32 devices in a mesh: au: 4 (over z), vert: 4 (over x, core), ch: 2 (over y).
Axes of the slice: x: 2, y: 2, z: 4, core: 2. Of those that a mesh axis runs over, the one named last changes fastest.
Arguments:
- visibilities: bfloat16 [512, 8, 512], P(('au', 'vert'), None, 'ch'), may hold values from -6 to 6
- tracks: bfloat16 [512, 2, 8], P(('au', 'vert')), may hold values from -10 to 10
- offset_u: int32 [512], P(('au', 'vert')), may hold values from 0 to 255
- offset_v: int32 [512], P(('au', 'vert')), may hold values from 0 to 255
- heading: int32 [512, 1], P(('au', 'vert')), may hold values from 0 to 4; in each aligned block of 32 rows (0 to 31, 32 to 63, ...) at most 8 rows name the same one
- baseline: int32 [512], P(('au', 'vert')), may hold values from 0 to 2015
- station_pair: int32 [2, 2016], replicated, may hold values from 0 to 63, as said below
- screens: bfloat16 [64, 4, 4096], P('ch'), may hold values from -4.1875 to 4.1875
Outputs:
- band_grid: float32 [2, 8, 1024, 1024], P('ch', None, 'au', 'vert')
The draws below stay inside these ranges and needn't reach their ends.
Inputs may be any that keep to these rules, and one draw needn't show every extreme that they name: Within the blocks of one tile (aligned runs of 32 rows) no heading occurs more than 8 times. `station_pair`: the two stations of a baseline differ.
All inputs are finite; a program needn't handle non-finite values.
Results may differ from the reference program's by a relative error of at most 0.0065.
Values may be sent and summed in bfloat16 or wider, within the bound.
A program may use at most 128 MiB of HBM per device.

```python
import math
import jax
import jax.numpy as jnp
import numpy as np
from jax import lax

S = 64
CH_DEV = 32
TB = 8
STATION_COUNT = 64
B_DEV = 32
TU = 256
TV = 256
K = 256
CHANNELS = 64
BASELINE_COUNT = 2016
BLOCK_COUNT = 512
NU = 1024
NV = 1024
N_AU = 4
N_VERT = 4
N_CH = 2


def draw_station_pair(key, part):
    key_leading, key_spacing = jax.random.split(jax.random.fold_in(key, 17))
    leading_station = jax.random.randint(key_leading, (BASELINE_COUNT,), 0, STATION_COUNT)
    station_spacing = jax.random.randint(key_spacing, (BASELINE_COUNT,), 1, STATION_COUNT)
    second_station = (leading_station + station_spacing) % STATION_COUNT
    return jnp.stack([leading_station, second_station]).astype(jnp.int32)


def place_ends(result, stream_key, least, largest):
    place = [jax.random.randint(jax.random.fold_in(stream_key, axis), (), 0, length) for axis, length in enumerate(result.shape)]
    main_axis = result.shape.index(max(result.shape))
    neighbour = place[:main_axis] + [(place[main_axis] + 1) % result.shape[main_axis]] + place[main_axis + 1:]
    return result.at[tuple(place)].set(least).at[tuple(neighbour)].set(largest)


def levels(stream_key, shape, shards, least, top_value):
    factor_of, own = 1.0, jax.random.fold_in(stream_key, 6)
    for dim, blocks in shards:
        steps = jnp.exp(jax.random.uniform(jax.random.fold_in(own, dim), (blocks,), jnp.float32, least / len(shards), top_value / len(shards)))
        factor_of = factor_of * jnp.repeat(steps, shape[dim] // blocks).reshape([-1 if axis == dim else 1 for axis in range(len(shape))])
    return factor_of


def deal_out(rng, own, number, rows, count, top, bound, skew):
    ranking = jax.random.permutation(rng, count)
    heavy_load, usual = portions_of(count, rows * top, bound, skew, True), portions_of(count, rows * top, bound, skew, False)
    places = jnp.arange(count)

    def named(sizes, turn):
        used = int((sizes > 0).sum())
        fixed = max(1, used // 4)
        passed = fixed + (places - fixed + turn * (used - fixed)) % max(1, count - fixed)
        return jnp.zeros((count,), jnp.int32).at[ranking[jnp.where(places < fixed, places, passed)]].set(jnp.asarray(sizes, jnp.int32))

    sizes = jnp.where(number % 4 == 0, named(heavy_load, number // 4), named(usual, number - number // 4 - 1))
    mixed = jax.random.permutation(jax.random.fold_in(own, 3), count)
    donor, receiver = mixed[0:count // 2 * 2:2], mixed[1:count // 2 * 2:2]
    room = jnp.minimum(sizes[donor] - 1, bound - sizes[receiver]) // 2
    room = jnp.where((donor == ranking[0]) | (receiver == ranking[0]) | (sizes[receiver] == 0), 0, jnp.maximum(room, 0))
    passed = jax.random.randint(jax.random.fold_in(own, 4), (count // 2,), 0, 1 << 20) % (room + 1)
    sizes = sizes.at[donor].add(-passed).at[receiver].add(passed)
    items = jnp.searchsorted(jnp.cumsum(sizes), jnp.arange(rows * top), side="right").astype(jnp.int32)
    listing = items.reshape(top, rows).T
    listing = listing[jax.random.permutation(jax.random.fold_in(own, 1), rows)]
    turn = jax.random.randint(jax.random.fold_in(own, 2), (rows, 1), 0, top)
    return jnp.take_along_axis(listing, (jnp.arange(top)[None, :] + turn) % top, axis=1)


def portions_of(count, total, reach, slope, full):
    loads = [(1 << 20) // math.isqrt(standing ** slope) + 1 for standing in range(1, count + 1)]
    largest = reach if full else min(reach, max(-(-total // count), total * loads[0] // sum(loads)))
    least = 1 if total - largest >= count - 1 else 0
    given, spare = [largest] + [least] * (count - 1), total - largest - least * (count - 1)
    while spare > 0:
        candidates = [i for i in range(1, count) if given[i] < largest] or [i for i in range(1, count) if given[i] < reach]
        pool, remaining = sum([loads[i] for i in candidates]), spare
        for i in candidates:
            addition = min(reach - given[i], max(1, remaining * loads[i] // pool), spare)
            given[i] = given[i] + addition
            spare = spare - addition
    return np.array(given)


def bell_draw(stream_key, dims, spread, most, cuts=(), kind=jnp.bfloat16):
    gain = levels(stream_key, dims, cuts, -0.22, 0.18) if cuts else 1.0
    entries = jax.random.normal(stream_key, dims, jnp.float32) * spread * gain
    return jnp.minimum(jnp.maximum(entries, -most), most).astype(kind)


def setup_inputs(seed: int = 0) -> dict:
    splits = jax.random.split(jax.random.key(seed), 9)
    visibilities = bell_draw(splits[0], (BLOCK_COUNT, 8, N_CH * K), 1.0, 6.0, ((0, 16), (2, 2)))
    tracks = jnp.clip(jax.random.uniform(splits[1], (BLOCK_COUNT, 2, TB), jnp.float32, -10.0, 10.0) * levels(splits[1], (BLOCK_COUNT, 2, TB), ((0, 16),), -0.4, 0.0), -10.0, 10.0).astype(jnp.bfloat16)
    offset_u = place_ends(jax.random.randint(splits[2], (BLOCK_COUNT,), 0, TU), jax.random.fold_in(splits[2], 1), 0, TU - 1).astype(jnp.int32)
    offset_v = place_ends(jax.random.randint(splits[3], (BLOCK_COUNT,), 0, TV), jax.random.fold_in(splits[3], 1), 0, TV - 1).astype(jnp.int32)
    heading_keys = jax.random.split(jax.random.fold_in(splits[4], 1), BLOCK_COUNT // B_DEV)
    heading_turns = jax.random.permutation(jax.random.fold_in(splits[4], 3), BLOCK_COUNT // B_DEV)
    heading = jax.vmap(lambda own, number: deal_out(jax.random.fold_in(splits[4], 2), own, number, B_DEV, 5, 1, B_DEV // 4, 2))(heading_keys, heading_turns).reshape((BLOCK_COUNT, 1))
    baseline = place_ends(jax.random.randint(splits[5], (BLOCK_COUNT,), 0, BASELINE_COUNT), jax.random.fold_in(splits[5], 1), 0, BASELINE_COUNT - 1).astype(jnp.int32)
    station_pair = draw_station_pair(jax.random.fold_in(splits[8], 71), 0)
    screens = bell_draw(splits[7], (STATION_COUNT, 4, S * S), 0.7, 4.1875, ((0, 2),))
    return {"visibilities": visibilities, "tracks": tracks, "offset_u": offset_u, "offset_v": offset_v, "heading": heading, "baseline": baseline, "station_pair": station_pair, "screens": screens}


def product_full(pattern, first_op, second_op):
    return jnp.einsum(pattern, first_op.astype(jnp.float32), second_op.astype(jnp.float32))

def phase_tables(track_rows, band_index, channels):
    channel = band_index * CH_DEV + jnp.arange(CH_DEV, dtype=jnp.int32)
    freq_ratio = 1.0 + channel.astype(jnp.float32) / jnp.float32(2 * channels)
    position = track_rows.astype(jnp.float32)[:, :, :, None] * freq_ratio[None, None, None, :]
    position = position.reshape(track_rows.shape[0], 2, TB * CH_DEV)
    pixels = (jnp.arange(S, dtype=jnp.float32) - jnp.float32(S // 2)) / jnp.float32(S)
    angles = jnp.float32(2.0 * math.pi) * position[:, :, :, None] * pixels[None, None, None, :]
    return (jnp.cos(angles).astype(jnp.bfloat16), jnp.sin(angles).astype(jnp.bfloat16))

def dft_table():
    centred = jnp.arange(S, dtype=jnp.int32) - S // 2
    product = centred[:, None] * centred[None, :] % S
    angles = jnp.float32(2.0 * math.pi / S) * product.astype(jnp.float32)
    root_scale = jnp.float32(1.0 / math.sqrt(S))
    return ((jnp.cos(angles) * root_scale).astype(jnp.bfloat16), (-jnp.sin(angles) * root_scale).astype(jnp.bfloat16))

def make_subgrids(samples, track_rows, leading_station, second_station, screens, band_index, channels):
    number = samples.shape[0]
    cos_table, sin_table = phase_tables(track_rows, band_index, channels)
    cos_u = cos_table[:, 0].astype(jnp.float32)[:, None]
    sin_u = sin_table[:, 0].astype(jnp.float32)[:, None]
    cos_v = cos_table[:, 1]
    sin_v = sin_table[:, 1]
    vis_re = samples[:, 0::2].astype(jnp.float32)[..., None]
    vis_im = samples[:, 1::2].astype(jnp.float32)[..., None]
    weigh_re = (vis_re * cos_u - vis_im * sin_u).astype(jnp.bfloat16)
    weigh_im = (vis_re * sin_u + vis_im * cos_u).astype(jnp.bfloat16)
    norm_scale = jnp.float32(1.0 / math.sqrt(TB * CH_DEV))
    pattern = 'npkl,nkm->nplm'
    image_re = (product_full(pattern, weigh_re, cos_v) - product_full(pattern, weigh_im, sin_v)) * norm_scale
    image_im = (product_full(pattern, weigh_re, sin_v) + product_full(pattern, weigh_im, cos_v)) * norm_scale
    screen_one = jnp.take(screens, leading_station, axis=0).astype(jnp.float32).reshape(number, 2, 2, S, S)
    screen_two = jnp.take(screens, second_station, axis=0).astype(jnp.float32).reshape(number, 2, 2, S, S)
    one_re = screen_one[:, :, 0][:, :, None]
    one_im = screen_one[:, :, 1][:, :, None]
    two_re = screen_two[:, :, 0][:, None, :]
    two_im = screen_two[:, :, 1][:, None, :]
    gain_re = (one_re * two_re + one_im * two_im).reshape(number, 4, S, S)
    gain_im = (one_im * two_re - one_re * two_im).reshape(number, 4, S, S)
    fixed_re = (image_re * gain_re - image_im * gain_im).astype(jnp.bfloat16)
    fixed_im = (image_re * gain_im + image_im * gain_re).astype(jnp.bfloat16)
    dft_re, dft_im = dft_table()
    left = 'kl,nplm->npkm'
    half_re = (product_full(left, dft_re, fixed_re) - product_full(left, dft_im, fixed_im)).astype(jnp.bfloat16)
    half_im = (product_full(left, dft_re, fixed_im) + product_full(left, dft_im, fixed_re)).astype(jnp.bfloat16)
    right = 'npkm,jm->npkj'
    out_re = product_full(right, half_re, dft_re) - product_full(right, half_im, dft_im)
    out_im = product_full(right, half_re, dft_im) + product_full(right, half_im, dft_re)
    return jnp.stack([out_re, out_im], axis=2).reshape(number, 8, S, S)

def reference(visibilities, tracks, offset_u, offset_v, heading, baseline, station_pair, screens):
    step_u = jnp.array([0, 1, -1, 0, 0], dtype=jnp.int32)
    step_v = jnp.array([0, 0, 0, 1, -1], dtype=jnp.int32)
    first_all = station_pair[0][baseline].astype(jnp.int32)
    second_all = station_pair[1][baseline].astype(jnp.int32)
    head_codes = heading[:, 0].astype(jnp.int32)
    band_grids = []
    for band_index in range(N_CH):
        band_vis = visibilities[:, :, band_index * K:(band_index + 1) * K]

        def one_source(source, padded):
            source = source.astype(jnp.int32)
            first_row = source * B_DEV

            def own_rows(array):
                return lax.dynamic_slice_in_dim(array, first_row, B_DEV, 0)
            subgrids = make_subgrids(own_rows(band_vis), own_rows(tracks), own_rows(first_all), own_rows(second_all), screens, band_index, CHANNELS)
            home_u = source // N_VERT
            home_v = source % N_VERT
            head_rows = own_rows(head_codes)
            dest_u = (home_u + step_u[head_rows]) % N_AU
            dest_v = (home_v + step_v[head_rows]) % N_VERT
            cell_u = (dest_u * TU + own_rows(offset_u)).astype(jnp.int32)
            cell_v = (dest_v * TV + own_rows(offset_v)).astype(jnp.int32)

            def add_one(slot_index, canvas):
                corner = (jnp.int32(0), cell_u[slot_index].astype(jnp.int32), cell_v[slot_index].astype(jnp.int32))
                window = lax.dynamic_slice(canvas, corner, (8, S, S))
                return lax.dynamic_update_slice(canvas, window + subgrids[slot_index], corner)
            return lax.fori_loop(0, B_DEV, add_one, padded)
        padded = lax.fori_loop(0, N_AU * N_VERT, one_source, jnp.zeros((8, NU + S, NV + S), jnp.float32))
        folded = padded[:, :NU, :]
        folded = folded.at[:, :S, :].add(padded[:, NU:, :])
        band_grid = folded[:, :, :NV]
        band_grid = band_grid.at[:, :, :S].add(folded[:, :, NV:])
        band_grids.append(band_grid)
    return jnp.stack(band_grids)
```

```python
import math

import jax
import jax.numpy as jnp
import ml_dtypes
import numpy as np
from jax import lax
from jax.experimental import pallas as pl
from jax.experimental.pallas import tpu as pltpu
from jax.sharding import PartitionSpec as P

S = 64
CH_DEV = 32
TB = 8
K = TB * CH_DEV
B_DEV = 32
CAP = B_DEV // 4
SLOTS = 5 * CAP
TU = 256
TV = 256
ROWS = 72
FIRST_PAIRS = 10
PARTS = 2
Y_PAIRS = (4, 10)
X_PAIRS = (11, 17)
MESH = pl.DeviceIdType.MESH
BF = jnp.bfloat16
F32 = jnp.float32


def series(values, degree):
    nodes = (np.cos(np.pi * (np.arange(400) + 0.5) / 400) + 1.0) * 0.125
    fitted = np.polynomial.chebyshev.Chebyshev.fit(nodes, values(nodes), degree, domain=[0, 0.25])
    return [float(c) for c in fitted.convert(kind=np.polynomial.Polynomial).coef]


COS_COEF = series(lambda q: np.cos(2 * np.pi * np.sqrt(q)), 7)
SIN_COEF = series(lambda q: np.sin(2 * np.pi * np.sqrt(q)) / np.sqrt(q), 6)


def horner(coefs, q):
    total = jnp.full_like(q, coefs[-1])
    for c in coefs[-2::-1]:
        total = total * q + jnp.float32(c)
    return total


def dft_tables():
    centred = np.arange(S) - S // 2
    product = (centred[:, None] * centred[None, :]) % S
    angles = np.float32(2.0 * math.pi / S) * product.astype(np.float32)
    scale = np.float32(1.0 / math.sqrt(S))
    re = (np.cos(angles) * scale).astype(ml_dtypes.bfloat16).astype(np.float32)
    im = (-np.sin(angles) * scale).astype(ml_dtypes.bfloat16).astype(np.float32)
    return re, im


def right_table():
    re, im = dft_tables()
    norm = np.float32(1.0 / math.sqrt(K))
    table = np.zeros((2 * S, 256), np.float32)
    table[:S, :S] = re.T * norm
    table[S:, :S] = im.T * norm
    return table


def left_table():
    re, im = dft_tables()
    order = np.concatenate([np.arange(0, S, 2), np.arange(1, S, 2)])
    re, im = re[:, order], im[:, order]
    table = np.zeros((8, 2, ROWS, 2 * S), np.float32)
    for shift in range(8):
        table[shift, 0, shift : shift + S, :S] = re
        table[shift, 0, shift : shift + S, S:] = -im
        table[shift, 1, shift : shift + S, :S] = im
        table[shift, 1, shift : shift + S, S:] = re
    return table.reshape(8, 2 * ROWS, 2 * S).astype(ml_dtypes.bfloat16)


def swap_halves(x):
    return pltpu.roll(x, S, x.ndim - 1)


def arrange_station(raw, tall):
    value = raw.astype(F32)
    for i in range(S // 2):
        tall[8 * i : 8 * i + 4, :] = value[:, 128 * i : 128 * (i + 1)]
    lane = lax.broadcasted_iota(jnp.int32, (S // 2, 128), 1)
    feeds = []
    for f in range(2):
        re = tall[pl.ds(2 * f, S // 2, stride=8), :]
        im = tall[pl.ds(2 * f + 1, S // 2, stride=8), :]
        even = jnp.where(lane < S, re, swap_halves(im))
        odd = jnp.where(lane < S, swap_halves(re), im)
        feeds.append(jnp.concatenate([even, odd], axis=0).astype(BF))
    return feeds


def pack_blocks(head, off_u, off_v, base, pairs, track, data):
    heads = head[...]
    kind = lax.broadcasted_iota(jnp.int32, (8, B_DEV), 0)
    named = jnp.where(kind == heads, 1.0, 0.0)
    before = lax.broadcasted_iota(jnp.int32, (B_DEV, B_DEV), 0)
    after = lax.broadcasted_iota(jnp.int32, (B_DEV, B_DEV), 1)
    strict = jnp.where(before < after, 1.0, 0.0).astype(BF)
    counts = jnp.dot(named.astype(BF), strict, preferred_element_type=F32)
    rank = jnp.sum(named * counts, axis=0, keepdims=True)
    slot = heads.astype(F32) * CAP + rank
    which = lax.broadcasted_iota(jnp.int32, (SLOTS, B_DEV), 0).astype(F32)
    chosen = jnp.where(which == slot, 1.0, 0.0).astype(BF)

    label = lax.broadcasted_iota(jnp.int32, (pairs.shape[1], B_DEV), 0)
    listed = jnp.where(label == base[...], 1.0, 0.0).astype(BF)
    station = jnp.dot(pairs[...].astype(F32).astype(BF), listed, preferred_element_type=F32)
    rows = jnp.concatenate(
        [
            jnp.ones((1, B_DEV), F32),
            off_u[...].astype(F32),
            off_v[...].astype(F32),
            station,
            jnp.zeros((3, B_DEV), F32),
            track[...].astype(F32),
            jnp.zeros((128 - 8 - 2 * TB, B_DEV), F32),
        ],
        axis=0,
    ).astype(BF)
    dims = (((1,), (1,)), ((), ()))
    labels = lax.dot_general(chosen, rows, dims, preferred_element_type=F32)

    owner = lax.broadcasted_iota(jnp.int32, (B_DEV, 8 * B_DEV), 0)
    column = lax.broadcasted_iota(jnp.int32, (B_DEV, 8 * B_DEV), 1)
    widen = jnp.where(owner == column // 8, 1.0, 0.0).astype(BF)
    wide = jnp.dot(
        jnp.broadcast_to(slot, (8, B_DEV)).astype(BF), widen, preferred_element_type=F32
    )[:1]
    lane = lax.broadcasted_iota(jnp.int32, (1, 8 * B_DEV), 1) % 8
    place = wide * 8.0 + lane.astype(F32)
    target = lax.broadcasted_iota(jnp.int32, (8 * SLOTS, 8 * B_DEV), 0).astype(F32)
    moved = jnp.where(target == place, 1.0, 0.0).astype(BF)
    return jnp.dot(moved, data[...], preferred_element_type=F32).astype(BF), labels


def list_blocks(labels):
    dims = (((1,), (1,)), ((), ()))
    quantity = lax.broadcasted_iota(jnp.int32, (8, 128), 0)
    lane = lax.broadcasted_iota(jnp.int32, (8, 128), 1)
    pick = jnp.where(quantity == lane, 1.0, 0.0).astype(BF)
    rows = lax.dot_general(pick, labels.astype(BF), dims, preferred_element_type=F32)
    filled, at_u, at_v = rows[0:1], rows[1:2], rows[2:3]
    past = jnp.logical_or(at_u > TU - S, at_v > TV - S)
    early = jnp.where(past, filled, 0.0)
    late = filled - early
    kind = lax.broadcasted_iota(jnp.int32, (8, SLOTS), 0)
    both = jnp.where(kind == 0, early, jnp.where(kind == 1, late, 0.0))
    before = lax.broadcasted_iota(jnp.int32, (SLOTS, SLOTS), 0)
    after = lax.broadcasted_iota(jnp.int32, (SLOTS, SLOTS), 1)
    strict = jnp.where(before < after, 1.0, 0.0).astype(BF)
    ahead = jnp.dot(both.astype(BF), strict, preferred_element_type=F32)
    number_early = jnp.sum(early, axis=1, keepdims=True)
    number = jnp.sum(filled, axis=1, keepdims=True)
    place = jnp.where(past, ahead[0:1], number_early + ahead[1:2])
    place = jnp.where(filled > 0.5, place, -1.0)
    target = lax.broadcasted_iota(jnp.int32, (128, SLOTS), 0).astype(F32)
    moved = jnp.where(target == place, 1.0, 0.0).astype(BF)
    slot = lax.broadcasted_iota(jnp.int32, (8, SLOTS), 1).astype(F32)
    rows = jnp.where(kind == 0, slot, rows)
    table = lax.dot_general(rows.astype(BF), moved, dims, preferred_element_type=F32)
    spare = jnp.where(lane.astype(F32) >= number, float(TU + S), 0.0)
    table = table + jnp.where(quantity == 1, spare, 0.0)
    pairs_early = jnp.floor((number_early + 1.0) * 0.5)
    pairs = jnp.floor((number + 1.0) * 0.5)
    pairs_early = jnp.maximum(pairs_early, jnp.minimum(pairs, float(FIRST_PAIRS)))
    table = jnp.where(quantity == 5, pairs_early, jnp.where(quantity == 6, pairs, table))
    return table.astype(jnp.int32)


def image_kernel(
    head, off_u, off_v, base, pairs, track, data, own_screens,
    images, screens, listing, canvas,
    packed, labels, got_data, got_labels, samples, spread, mult, raw, tall,
    own_sems, send_sems, recv_sems, y_send, y_recv, x_send, x_recv, c_send, c_recv,
):
    au, vert, band = (lax.axis_index(axis) for axis in ("au", "vert", "ch"))
    n_au, n_vert, n_ch = (lax.axis_size(axis) for axis in ("au", "vert", "ch"))
    here = own_screens.shape[0]
    piece = here // n_vert
    part = piece // PARTS
    n_x = n_vert // 2

    def turned(step):
        return lax.rem(vert + step, n_vert)

    near = (
        {"au": lax.rem(au + 1, n_au)},
        {"au": lax.rem(au + n_au - 1, n_au)},
        {"vert": turned(1)},
        {"vert": turned(n_vert - 1)},
    )
    across = {"ch": lax.rem(band + 1, n_ch)}
    sibling = {"vert": vert + 1 - 2 * lax.rem(vert, 2)}
    beside = [{"vert": turned(2 * j)} for j in range(1, n_x)]

    fetches = []
    for j in range(n_vert):
        rows = pl.ds(turned(j) * piece, piece)
        fetches.append(
            pltpu.make_async_copy(own_screens.at[rows], raw.at[rows], own_sems.at[j])
        )
        fetches[-1].start()
    barrier = pltpu.get_barrier_semaphore()
    for device in (*near, across, *beside):
        pl.semaphore_signal(barrier, inc=1, device_id=device, device_id_type=MESH)

    values, rows = pack_blocks(head, off_u, off_v, base, pairs, track, data)
    packed[...] = values
    labels[...] = rows

    def arrange(first, number):
        def one(pair, carry):
            for i in range(2):
                station = lax.rem(first + 2 * pair + i, here)
                feeds = arrange_station(raw[station], tall.at[i])
                for f in range(2):
                    screens[station, f] = feeds[f]
            return carry

        lax.fori_loop(0, number // 2, one, 0)

    fetches[0].wait()
    arrange(vert * piece, piece)
    pl.semaphore_wait(barrier, 5 + len(beside))

    def moves(i):
        pairs_of = ((packed, got_data, 8 * CAP), (labels, got_labels, CAP))
        for j, (source, target, rows) in enumerate(pairs_of):
            where = pl.ds((i + 1) * rows, rows)
            yield pltpu.make_async_remote_copy(
                src_ref=source.at[where],
                dst_ref=target.at[where],
                send_sem=send_sems.at[i, j],
                recv_sem=recv_sems.at[i, j],
                device_id=near[i],
                device_id_type=MESH,
            )

    def to_other(source, owner, k, send, recv, device):
        return pltpu.make_async_remote_copy(
            src_ref=screens.at[pl.ds(source * piece + k * part, part)],
            dst_ref=screens.at[pl.ds(here + owner * piece + k * part, part)],
            send_sem=send,
            recv_sem=recv,
            device_id=device,
            device_id_type=MESH,
        )

    def y_copy(k):
        return to_other(vert, vert, k, y_send.at[k], y_recv.at[k], across)

    def x_copy(j, k, owner):
        return to_other(
            n_vert + owner, owner, k, x_send.at[j - 1, k], x_recv.at[j - 1, k], beside[j - 1]
        )

    def c_copy(j, k, owner):
        return to_other(
            n_vert + owner, owner, k, c_send.at[j, k], c_recv.at[j, k], sibling
        )

    for i in range(4):
        for copy in moves(i):
            copy.start()
    for k in range(PARTS):
        y_copy(k).start()

    canvas[...] = jnp.zeros_like(canvas)
    for copy in fetches[1:]:
        copy.wait()
    arrange((vert + 1) * piece, here - piece)

    row = lax.broadcasted_iota(jnp.int32, (32, K), 0)
    channel = band * CH_DEV + lax.broadcasted_iota(jnp.int32, (32, K), 1) % CH_DEV
    ratio = 1.0 + channel.astype(F32) / jnp.float32(2 * CH_DEV * n_ch)
    coarse = row - 8
    coarse_u = 16 * (coarse % 4) + coarse // 4 - S // 2
    fine_v = row - 16
    coarse_v = (row - 24) * 8 - S // 2
    step = jnp.where(
        row < 16, jnp.where(row < 8, 2 * row, coarse_u), jnp.where(row < 24, fine_v, coarse_v)
    )
    mult[...] = step.astype(F32) / S * ratio

    def widen(rows):
        source = lax.broadcasted_iota(jnp.int32, (128, 2 * K), 0)
        column = lax.broadcasted_iota(jnp.int32, (128, 2 * K), 1)
        chosen = jnp.where(source == 8 + column // CH_DEV, 1.0, 0.0).astype(BF)
        lane = lax.broadcasted_iota(jnp.int32, rows.shape, 1)
        only = jnp.where(lane < 8, 0.0, rows).astype(BF)
        return jnp.dot(only, chosen, preferred_element_type=F32)

    got_labels[:CAP] = labels[:CAP]
    samples[: 8 * CAP] = packed[: 8 * CAP].astype(F32)
    spread[:CAP] = widen(labels[:CAP])

    def block(slot):
        sample = samples[pl.ds(8 * slot, 8), :]
        track = spread[pl.ds(slot, 1), :]
        turns = jnp.concatenate(
            [track[:, :K] * mult[:16], track[:, K:] * mult[16:]], axis=0
        )
        frac = turns - jnp.floor(turns + 0.5)
        square = frac * frac
        cos = horner(COS_COEF, square)
        sin = horner(SIN_COEF, square) * frac

        def phasors(first):
            cos_fine, sin_fine = cos[first : first + 8], sin[first : first + 8]
            all_cos, all_sin = [], []
            for a in range(8):
                at = first + 8 + a
                cos_a, sin_a = cos[at : at + 1], sin[at : at + 1]
                all_cos.append(cos_fine * cos_a - sin_fine * sin_a)
                all_sin.append(sin_fine * cos_a + cos_fine * sin_a)
            return (
                jnp.concatenate(all_cos, axis=0).astype(BF),
                jnp.concatenate(all_sin, axis=0).astype(BF),
            )

        cos_u, sin_u = phasors(0)
        cos_u, sin_u = cos_u.astype(F32), sin_u.astype(F32)
        cos_v, sin_v = phasors(16)
        table_re = jnp.concatenate([cos_v, sin_v], axis=0)
        table_im = jnp.concatenate([-sin_v, cos_v], axis=0)
        weigh_re, weigh_im = [], []
        for p in range(4):
            re, im = sample[2 * p : 2 * p + 1], sample[2 * p + 1 : 2 * p + 2]
            weigh_re.append((re * cos_u - im * sin_u).astype(BF))
            weigh_im.append((re * sin_u + im * cos_u).astype(BF))
        dims = (((1,), (1,)), ((), ()))
        image = lax.dot_general(
            jnp.concatenate(weigh_re, axis=0), table_re, dims, preferred_element_type=F32
        ) + lax.dot_general(
            jnp.concatenate(weigh_im, axis=0), table_im, dims, preferred_element_type=F32
        )
        return image.astype(BF)

    def forward_y(k):
        y_copy(k).wait_recv()
        for j in range(1, n_x):
            x_copy(j, k, vert).start()
        c_copy(0, k, vert).start()

    def forward_x(k):
        for j in range(1, n_x):
            owner = turned(n_vert - 2 * j)
            x_copy(j, k, owner).wait_recv()
            c_copy(j, k, owner).start()

    def loop(pair, carry):
        @pl.when(pair == CAP // 2)
        def _():
            for i in range(4):
                for copy in moves(i):
                    copy.wait_recv()
            samples[8 * CAP :] = got_data[8 * CAP :].astype(F32)
            spread[CAP:] = widen(got_labels[CAP:])

        for k in range(PARTS):

            @pl.when(pair == Y_PAIRS[k])
            def _():
                forward_y(k)

            @pl.when(pair == X_PAIRS[k])
            def _():
                forward_x(k)

        first, second = block(2 * pair), block(2 * pair + 1)
        images[2 * pair] = first
        images[2 * pair + 1] = second
        return carry

    lax.fori_loop(0, SLOTS // 2, loop, 0)
    listing[...] = list_blocks(got_labels[...])
    for i in range(4):
        for copy in moves(i):
            copy.wait_send()
    for k in range(PARTS):
        y_copy(k).wait_send()
        for j in range(1, n_x):
            x_copy(j, k, vert).wait_send()
        for j in range(n_x):
            c_copy(j, k, turned(n_vert - 2 * j)).wait_send()
            mine = turned(n_vert - 2 * j)
            theirs = mine + 1 - 2 * lax.rem(mine, 2)
            c_copy(j, k, theirs).wait_recv()


def folded(x):
    middle = x.shape[1] // 2
    lane = lax.broadcasted_iota(jnp.int32, (1, 1, 128), 2)
    return jnp.where(lane < S, x[:, :middle], swap_halves(x[:, middle:])).astype(BF)


def early_kernel(
    listing, images, screens, right, left, canvas_in, canvas, edge_u, edge_v, corner
):
    grid_blocks(images, screens, canvas, right, left, listing, 0, listing[5, 0])
    edge_u[...] = canvas[:, TU : TU + S, :TV].astype(BF)
    edge_v[...] = folded(canvas[:, :TU, TV:])
    corner[...] = folded(canvas[:, TU : TU + S, TV:])


def late_kernel(listing, images, screens, right, left, canvas_in, canvas):
    grid_blocks(images, screens, canvas, right, left, listing, listing[5, 0], listing[6, 0])


def grid_blocks(images, screens, canvas, right, left, listing, first, last):
    here = screens.shape[0] // 2
    band = lax.axis_index("ch")

    def screen_place(station):
        owner = station // here
        local = station - owner * here
        return jnp.where(owner == band, local, here + local)

    def block(index):
        slot = listing[0, index]
        off_u = listing[1, index]
        off_v = listing[2, index]
        one = screen_place(listing[3, index])
        two = screen_place(listing[4, index])
        two_s = [screens[two, f].astype(F32) for f in range(2)]
        fixed = []
        for f in range(2):
            one_s = screens[one, f].astype(F32)
            one_swapped = swap_halves(one_s)
            for e in range(2):
                p = 2 * f + e
                same = one_s * two_s[e]
                cross = one_swapped * two_s[e]
                gain_re = same + swap_halves(same)
                gain_im = swap_halves(cross) - cross
                part = images[slot, p * S : (p + 1) * S].astype(F32)
                fixed.append((part * gain_re + swap_halves(part) * gain_im).astype(BF))
        lanes = off_v // 128
        moved = pltpu.roll(right[...], off_v - lanes * 128, 1).astype(BF)
        table_re, table_im = moved[:S], moved[S:]
        shifted = jnp.concatenate(
            [
                jnp.concatenate([table_re, -table_im], axis=0),
                jnp.concatenate([table_im, table_re], axis=0),
            ],
            axis=1,
        )
        half = jnp.dot(
            jnp.concatenate(fixed, axis=0), shifted, preferred_element_type=F32
        ).astype(BF)
        eighth = off_u // 8
        placed = left[off_u - eighth * 8]
        start_u = pl.multiple_of(eighth * 8, 8)
        start_v = pl.multiple_of(lanes * 128, 128)
        return start_u, start_v, placed, half

    def loop(pair, carry):
        ready = [block(2 * pair), block(2 * pair + 1)]
        for start_u, start_v, placed, half in ready:
            for p in range(4):
                part = half[p * S : (p + 1) * S]
                both = jnp.concatenate([part[:, :256], part[:, 256:]], axis=0)
                grid = jnp.dot(placed, both, preferred_element_type=F32)
                for r in range(2):
                    where = (2 * p + r, pl.ds(start_u, ROWS), pl.ds(start_v, 256))
                    canvas[where] += grid[r * ROWS : (r + 1) * ROWS]
        return carry

    lax.fori_loop(first, last, loop, 0)


def finish_kernel(canvas, got_u, got_v, got_c, out, top, side, sems):
    rest = pltpu.make_async_copy(
        canvas.at[:, S:TU, 128:TV], out.at[:, S:, 128:], sems.at[2]
    )
    rest.start()
    lane = lax.broadcasted_iota(jnp.int32, (1, 1, 128), 2)

    def unfolded(x):
        x = x.astype(F32)
        low = jnp.where(lane < S, x, 0.0)
        high = jnp.where(lane < S, swap_halves(x), 0.0)
        return low, high

    low, high = unfolded(got_v[...])
    first, second = unfolded(got_c[...])
    side[:, : TU // 2 - S] = canvas[:, S : TU // 2, :128] + low[:, S:]
    side[:, TU // 2 - S :] = canvas[:, TU // 2 : TU, :128] + high
    store_side = pltpu.make_async_copy(side, out.at[:, S:, :128], sems.at[1])
    store_side.start()
    top[...] = canvas[:, :S, :TV] + got_u[...].astype(F32)
    top[:, :, :128] += low[:, :S] + jnp.concatenate([first, second], axis=1)
    store_top = pltpu.make_async_copy(top, out.at[:, :S, :], sems.at[0])
    store_top.start()
    rest.wait()
    store_side.wait()
    store_top.wait()


def body(visibilities, tracks, offset_u, offset_v, heading, baseline, station_pair, screens):
    smem = pl.BlockSpec(memory_space=pltpu.SMEM)
    vmem = pl.BlockSpec(memory_space=pltpu.VMEM)
    anywhere = pl.BlockSpec(memory_space=pl.ANY)
    n_au, n_vert = (lax.axis_size(axis) for axis in ("au", "vert"))
    n_x = n_vert // 2
    here = screens.shape[0]
    canvas_shape = jax.ShapeDtypeStruct((8, TU + S + ROWS, TV + 128), F32)
    dma = pltpu.SemaphoreType.DMA
    images, all_screens, listing, canvas = pl.pallas_call(
        image_kernel,
        out_shape=(
            jax.ShapeDtypeStruct((SLOTS, 4 * S, 2 * S), BF),
            jax.ShapeDtypeStruct((2 * here, 2, S, 2 * S), BF),
            jax.ShapeDtypeStruct((8, 128), jnp.int32),
            canvas_shape,
        ),
        in_specs=[vmem] * 7 + [anywhere],
        out_specs=(vmem,) * 4,
        scratch_shapes=[
            pltpu.VMEM((8 * SLOTS, K), BF),
            pltpu.VMEM((SLOTS, 128), F32),
            pltpu.VMEM((8 * SLOTS, K), BF),
            pltpu.VMEM((SLOTS, 128), F32),
            pltpu.VMEM((8 * SLOTS, K), F32),
            pltpu.VMEM((SLOTS, 2 * K), F32),
            pltpu.VMEM((32, K), F32),
            pltpu.VMEM((here, 4, S * S), BF),
            pltpu.VMEM((2, 4 * S, 128), F32),
            dma((n_vert,)),
            dma((4, 2)),
            dma((4, 2)),
            dma((PARTS,)),
            dma((PARTS,)),
            dma((n_x - 1, PARTS)),
            dma((n_x - 1, PARTS)),
            dma((n_x, PARTS)),
            dma((n_x, PARTS)),
        ],
        compiler_params=pltpu.CompilerParams(
            collective_id=0, has_side_effects=True, vmem_limit_bytes=20 << 20
        ),
    )(
        heading.reshape(1, B_DEV), offset_u[None], offset_v[None], baseline[None],
        station_pair, tracks.transpose(1, 2, 0).reshape(2 * TB, B_DEV),
        visibilities.reshape(8 * B_DEV, K), screens,
    )
    right, left = jnp.asarray(right_table()), jnp.asarray(left_table())
    canvas, edge_u, edge_v, corner = pl.pallas_call(
        early_kernel,
        out_shape=(
            canvas_shape,
            jax.ShapeDtypeStruct((8, S, TV), BF),
            jax.ShapeDtypeStruct((8, TU // 2, 128), BF),
            jax.ShapeDtypeStruct((8, S // 2, 128), BF),
        ),
        in_specs=[smem] + [vmem] * 5,
        out_specs=(vmem,) * 4,
        input_output_aliases={5: 0},
        compiler_params=pltpu.CompilerParams(vmem_limit_bytes=12 << 20),
    )(listing, images, all_screens, right, left, canvas)
    got_u = lax.ppermute(edge_u, "au", [(i, (i + 1) % n_au) for i in range(n_au)])
    got_v = lax.ppermute(edge_v, "vert", [(i, (i + 1) % n_vert) for i in range(n_vert)])
    diagonal = [
        (u * n_vert + v, (u + 1) % n_au * n_vert + (v + 1) % n_vert)
        for u in range(n_au)
        for v in range(n_vert)
    ]
    got_c = lax.ppermute(corner, ("au", "vert"), diagonal)
    canvas = pl.pallas_call(
        late_kernel,
        out_shape=canvas_shape,
        in_specs=[smem] + [vmem] * 5,
        out_specs=vmem,
        input_output_aliases={5: 0},
        compiler_params=pltpu.CompilerParams(vmem_limit_bytes=12 << 20),
        cost_estimate=pl.CostEstimate(
            flops=SLOTS * 2 * 256 * 512 * 128 * 8, bytes_accessed=8 << 20, transcendentals=0
        ),
    )(listing, images, all_screens, right, left, canvas)
    out = pl.pallas_call(
        finish_kernel,
        out_shape=jax.ShapeDtypeStruct((8, TU, TV), F32),
        in_specs=[vmem] * 4,
        out_specs=anywhere,
        scratch_shapes=[
            pltpu.VMEM((8, S, TV), F32),
            pltpu.VMEM((8, TU - S, 128), F32),
            dma((3,)),
        ],
        compiler_params=pltpu.CompilerParams(vmem_limit_bytes=8 << 20),
    )(canvas, got_u, got_v, got_c)
    return out[None]


def solution(mesh):
    placed = (
        P(("au", "vert"), None, "ch"),
        P(("au", "vert"), None, None),
        P(("au", "vert")),
        P(("au", "vert")),
        P(("au", "vert"), None),
        P(("au", "vert")),
        P(),
        P("ch", None, None),
    )
    return jax.shard_map(
        body, mesh=mesh, in_specs=placed, out_specs=P("ch", None, "au", "vert"), check_vma=False
    )
```

```python
import math

import jax
import jax.numpy as jnp
import ml_dtypes
import numpy as np
from jax import lax
from jax.experimental import pallas as pl
from jax.experimental.pallas import tpu as pltpu
from jax.sharding import PartitionSpec as P

S = 64
CH_DEV = 32
TB = 8
K = TB * CH_DEV
B_DEV = 32
CAP = B_DEV // 4
SLOTS = 5 * CAP
TU = 256
TV = 256
ROWS = 72
U_PAIRS = 5
V_PAIRS = 10
PARTS = 2
V_SPLIT = 2
Y_PAIRS = (4, 10)
X_PAIRS = (11, 17)
MESH = pl.DeviceIdType.MESH
BF = jnp.bfloat16
F32 = jnp.float32


def series(values, degree):
    nodes = (np.cos(np.pi * (np.arange(400) + 0.5) / 400) + 1.0) * 0.125
    fitted = np.polynomial.chebyshev.Chebyshev.fit(nodes, values(nodes), degree, domain=[0, 0.25])
    return [float(c) for c in fitted.convert(kind=np.polynomial.Polynomial).coef]


COS_COEF = series(lambda q: np.cos(2 * np.pi * np.sqrt(q)), 7)
SIN_COEF = series(lambda q: np.sin(2 * np.pi * np.sqrt(q)) / np.sqrt(q), 6)


def horner(coefs, q):
    total = jnp.full_like(q, coefs[-1])
    for c in coefs[-2::-1]:
        total = total * q + jnp.float32(c)
    return total


def dft_tables():
    centred = np.arange(S) - S // 2
    product = (centred[:, None] * centred[None, :]) % S
    angles = np.float32(2.0 * math.pi / S) * product.astype(np.float32)
    scale = np.float32(1.0 / math.sqrt(S))
    re = (np.cos(angles) * scale).astype(ml_dtypes.bfloat16).astype(np.float32)
    im = (-np.sin(angles) * scale).astype(ml_dtypes.bfloat16).astype(np.float32)
    return re, im


def right_table():
    re, im = dft_tables()
    norm = np.float32(1.0 / math.sqrt(K))
    table = np.zeros((2 * S, 256), np.float32)
    table[:S, :S] = re.T * norm
    table[S:, :S] = im.T * norm
    return table


def left_table():
    re, im = dft_tables()
    order = np.concatenate([np.arange(0, S, 2), np.arange(1, S, 2)])
    re, im = re[:, order], im[:, order]
    table = np.zeros((8, 2, ROWS, 2 * S), np.float32)
    for shift in range(8):
        table[shift, 0, shift : shift + S, :S] = re
        table[shift, 0, shift : shift + S, S:] = -im
        table[shift, 1, shift : shift + S, :S] = im
        table[shift, 1, shift : shift + S, S:] = re
    return table.reshape(8, 2 * ROWS, 2 * S).astype(ml_dtypes.bfloat16)


def swap_halves(x):
    return pltpu.roll(x, S, x.ndim - 1)


def arrange_station(raw, tall):
    value = raw.astype(F32)
    for i in range(S // 2):
        tall[8 * i : 8 * i + 4, :] = value[:, 128 * i : 128 * (i + 1)]
    lane = lax.broadcasted_iota(jnp.int32, (S // 2, 128), 1)
    feeds = []
    for f in range(2):
        re = tall[pl.ds(2 * f, S // 2, stride=8), :]
        im = tall[pl.ds(2 * f + 1, S // 2, stride=8), :]
        even = jnp.where(lane < S, re, swap_halves(im))
        odd = jnp.where(lane < S, swap_halves(re), im)
        feeds.append(jnp.concatenate([even, odd], axis=0).astype(BF))
    return feeds


def pack_blocks(head, off_u, off_v, base, pairs, track, data):
    heads = head[...]
    kind = lax.broadcasted_iota(jnp.int32, (8, B_DEV), 0)
    named = jnp.where(kind == heads, 1.0, 0.0)
    before = lax.broadcasted_iota(jnp.int32, (B_DEV, B_DEV), 0)
    after = lax.broadcasted_iota(jnp.int32, (B_DEV, B_DEV), 1)
    strict = jnp.where(before < after, 1.0, 0.0).astype(BF)
    counts = jnp.dot(named.astype(BF), strict, preferred_element_type=F32)
    rank = jnp.sum(named * counts, axis=0, keepdims=True)
    slot = heads.astype(F32) * CAP + rank
    which = lax.broadcasted_iota(jnp.int32, (SLOTS, B_DEV), 0).astype(F32)
    chosen = jnp.where(which == slot, 1.0, 0.0).astype(BF)

    label = lax.broadcasted_iota(jnp.int32, (pairs.shape[1], B_DEV), 0)
    listed = jnp.where(label == base[...], 1.0, 0.0).astype(BF)
    station = jnp.dot(pairs[...].astype(F32).astype(BF), listed, preferred_element_type=F32)
    rows = jnp.concatenate(
        [
            jnp.ones((1, B_DEV), F32),
            off_u[...].astype(F32),
            off_v[...].astype(F32),
            station,
            jnp.zeros((3, B_DEV), F32),
            track[...].astype(F32),
            jnp.zeros((128 - 8 - 2 * TB, B_DEV), F32),
        ],
        axis=0,
    ).astype(BF)
    dims = (((1,), (1,)), ((), ()))
    labels = lax.dot_general(chosen, rows, dims, preferred_element_type=F32)

    owner = lax.broadcasted_iota(jnp.int32, (B_DEV, 8 * B_DEV), 0)
    column = lax.broadcasted_iota(jnp.int32, (B_DEV, 8 * B_DEV), 1)
    widen = jnp.where(owner == column // 8, 1.0, 0.0).astype(BF)
    wide = jnp.dot(
        jnp.broadcast_to(slot, (8, B_DEV)).astype(BF), widen, preferred_element_type=F32
    )[:1]
    lane = lax.broadcasted_iota(jnp.int32, (1, 8 * B_DEV), 1) % 8
    place = wide * 8.0 + lane.astype(F32)
    target = lax.broadcasted_iota(jnp.int32, (8 * SLOTS, 8 * B_DEV), 0).astype(F32)
    moved = jnp.where(target == place, 1.0, 0.0).astype(BF)
    return jnp.dot(moved, data[...], preferred_element_type=F32).astype(BF), labels


def list_blocks(labels):
    dims = (((1,), (1,)), ((), ()))
    quantity = lax.broadcasted_iota(jnp.int32, (8, 128), 0)
    lane = lax.broadcasted_iota(jnp.int32, (8, 128), 1)
    pick = jnp.where(quantity == lane, 1.0, 0.0).astype(BF)
    rows = lax.dot_general(pick, labels.astype(BF), dims, preferred_element_type=F32)
    filled, at_u, at_v = rows[0:1], rows[1:2], rows[2:3]
    past_u = at_u > TU - S
    past = jnp.logical_or(past_u, at_v > TV - S)
    first = jnp.where(past_u, filled, 0.0)
    early = jnp.where(past, filled, 0.0)
    kind = lax.broadcasted_iota(jnp.int32, (8, SLOTS), 0)
    both = jnp.where(
        kind == 0,
        first,
        jnp.where(kind == 1, early - first, jnp.where(kind == 2, filled - early, 0.0)),
    )
    before = lax.broadcasted_iota(jnp.int32, (SLOTS, SLOTS), 0)
    after = lax.broadcasted_iota(jnp.int32, (SLOTS, SLOTS), 1)
    strict = jnp.where(before < after, 1.0, 0.0).astype(BF)
    ahead = jnp.dot(both.astype(BF), strict, preferred_element_type=F32)
    number_first = jnp.sum(first, axis=1, keepdims=True)
    number_early = jnp.sum(early, axis=1, keepdims=True)
    number = jnp.sum(filled, axis=1, keepdims=True)
    place = jnp.where(past, number_first + ahead[1:2], number_early + ahead[2:3])
    place = jnp.where(past_u, ahead[0:1], place)
    place = jnp.where(filled > 0.5, place, -1.0)
    target = lax.broadcasted_iota(jnp.int32, (128, SLOTS), 0).astype(F32)
    moved = jnp.where(target == place, 1.0, 0.0).astype(BF)
    slot = lax.broadcasted_iota(jnp.int32, (8, SLOTS), 1).astype(F32)
    rows = jnp.where(kind == 0, slot, rows)
    table = lax.dot_general(rows.astype(BF), moved, dims, preferred_element_type=F32)
    spare = jnp.where(lane.astype(F32) >= number, float(TU + S), 0.0)
    table = table + jnp.where(quantity == 1, spare, 0.0)
    pairs = jnp.floor((number + 1.0) * 0.5)
    ends = []
    for count, least in ((number_first, U_PAIRS), (number_early, V_PAIRS)):
        enough = jnp.minimum(pairs, float(least))
        ends.append(jnp.maximum(jnp.floor((count + 1.0) * 0.5), enough))
    for row, end in enumerate((*ends, pairs)):
        table = jnp.where(quantity == 5 + row, end, table)
    return table.astype(jnp.int32)


def image_kernel(
    head_in, off_u_in, off_v_in, base_in, pairs_in, track_in, data_in, own_screens,
    right_in, left_in,
    images, screens, listing, canvas, right, left,
    head, off_u, off_v, base, pairs, track, data, in_sems,
    packed, labels, got_data, got_labels, samples, spread, mult, raw, tall,
    own_sems, send_sems, recv_sems, y_send, y_recv, x_send, x_recv, c_send, c_recv,
):
    au, vert, band = (lax.axis_index(axis) for axis in ("au", "vert", "ch"))
    n_au, n_vert, n_ch = (lax.axis_size(axis) for axis in ("au", "vert", "ch"))
    here = own_screens.shape[0]
    piece = here // n_vert
    part = piece // PARTS
    n_x = n_vert // 2

    def turned(step):
        return lax.rem(vert + step, n_vert)

    near = (
        {"au": lax.rem(au + 1, n_au)},
        {"au": lax.rem(au + n_au - 1, n_au)},
        {"vert": turned(1)},
        {"vert": turned(n_vert - 1)},
    )
    across = {"ch": lax.rem(band + 1, n_ch)}
    sibling = {"vert": vert + 1 - 2 * lax.rem(vert, 2)}
    beside = [{"vert": turned(2 * j)} for j in range(1, n_x)]

    inputs = (
        (head_in, head), (off_u_in, off_u), (off_v_in, off_v), (base_in, base),
        (pairs_in, pairs), (track_in, track), (data_in, data),
        (right_in, right), (left_in, left),
    )
    loads = [
        pltpu.make_async_copy(source, target, in_sems.at[j])
        for j, (source, target) in enumerate(inputs)
    ]
    for copy in loads:
        copy.start()
    fetches = []
    for j in range(n_vert):
        rows = pl.ds(turned(j) * piece, piece)
        fetches.append(
            pltpu.make_async_copy(own_screens.at[rows], raw.at[rows], own_sems.at[j])
        )
        fetches[-1].start()
    barrier = pltpu.get_barrier_semaphore()
    for device in (*near, across, *beside):
        pl.semaphore_signal(barrier, inc=1, device_id=device, device_id_type=MESH)

    for copy in loads[:7]:
        copy.wait()
    values, rows = pack_blocks(head, off_u, off_v, base, pairs, track, data)
    packed[...] = values
    labels[...] = rows

    def arrange(first, number):
        def one(pair, carry):
            for i in range(2):
                station = lax.rem(first + 2 * pair + i, here)
                feeds = arrange_station(raw[station], tall.at[i])
                for f in range(2):
                    screens[station, f] = feeds[f]
            return carry

        lax.fori_loop(0, number // 2, one, 0)

    fetches[0].wait()
    arrange(vert * piece, piece)
    pl.semaphore_wait(barrier, 5 + len(beside))

    def moves(i):
        pairs_of = ((packed, got_data, 8 * CAP), (labels, got_labels, CAP))
        for j, (source, target, rows) in enumerate(pairs_of):
            where = pl.ds((i + 1) * rows, rows)
            yield pltpu.make_async_remote_copy(
                src_ref=source.at[where],
                dst_ref=target.at[where],
                send_sem=send_sems.at[i, j],
                recv_sem=recv_sems.at[i, j],
                device_id=near[i],
                device_id_type=MESH,
            )

    def to_other(source, owner, k, send, recv, device):
        return pltpu.make_async_remote_copy(
            src_ref=screens.at[pl.ds(source * piece + k * part, part)],
            dst_ref=screens.at[pl.ds(here + owner * piece + k * part, part)],
            send_sem=send,
            recv_sem=recv,
            device_id=device,
            device_id_type=MESH,
        )

    def y_copy(k):
        return to_other(vert, vert, k, y_send.at[k], y_recv.at[k], across)

    def x_copy(j, k, owner):
        return to_other(
            n_vert + owner, owner, k, x_send.at[j - 1, k], x_recv.at[j - 1, k], beside[j - 1]
        )

    def c_copy(j, k, owner):
        return to_other(
            n_vert + owner, owner, k, c_send.at[j, k], c_recv.at[j, k], sibling
        )

    for i in range(4):
        for copy in moves(i):
            copy.start()
    for k in range(PARTS):
        y_copy(k).start()

    canvas[...] = jnp.zeros_like(canvas)
    for copy in fetches[1:]:
        copy.wait()
    arrange((vert + 1) * piece, here - piece)

    row = lax.broadcasted_iota(jnp.int32, (32, K), 0)
    channel = band * CH_DEV + lax.broadcasted_iota(jnp.int32, (32, K), 1) % CH_DEV
    ratio = 1.0 + channel.astype(F32) / jnp.float32(2 * CH_DEV * n_ch)
    coarse = row - 8
    coarse_u = 16 * (coarse % 4) + coarse // 4 - S // 2
    fine_v = row - 16
    coarse_v = (row - 24) * 8 - S // 2
    step = jnp.where(
        row < 16, jnp.where(row < 8, 2 * row, coarse_u), jnp.where(row < 24, fine_v, coarse_v)
    )
    mult[...] = step.astype(F32) / S * ratio

    def widen(rows):
        source = lax.broadcasted_iota(jnp.int32, (128, 2 * K), 0)
        column = lax.broadcasted_iota(jnp.int32, (128, 2 * K), 1)
        chosen = jnp.where(source == 8 + column // CH_DEV, 1.0, 0.0).astype(BF)
        lane = lax.broadcasted_iota(jnp.int32, rows.shape, 1)
        only = jnp.where(lane < 8, 0.0, rows).astype(BF)
        return jnp.dot(only, chosen, preferred_element_type=F32)

    got_labels[:CAP] = labels[:CAP]
    samples[: 8 * CAP] = packed[: 8 * CAP].astype(F32)
    spread[:CAP] = widen(labels[:CAP])

    def block(slot):
        sample = samples[pl.ds(8 * slot, 8), :]
        track = spread[pl.ds(slot, 1), :]
        turns = jnp.concatenate(
            [track[:, :K] * mult[:16], track[:, K:] * mult[16:]], axis=0
        )
        frac = turns - jnp.floor(turns + 0.5)
        square = frac * frac
        cos = horner(COS_COEF, square)
        sin = horner(SIN_COEF, square) * frac

        def phasors(first):
            cos_fine, sin_fine = cos[first : first + 8], sin[first : first + 8]
            all_cos, all_sin = [], []
            for a in range(8):
                at = first + 8 + a
                cos_a, sin_a = cos[at : at + 1], sin[at : at + 1]
                all_cos.append(cos_fine * cos_a - sin_fine * sin_a)
                all_sin.append(sin_fine * cos_a + cos_fine * sin_a)
            return (
                jnp.concatenate(all_cos, axis=0).astype(BF),
                jnp.concatenate(all_sin, axis=0).astype(BF),
            )

        cos_u, sin_u = phasors(0)
        cos_u, sin_u = cos_u.astype(F32), sin_u.astype(F32)
        cos_v, sin_v = phasors(16)
        table_re = jnp.concatenate([cos_v, sin_v], axis=0)
        table_im = jnp.concatenate([-sin_v, cos_v], axis=0)
        weigh_re, weigh_im = [], []
        for p in range(4):
            re, im = sample[2 * p : 2 * p + 1], sample[2 * p + 1 : 2 * p + 2]
            weigh_re.append((re * cos_u - im * sin_u).astype(BF))
            weigh_im.append((re * sin_u + im * cos_u).astype(BF))
        dims = (((1,), (1,)), ((), ()))
        image = lax.dot_general(
            jnp.concatenate(weigh_re, axis=0), table_re, dims, preferred_element_type=F32
        ) + lax.dot_general(
            jnp.concatenate(weigh_im, axis=0), table_im, dims, preferred_element_type=F32
        )
        return image.astype(BF)

    def forward_y(k):
        y_copy(k).wait_recv()
        for j in range(1, n_x):
            x_copy(j, k, vert).start()
        c_copy(0, k, vert).start()

    def forward_x(k):
        for j in range(1, n_x):
            owner = turned(n_vert - 2 * j)
            x_copy(j, k, owner).wait_recv()
            c_copy(j, k, owner).start()

    def loop(pair, carry):
        @pl.when(pair == CAP // 2)
        def _():
            for i in range(4):
                for copy in moves(i):
                    copy.wait_recv()
            samples[8 * CAP :] = got_data[8 * CAP :].astype(F32)
            spread[CAP:] = widen(got_labels[CAP:])

        for k in range(PARTS):

            @pl.when(pair == Y_PAIRS[k])
            def _():
                forward_y(k)

            @pl.when(pair == X_PAIRS[k])
            def _():
                forward_x(k)

        first, second = block(2 * pair), block(2 * pair + 1)
        images[2 * pair] = first
        images[2 * pair + 1] = second
        return carry

    lax.fori_loop(0, SLOTS // 2, loop, 0)
    listing[...] = list_blocks(got_labels[...])
    for copy in loads[7:]:
        copy.wait()
    for i in range(4):
        for copy in moves(i):
            copy.wait_send()
    for k in range(PARTS):
        y_copy(k).wait_send()
        for j in range(1, n_x):
            x_copy(j, k, vert).wait_send()
        for j in range(n_x):
            c_copy(j, k, turned(n_vert - 2 * j)).wait_send()
            mine = turned(n_vert - 2 * j)
            theirs = mine + 1 - 2 * lax.rem(mine, 2)
            c_copy(j, k, theirs).wait_recv()


def folded(x):
    middle = x.shape[1] // 2
    lane = lax.broadcasted_iota(jnp.int32, (1, 1, 128), 2)
    return jnp.where(lane < S, x[:, :middle], swap_halves(x[:, middle:])).astype(BF)


def edge_u_kernel(listing, images, screens, right, left, canvas_in, canvas, edge_u, corner):
    grid_blocks(images, screens, canvas, right, left, listing, 0, listing[5, 0])
    edge_u[...] = canvas[:, TU : TU + S, :TV].astype(BF)
    corner[...] = folded(canvas[:, TU : TU + S, TV:])


def edge_v_kernel(listing, images, screens, right, left, canvas_in, canvas, *edge_v):
    grid_blocks(images, screens, canvas, right, left, listing, listing[5, 0], listing[6, 0])
    each = 8 // V_SPLIT
    for i, edge in enumerate(edge_v):
        edge[...] = folded(canvas[i * each : (i + 1) * each, :TU, TV:])


def late_kernel(listing, images, screens, right, left, canvas_in, canvas):
    grid_blocks(images, screens, canvas, right, left, listing, listing[6, 0], listing[7, 0])


def grid_blocks(images, screens, canvas, right, left, listing, first, last):
    here = screens.shape[0] // 2
    band = lax.axis_index("ch")

    def screen_place(station):
        owner = station // here
        local = station - owner * here
        return jnp.where(owner == band, local, here + local)

    def block(index):
        slot = listing[0, index]
        off_u = listing[1, index]
        off_v = listing[2, index]
        one = screen_place(listing[3, index])
        two = screen_place(listing[4, index])
        two_s = [screens[two, f].astype(F32) for f in range(2)]
        fixed = []
        for f in range(2):
            one_s = screens[one, f].astype(F32)
            one_swapped = swap_halves(one_s)
            for e in range(2):
                p = 2 * f + e
                same = one_s * two_s[e]
                cross = one_swapped * two_s[e]
                gain_re = same + swap_halves(same)
                gain_im = swap_halves(cross) - cross
                part = images[slot, p * S : (p + 1) * S].astype(F32)
                fixed.append((part * gain_re + swap_halves(part) * gain_im).astype(BF))
        lanes = off_v // 128
        moved = pltpu.roll(right[...], off_v - lanes * 128, 1).astype(BF)
        table_re, table_im = moved[:S], moved[S:]
        shifted = jnp.concatenate(
            [
                jnp.concatenate([table_re, -table_im], axis=0),
                jnp.concatenate([table_im, table_re], axis=0),
            ],
            axis=1,
        )
        half = jnp.dot(
            jnp.concatenate(fixed, axis=0), shifted, preferred_element_type=F32
        ).astype(BF)
        eighth = off_u // 8
        placed = left[off_u - eighth * 8]
        start_u = pl.multiple_of(eighth * 8, 8)
        start_v = pl.multiple_of(lanes * 128, 128)
        return start_u, start_v, placed, half

    def loop(pair, carry):
        ready = [block(2 * pair), block(2 * pair + 1)]
        for start_u, start_v, placed, half in ready:
            for p in range(4):
                part = half[p * S : (p + 1) * S]
                both = jnp.concatenate([part[:, :256], part[:, 256:]], axis=0)
                grid = jnp.dot(placed, both, preferred_element_type=F32)
                for r in range(2):
                    where = (2 * p + r, pl.ds(start_u, ROWS), pl.ds(start_v, 256))
                    canvas[where] += grid[r * ROWS : (r + 1) * ROWS]
        return carry

    lax.fori_loop(first, last, loop, 0)


def finish_kernel(canvas, got_u, got_c, *rest):
    *got_v, out, top, side, sems = rest
    rest = pltpu.make_async_copy(
        canvas.at[:, S:TU, 128:TV], out.at[:, S:, 128:], sems.at[2]
    )
    rest.start()
    lane = lax.broadcasted_iota(jnp.int32, (1, 1, 128), 2)

    def unfolded(x):
        x = x.astype(F32)
        low = jnp.where(lane < S, x, 0.0)
        high = jnp.where(lane < S, swap_halves(x), 0.0)
        return low, high

    low, high = unfolded(jnp.concatenate([x[...] for x in got_v], axis=0))
    first, second = unfolded(got_c[...])
    side[:, : TU // 2 - S] = canvas[:, S : TU // 2, :128] + low[:, S:]
    side[:, TU // 2 - S :] = canvas[:, TU // 2 : TU, :128] + high
    store_side = pltpu.make_async_copy(side, out.at[:, S:, :128], sems.at[1])
    store_side.start()
    top[...] = canvas[:, :S, :TV] + got_u[...].astype(F32)
    top[:, :, :128] += low[:, :S] + jnp.concatenate([first, second], axis=1)
    store_top = pltpu.make_async_copy(top, out.at[:, :S, :], sems.at[0])
    store_top.start()
    rest.wait()
    store_side.wait()
    store_top.wait()


def body(visibilities, tracks, offset_u, offset_v, heading, baseline, station_pair, screens):
    smem = pl.BlockSpec(memory_space=pltpu.SMEM)
    vmem = pl.BlockSpec(memory_space=pltpu.VMEM)
    hbm = pl.BlockSpec(memory_space=pltpu.HBM)
    n_au, n_vert = (lax.axis_size(axis) for axis in ("au", "vert"))
    n_x = n_vert // 2
    here = screens.shape[0]
    canvas_shape = jax.ShapeDtypeStruct((8, TU + S + ROWS, TV + 128), F32)
    right_shape = jax.ShapeDtypeStruct((2 * S, 256), F32)
    left_shape = jax.ShapeDtypeStruct((8, 2 * ROWS, 2 * S), BF)
    dma = pltpu.SemaphoreType.DMA
    number = pltpu.VMEM((1, B_DEV), jnp.int32)
    images, all_screens, listing, canvas, right, left = pl.pallas_call(
        image_kernel,
        out_shape=(
            jax.ShapeDtypeStruct((SLOTS, 4 * S, 2 * S), BF),
            jax.ShapeDtypeStruct((2 * here, 2, S, 2 * S), BF),
            jax.ShapeDtypeStruct((8, 128), jnp.int32),
            canvas_shape,
            right_shape,
            left_shape,
        ),
        in_specs=[hbm] * 10,
        out_specs=(vmem,) * 6,
        scratch_shapes=[
            number,
            number,
            number,
            number,
            pltpu.VMEM(station_pair.shape, jnp.int32),
            pltpu.VMEM((2 * TB, B_DEV), BF),
            pltpu.VMEM((8 * B_DEV, K), BF),
            dma((9,)),
            pltpu.VMEM((8 * SLOTS, K), BF),
            pltpu.VMEM((SLOTS, 128), F32),
            pltpu.VMEM((8 * SLOTS, K), BF),
            pltpu.VMEM((SLOTS, 128), F32),
            pltpu.VMEM((8 * SLOTS, K), F32),
            pltpu.VMEM((SLOTS, 2 * K), F32),
            pltpu.VMEM((32, K), F32),
            pltpu.VMEM((here, 4, S * S), BF),
            pltpu.VMEM((2, 4 * S, 128), F32),
            dma((n_vert,)),
            dma((4, 2)),
            dma((4, 2)),
            dma((PARTS,)),
            dma((PARTS,)),
            dma((n_x - 1, PARTS)),
            dma((n_x - 1, PARTS)),
            dma((n_x, PARTS)),
            dma((n_x, PARTS)),
        ],
        compiler_params=pltpu.CompilerParams(
            collective_id=0, has_side_effects=True, vmem_limit_bytes=20 << 20
        ),
    )(*(pltpu.with_memory_space_constraint(x, pltpu.HBM) for x in (
        heading.reshape(1, B_DEV), offset_u[None], offset_v[None], baseline[None],
        station_pair, tracks.transpose(1, 2, 0).reshape(2 * TB, B_DEV),
        visibilities.reshape(8 * B_DEV, K), screens,
        jnp.asarray(right_table()), jnp.asarray(left_table()),
    )))

    def grid(kernel, canvas, flops, *edges):
        return pl.pallas_call(
            kernel,
            out_shape=(canvas_shape, *edges),
            in_specs=[smem] + [vmem] * 5,
            out_specs=(vmem,) * (1 + len(edges)),
            input_output_aliases={5: 0},
            compiler_params=pltpu.CompilerParams(vmem_limit_bytes=12 << 20),
            cost_estimate=pl.CostEstimate(
                flops=flops, bytes_accessed=1 << 20, transcendentals=0
            ),
        )(listing, images, all_screens, right, left, canvas)

    canvas, edge_u, corner = grid(
        edge_u_kernel,
        canvas,
        10**9,
        jax.ShapeDtypeStruct((8, S, TV), BF),
        jax.ShapeDtypeStruct((8, S // 2, 128), BF),
    )
    got_u = lax.ppermute(edge_u, "au", [(i, (i + 1) % n_au) for i in range(n_au)])
    diagonal = [
        (u * n_vert + v, (u + 1) % n_au * n_vert + (v + 1) % n_vert)
        for u in range(n_au)
        for v in range(n_vert)
    ]
    got_c = lax.ppermute(corner, ("au", "vert"), diagonal)
    canvas, *edge_v = grid(
        edge_v_kernel, canvas, 4 * 10**9, *[jax.ShapeDtypeStruct((8 // V_SPLIT, TU // 2, 128), BF)] * V_SPLIT
    )
    got_v = [
        lax.ppermute(x, "vert", [(i, (i + 1) % n_vert) for i in range(n_vert)]) for x in edge_v
    ]
    (canvas,) = grid(late_kernel, canvas, 10**6)
    out = pl.pallas_call(
        finish_kernel,
        out_shape=jax.ShapeDtypeStruct((8, TU, TV), F32),
        in_specs=[vmem] * (3 + V_SPLIT),
        out_specs=pl.BlockSpec(memory_space=pl.ANY),
        scratch_shapes=[
            pltpu.VMEM((8, S, TV), F32),
            pltpu.VMEM((8, TU - S, 128), F32),
            dma((3,)),
        ],
        compiler_params=pltpu.CompilerParams(vmem_limit_bytes=8 << 20),
    )(canvas, got_u, got_c, *got_v)
    return out[None]


def solution(mesh):
    placed = (
        P(("au", "vert"), None, "ch"),
        P(("au", "vert"), None, None),
        P(("au", "vert")),
        P(("au", "vert")),
        P(("au", "vert"), None),
        P(("au", "vert")),
        P(),
        P("ch", None, None),
    )
    return jax.shard_map(
        body, mesh=mesh, in_specs=placed, out_specs=P("ch", None, "au", "vert"), check_vma=False
    )
```

```python
import math

import jax
import jax.numpy as jnp
import ml_dtypes
import numpy as np
from jax import lax
from jax.experimental import pallas as pl
from jax.experimental.pallas import tpu as pltpu
from jax.sharding import PartitionSpec as P

S = 64
CH_DEV = 32
TB = 8
K = TB * CH_DEV
B_DEV = 32
CAP = B_DEV // 4
SLOTS = 5 * CAP
TU = 256
TV = 256
ROWS = 72
AT_ONCE = 4
U_GROUPS = 3
V_GROUPS = 5
PARTS = 2
V_SPLIT = 2
Y_AT = (2, 5)
X_AT = (6, 8)
MESH = pl.DeviceIdType.MESH
BF = jnp.bfloat16
F32 = jnp.float32


def series(values, degree):
    nodes = (np.cos(np.pi * (np.arange(400) + 0.5) / 400) + 1.0) * 0.125
    fitted = np.polynomial.chebyshev.Chebyshev.fit(nodes, values(nodes), degree, domain=[0, 0.25])
    return [float(c) for c in fitted.convert(kind=np.polynomial.Polynomial).coef]


COS_COEF = series(lambda q: np.cos(2 * np.pi * np.sqrt(q)), 5)
SIN_COEF = series(lambda q: np.sin(2 * np.pi * np.sqrt(q)) / np.sqrt(q), 5)


def horner(coefs, q):
    total = jnp.full_like(q, coefs[-1])
    for c in coefs[-2::-1]:
        total = total * q + jnp.float32(c)
    return total


def dft_tables():
    centred = np.arange(S) - S // 2
    product = (centred[:, None] * centred[None, :]) % S
    angles = np.float32(2.0 * math.pi / S) * product.astype(np.float32)
    scale = np.float32(1.0 / math.sqrt(S))
    re = (np.cos(angles) * scale).astype(ml_dtypes.bfloat16).astype(np.float32)
    im = (-np.sin(angles) * scale).astype(ml_dtypes.bfloat16).astype(np.float32)
    return re, im


def right_table():
    re, im = dft_tables()
    norm = np.float32(1.0 / math.sqrt(K))
    table = np.zeros((2 * S, 128), np.float32)
    table[:S, :S] = re.T * norm
    table[S:, :S] = im.T * norm
    return table


def left_table():
    re, im = dft_tables()
    order = np.concatenate([np.arange(0, S, 2), np.arange(1, S, 2)])
    re, im = re[:, order], im[:, order]
    table = np.zeros((8, 2, ROWS, 2 * S), np.float32)
    for shift in range(8):
        table[shift, 0, shift : shift + S, :S] = re
        table[shift, 0, shift : shift + S, S:] = -im
        table[shift, 1, shift : shift + S, :S] = im
        table[shift, 1, shift : shift + S, S:] = re
    return table.reshape(8, 2 * ROWS, 2 * S).astype(ml_dtypes.bfloat16)


def swap_halves(x):
    return pltpu.roll(x, S, x.ndim - 1)


def arrange_station(raw, tall):
    value = raw.astype(F32)
    for i in range(S // 2):
        tall[8 * i : 8 * i + 4, :] = value[:, 128 * i : 128 * (i + 1)]
    lane = lax.broadcasted_iota(jnp.int32, (S // 2, 128), 1)
    feeds = []
    for f in range(2):
        re = tall[pl.ds(2 * f, S // 2, stride=8), :]
        im = tall[pl.ds(2 * f + 1, S // 2, stride=8), :]
        even = jnp.where(lane < S, re, swap_halves(im))
        odd = jnp.where(lane < S, swap_halves(re), im)
        feeds.append(jnp.concatenate([even, odd], axis=0).astype(BF))
    return feeds


def pack_blocks(head, off_u, off_v, base, pairs, track, data):
    heads = head[...]
    kind = lax.broadcasted_iota(jnp.int32, (8, B_DEV), 0)
    named = jnp.where(kind == heads, 1.0, 0.0)
    before = lax.broadcasted_iota(jnp.int32, (B_DEV, B_DEV), 0)
    after = lax.broadcasted_iota(jnp.int32, (B_DEV, B_DEV), 1)
    strict = jnp.where(before < after, 1.0, 0.0).astype(BF)
    counts = jnp.dot(named.astype(BF), strict, preferred_element_type=F32)
    rank = jnp.sum(named * counts, axis=0, keepdims=True)
    slot = heads.astype(F32) * CAP + rank
    which = lax.broadcasted_iota(jnp.int32, (SLOTS, B_DEV), 0).astype(F32)
    chosen = jnp.where(which == slot, 1.0, 0.0).astype(BF)

    label = lax.broadcasted_iota(jnp.int32, (pairs.shape[1], B_DEV), 0)
    listed = jnp.where(label == base[...], 1.0, 0.0).astype(BF)
    station = jnp.dot(pairs[...].astype(F32).astype(BF), listed, preferred_element_type=F32)
    rows = jnp.concatenate(
        [
            jnp.ones((1, B_DEV), F32),
            off_u[...].astype(F32),
            off_v[...].astype(F32),
            station,
            jnp.zeros((3, B_DEV), F32),
            track[...].astype(F32),
            jnp.zeros((128 - 8 - 2 * TB, B_DEV), F32),
        ],
        axis=0,
    ).astype(BF)
    dims = (((1,), (1,)), ((), ()))
    labels = lax.dot_general(chosen, rows, dims, preferred_element_type=F32)

    owner = lax.broadcasted_iota(jnp.int32, (B_DEV, 8 * B_DEV), 0)
    column = lax.broadcasted_iota(jnp.int32, (B_DEV, 8 * B_DEV), 1)
    widen = jnp.where(owner == column // 8, 1.0, 0.0).astype(BF)
    wide = jnp.dot(
        jnp.broadcast_to(slot, (8, B_DEV)).astype(BF), widen, preferred_element_type=F32
    )[:1]
    lane = lax.broadcasted_iota(jnp.int32, (1, 8 * B_DEV), 1) % 8
    place = wide * 8.0 + lane.astype(F32)
    target = lax.broadcasted_iota(jnp.int32, (8 * SLOTS, 8 * B_DEV), 0).astype(F32)
    moved = jnp.where(target == place, 1.0, 0.0).astype(BF)
    return jnp.dot(moved, data[...], preferred_element_type=F32).astype(BF), labels


def list_blocks(labels):
    dims = (((1,), (1,)), ((), ()))
    quantity = lax.broadcasted_iota(jnp.int32, (8, 128), 0)
    lane = lax.broadcasted_iota(jnp.int32, (8, 128), 1)
    pick = jnp.where(quantity == lane, 1.0, 0.0).astype(BF)
    rows = lax.dot_general(pick, labels.astype(BF), dims, preferred_element_type=F32)
    filled, at_u, at_v = rows[0:1], rows[1:2], rows[2:3]
    past_u = at_u > TU - S
    past = jnp.logical_or(past_u, at_v > TV - S)
    first = jnp.where(past_u, filled, 0.0)
    early = jnp.where(past, filled, 0.0)
    kind = lax.broadcasted_iota(jnp.int32, (8, SLOTS), 0)
    both = jnp.where(
        kind == 0,
        first,
        jnp.where(kind == 1, early - first, jnp.where(kind == 2, filled - early, 0.0)),
    )
    before = lax.broadcasted_iota(jnp.int32, (SLOTS, SLOTS), 0)
    after = lax.broadcasted_iota(jnp.int32, (SLOTS, SLOTS), 1)
    strict = jnp.where(before < after, 1.0, 0.0).astype(BF)
    ahead = jnp.dot(both.astype(BF), strict, preferred_element_type=F32)
    number_first = jnp.sum(first, axis=1, keepdims=True)
    number_early = jnp.sum(early, axis=1, keepdims=True)
    number = jnp.sum(filled, axis=1, keepdims=True)
    place = jnp.where(past, number_first + ahead[1:2], number_early + ahead[2:3])
    place = jnp.where(past_u, ahead[0:1], place)
    place = jnp.where(filled > 0.5, place, -1.0)
    target = lax.broadcasted_iota(jnp.int32, (128, SLOTS), 0).astype(F32)
    moved = jnp.where(target == place, 1.0, 0.0).astype(BF)
    slot = lax.broadcasted_iota(jnp.int32, (8, SLOTS), 1).astype(F32)
    rows = jnp.where(kind == 0, slot, rows)
    table = lax.dot_general(rows.astype(BF), moved, dims, preferred_element_type=F32)
    spare = jnp.where(lane.astype(F32) >= number, float(TU + S), 0.0)
    table = table + jnp.where(quantity == 1, spare, 0.0)
    groups = jnp.floor((number + (AT_ONCE - 1.0)) / AT_ONCE)
    ends = []
    for count, least in ((number_first, U_GROUPS), (number_early, V_GROUPS)):
        enough = jnp.minimum(groups, float(least))
        needed = jnp.floor((count + (AT_ONCE - 1.0)) / AT_ONCE)
        ends.append(jnp.maximum(needed, enough))
    for row, end in enumerate((*ends, groups)):
        table = jnp.where(quantity == 5 + row, end, table)
    return table.astype(jnp.int32)


def image_kernel(
    head_in, off_u_in, off_v_in, base_in, pairs_in, track_in, data_in, own_screens,
    right_in, left_in,
    images, screens, listing, canvas, right, left,
    head, off_u, off_v, base, pairs, track, data, in_sems,
    packed, labels, got_data, got_labels, samples, spread, mult, raw, tall,
    own_sems, send_sems, recv_sems, y_send, y_recv, x_send, x_recv, c_send, c_recv,
):
    au, vert, band = (lax.axis_index(axis) for axis in ("au", "vert", "ch"))
    n_au, n_vert, n_ch = (lax.axis_size(axis) for axis in ("au", "vert", "ch"))
    here = own_screens.shape[0]
    piece = here // n_vert
    part = piece // PARTS
    n_x = n_vert // 2

    def turned(step):
        return lax.rem(vert + step, n_vert)

    near = (
        {"au": lax.rem(au + 1, n_au)},
        {"au": lax.rem(au + n_au - 1, n_au)},
        {"vert": turned(1)},
        {"vert": turned(n_vert - 1)},
    )
    across = {"ch": lax.rem(band + 1, n_ch)}
    sibling = {"vert": vert + 1 - 2 * lax.rem(vert, 2)}
    beside = [{"vert": turned(2 * j)} for j in range(1, n_x)]

    inputs = (
        (head_in, head), (off_u_in, off_u), (off_v_in, off_v), (base_in, base),
        (pairs_in, pairs), (track_in, track), (data_in, data),
        (right_in, right), (left_in, left),
    )
    loads = [
        pltpu.make_async_copy(source, target, in_sems.at[j])
        for j, (source, target) in enumerate(inputs)
    ]
    for copy in loads:
        copy.start()
    fetches = []
    for j in range(n_vert):
        rows = pl.ds(turned(j) * piece, piece)
        fetches.append(
            pltpu.make_async_copy(own_screens.at[rows], raw.at[rows], own_sems.at[j])
        )
        fetches[-1].start()
    barrier = pltpu.get_barrier_semaphore()
    for device in (*near, across, *beside):
        pl.semaphore_signal(barrier, inc=1, device_id=device, device_id_type=MESH)

    for copy in loads[:7]:
        copy.wait()
    values, rows = pack_blocks(head, off_u, off_v, base, pairs, track, data)
    packed[...] = values
    labels[...] = rows

    def arrange(first, number):
        def one(pair, carry):
            for i in range(2):
                station = lax.rem(first + 2 * pair + i, here)
                feeds = arrange_station(raw[station], tall.at[i])
                for f in range(2):
                    screens[station, f] = feeds[f]
            return carry

        lax.fori_loop(0, number // 2, one, 0)

    fetches[0].wait()
    arrange(vert * piece, piece)
    pl.semaphore_wait(barrier, 5 + len(beside))

    def moves(i):
        pairs_of = ((packed, got_data, 8 * CAP), (labels, got_labels, CAP))
        for j, (source, target, rows) in enumerate(pairs_of):
            where = pl.ds((i + 1) * rows, rows)
            yield pltpu.make_async_remote_copy(
                src_ref=source.at[where],
                dst_ref=target.at[where],
                send_sem=send_sems.at[i, j],
                recv_sem=recv_sems.at[i, j],
                device_id=near[i],
                device_id_type=MESH,
            )

    def to_other(source, owner, k, send, recv, device):
        return pltpu.make_async_remote_copy(
            src_ref=screens.at[pl.ds(source * piece + k * part, part)],
            dst_ref=screens.at[pl.ds(here + owner * piece + k * part, part)],
            send_sem=send,
            recv_sem=recv,
            device_id=device,
            device_id_type=MESH,
        )

    def y_copy(k):
        return to_other(vert, vert, k, y_send.at[k], y_recv.at[k], across)

    def x_copy(j, k, owner):
        return to_other(
            n_vert + owner, owner, k, x_send.at[j - 1, k], x_recv.at[j - 1, k], beside[j - 1]
        )

    def c_copy(j, k, owner):
        return to_other(
            n_vert + owner, owner, k, c_send.at[j, k], c_recv.at[j, k], sibling
        )

    for i in range(4):
        for copy in moves(i):
            copy.start()
    for k in range(PARTS):
        y_copy(k).start()

    canvas[...] = jnp.zeros_like(canvas)
    for copy in fetches[1:]:
        copy.wait()
    arrange((vert + 1) * piece, here - piece)

    row = lax.broadcasted_iota(jnp.int32, (32, K), 0)
    channel = band * CH_DEV + lax.broadcasted_iota(jnp.int32, (32, K), 1) % CH_DEV
    ratio = 1.0 + channel.astype(F32) / jnp.float32(2 * CH_DEV * n_ch)
    coarse = row - 8
    coarse_u = 16 * (coarse % 4) + coarse // 4 - S // 2
    fine_v = row - 16
    coarse_v = (row - 24) * 8 - S // 2
    step = jnp.where(
        row < 16, jnp.where(row < 8, 2 * row, coarse_u), jnp.where(row < 24, fine_v, coarse_v)
    )
    mult[...] = step.astype(F32) / S * ratio

    def widen(rows):
        source = lax.broadcasted_iota(jnp.int32, (128, 2 * K), 0)
        column = lax.broadcasted_iota(jnp.int32, (128, 2 * K), 1)
        chosen = jnp.where(source == 8 + column // CH_DEV, 1.0, 0.0).astype(BF)
        lane = lax.broadcasted_iota(jnp.int32, rows.shape, 1)
        only = jnp.where(lane < 8, 0.0, rows).astype(BF)
        return jnp.dot(only, chosen, preferred_element_type=F32)

    got_labels[:CAP] = labels[:CAP]
    samples[: 8 * CAP] = packed[: 8 * CAP].astype(F32)
    spread[:CAP] = widen(labels[:CAP])

    def block(slot):
        sample = samples[pl.ds(8 * slot, 8), :]
        track = spread[pl.ds(slot, 1), :]
        turns = jnp.concatenate(
            [track[:, :K] * mult[:16], track[:, K:] * mult[16:]], axis=0
        )
        frac = turns - jnp.floor(turns + 0.5)
        square = frac * frac
        cos = horner(COS_COEF, square)
        sin = horner(SIN_COEF, square) * frac

        def phasors(first):
            cos_fine, sin_fine = cos[first : first + 8], sin[first : first + 8]
            all_cos, all_sin = [], []
            for a in range(8):
                at = first + 8 + a
                cos_a, sin_a = cos[at : at + 1], sin[at : at + 1]
                all_cos.append(cos_fine * cos_a - sin_fine * sin_a)
                all_sin.append(sin_fine * cos_a + cos_fine * sin_a)
            return (
                jnp.concatenate(all_cos, axis=0).astype(BF),
                jnp.concatenate(all_sin, axis=0).astype(BF),
            )

        cos_u, sin_u = phasors(0)
        cos_v, sin_v = phasors(16)
        table = jnp.concatenate(
            [
                jnp.concatenate([cos_v, -sin_v], axis=1),
                jnp.concatenate([sin_v, cos_v], axis=1),
            ],
            axis=0,
        )

        def spread_row(r):
            row = jnp.broadcast_to(sample[r : r + 1], (16, K)).astype(BF)
            return jnp.concatenate([row] * (S // 16), axis=0)

        weighed = []
        for p in range(4):
            re, im = spread_row(2 * p), spread_row(2 * p + 1)
            weighed.append(
                jnp.concatenate([re * cos_u - im * sin_u, re * sin_u + im * cos_u], axis=1)
            )
        dims = (((1,), (1,)), ((), ()))
        image = lax.dot_general(
            jnp.concatenate(weighed, axis=0), table, dims, preferred_element_type=F32
        )
        return image.astype(BF)

    def forward_y(k):
        y_copy(k).wait_recv()
        for j in range(1, n_x):
            x_copy(j, k, vert).start()
        c_copy(0, k, vert).start()

    def forward_x(k):
        for j in range(1, n_x):
            owner = turned(n_vert - 2 * j)
            x_copy(j, k, owner).wait_recv()
            c_copy(j, k, owner).start()

    def loop(group, carry):
        @pl.when(group == CAP // AT_ONCE)
        def _():
            for i in range(4):
                for copy in moves(i):
                    copy.wait_recv()
            samples[8 * CAP :] = got_data[8 * CAP :].astype(F32)
            spread[CAP:] = widen(got_labels[CAP:])

        for k in range(PARTS):

            @pl.when(group == Y_AT[k])
            def _():
                forward_y(k)

            @pl.when(group == X_AT[k])
            def _():
                forward_x(k)

        made = [block(AT_ONCE * group + i) for i in range(AT_ONCE)]
        for i in range(AT_ONCE):
            images[AT_ONCE * group + i] = made[i]
        return carry

    lax.fori_loop(0, SLOTS // AT_ONCE, loop, 0)
    listing[...] = list_blocks(got_labels[...])
    for copy in loads[7:]:
        copy.wait()
    for i in range(4):
        for copy in moves(i):
            copy.wait_send()
    for k in range(PARTS):
        y_copy(k).wait_send()
        for j in range(1, n_x):
            x_copy(j, k, vert).wait_send()
        for j in range(n_x):
            c_copy(j, k, turned(n_vert - 2 * j)).wait_send()
            mine = turned(n_vert - 2 * j)
            theirs = mine + 1 - 2 * lax.rem(mine, 2)
            c_copy(j, k, theirs).wait_recv()


def folded(x):
    middle = x.shape[1] // 2
    lane = lax.broadcasted_iota(jnp.int32, (1, 1, 128), 2)
    return jnp.where(lane < S, x[:, :middle], swap_halves(x[:, middle:])).astype(BF)


def edge_u_kernel(listing, images, screens, right, left, canvas_in, canvas, edge_u, corner):
    grid_blocks(images, screens, canvas, right, left, listing, 0, listing[5, 0])
    edge_u[...] = canvas[:, TU : TU + S, :TV].astype(BF)
    corner[...] = folded(canvas[:, TU : TU + S, TV:])


def edge_v_kernel(listing, images, screens, right, left, canvas_in, canvas, *edge_v):
    grid_blocks(images, screens, canvas, right, left, listing, listing[5, 0], listing[6, 0])
    each = 8 // V_SPLIT
    for i, edge in enumerate(edge_v):
        edge[...] = folded(canvas[i * each : (i + 1) * each, :TU, TV:])


def late_kernel(listing, images, screens, right, left, canvas_in, canvas):
    grid_blocks(images, screens, canvas, right, left, listing, listing[6, 0], listing[7, 0])


def grid_blocks(images, screens, canvas, right, left, listing, first, last):
    here = screens.shape[0] // 2
    band = lax.axis_index("ch")

    def screen_place(station):
        owner = station // here
        local = station - owner * here
        return jnp.where(owner == band, local, here + local)

    def block(index):
        slot = listing[0, index]
        off_u = listing[1, index]
        off_v = listing[2, index]
        one = screen_place(listing[3, index])
        two = screen_place(listing[4, index])
        two_s = [screens[two, f].astype(F32) for f in range(2)]
        fixed = []
        for f in range(2):
            one_s = screens[one, f].astype(F32)
            one_swapped = swap_halves(one_s)
            for e in range(2):
                p = 2 * f + e
                same = one_s * two_s[e]
                cross = one_swapped * two_s[e]
                gain_re = same + swap_halves(same)
                gain_im = swap_halves(cross) - cross
                part = images[slot, p * S : (p + 1) * S].astype(F32)
                fixed.append((part * gain_re + swap_halves(part) * gain_im).astype(BF))
        tile = off_v // 128
        shift = off_v - tile * 128
        moved = pltpu.roll(right[...], shift, 1).astype(BF)
        table_re, table_im = moved[:S], moved[S:]
        shifted = jnp.concatenate(
            [
                jnp.concatenate([table_re, -table_im], axis=0),
                jnp.concatenate([table_im, table_re], axis=0),
            ],
            axis=1,
        )
        half = jnp.dot(
            jnp.concatenate(fixed, axis=0), shifted, preferred_element_type=F32
        ).astype(BF)
        eighth = off_u // 8
        placed = left[off_u - eighth * 8]
        start_u = pl.multiple_of(eighth * 8, 8)
        start_v = pl.multiple_of(tile * 128, 128)
        return start_u, start_v, shift, placed, half

    lane = lax.broadcasted_iota(jnp.int32, (1, 128), 1)

    def loop(group, carry):
        ready = [block(AT_ONCE * group + i) for i in range(AT_ONCE)]
        for start_u, start_v, shift, placed, half in ready:
            for f in range(2):
                both = []
                for p in (2 * f, 2 * f + 1):
                    part = half[p * S : (p + 1) * S]
                    both.append(jnp.concatenate([part[:, :128], part[:, 128:]], axis=0))
                grid = jnp.dot(
                    placed, jnp.concatenate(both, axis=1), preferred_element_type=F32
                )
                for e in range(2):
                    for r in range(2):
                        cells = grid[r * ROWS : (r + 1) * ROWS, 128 * e : 128 * (e + 1)]
                        cells = jnp.concatenate(
                            [
                                jnp.where(lane >= shift, cells, 0.0),
                                jnp.where(lane < shift, cells, 0.0),
                            ],
                            axis=1,
                        )
                        where = (
                            4 * f + 2 * e + r, pl.ds(start_u, ROWS), pl.ds(start_v, 256)
                        )
                        canvas[where] += cells
        return carry

    lax.fori_loop(first, last, loop, 0)


def finish_kernel(canvas, got_u, got_c, *rest):
    *got_v, out, top, side, sems = rest
    rest = pltpu.make_async_copy(
        canvas.at[:, S:TU, 128:TV], out.at[:, S:, 128:], sems.at[2]
    )
    rest.start()
    lane = lax.broadcasted_iota(jnp.int32, (1, 1, 128), 2)

    def unfolded(x):
        x = x.astype(F32)
        low = jnp.where(lane < S, x, 0.0)
        high = jnp.where(lane < S, swap_halves(x), 0.0)
        return low, high

    low, high = unfolded(jnp.concatenate([x[...] for x in got_v], axis=0))
    first, second = unfolded(got_c[...])
    side[:, : TU // 2 - S] = canvas[:, S : TU // 2, :128] + low[:, S:]
    side[:, TU // 2 - S :] = canvas[:, TU // 2 : TU, :128] + high
    store_side = pltpu.make_async_copy(side, out.at[:, S:, :128], sems.at[1])
    store_side.start()
    top[...] = canvas[:, :S, :TV] + got_u[...].astype(F32)
    top[:, :, :128] += low[:, :S] + jnp.concatenate([first, second], axis=1)
    store_top = pltpu.make_async_copy(top, out.at[:, :S, :], sems.at[0])
    store_top.start()
    rest.wait()
    store_side.wait()
    store_top.wait()


def body(visibilities, tracks, offset_u, offset_v, heading, baseline, station_pair, screens):
    smem = pl.BlockSpec(memory_space=pltpu.SMEM)
    vmem = pl.BlockSpec(memory_space=pltpu.VMEM)
    hbm = pl.BlockSpec(memory_space=pltpu.HBM)
    n_au, n_vert = (lax.axis_size(axis) for axis in ("au", "vert"))
    n_x = n_vert // 2
    here = screens.shape[0]
    canvas_shape = jax.ShapeDtypeStruct((8, TU + S + ROWS, TV + 128), F32)
    right_shape = jax.ShapeDtypeStruct((2 * S, 128), F32)
    left_shape = jax.ShapeDtypeStruct((8, 2 * ROWS, 2 * S), BF)
    dma = pltpu.SemaphoreType.DMA
    number = pltpu.VMEM((1, B_DEV), jnp.int32)
    images, all_screens, listing, canvas, right, left = pl.pallas_call(
        image_kernel,
        out_shape=(
            jax.ShapeDtypeStruct((SLOTS, 4 * S, 2 * S), BF),
            jax.ShapeDtypeStruct((2 * here, 2, S, 2 * S), BF),
            jax.ShapeDtypeStruct((8, 128), jnp.int32),
            canvas_shape,
            right_shape,
            left_shape,
        ),
        in_specs=[hbm] * 10,
        out_specs=(vmem,) * 6,
        scratch_shapes=[
            number,
            number,
            number,
            number,
            pltpu.VMEM(station_pair.shape, jnp.int32),
            pltpu.VMEM((2 * TB, B_DEV), BF),
            pltpu.VMEM((8 * B_DEV, K), BF),
            dma((9,)),
            pltpu.VMEM((8 * SLOTS, K), BF),
            pltpu.VMEM((SLOTS, 128), F32),
            pltpu.VMEM((8 * SLOTS, K), BF),
            pltpu.VMEM((SLOTS, 128), F32),
            pltpu.VMEM((8 * SLOTS, K), F32),
            pltpu.VMEM((SLOTS, 2 * K), F32),
            pltpu.VMEM((32, K), F32),
            pltpu.VMEM((here, 4, S * S), BF),
            pltpu.VMEM((2, 4 * S, 128), F32),
            dma((n_vert,)),
            dma((4, 2)),
            dma((4, 2)),
            dma((PARTS,)),
            dma((PARTS,)),
            dma((n_x - 1, PARTS)),
            dma((n_x - 1, PARTS)),
            dma((n_x, PARTS)),
            dma((n_x, PARTS)),
        ],
        compiler_params=pltpu.CompilerParams(
            collective_id=0, has_side_effects=True, vmem_limit_bytes=20 << 20
        ),
    )(*(pltpu.with_memory_space_constraint(x, pltpu.HBM) for x in (
        heading.reshape(1, B_DEV), offset_u[None], offset_v[None], baseline[None],
        station_pair, tracks.transpose(1, 2, 0).reshape(2 * TB, B_DEV),
        visibilities.reshape(8 * B_DEV, K), screens,
        jnp.asarray(right_table()), jnp.asarray(left_table()),
    )))

    def grid(kernel, canvas, flops, *edges):
        return pl.pallas_call(
            kernel,
            out_shape=(canvas_shape, *edges),
            in_specs=[smem] + [vmem] * 5,
            out_specs=(vmem,) * (1 + len(edges)),
            input_output_aliases={5: 0},
            compiler_params=pltpu.CompilerParams(vmem_limit_bytes=12 << 20),
            cost_estimate=pl.CostEstimate(
                flops=flops, bytes_accessed=1 << 20, transcendentals=0
            ),
        )(listing, images, all_screens, right, left, canvas)

    canvas, edge_u, corner = grid(
        edge_u_kernel,
        canvas,
        10**9,
        jax.ShapeDtypeStruct((8, S, TV), BF),
        jax.ShapeDtypeStruct((8, S // 2, 128), BF),
    )
    got_u = lax.ppermute(edge_u, "au", [(i, (i + 1) % n_au) for i in range(n_au)])
    diagonal = [
        (u * n_vert + v, (u + 1) % n_au * n_vert + (v + 1) % n_vert)
        for u in range(n_au)
        for v in range(n_vert)
    ]
    got_c = lax.ppermute(corner, ("au", "vert"), diagonal)
    canvas, *edge_v = grid(
        edge_v_kernel, canvas, 4 * 10**9, *[jax.ShapeDtypeStruct((8 // V_SPLIT, TU // 2, 128), BF)] * V_SPLIT
    )
    got_v = [
        lax.ppermute(x, "vert", [(i, (i + 1) % n_vert) for i in range(n_vert)]) for x in edge_v
    ]
    (canvas,) = grid(late_kernel, canvas, 10**6)
    out = pl.pallas_call(
        finish_kernel,
        out_shape=jax.ShapeDtypeStruct((8, TU, TV), F32),
        in_specs=[vmem] * (3 + V_SPLIT),
        out_specs=pl.BlockSpec(memory_space=pl.ANY),
        scratch_shapes=[
            pltpu.VMEM((8, S, TV), F32),
            pltpu.VMEM((8, TU - S, 128), F32),
            dma((3,)),
        ],
        compiler_params=pltpu.CompilerParams(vmem_limit_bytes=8 << 20),
    )(canvas, got_u, got_c, *got_v)
    return out[None]


def solution(mesh):
    placed = (
        P(("au", "vert"), None, "ch"),
        P(("au", "vert"), None, None),
        P(("au", "vert")),
        P(("au", "vert")),
        P(("au", "vert"), None),
        P(("au", "vert")),
        P(),
        P("ch", None, None),
    )
    return jax.shard_map(
        body, mesh=mesh, in_specs=placed, out_specs=P("ch", None, "au", "vert"), check_vma=False
    )
```

```python
import math

import jax
import jax.numpy as jnp
import ml_dtypes
import numpy as np
from jax import lax
from jax.experimental import pallas as pl
from jax.experimental.pallas import tpu as pltpu
from jax.sharding import PartitionSpec as P

S = 64
CH_DEV = 32
TB = 8
K = TB * CH_DEV
B_DEV = 32
CAP = B_DEV // 4
SLOTS = 5 * CAP
TU = 256
TV = 256
ROWS = 72
AT_ONCE = 4
U_GROUPS = 3
V_GROUPS = 5
V_SPLIT = 2
RELAY_AT = (0, 2, 3, 5, 6, 8)
MESH = pl.DeviceIdType.MESH
BF = jnp.bfloat16
F32 = jnp.float32


def series(values, degree):
    nodes = (np.cos(np.pi * (np.arange(400) + 0.5) / 400) + 1.0) * 0.125
    fitted = np.polynomial.chebyshev.Chebyshev.fit(nodes, values(nodes), degree, domain=[0, 0.25])
    return [float(c) for c in fitted.convert(kind=np.polynomial.Polynomial).coef]


COS_COEF = series(lambda q: np.cos(2 * np.pi * np.sqrt(q)), 5)
SIN_COEF = series(lambda q: np.sin(2 * np.pi * np.sqrt(q)) / np.sqrt(q), 5)


def horner(coefs, q):
    total = jnp.full_like(q, coefs[-1])
    for c in coefs[-2::-1]:
        total = total * q + jnp.float32(c)
    return total


def dft_tables():
    centred = np.arange(S) - S // 2
    product = (centred[:, None] * centred[None, :]) % S
    angles = np.float32(2.0 * math.pi / S) * product.astype(np.float32)
    scale = np.float32(1.0 / math.sqrt(S))
    re = (np.cos(angles) * scale).astype(ml_dtypes.bfloat16).astype(np.float32)
    im = (-np.sin(angles) * scale).astype(ml_dtypes.bfloat16).astype(np.float32)
    return re, im


def right_table():
    re, im = dft_tables()
    norm = np.float32(1.0 / math.sqrt(K))
    table = np.zeros((2 * S, 128), np.float32)
    table[:S, :S] = re.T * norm
    table[S:, :S] = im.T * norm
    return table


def left_table():
    re, im = dft_tables()
    order = np.concatenate([np.arange(0, S, 2), np.arange(1, S, 2)])
    re, im = re[:, order], im[:, order]
    table = np.zeros((8, 2, ROWS, 2 * S), np.float32)
    for shift in range(8):
        table[shift, 0, shift : shift + S, :S] = re
        table[shift, 0, shift : shift + S, S:] = -im
        table[shift, 1, shift : shift + S, :S] = im
        table[shift, 1, shift : shift + S, S:] = re
    return table.reshape(8, 2 * ROWS, 2 * S).astype(ml_dtypes.bfloat16)


def swap_halves(x):
    return pltpu.roll(x, S, x.ndim - 1)


def arrange_station(raw, tall):
    value = raw.astype(F32)
    for i in range(S // 2):
        tall[8 * i : 8 * i + 4, :] = value[:, 128 * i : 128 * (i + 1)]
    lane = lax.broadcasted_iota(jnp.int32, (S // 2, 128), 1)
    feeds = []
    for f in range(2):
        re = tall[pl.ds(2 * f, S // 2, stride=8), :]
        im = tall[pl.ds(2 * f + 1, S // 2, stride=8), :]
        even = jnp.where(lane < S, re, swap_halves(im))
        odd = jnp.where(lane < S, swap_halves(re), im)
        feeds.append(jnp.concatenate([even, odd], axis=0).astype(BF))
    return feeds


def pack_blocks(head, off_u, off_v, base, pairs, track, data):
    heads = head[...]
    kind = lax.broadcasted_iota(jnp.int32, (8, B_DEV), 0)
    named = jnp.where(kind == heads, 1.0, 0.0)
    before = lax.broadcasted_iota(jnp.int32, (B_DEV, B_DEV), 0)
    after = lax.broadcasted_iota(jnp.int32, (B_DEV, B_DEV), 1)
    strict = jnp.where(before < after, 1.0, 0.0).astype(BF)
    counts = jnp.dot(named.astype(BF), strict, preferred_element_type=F32)
    rank = jnp.sum(named * counts, axis=0, keepdims=True)
    slot = heads.astype(F32) * CAP + rank
    which = lax.broadcasted_iota(jnp.int32, (SLOTS, B_DEV), 0).astype(F32)
    chosen = jnp.where(which == slot, 1.0, 0.0).astype(BF)

    label = lax.broadcasted_iota(jnp.int32, (pairs.shape[1], B_DEV), 0)
    listed = jnp.where(label == base[...], 1.0, 0.0).astype(BF)
    station = jnp.dot(pairs[...].astype(F32).astype(BF), listed, preferred_element_type=F32)
    rows = jnp.concatenate(
        [
            jnp.ones((1, B_DEV), F32),
            off_u[...].astype(F32),
            off_v[...].astype(F32),
            station,
            jnp.zeros((3, B_DEV), F32),
            track[...].astype(F32),
            jnp.zeros((128 - 8 - 2 * TB, B_DEV), F32),
        ],
        axis=0,
    ).astype(BF)
    dims = (((1,), (1,)), ((), ()))
    labels = lax.dot_general(chosen, rows, dims, preferred_element_type=F32)

    owner = lax.broadcasted_iota(jnp.int32, (B_DEV, 8 * B_DEV), 0)
    column = lax.broadcasted_iota(jnp.int32, (B_DEV, 8 * B_DEV), 1)
    widen = jnp.where(owner == column // 8, 1.0, 0.0).astype(BF)
    wide = jnp.dot(
        jnp.broadcast_to(slot, (8, B_DEV)).astype(BF), widen, preferred_element_type=F32
    )[:1]
    lane = lax.broadcasted_iota(jnp.int32, (1, 8 * B_DEV), 1) % 8
    place = wide * 8.0 + lane.astype(F32)
    target = lax.broadcasted_iota(jnp.int32, (8 * SLOTS, 8 * B_DEV), 0).astype(F32)
    moved = jnp.where(target == place, 1.0, 0.0).astype(BF)
    return jnp.dot(moved, data[...], preferred_element_type=F32).astype(BF), labels


def list_blocks(labels):
    dims = (((1,), (1,)), ((), ()))
    quantity = lax.broadcasted_iota(jnp.int32, (8, 128), 0)
    lane = lax.broadcasted_iota(jnp.int32, (8, 128), 1)
    pick = jnp.where(quantity == lane, 1.0, 0.0).astype(BF)
    rows = lax.dot_general(pick, labels.astype(BF), dims, preferred_element_type=F32)
    filled, at_u, at_v = rows[0:1], rows[1:2], rows[2:3]
    past_u = at_u > TU - S
    past = jnp.logical_or(past_u, at_v > TV - S)
    first = jnp.where(past_u, filled, 0.0)
    early = jnp.where(past, filled, 0.0)
    kind = lax.broadcasted_iota(jnp.int32, (8, SLOTS), 0)
    both = jnp.where(
        kind == 0,
        first,
        jnp.where(kind == 1, early - first, jnp.where(kind == 2, filled - early, 0.0)),
    )
    before = lax.broadcasted_iota(jnp.int32, (SLOTS, SLOTS), 0)
    after = lax.broadcasted_iota(jnp.int32, (SLOTS, SLOTS), 1)
    strict = jnp.where(before < after, 1.0, 0.0).astype(BF)
    ahead = jnp.dot(both.astype(BF), strict, preferred_element_type=F32)
    number_first = jnp.sum(first, axis=1, keepdims=True)
    number_early = jnp.sum(early, axis=1, keepdims=True)
    number = jnp.sum(filled, axis=1, keepdims=True)
    place = jnp.where(past, number_first + ahead[1:2], number_early + ahead[2:3])
    place = jnp.where(past_u, ahead[0:1], place)
    place = jnp.where(filled > 0.5, place, -1.0)
    target = lax.broadcasted_iota(jnp.int32, (128, SLOTS), 0).astype(F32)
    moved = jnp.where(target == place, 1.0, 0.0).astype(BF)
    slot = lax.broadcasted_iota(jnp.int32, (8, SLOTS), 1).astype(F32)
    rows = jnp.where(kind == 0, slot, rows)
    table = lax.dot_general(rows.astype(BF), moved, dims, preferred_element_type=F32)
    spare = jnp.where(lane.astype(F32) >= number, float(TU + S), 0.0)
    table = table + jnp.where(quantity == 1, spare, 0.0)
    groups = jnp.floor((number + (AT_ONCE - 1.0)) / AT_ONCE)
    ends = []
    for count, least in ((number_first, U_GROUPS), (number_early, V_GROUPS)):
        enough = jnp.minimum(groups, float(least))
        needed = jnp.floor((count + (AT_ONCE - 1.0)) / AT_ONCE)
        ends.append(jnp.maximum(needed, enough))
    for row, end in enumerate((*ends, groups)):
        table = jnp.where(quantity == 5 + row, end, table)
    return table.astype(jnp.int32)


def image_kernel(
    head_in, off_u_in, off_v_in, base_in, pairs_in, track_in, data_in, own_screens,
    right_in, left_in,
    images, screens, listing, canvas, right, left,
    head, off_u, off_v, base, pairs, track, data, in_sems,
    packed, labels, got_data, got_labels, samples, spread, mult, raw, tall,
    own_sems, send_sems, recv_sems, y_send, y_recv, x_send, x_recv, z_send, z_recv,
    xd_send, xd_recv, zd_send, zd_recv, c_send, c_recv,
):
    au, vert, band = (lax.axis_index(axis) for axis in ("au", "vert", "ch"))
    n_au, n_vert, n_ch = (lax.axis_size(axis) for axis in ("au", "vert", "ch"))
    here = own_screens.shape[0]
    quarter = here // n_vert // 4
    half = 2 * quarter
    side = lax.rem(au, 2)
    n_x = n_vert // 2

    def turned(step):
        return lax.rem(vert + step, n_vert)

    near = (
        {"au": lax.rem(au + 1, n_au)},
        {"au": lax.rem(au + n_au - 1, n_au)},
        {"vert": turned(1)},
        {"vert": turned(n_vert - 1)},
    )
    across = {"ch": lax.rem(band + 1, n_ch)}
    sibling = {"vert": vert + 1 - 2 * lax.rem(vert, 2)}
    along = {"au": au + 1 - 2 * side}
    beside = [{"vert": turned(2 * j)} for j in range(1, n_x)]

    inputs = (
        (head_in, head), (off_u_in, off_u), (off_v_in, off_v), (base_in, base),
        (pairs_in, pairs), (track_in, track), (data_in, data),
        (right_in, right), (left_in, left),
    )
    loads = [
        pltpu.make_async_copy(source, target, in_sems.at[j])
        for j, (source, target) in enumerate(inputs)
    ]
    for copy in loads:
        copy.start()
    fetches = []
    for j in range(2 * n_vert):
        rows = pl.ds(lax.rem(2 * vert + side + j, 2 * n_vert) * half, half)
        fetches.append(
            pltpu.make_async_copy(own_screens.at[rows], raw.at[rows], own_sems.at[j])
        )
        fetches[-1].start()
    barrier = pltpu.get_barrier_semaphore()
    for device in (*near, across, *beside):
        pl.semaphore_signal(barrier, inc=1, device_id=device, device_id_type=MESH)

    def arrange(first, number):
        def one(pair, carry):
            for i in range(2):
                station = lax.rem(first + 2 * pair + i, here)
                feeds = arrange_station(raw[station], tall.at[i])
                for f in range(2):
                    screens[station, f] = feeds[f]
            return carry

        lax.fori_loop(0, number // 2, one, 0)

    fetches[0].wait()
    arrange((2 * vert + side) * half, half)
    pl.semaphore_wait(barrier, 5 + len(beside))

    def moves(i):
        pairs_of = ((packed, got_data, 8 * CAP), (labels, got_labels, CAP))
        for j, (source, target, rows) in enumerate(pairs_of):
            where = pl.ds((i + 1) * rows, rows)
            yield pltpu.make_async_remote_copy(
                src_ref=source.at[where],
                dst_ref=target.at[where],
                send_sem=send_sems.at[i, j],
                recv_sem=recv_sems.at[i, j],
                device_id=near[i],
                device_id_type=MESH,
            )

    def send(number, count, send_sem, recv_sem, device, own=False):
        where = number * quarter
        return pltpu.make_async_remote_copy(
            src_ref=screens.at[pl.ds(where if own else here + where, count * quarter)],
            dst_ref=screens.at[pl.ds(here + where, count * quarter)],
            send_sem=send_sem,
            recv_sem=recv_sem,
            device_id=device,
            device_id_type=MESH,
        )

    def y_copy(k):
        return send(4 * vert + 2 * side + k, 1, y_send.at[k], y_recv.at[k], across, True)

    def x_copy(j, k, owner):
        at = (j - 1, k)
        return send(4 * owner + 2 * side + k, 1, x_send.at[at], x_recv.at[at], beside[j - 1])

    def z_copy(k, half_of):
        return send(4 * vert + 2 * half_of + k, 1, z_send.at[k], z_recv.at[k], along)

    def x_relay(j, owner):
        at = j - 1
        return send(4 * owner + 2 * other, 1, xd_send.at[at], xd_recv.at[at], beside[at])

    def z_relay(j, half_of):
        at = j - 1
        number = 4 * behind(j) + 2 * half_of + 1
        return send(number, 1, zd_send.at[at], zd_recv.at[at], along)

    def c_copy(j, k, owner):
        number = 4 * owner + (2 * side if k == 0 else 2 * other + k - 1)
        return send(number, 2 if k == 0 else 1, c_send.at[j, k], c_recv.at[j, k], sibling)

    def behind(j):
        return turned(n_vert - 2 * j)

    other = 1 - side
    for k in range(2):
        y_copy(k).start()

    for copy in loads[:7]:
        copy.wait()
    values, rows = pack_blocks(head, off_u, off_v, base, pairs, track, data)
    packed[...] = values
    labels[...] = rows

    for i in range(4):
        for copy in moves(i):
            copy.start()

    canvas[...] = jnp.zeros_like(canvas)
    for copy in fetches[1:]:
        copy.wait()
    arrange((2 * vert + side + 1) * half, here - half)

    row = lax.broadcasted_iota(jnp.int32, (32, K), 0)
    channel = band * CH_DEV + lax.broadcasted_iota(jnp.int32, (32, K), 1) % CH_DEV
    ratio = 1.0 + channel.astype(F32) / jnp.float32(2 * CH_DEV * n_ch)
    coarse = row - 8
    coarse_u = 16 * (coarse % 4) + coarse // 4 - S // 2
    fine_v = row - 16
    coarse_v = (row - 24) * 8 - S // 2
    step = jnp.where(
        row < 16, jnp.where(row < 8, 2 * row, coarse_u), jnp.where(row < 24, fine_v, coarse_v)
    )
    mult[...] = step.astype(F32) / S * ratio

    def widen(rows):
        source = lax.broadcasted_iota(jnp.int32, (128, 2 * K), 0)
        column = lax.broadcasted_iota(jnp.int32, (128, 2 * K), 1)
        chosen = jnp.where(source == 8 + column // CH_DEV, 1.0, 0.0).astype(BF)
        lane = lax.broadcasted_iota(jnp.int32, rows.shape, 1)
        only = jnp.where(lane < 8, 0.0, rows).astype(BF)
        return jnp.dot(only, chosen, preferred_element_type=F32)

    got_labels[:CAP] = labels[:CAP]
    samples[: 8 * CAP] = packed[: 8 * CAP].astype(F32)
    spread[:CAP] = widen(labels[:CAP])

    def block(slot):
        sample = samples[pl.ds(8 * slot, 8), :]
        track = spread[pl.ds(slot, 1), :]
        turns = jnp.concatenate(
            [track[:, :K] * mult[:16], track[:, K:] * mult[16:]], axis=0
        )
        frac = turns - jnp.floor(turns + 0.5)
        square = frac * frac
        cos = horner(COS_COEF, square)
        sin = horner(SIN_COEF, square) * frac

        def phasors(first):
            cos_fine, sin_fine = cos[first : first + 8], sin[first : first + 8]
            all_cos, all_sin = [], []
            for a in range(8):
                at = first + 8 + a
                cos_a, sin_a = cos[at : at + 1], sin[at : at + 1]
                all_cos.append(cos_fine * cos_a - sin_fine * sin_a)
                all_sin.append(sin_fine * cos_a + cos_fine * sin_a)
            return (
                jnp.concatenate(all_cos, axis=0).astype(BF),
                jnp.concatenate(all_sin, axis=0).astype(BF),
            )

        cos_u, sin_u = phasors(0)
        cos_v, sin_v = phasors(16)
        table = jnp.concatenate(
            [
                jnp.concatenate([cos_v, -sin_v], axis=1),
                jnp.concatenate([sin_v, cos_v], axis=1),
            ],
            axis=0,
        )

        def spread_row(r):
            row = jnp.broadcast_to(sample[r : r + 1], (16, K)).astype(BF)
            return jnp.concatenate([row] * (S // 16), axis=0)

        weighed = []
        for p in range(4):
            re, im = spread_row(2 * p), spread_row(2 * p + 1)
            weighed.append(
                jnp.concatenate([re * cos_u - im * sin_u, re * sin_u + im * cos_u], axis=1)
            )
        dims = (((1,), (1,)), ((), ()))
        image = lax.dot_general(
            jnp.concatenate(weighed, axis=0), table, dims, preferred_element_type=F32
        )
        return image.astype(BF)

    def relay(stage):
        if stage < 2:
            y_copy(stage).wait_recv()
            for j in range(1, n_x):
                x_copy(j, stage, vert).start()
            z_copy(stage, side).start()
            if stage == 1:
                c_copy(0, 0, vert).start()
        elif stage == 2:
            z_copy(0, other).wait_recv()
            for j in range(1, n_x):
                x_relay(j, vert).start()
            c_copy(0, 1, vert).start()
        elif stage == 3:
            for j in range(1, n_x):
                for k in range(2):
                    x_copy(j, k, behind(j)).wait_recv()
                z_relay(j, side).start()
                c_copy(j, 0, behind(j)).start()
        elif stage == 4:
            z_copy(1, other).wait_recv()
            c_copy(0, 2, vert).start()
        else:
            for j in range(1, n_x):
                x_relay(j, behind(j)).wait_recv()
                c_copy(j, 1, behind(j)).start()
                z_relay(j, other).wait_recv()
                c_copy(j, 2, behind(j)).start()

    def loop(group, carry):
        @pl.when(group == CAP // AT_ONCE)
        def _():
            for i in range(4):
                for copy in moves(i):
                    copy.wait_recv()
            samples[8 * CAP :] = got_data[8 * CAP :].astype(F32)
            spread[CAP:] = widen(got_labels[CAP:])

        for stage, at in enumerate(RELAY_AT):

            @pl.when(group == at)
            def _():
                relay(stage)

        made = [block(AT_ONCE * group + i) for i in range(AT_ONCE)]
        for i in range(AT_ONCE):
            images[AT_ONCE * group + i] = made[i]
        return carry

    lax.fori_loop(0, SLOTS // AT_ONCE, loop, 0)
    listing[...] = list_blocks(got_labels[...])
    for copy in loads[7:]:
        copy.wait()
    for i in range(4):
        for copy in moves(i):
            copy.wait_send()
    for k in range(2):
        y_copy(k).wait_send()
        z_copy(k, side).wait_send()
        for j in range(1, n_x):
            x_copy(j, k, vert).wait_send()
    for j in range(1, n_x):
        x_relay(j, vert).wait_send()
        z_relay(j, side).wait_send()
    for j in range(n_x):
        for k in range(3):
            c_copy(j, k, behind(j)).wait_send()
            mine = behind(j)
            c_copy(j, k, mine + 1 - 2 * lax.rem(mine, 2)).wait_recv()


def folded(x):
    middle = x.shape[1] // 2
    lane = lax.broadcasted_iota(jnp.int32, (1, 1, 128), 2)
    return jnp.where(lane < S, x[:, :middle], swap_halves(x[:, middle:])).astype(BF)


def edge_u_kernel(listing, images, screens, right, left, canvas_in, canvas, edge_u, corner):
    grid_blocks(images, screens, canvas, right, left, listing, 0, listing[5, 0])
    edge_u[...] = canvas[:, TU : TU + S, :TV].astype(BF)
    corner[...] = folded(canvas[:, TU : TU + S, TV:])


def edge_v_kernel(listing, images, screens, right, left, canvas_in, canvas, *edge_v):
    grid_blocks(images, screens, canvas, right, left, listing, listing[5, 0], listing[6, 0])
    each = 8 // V_SPLIT
    for i, edge in enumerate(edge_v):
        edge[...] = folded(canvas[i * each : (i + 1) * each, :TU, TV:])


def late_kernel(listing, images, screens, right, left, canvas_in, canvas):
    grid_blocks(images, screens, canvas, right, left, listing, listing[6, 0], listing[7, 0])


def grid_blocks(images, screens, canvas, right, left, listing, first, last):
    here = screens.shape[0] // 2
    band = lax.axis_index("ch")

    def screen_place(station):
        owner = station // here
        local = station - owner * here
        return jnp.where(owner == band, local, here + local)

    def block(index):
        slot = listing[0, index]
        off_u = listing[1, index]
        off_v = listing[2, index]
        one = screen_place(listing[3, index])
        two = screen_place(listing[4, index])
        two_s = [screens[two, f].astype(F32) for f in range(2)]
        fixed = []
        for f in range(2):
            one_s = screens[one, f].astype(F32)
            one_swapped = swap_halves(one_s)
            for e in range(2):
                p = 2 * f + e
                same = one_s * two_s[e]
                cross = one_swapped * two_s[e]
                gain_re = same + swap_halves(same)
                gain_im = swap_halves(cross) - cross
                part = images[slot, p * S : (p + 1) * S].astype(F32)
                fixed.append((part * gain_re + swap_halves(part) * gain_im).astype(BF))
        tile = off_v // 128
        shift = off_v - tile * 128
        moved = pltpu.roll(right[...], shift, 1).astype(BF)
        table_re, table_im = moved[:S], moved[S:]
        shifted = jnp.concatenate(
            [
                jnp.concatenate([table_re, -table_im], axis=0),
                jnp.concatenate([table_im, table_re], axis=0),
            ],
            axis=1,
        )
        half = jnp.dot(
            jnp.concatenate(fixed, axis=0), shifted, preferred_element_type=F32
        ).astype(BF)
        eighth = off_u // 8
        placed = left[off_u - eighth * 8]
        start_u = pl.multiple_of(eighth * 8, 8)
        start_v = pl.multiple_of(tile * 128, 128)
        return start_u, start_v, shift, placed, half

    lane = lax.broadcasted_iota(jnp.int32, (1, 128), 1)

    def loop(group, carry):
        ready = [block(AT_ONCE * group + i) for i in range(AT_ONCE)]
        for start_u, start_v, shift, placed, half in ready:
            for f in range(2):
                both = []
                for p in (2 * f, 2 * f + 1):
                    part = half[p * S : (p + 1) * S]
                    both.append(jnp.concatenate([part[:, :128], part[:, 128:]], axis=0))
                grid = jnp.dot(
                    placed, jnp.concatenate(both, axis=1), preferred_element_type=F32
                )
                for e in range(2):
                    for r in range(2):
                        cells = grid[r * ROWS : (r + 1) * ROWS, 128 * e : 128 * (e + 1)]
                        cells = jnp.concatenate(
                            [
                                jnp.where(lane >= shift, cells, 0.0),
                                jnp.where(lane < shift, cells, 0.0),
                            ],
                            axis=1,
                        )
                        where = (
                            4 * f + 2 * e + r, pl.ds(start_u, ROWS), pl.ds(start_v, 256)
                        )
                        canvas[where] += cells
        return carry

    lax.fori_loop(first, last, loop, 0)


def finish_kernel(canvas, got_u, got_c, *rest):
    *got_v, out, top, side, sems = rest
    rest = pltpu.make_async_copy(
        canvas.at[:, S:TU, 128:TV], out.at[:, S:, 128:], sems.at[2]
    )
    rest.start()
    lane = lax.broadcasted_iota(jnp.int32, (1, 1, 128), 2)

    def unfolded(x):
        x = x.astype(F32)
        low = jnp.where(lane < S, x, 0.0)
        high = jnp.where(lane < S, swap_halves(x), 0.0)
        return low, high

    low, high = unfolded(jnp.concatenate([x[...] for x in got_v], axis=0))
    first, second = unfolded(got_c[...])
    side[:, : TU // 2 - S] = canvas[:, S : TU // 2, :128] + low[:, S:]
    side[:, TU // 2 - S :] = canvas[:, TU // 2 : TU, :128] + high
    store_side = pltpu.make_async_copy(side, out.at[:, S:, :128], sems.at[1])
    store_side.start()
    top[...] = canvas[:, :S, :TV] + got_u[...].astype(F32)
    top[:, :, :128] += low[:, :S] + jnp.concatenate([first, second], axis=1)
    store_top = pltpu.make_async_copy(top, out.at[:, :S, :], sems.at[0])
    store_top.start()
    rest.wait()
    store_side.wait()
    store_top.wait()


def body(visibilities, tracks, offset_u, offset_v, heading, baseline, station_pair, screens):
    smem = pl.BlockSpec(memory_space=pltpu.SMEM)
    vmem = pl.BlockSpec(memory_space=pltpu.VMEM)
    hbm = pl.BlockSpec(memory_space=pltpu.HBM)
    n_au, n_vert = (lax.axis_size(axis) for axis in ("au", "vert"))
    n_x = n_vert // 2
    here = screens.shape[0]
    canvas_shape = jax.ShapeDtypeStruct((8, TU + S + ROWS, TV + 128), F32)
    right_shape = jax.ShapeDtypeStruct((2 * S, 128), F32)
    left_shape = jax.ShapeDtypeStruct((8, 2 * ROWS, 2 * S), BF)
    dma = pltpu.SemaphoreType.DMA
    number = pltpu.VMEM((1, B_DEV), jnp.int32)
    images, all_screens, listing, canvas, right, left = pl.pallas_call(
        image_kernel,
        out_shape=(
            jax.ShapeDtypeStruct((SLOTS, 4 * S, 2 * S), BF),
            jax.ShapeDtypeStruct((2 * here, 2, S, 2 * S), BF),
            jax.ShapeDtypeStruct((8, 128), jnp.int32),
            canvas_shape,
            right_shape,
            left_shape,
        ),
        in_specs=[hbm] * 10,
        out_specs=(vmem,) * 6,
        scratch_shapes=[
            number,
            number,
            number,
            number,
            pltpu.VMEM(station_pair.shape, jnp.int32),
            pltpu.VMEM((2 * TB, B_DEV), BF),
            pltpu.VMEM((8 * B_DEV, K), BF),
            dma((9,)),
            pltpu.VMEM((8 * SLOTS, K), BF),
            pltpu.VMEM((SLOTS, 128), F32),
            pltpu.VMEM((8 * SLOTS, K), BF),
            pltpu.VMEM((SLOTS, 128), F32),
            pltpu.VMEM((8 * SLOTS, K), F32),
            pltpu.VMEM((SLOTS, 2 * K), F32),
            pltpu.VMEM((32, K), F32),
            pltpu.VMEM((here, 4, S * S), BF),
            pltpu.VMEM((2, 4 * S, 128), F32),
            dma((2 * n_vert,)),
            dma((4, 2)),
            dma((4, 2)),
            dma((2,)),
            dma((2,)),
            dma((n_x - 1, 2)),
            dma((n_x - 1, 2)),
            dma((2,)),
            dma((2,)),
            dma((n_x - 1,)),
            dma((n_x - 1,)),
            dma((n_x - 1,)),
            dma((n_x - 1,)),
            dma((n_x, 3)),
            dma((n_x, 3)),
        ],
        compiler_params=pltpu.CompilerParams(
            collective_id=0, has_side_effects=True, vmem_limit_bytes=20 << 20
        ),
    )(*(pltpu.with_memory_space_constraint(x, pltpu.HBM) for x in (
        heading.reshape(1, B_DEV), offset_u[None], offset_v[None], baseline[None],
        station_pair, tracks.transpose(1, 2, 0).reshape(2 * TB, B_DEV),
        visibilities.reshape(8 * B_DEV, K), screens,
        jnp.asarray(right_table()), jnp.asarray(left_table()),
    )))

    def grid(kernel, canvas, flops, *edges):
        return pl.pallas_call(
            kernel,
            out_shape=(canvas_shape, *edges),
            in_specs=[smem] + [vmem] * 5,
            out_specs=(vmem,) * (1 + len(edges)),
            input_output_aliases={5: 0},
            compiler_params=pltpu.CompilerParams(vmem_limit_bytes=12 << 20),
            cost_estimate=pl.CostEstimate(
                flops=flops, bytes_accessed=1 << 20, transcendentals=0
            ),
        )(listing, images, all_screens, right, left, canvas)

    canvas, edge_u, corner = grid(
        edge_u_kernel,
        canvas,
        10**9,
        jax.ShapeDtypeStruct((8, S, TV), BF),
        jax.ShapeDtypeStruct((8, S // 2, 128), BF),
    )
    got_u = lax.ppermute(edge_u, "au", [(i, (i + 1) % n_au) for i in range(n_au)])
    diagonal = [
        (u * n_vert + v, (u + 1) % n_au * n_vert + (v + 1) % n_vert)
        for u in range(n_au)
        for v in range(n_vert)
    ]
    got_c = lax.ppermute(corner, ("au", "vert"), diagonal)
    canvas, *edge_v = grid(
        edge_v_kernel, canvas, 4 * 10**9, *[jax.ShapeDtypeStruct((8 // V_SPLIT, TU // 2, 128), BF)] * V_SPLIT
    )
    got_v = [
        lax.ppermute(x, "vert", [(i, (i + 1) % n_vert) for i in range(n_vert)]) for x in edge_v
    ]
    (canvas,) = grid(late_kernel, canvas, 10**6)
    out = pl.pallas_call(
        finish_kernel,
        out_shape=jax.ShapeDtypeStruct((8, TU, TV), F32),
        in_specs=[vmem] * (3 + V_SPLIT),
        out_specs=pl.BlockSpec(memory_space=pl.ANY),
        scratch_shapes=[
            pltpu.VMEM((8, S, TV), F32),
            pltpu.VMEM((8, TU - S, 128), F32),
            dma((3,)),
        ],
        compiler_params=pltpu.CompilerParams(vmem_limit_bytes=8 << 20),
    )(canvas, got_u, got_c, *got_v)
    return out[None]


def solution(mesh):
    placed = (
        P(("au", "vert"), None, "ch"),
        P(("au", "vert"), None, None),
        P(("au", "vert")),
        P(("au", "vert")),
        P(("au", "vert"), None),
        P(("au", "vert")),
        P(),
        P("ch", None, None),
    )
    return jax.shard_map(
        body, mesh=mesh, in_specs=placed, out_specs=P("ch", None, "au", "vert"), check_vma=False
    )
```

```python
import math

import jax
import jax.numpy as jnp
import ml_dtypes
import numpy as np
from jax import lax
from jax.experimental import pallas as pl
from jax.experimental.pallas import tpu as pltpu
from jax.sharding import PartitionSpec as P

S = 64
CH_DEV = 32
TB = 8
K = TB * CH_DEV
B_DEV = 32
CAP = B_DEV // 4
SLOTS = 5 * CAP
TU = 256
TV = 256
ROWS = 72
AT_ONCE = 4
U_GROUPS = 3
V_GROUPS = 5
V_SPLIT = 2
RELAY_AT = (0, 1, 3, 4, 6, 8)
MESH = pl.DeviceIdType.MESH
BF = jnp.bfloat16
F32 = jnp.float32


def series(values, degree):
    nodes = (np.cos(np.pi * (np.arange(400) + 0.5) / 400) + 1.0) * 0.125
    fitted = np.polynomial.chebyshev.Chebyshev.fit(nodes, values(nodes), degree, domain=[0, 0.25])
    return [float(c) for c in fitted.convert(kind=np.polynomial.Polynomial).coef]


COS_COEF = series(lambda q: np.cos(2 * np.pi * np.sqrt(q)), 5)
SIN_COEF = series(lambda q: np.sin(2 * np.pi * np.sqrt(q)) / np.sqrt(q), 5)


def horner(coefs, q):
    total = jnp.full_like(q, coefs[-1])
    for c in coefs[-2::-1]:
        total = total * q + jnp.float32(c)
    return total


def dft_tables():
    centred = np.arange(S) - S // 2
    product = (centred[:, None] * centred[None, :]) % S
    angles = np.float32(2.0 * math.pi / S) * product.astype(np.float32)
    scale = np.float32(1.0 / math.sqrt(S))
    re = (np.cos(angles) * scale).astype(ml_dtypes.bfloat16).astype(np.float32)
    im = (-np.sin(angles) * scale).astype(ml_dtypes.bfloat16).astype(np.float32)
    return re, im


def right_table():
    re, im = dft_tables()
    norm = np.float32(1.0 / math.sqrt(K))
    table = np.zeros((2 * S, 128), np.float32)
    table[:S, :S] = re.T * norm
    table[S:, :S] = im.T * norm
    return table


def left_table():
    re, im = dft_tables()
    order = np.concatenate([np.arange(0, S, 2), np.arange(1, S, 2)])
    re, im = re[:, order], im[:, order]
    table = np.zeros((8, 2, ROWS, 2 * S), np.float32)
    for shift in range(8):
        table[shift, 0, shift : shift + S, :S] = re
        table[shift, 0, shift : shift + S, S:] = -im
        table[shift, 1, shift : shift + S, :S] = im
        table[shift, 1, shift : shift + S, S:] = re
    return table.reshape(8, 2 * ROWS, 2 * S).astype(ml_dtypes.bfloat16)


def swap_halves(x):
    return pltpu.roll(x, S, x.ndim - 1)


def arrange_station(raw, tall):
    value = raw.astype(F32)
    for i in range(S // 2):
        tall[8 * i : 8 * i + 4, :] = value[:, 128 * i : 128 * (i + 1)]
    lane = lax.broadcasted_iota(jnp.int32, (S // 2, 128), 1)
    feeds = []
    for f in range(2):
        re = tall[pl.ds(2 * f, S // 2, stride=8), :]
        im = tall[pl.ds(2 * f + 1, S // 2, stride=8), :]
        even = jnp.where(lane < S, re, swap_halves(im))
        odd = jnp.where(lane < S, swap_halves(re), im)
        feeds.append(jnp.concatenate([even, odd], axis=0).astype(BF))
    return feeds


def pack_blocks(head, off_u, off_v, base, pairs, track, data):
    heads = head[...]
    kind = lax.broadcasted_iota(jnp.int32, (8, B_DEV), 0)
    named = jnp.where(kind == heads, 1.0, 0.0)
    before = lax.broadcasted_iota(jnp.int32, (B_DEV, B_DEV), 0)
    after = lax.broadcasted_iota(jnp.int32, (B_DEV, B_DEV), 1)
    strict = jnp.where(before < after, 1.0, 0.0).astype(BF)
    counts = jnp.dot(named.astype(BF), strict, preferred_element_type=F32)
    rank = jnp.sum(named * counts, axis=0, keepdims=True)
    slot = heads.astype(F32) * CAP + rank
    which = lax.broadcasted_iota(jnp.int32, (SLOTS, B_DEV), 0).astype(F32)
    chosen = jnp.where(which == slot, 1.0, 0.0).astype(BF)

    label = lax.broadcasted_iota(jnp.int32, (pairs.shape[1], B_DEV), 0)
    listed = jnp.where(label == base[...], 1.0, 0.0).astype(BF)
    station = jnp.dot(pairs[...].astype(F32).astype(BF), listed, preferred_element_type=F32)
    rows = jnp.concatenate(
        [
            jnp.ones((1, B_DEV), F32),
            off_u[...].astype(F32),
            off_v[...].astype(F32),
            station,
            jnp.zeros((3, B_DEV), F32),
            track[...].astype(F32),
            jnp.zeros((128 - 8 - 2 * TB, B_DEV), F32),
        ],
        axis=0,
    ).astype(BF)
    dims = (((1,), (1,)), ((), ()))
    labels = lax.dot_general(chosen, rows, dims, preferred_element_type=F32)

    owner = lax.broadcasted_iota(jnp.int32, (B_DEV, 8 * B_DEV), 0)
    column = lax.broadcasted_iota(jnp.int32, (B_DEV, 8 * B_DEV), 1)
    widen = jnp.where(owner == column // 8, 1.0, 0.0).astype(BF)
    wide = jnp.dot(
        jnp.broadcast_to(slot, (8, B_DEV)).astype(BF), widen, preferred_element_type=F32
    )[:1]
    lane = lax.broadcasted_iota(jnp.int32, (1, 8 * B_DEV), 1) % 8
    place = wide * 8.0 + lane.astype(F32)
    target = lax.broadcasted_iota(jnp.int32, (8 * SLOTS, 8 * B_DEV), 0).astype(F32)
    moved = jnp.where(target == place, 1.0, 0.0).astype(BF)
    return jnp.dot(moved, data[...], preferred_element_type=F32).astype(BF), labels


def list_blocks(labels):
    dims = (((1,), (1,)), ((), ()))
    quantity = lax.broadcasted_iota(jnp.int32, (8, 128), 0)
    lane = lax.broadcasted_iota(jnp.int32, (8, 128), 1)
    pick = jnp.where(quantity == lane, 1.0, 0.0).astype(BF)
    rows = lax.dot_general(pick, labels.astype(BF), dims, preferred_element_type=F32)
    filled, at_u, at_v = rows[0:1], rows[1:2], rows[2:3]
    past_u = at_u > TU - S
    past = jnp.logical_or(past_u, at_v > TV - S)
    first = jnp.where(past_u, filled, 0.0)
    early = jnp.where(past, filled, 0.0)
    kind = lax.broadcasted_iota(jnp.int32, (8, SLOTS), 0)
    both = jnp.where(
        kind == 0,
        first,
        jnp.where(kind == 1, early - first, jnp.where(kind == 2, filled - early, 0.0)),
    )
    before = lax.broadcasted_iota(jnp.int32, (SLOTS, SLOTS), 0)
    after = lax.broadcasted_iota(jnp.int32, (SLOTS, SLOTS), 1)
    strict = jnp.where(before < after, 1.0, 0.0).astype(BF)
    ahead = jnp.dot(both.astype(BF), strict, preferred_element_type=F32)
    number_first = jnp.sum(first, axis=1, keepdims=True)
    number_early = jnp.sum(early, axis=1, keepdims=True)
    number = jnp.sum(filled, axis=1, keepdims=True)
    place = jnp.where(past, number_first + ahead[1:2], number_early + ahead[2:3])
    place = jnp.where(past_u, ahead[0:1], place)
    place = jnp.where(filled > 0.5, place, -1.0)
    target = lax.broadcasted_iota(jnp.int32, (128, SLOTS), 0).astype(F32)
    moved = jnp.where(target == place, 1.0, 0.0).astype(BF)
    slot = lax.broadcasted_iota(jnp.int32, (8, SLOTS), 1).astype(F32)
    rows = jnp.where(kind == 0, slot, rows)
    table = lax.dot_general(rows.astype(BF), moved, dims, preferred_element_type=F32)
    spare = jnp.where(lane.astype(F32) >= number, float(TU + S), 0.0)
    table = table + jnp.where(quantity == 1, spare, 0.0)
    groups = jnp.floor((number + (AT_ONCE - 1.0)) / AT_ONCE)
    ends = []
    for count, least in ((number_first, U_GROUPS), (number_early, V_GROUPS)):
        enough = jnp.minimum(groups, float(least))
        needed = jnp.floor((count + (AT_ONCE - 1.0)) / AT_ONCE)
        ends.append(jnp.maximum(needed, enough))
    for row, end in enumerate((*ends, groups)):
        table = jnp.where(quantity == 5 + row, end, table)
    return table.astype(jnp.int32)


def image_kernel(
    head_in, off_u_in, off_v_in, base_in, pairs_in, track_in, data_in, own_screens,
    right_in, left_in,
    images, screens, listing, canvas, right, left,
    head, off_u, off_v, base, pairs, track, data, in_sems,
    packed, labels, got_data, got_labels, samples, spread, mult, raw, tall,
    own_sems, send_sems, recv_sems, y_send, y_recv, relay_send, relay_recv, c_send, c_recv,
):
    au, vert, band = (lax.axis_index(axis) for axis in ("au", "vert", "ch"))
    n_au, n_vert, n_ch = (lax.axis_size(axis) for axis in ("au", "vert", "ch"))
    here = own_screens.shape[0]
    chunk = here // 16
    core = lax.rem(vert, 2)
    colour = lax.rem(vert // 2 + au, 2)
    mine = 8 * core + 4 * colour
    others = 8 * core + 4 * (1 - colour)

    def turned(step):
        return lax.rem(vert + step, n_vert)

    near = (
        {"au": lax.rem(au + 1, n_au)},
        {"au": lax.rem(au + n_au - 1, n_au)},
        {"vert": turned(1)},
        {"vert": turned(n_vert - 1)},
    )
    across = {"ch": lax.rem(band + 1, n_ch)}
    sibling = {"vert": vert + 1 - 2 * core}
    beside = {"vert": vert + 2 - 4 * lax.rem(vert // 2, 2)}
    along = {"au": au + 1 - 2 * lax.rem(au, 2)}

    inputs = (
        (head_in, head), (off_u_in, off_u), (off_v_in, off_v), (base_in, base),
        (pairs_in, pairs), (track_in, track), (data_in, data),
        (right_in, right), (left_in, left),
    )
    loads = [
        pltpu.make_async_copy(source, target, in_sems.at[j])
        for j, (source, target) in enumerate(inputs)
    ]
    for copy in loads:
        copy.start()
    fetches = []
    for j in range(4):
        rows = pl.ds(lax.rem(mine + 4 * j, 16) * chunk, 4 * chunk)
        fetches.append(
            pltpu.make_async_copy(own_screens.at[rows], raw.at[rows], own_sems.at[j])
        )
        fetches[-1].start()
    barrier = pltpu.get_barrier_semaphore()
    for device in (*near, across, beside):
        pl.semaphore_signal(barrier, inc=1, device_id=device, device_id_type=MESH)

    def arrange(first, number):
        def one(pair, carry):
            for i in range(2):
                station = lax.rem(first + 2 * pair + i, here)
                feeds = arrange_station(raw[station], tall.at[i])
                for f in range(2):
                    screens[station, f] = feeds[f]
            return carry

        lax.fori_loop(0, number // 2, one, 0)

    fetches[0].wait()
    arrange(mine * chunk, 4 * chunk)
    pl.semaphore_wait(barrier, 6)

    def moves(i):
        pairs_of = ((packed, got_data, 8 * CAP), (labels, got_labels, CAP))
        for j, (source, target, rows) in enumerate(pairs_of):
            where = pl.ds((i + 1) * rows, rows)
            yield pltpu.make_async_remote_copy(
                src_ref=source.at[where],
                dst_ref=target.at[where],
                send_sem=send_sems.at[i, j],
                recv_sem=recv_sems.at[i, j],
                device_id=near[i],
                device_id_type=MESH,
            )

    def send(number, count, send_sem, recv_sem, device, own=False):
        where = number * chunk
        return pltpu.make_async_remote_copy(
            src_ref=screens.at[pl.ds(where if own else here + where, count * chunk)],
            dst_ref=screens.at[pl.ds(here + where, count * chunk)],
            send_sem=send_sem,
            recv_sem=recv_sem,
            device_id=device,
            device_id_type=MESH,
        )

    def y_copy(k):
        return send(mine + k, 1, y_send.at[k], y_recv.at[k], across, True)

    def relayed(k, first):
        device = beside if k % 2 == 0 else along
        return send(first + k, 1, relay_send.at[k], relay_recv.at[k], device)

    def c_copy(k, first):
        return send(first + 2 * (k % 2), 2, c_send.at[k], c_recv.at[k], sibling)

    for k in range(4):
        y_copy(k).start()

    for copy in loads[:7]:
        copy.wait()
    values, rows = pack_blocks(head, off_u, off_v, base, pairs, track, data)
    packed[...] = values
    labels[...] = rows

    for i in range(4):
        for copy in moves(i):
            copy.start()

    canvas[...] = jnp.zeros_like(canvas)
    for copy in fetches[1:]:
        copy.wait()
    arrange((mine + 4) * chunk, here - 4 * chunk)

    row = lax.broadcasted_iota(jnp.int32, (32, K), 0)
    channel = band * CH_DEV + lax.broadcasted_iota(jnp.int32, (32, K), 1) % CH_DEV
    ratio = 1.0 + channel.astype(F32) / jnp.float32(2 * CH_DEV * n_ch)
    coarse = row - 8
    coarse_u = 16 * (coarse % 4) + coarse // 4 - S // 2
    fine_v = row - 16
    coarse_v = (row - 24) * 8 - S // 2
    step = jnp.where(
        row < 16, jnp.where(row < 8, 2 * row, coarse_u), jnp.where(row < 24, fine_v, coarse_v)
    )
    mult[...] = step.astype(F32) / S * ratio

    def widen(rows):
        source = lax.broadcasted_iota(jnp.int32, (128, 2 * K), 0)
        column = lax.broadcasted_iota(jnp.int32, (128, 2 * K), 1)
        chosen = jnp.where(source == 8 + column // CH_DEV, 1.0, 0.0).astype(BF)
        lane = lax.broadcasted_iota(jnp.int32, rows.shape, 1)
        only = jnp.where(lane < 8, 0.0, rows).astype(BF)
        return jnp.dot(only, chosen, preferred_element_type=F32)

    got_labels[:CAP] = labels[:CAP]
    samples[: 8 * CAP] = packed[: 8 * CAP].astype(F32)
    spread[:CAP] = widen(labels[:CAP])

    def block(slot):
        sample = samples[pl.ds(8 * slot, 8), :]
        track = spread[pl.ds(slot, 1), :]
        turns = jnp.concatenate(
            [track[:, :K] * mult[:16], track[:, K:] * mult[16:]], axis=0
        )
        frac = turns - jnp.floor(turns + 0.5)
        square = frac * frac
        cos = horner(COS_COEF, square)
        sin = horner(SIN_COEF, square) * frac

        def phasors(first):
            cos_fine, sin_fine = cos[first : first + 8], sin[first : first + 8]
            all_cos, all_sin = [], []
            for a in range(8):
                at = first + 8 + a
                cos_a, sin_a = cos[at : at + 1], sin[at : at + 1]
                all_cos.append(cos_fine * cos_a - sin_fine * sin_a)
                all_sin.append(sin_fine * cos_a + cos_fine * sin_a)
            return (
                jnp.concatenate(all_cos, axis=0).astype(BF),
                jnp.concatenate(all_sin, axis=0).astype(BF),
            )

        cos_u, sin_u = phasors(0)
        cos_v, sin_v = phasors(16)
        table = jnp.concatenate(
            [
                jnp.concatenate([cos_v, -sin_v], axis=1),
                jnp.concatenate([sin_v, cos_v], axis=1),
            ],
            axis=0,
        )

        def spread_row(r):
            row = jnp.broadcast_to(sample[r : r + 1], (16, K)).astype(BF)
            return jnp.concatenate([row] * (S // 16), axis=0)

        weighed = []
        for p in range(4):
            re, im = spread_row(2 * p), spread_row(2 * p + 1)
            weighed.append(
                jnp.concatenate([re * cos_u - im * sin_u, re * sin_u + im * cos_u], axis=1)
            )
        dims = (((1,), (1,)), ((), ()))
        image = lax.dot_general(
            jnp.concatenate(weighed, axis=0), table, dims, preferred_element_type=F32
        )
        return image.astype(BF)

    def relay(stage):
        if stage < 4:
            y_copy(stage).wait_recv()
            relayed(stage, mine).start()
            if stage % 2 == 1:
                c_copy(stage // 2, mine).start()
        else:
            for k in (2 * stage - 8, 2 * stage - 7):
                relayed(k, others).wait_recv()
            c_copy(stage - 2, others).start()

    def loop(group, carry):
        @pl.when(group == CAP // AT_ONCE)
        def _():
            for i in range(4):
                for copy in moves(i):
                    copy.wait_recv()
            samples[8 * CAP :] = got_data[8 * CAP :].astype(F32)
            spread[CAP:] = widen(got_labels[CAP:])

        for stage, at in enumerate(RELAY_AT):

            @pl.when(group == at)
            def _():
                relay(stage)

        made = [block(AT_ONCE * group + i) for i in range(AT_ONCE)]
        for i in range(AT_ONCE):
            images[AT_ONCE * group + i] = made[i]
        return carry

    lax.fori_loop(0, SLOTS // AT_ONCE, loop, 0)
    listing[...] = list_blocks(got_labels[...])
    for copy in loads[7:]:
        copy.wait()
    for i in range(4):
        for copy in moves(i):
            copy.wait_send()
    for k in range(4):
        y_copy(k).wait_send()
        relayed(k, mine).wait_send()
        first = mine if k < 2 else others
        c_copy(k, first).wait_send()
        c_copy(k, first + 8 - 16 * core).wait_recv()


def folded(x):
    middle = x.shape[1] // 2
    lane = lax.broadcasted_iota(jnp.int32, (1, 1, 128), 2)
    return jnp.where(lane < S, x[:, :middle], swap_halves(x[:, middle:])).astype(BF)


def edge_u_kernel(listing, images, screens, right, left, canvas_in, canvas, edge_u, corner):
    grid_blocks(images, screens, canvas, right, left, listing, 0, listing[5, 0])
    edge_u[...] = canvas[:, TU : TU + S, :TV].astype(BF)
    corner[...] = canvas[:, TU : TU + S, TV:].astype(BF)


def edge_v_kernel(listing, images, screens, right, left, canvas_in, canvas, *edge_v):
    grid_blocks(images, screens, canvas, right, left, listing, listing[5, 0], listing[6, 0])
    each = 8 // V_SPLIT
    for i, edge in enumerate(edge_v):
        edge[...] = folded(canvas[i * each : (i + 1) * each, :TU, TV:])


def late_kernel(listing, images, screens, right, left, canvas_in, canvas):
    grid_blocks(images, screens, canvas, right, left, listing, listing[6, 0], listing[7, 0])


def grid_blocks(images, screens, canvas, right, left, listing, first, last):
    here = screens.shape[0] // 2
    band = lax.axis_index("ch")

    def screen_place(station):
        owner = station // here
        local = station - owner * here
        return jnp.where(owner == band, local, here + local)

    def block(index):
        slot = listing[0, index]
        off_u = listing[1, index]
        off_v = listing[2, index]
        one = screen_place(listing[3, index])
        two = screen_place(listing[4, index])
        two_s = [screens[two, f].astype(F32) for f in range(2)]
        fixed = []
        for f in range(2):
            one_s = screens[one, f].astype(F32)
            one_swapped = swap_halves(one_s)
            for e in range(2):
                p = 2 * f + e
                same = one_s * two_s[e]
                cross = one_swapped * two_s[e]
                gain_re = same + swap_halves(same)
                gain_im = swap_halves(cross) - cross
                part = images[slot, p * S : (p + 1) * S].astype(F32)
                fixed.append((part * gain_re + swap_halves(part) * gain_im).astype(BF))
        tile = off_v // 128
        shift = off_v - tile * 128
        moved = pltpu.roll(right[...], shift, 1).astype(BF)
        table_re, table_im = moved[:S], moved[S:]
        shifted = jnp.concatenate(
            [
                jnp.concatenate([table_re, -table_im], axis=0),
                jnp.concatenate([table_im, table_re], axis=0),
            ],
            axis=1,
        )
        half = jnp.dot(
            jnp.concatenate(fixed, axis=0), shifted, preferred_element_type=F32
        ).astype(BF)
        eighth = off_u // 8
        placed = left[off_u - eighth * 8]
        start_u = pl.multiple_of(eighth * 8, 8)
        start_v = pl.multiple_of(tile * 128, 128)
        return start_u, start_v, shift, placed, half

    lane = lax.broadcasted_iota(jnp.int32, (1, 128), 1)

    def loop(group, carry):
        ready = [block(AT_ONCE * group + i) for i in range(AT_ONCE)]
        for start_u, start_v, shift, placed, half in ready:
            for f in range(2):
                both = []
                for p in (2 * f, 2 * f + 1):
                    part = half[p * S : (p + 1) * S]
                    both.append(jnp.concatenate([part[:, :128], part[:, 128:]], axis=0))
                grid = jnp.dot(
                    placed, jnp.concatenate(both, axis=1), preferred_element_type=F32
                )
                for e in range(2):
                    for r in range(2):
                        cells = grid[r * ROWS : (r + 1) * ROWS, 128 * e : 128 * (e + 1)]
                        cells = jnp.concatenate(
                            [
                                jnp.where(lane >= shift, cells, 0.0),
                                jnp.where(lane < shift, cells, 0.0),
                            ],
                            axis=1,
                        )
                        where = (
                            4 * f + 2 * e + r, pl.ds(start_u, ROWS), pl.ds(start_v, 256)
                        )
                        canvas[where] += cells
        return carry

    lax.fori_loop(first, last, loop, 0)


def finish_kernel(canvas, got_u, got_c, *rest):
    *got_v, out, top, side, sems = rest
    rest = pltpu.make_async_copy(
        canvas.at[:, S:TU, 128:TV], out.at[:, S:, 128:], sems.at[2]
    )
    rest.start()
    lane = lax.broadcasted_iota(jnp.int32, (1, 1, 128), 2)

    def unfolded(x):
        x = x.astype(F32)
        low = jnp.where(lane < S, x, 0.0)
        high = jnp.where(lane < S, swap_halves(x), 0.0)
        return low, high

    low, high = unfolded(jnp.concatenate([x[...] for x in got_v], axis=0))
    side[:, : TU // 2 - S] = canvas[:, S : TU // 2, :128] + low[:, S:]
    side[:, TU // 2 - S :] = canvas[:, TU // 2 : TU, :128] + high
    store_side = pltpu.make_async_copy(side, out.at[:, S:, :128], sems.at[1])
    store_side.start()
    top[...] = canvas[:, :S, :TV] + got_u[...].astype(F32)
    top[:, :, :128] += low[:, :S] + got_c[...].astype(F32)
    store_top = pltpu.make_async_copy(top, out.at[:, :S, :], sems.at[0])
    store_top.start()
    rest.wait()
    store_side.wait()
    store_top.wait()


def body(visibilities, tracks, offset_u, offset_v, heading, baseline, station_pair, screens):
    smem = pl.BlockSpec(memory_space=pltpu.SMEM)
    vmem = pl.BlockSpec(memory_space=pltpu.VMEM)
    hbm = pl.BlockSpec(memory_space=pltpu.HBM)
    n_au, n_vert = (lax.axis_size(axis) for axis in ("au", "vert"))
    here = screens.shape[0]
    canvas_shape = jax.ShapeDtypeStruct((8, TU + S + ROWS, TV + 128), F32)
    right_shape = jax.ShapeDtypeStruct((2 * S, 128), F32)
    left_shape = jax.ShapeDtypeStruct((8, 2 * ROWS, 2 * S), BF)
    dma = pltpu.SemaphoreType.DMA
    number = pltpu.VMEM((1, B_DEV), jnp.int32)
    images, all_screens, listing, canvas, right, left = pl.pallas_call(
        image_kernel,
        out_shape=(
            jax.ShapeDtypeStruct((SLOTS, 4 * S, 2 * S), BF),
            jax.ShapeDtypeStruct((2 * here, 2, S, 2 * S), BF),
            jax.ShapeDtypeStruct((8, 128), jnp.int32),
            canvas_shape,
            right_shape,
            left_shape,
        ),
        in_specs=[hbm] * 10,
        out_specs=(vmem,) * 6,
        scratch_shapes=[
            number,
            number,
            number,
            number,
            pltpu.VMEM(station_pair.shape, jnp.int32),
            pltpu.VMEM((2 * TB, B_DEV), BF),
            pltpu.VMEM((8 * B_DEV, K), BF),
            dma((9,)),
            pltpu.VMEM((8 * SLOTS, K), BF),
            pltpu.VMEM((SLOTS, 128), F32),
            pltpu.VMEM((8 * SLOTS, K), BF),
            pltpu.VMEM((SLOTS, 128), F32),
            pltpu.VMEM((8 * SLOTS, K), F32),
            pltpu.VMEM((SLOTS, 2 * K), F32),
            pltpu.VMEM((32, K), F32),
            pltpu.VMEM((here, 4, S * S), BF),
            pltpu.VMEM((2, 4 * S, 128), F32),
            dma((4,)),
            dma((4, 2)),
            dma((4, 2)),
            dma((4,)),
            dma((4,)),
            dma((4,)),
            dma((4,)),
            dma((4,)),
            dma((4,)),
        ],
        compiler_params=pltpu.CompilerParams(
            collective_id=0, has_side_effects=True, vmem_limit_bytes=20 << 20
        ),
    )(*(pltpu.with_memory_space_constraint(x, pltpu.HBM) for x in (
        heading.reshape(1, B_DEV), offset_u[None], offset_v[None], baseline[None],
        station_pair, tracks.transpose(1, 2, 0).reshape(2 * TB, B_DEV),
        visibilities.reshape(8 * B_DEV, K), screens,
        jnp.asarray(right_table()), jnp.asarray(left_table()),
    )))

    def grid(kernel, canvas, flops, *edges):
        return pl.pallas_call(
            kernel,
            out_shape=(canvas_shape, *edges),
            in_specs=[smem] + [vmem] * 5,
            out_specs=(vmem,) * (1 + len(edges)),
            input_output_aliases={5: 0},
            compiler_params=pltpu.CompilerParams(vmem_limit_bytes=12 << 20),
            cost_estimate=pl.CostEstimate(
                flops=flops, bytes_accessed=1 << 20, transcendentals=0
            ),
        )(listing, images, all_screens, right, left, canvas)

    canvas, edge_u, corner = grid(
        edge_u_kernel,
        canvas,
        10**9,
        jax.ShapeDtypeStruct((8, S, TV), BF),
        jax.ShapeDtypeStruct((8, S, 128), BF),
    )
    got_u = lax.ppermute(edge_u, "au", [(i, (i + 1) % n_au) for i in range(n_au)])
    diagonal = [
        (u * n_vert + v, (u + 1) % n_au * n_vert + (v + 1) % n_vert)
        for u in range(n_au)
        for v in range(n_vert)
    ]
    got_c = lax.ppermute(corner, ("au", "vert"), diagonal)
    canvas, *edge_v = grid(
        edge_v_kernel, canvas, 4 * 10**9, *[jax.ShapeDtypeStruct((8 // V_SPLIT, TU // 2, 128), BF)] * V_SPLIT
    )
    got_v = [
        lax.ppermute(x, "vert", [(i, (i + 1) % n_vert) for i in range(n_vert)]) for x in edge_v
    ]
    (canvas,) = grid(late_kernel, canvas, 10**6)
    out = pl.pallas_call(
        finish_kernel,
        out_shape=jax.ShapeDtypeStruct((8, TU, TV), F32),
        in_specs=[vmem] * (3 + V_SPLIT),
        out_specs=pl.BlockSpec(memory_space=pl.ANY),
        scratch_shapes=[
            pltpu.VMEM((8, S, TV), F32),
            pltpu.VMEM((8, TU - S, 128), F32),
            dma((3,)),
        ],
        compiler_params=pltpu.CompilerParams(vmem_limit_bytes=8 << 20),
    )(canvas, got_u, got_c, *got_v)
    return out[None]


def solution(mesh):
    placed = (
        P(("au", "vert"), None, "ch"),
        P(("au", "vert"), None, None),
        P(("au", "vert")),
        P(("au", "vert")),
        P(("au", "vert"), None),
        P(("au", "vert")),
        P(),
        P("ch", None, None),
    )
    return jax.shard_map(
        body, mesh=mesh, in_specs=placed, out_specs=P("ch", None, "au", "vert"), check_vma=False
    )
```

```python
import math

import jax
import jax.numpy as jnp
import ml_dtypes
import numpy as np
from jax import lax
from jax.experimental import pallas as pl
from jax.experimental.pallas import tpu as pltpu
from jax.sharding import PartitionSpec as P

S = 64
CH_DEV = 32
TB = 8
K = TB * CH_DEV
B_DEV = 32
CAP = B_DEV // 4
SLOTS = 5 * CAP
TU = 256
TV = 256
ROWS = 72
AT_ONCE = 4
U_GROUPS = 3
V_GROUPS = 5
V_SPLIT = 2
IMAGES_AT_ONCE = 8
RELAY_AT = (0, 1, 2, 3, 4)
MESH = pl.DeviceIdType.MESH
BF = jnp.bfloat16
F32 = jnp.float32


def series(values, degree):
    nodes = (np.cos(np.pi * (np.arange(400) + 0.5) / 400) + 1.0) * 0.125
    fitted = np.polynomial.chebyshev.Chebyshev.fit(nodes, values(nodes), degree, domain=[0, 0.25])
    return [float(c) for c in fitted.convert(kind=np.polynomial.Polynomial).coef]


COS_COEF = series(lambda q: np.cos(2 * np.pi * np.sqrt(q)), 5)
SIN_COEF = series(lambda q: np.sin(2 * np.pi * np.sqrt(q)) / np.sqrt(q), 5)


def horner(coefs, q):
    total = jnp.full_like(q, coefs[-1])
    for c in coefs[-2::-1]:
        total = total * q + jnp.float32(c)
    return total


def dft_tables():
    centred = np.arange(S) - S // 2
    product = (centred[:, None] * centred[None, :]) % S
    angles = np.float32(2.0 * math.pi / S) * product.astype(np.float32)
    scale = np.float32(1.0 / math.sqrt(S))
    re = (np.cos(angles) * scale).astype(ml_dtypes.bfloat16).astype(np.float32)
    im = (-np.sin(angles) * scale).astype(ml_dtypes.bfloat16).astype(np.float32)
    return re, im


def right_table():
    re, im = dft_tables()
    norm = np.float32(1.0 / math.sqrt(K))
    table = np.zeros((2 * S, 128), np.float32)
    table[:S, :S] = re.T * norm
    table[S:, :S] = im.T * norm
    return table


def left_table():
    re, im = dft_tables()
    order = np.concatenate([np.arange(0, S, 2), np.arange(1, S, 2)])
    re, im = re[:, order], im[:, order]
    table = np.zeros((8, 2, ROWS, 2 * S), np.float32)
    for shift in range(8):
        table[shift, 0, shift : shift + S, :S] = re
        table[shift, 0, shift : shift + S, S:] = -im
        table[shift, 1, shift : shift + S, :S] = im
        table[shift, 1, shift : shift + S, S:] = re
    return table.reshape(8, 2 * ROWS, 2 * S).astype(ml_dtypes.bfloat16)


def swap_halves(x):
    return pltpu.roll(x, S, x.ndim - 1)


def arrange_station(raw, tall):
    value = raw.astype(F32)
    for i in range(S // 2):
        tall[8 * i : 8 * i + 4, :] = value[:, 128 * i : 128 * (i + 1)]
    lane = lax.broadcasted_iota(jnp.int32, (S // 2, 128), 1)
    feeds = []
    for f in range(2):
        re = tall[pl.ds(2 * f, S // 2, stride=8), :]
        im = tall[pl.ds(2 * f + 1, S // 2, stride=8), :]
        even = jnp.where(lane < S, re, swap_halves(im))
        odd = jnp.where(lane < S, swap_halves(re), im)
        feeds.append(jnp.concatenate([even, odd], axis=0).astype(BF))
    return feeds


def pack_blocks(head, off_u, off_v, base, pairs, track, data):
    heads = head[...]
    kind = lax.broadcasted_iota(jnp.int32, (8, B_DEV), 0)
    named = jnp.where(kind == heads, 1.0, 0.0)
    before = lax.broadcasted_iota(jnp.int32, (B_DEV, B_DEV), 0)
    after = lax.broadcasted_iota(jnp.int32, (B_DEV, B_DEV), 1)
    strict = jnp.where(before < after, 1.0, 0.0).astype(BF)
    counts = jnp.dot(named.astype(BF), strict, preferred_element_type=F32)
    rank = jnp.sum(named * counts, axis=0, keepdims=True)
    slot = heads.astype(F32) * CAP + rank
    which = lax.broadcasted_iota(jnp.int32, (SLOTS, B_DEV), 0).astype(F32)
    chosen = jnp.where(which == slot, 1.0, 0.0).astype(BF)

    label = lax.broadcasted_iota(jnp.int32, (pairs.shape[1], B_DEV), 0)
    listed = jnp.where(label == base[...], 1.0, 0.0).astype(BF)
    station = jnp.dot(pairs[...].astype(F32).astype(BF), listed, preferred_element_type=F32)
    rows = jnp.concatenate(
        [
            jnp.ones((1, B_DEV), F32),
            off_u[...].astype(F32),
            off_v[...].astype(F32),
            station,
            jnp.zeros((3, B_DEV), F32),
            track[...].astype(F32),
            jnp.zeros((128 - 8 - 2 * TB, B_DEV), F32),
        ],
        axis=0,
    ).astype(BF)
    dims = (((1,), (1,)), ((), ()))
    labels = lax.dot_general(chosen, rows, dims, preferred_element_type=F32)

    owner = lax.broadcasted_iota(jnp.int32, (B_DEV, 8 * B_DEV), 0)
    column = lax.broadcasted_iota(jnp.int32, (B_DEV, 8 * B_DEV), 1)
    widen = jnp.where(owner == column // 8, 1.0, 0.0).astype(BF)
    wide = jnp.dot(
        jnp.broadcast_to(slot, (8, B_DEV)).astype(BF), widen, preferred_element_type=F32
    )[:1]
    lane = lax.broadcasted_iota(jnp.int32, (1, 8 * B_DEV), 1) % 8
    place = wide * 8.0 + lane.astype(F32)
    target = lax.broadcasted_iota(jnp.int32, (8 * SLOTS, 8 * B_DEV), 0).astype(F32)
    moved = jnp.where(target == place, 1.0, 0.0).astype(BF)
    return jnp.dot(moved, data[...], preferred_element_type=F32).astype(BF), labels


def list_blocks(labels):
    dims = (((1,), (1,)), ((), ()))
    quantity = lax.broadcasted_iota(jnp.int32, (8, 128), 0)
    lane = lax.broadcasted_iota(jnp.int32, (8, 128), 1)
    pick = jnp.where(quantity == lane, 1.0, 0.0).astype(BF)
    rows = lax.dot_general(pick, labels.astype(BF), dims, preferred_element_type=F32)
    filled, at_u, at_v = rows[0:1], rows[1:2], rows[2:3]
    past_u = at_u > TU - S
    past = jnp.logical_or(past_u, at_v > TV - S)
    first = jnp.where(past_u, filled, 0.0)
    early = jnp.where(past, filled, 0.0)
    kind = lax.broadcasted_iota(jnp.int32, (8, SLOTS), 0)
    both = jnp.where(
        kind == 0,
        first,
        jnp.where(kind == 1, early - first, jnp.where(kind == 2, filled - early, 0.0)),
    )
    before = lax.broadcasted_iota(jnp.int32, (SLOTS, SLOTS), 0)
    after = lax.broadcasted_iota(jnp.int32, (SLOTS, SLOTS), 1)
    strict = jnp.where(before < after, 1.0, 0.0).astype(BF)
    ahead = jnp.dot(both.astype(BF), strict, preferred_element_type=F32)
    number_first = jnp.sum(first, axis=1, keepdims=True)
    number_early = jnp.sum(early, axis=1, keepdims=True)
    number = jnp.sum(filled, axis=1, keepdims=True)
    place = jnp.where(past, number_first + ahead[1:2], number_early + ahead[2:3])
    place = jnp.where(past_u, ahead[0:1], place)
    place = jnp.where(filled > 0.5, place, -1.0)
    target = lax.broadcasted_iota(jnp.int32, (128, SLOTS), 0).astype(F32)
    moved = jnp.where(target == place, 1.0, 0.0).astype(BF)
    slot = lax.broadcasted_iota(jnp.int32, (8, SLOTS), 1).astype(F32)
    rows = jnp.where(kind == 0, slot, rows)
    table = lax.dot_general(rows.astype(BF), moved, dims, preferred_element_type=F32)
    spare = jnp.where(lane.astype(F32) >= number, float(TU + S), 0.0)
    table = table + jnp.where(quantity == 1, spare, 0.0)
    groups = jnp.floor((number + (AT_ONCE - 1.0)) / AT_ONCE)
    ends = []
    for count, least in ((number_first, U_GROUPS), (number_early, V_GROUPS)):
        enough = jnp.minimum(groups, float(least))
        needed = jnp.floor((count + (AT_ONCE - 1.0)) / AT_ONCE)
        ends.append(jnp.maximum(needed, enough))
    for row, end in enumerate((*ends, groups)):
        table = jnp.where(quantity == 5 + row, end, table)
    return table.astype(jnp.int32)


def image_kernel(
    head_in, off_u_in, off_v_in, base_in, pairs_in, track_in, data_in, own_screens,
    right_in, left_in,
    images, screens, listing, canvas, right, left,
    head, off_u, off_v, base, pairs, track, data, in_sems,
    packed, labels, got_data, got_labels, samples, spread, mult, raw, tall,
    own_sems, send_sems, recv_sems, y_send, y_recv, relay_send, relay_recv, c_send, c_recv,
):
    au, vert, band = (lax.axis_index(axis) for axis in ("au", "vert", "ch"))
    n_au, n_vert, n_ch = (lax.axis_size(axis) for axis in ("au", "vert", "ch"))
    here = own_screens.shape[0]
    unit = here // 32
    core = lax.rem(vert, 2)
    colour = lax.rem(vert // 2 + au, 2)
    mine = 16 * core + 10 * colour
    common = 16 * core + 6
    others = 16 * core + 10 * (1 - colour)

    def turned(step):
        return lax.rem(vert + step, n_vert)

    near = (
        {"au": lax.rem(au + 1, n_au)},
        {"au": lax.rem(au + n_au - 1, n_au)},
        {"vert": turned(1)},
        {"vert": turned(n_vert - 1)},
    )
    across = {"ch": lax.rem(band + 1, n_ch)}
    sibling = {"vert": vert + 1 - 2 * core}
    beside = {"vert": vert + 2 - 4 * lax.rem(vert // 2, 2)}
    along = {"au": au + 1 - 2 * lax.rem(au, 2)}

    inputs = (
        (head_in, head), (off_u_in, off_u), (off_v_in, off_v), (base_in, base),
        (pairs_in, pairs), (track_in, track), (data_in, data),
        (right_in, right), (left_in, left),
    )
    loads = [
        pltpu.make_async_copy(source, target, in_sems.at[j])
        for j, (source, target) in enumerate(inputs)
    ]
    for copy in loads:
        copy.start()
    fetches = []
    spans = ((mine, 6), (common, 4), (others, 6), (16 * (1 - core), 16))
    for j, (first, count) in enumerate(spans):
        rows = pl.ds(first * unit, count * unit)
        fetches.append(
            pltpu.make_async_copy(own_screens.at[rows], raw.at[rows], own_sems.at[j])
        )
        fetches[-1].start()
    barrier = pltpu.get_barrier_semaphore()
    for device in (*near, across, beside):
        pl.semaphore_signal(barrier, inc=1, device_id=device, device_id_type=MESH)

    def arrange(first, number):
        def one(pair, carry):
            for i in range(2):
                station = first * unit + 2 * pair + i
                feeds = arrange_station(raw[station], tall.at[i])
                for f in range(2):
                    screens[station, f] = feeds[f]
            return carry

        lax.fori_loop(0, number * unit // 2, one, 0)

    fetches[0].wait()
    arrange(mine, 6)
    fetches[1].wait()
    arrange(common, 4)
    pl.semaphore_wait(barrier, 6)

    def moves(i):
        pairs_of = ((packed, got_data, 8 * CAP), (labels, got_labels, CAP))
        for j, (source, target, rows) in enumerate(pairs_of):
            where = pl.ds((i + 1) * rows, rows)
            yield pltpu.make_async_remote_copy(
                src_ref=source.at[where],
                dst_ref=target.at[where],
                send_sem=send_sems.at[i, j],
                recv_sem=recv_sems.at[i, j],
                device_id=near[i],
                device_id_type=MESH,
            )

    def send(number, count, send_sem, recv_sem, device, own=False):
        where = number * unit
        return pltpu.make_async_remote_copy(
            src_ref=screens.at[pl.ds(where if own else here + where, count * unit)],
            dst_ref=screens.at[pl.ds(here + where, count * unit)],
            send_sem=send_sem,
            recv_sem=recv_sem,
            device_id=device,
            device_id_type=MESH,
        )

    runs = ((0, 2), (2, 2), (4, 1), (5, 1))

    def y_copy(k):
        first, count = (common, 4) if k == 4 else (mine + runs[k][0], runs[k][1])
        return send(first, count, y_send.at[k], y_recv.at[k], across, True)

    def relayed(k, first):
        device = beside if k % 2 == 0 else along
        start, count = runs[k]
        return send(first + start, count, relay_send.at[k], relay_recv.at[k], device)

    def c_copy(k, half):
        first = (
            half + 10 * colour, half + 6, half + 10 * (1 - colour), half + 10 * (1 - colour) + 4
        )[k]
        return send(first, (6, 4, 4, 2)[k], c_send.at[k], c_recv.at[k], sibling)

    for k in range(5):
        y_copy(k).start()

    for copy in loads[:7]:
        copy.wait()
    values, rows = pack_blocks(head, off_u, off_v, base, pairs, track, data)
    packed[...] = values
    labels[...] = rows

    for i in range(4):
        for copy in moves(i):
            copy.start()

    canvas[...] = jnp.zeros_like(canvas)
    for copy in fetches[2:]:
        copy.wait()
    arrange(others, 6)
    arrange(16 * (1 - core), 16)

    row = lax.broadcasted_iota(jnp.int32, (32, K), 0)
    channel = band * CH_DEV + lax.broadcasted_iota(jnp.int32, (32, K), 1) % CH_DEV
    ratio = 1.0 + channel.astype(F32) / jnp.float32(2 * CH_DEV * n_ch)
    coarse = row - 8
    coarse_u = 16 * (coarse % 4) + coarse // 4 - S // 2
    fine_v = row - 16
    coarse_v = (row - 24) * 8 - S // 2
    step = jnp.where(
        row < 16, jnp.where(row < 8, 2 * row, coarse_u), jnp.where(row < 24, fine_v, coarse_v)
    )
    mult[...] = step.astype(F32) / S * ratio

    def widen(rows):
        source = lax.broadcasted_iota(jnp.int32, (128, 2 * K), 0)
        column = lax.broadcasted_iota(jnp.int32, (128, 2 * K), 1)
        chosen = jnp.where(source == 8 + column // CH_DEV, 1.0, 0.0).astype(BF)
        lane = lax.broadcasted_iota(jnp.int32, rows.shape, 1)
        only = jnp.where(lane < 8, 0.0, rows).astype(BF)
        return jnp.dot(only, chosen, preferred_element_type=F32)

    got_labels[:CAP] = labels[:CAP]
    samples[: 8 * CAP] = packed[: 8 * CAP].astype(F32)
    spread[:CAP] = widen(labels[:CAP])

    def block(slot):
        sample = samples[pl.ds(8 * slot, 8), :]
        track = spread[pl.ds(slot, 1), :]
        turns = jnp.concatenate(
            [track[:, :K] * mult[:16], track[:, K:] * mult[16:]], axis=0
        )
        frac = turns - jnp.floor(turns + 0.5)
        square = frac * frac
        cos = horner(COS_COEF, square)
        sin = horner(SIN_COEF, square) * frac

        def phasors(first):
            cos_fine, sin_fine = cos[first : first + 8], sin[first : first + 8]
            all_cos, all_sin = [], []
            for a in range(8):
                at = first + 8 + a
                cos_a, sin_a = cos[at : at + 1], sin[at : at + 1]
                all_cos.append(cos_fine * cos_a - sin_fine * sin_a)
                all_sin.append(sin_fine * cos_a + cos_fine * sin_a)
            return (
                jnp.concatenate(all_cos, axis=0).astype(BF),
                jnp.concatenate(all_sin, axis=0).astype(BF),
            )

        cos_u, sin_u = phasors(0)
        cos_v, sin_v = phasors(16)
        table = jnp.concatenate(
            [
                jnp.concatenate([cos_v, -sin_v], axis=1),
                jnp.concatenate([sin_v, cos_v], axis=1),
            ],
            axis=0,
        )

        def spread_row(r):
            row = jnp.broadcast_to(sample[r : r + 1], (16, K)).astype(BF)
            return jnp.concatenate([row] * (S // 16), axis=0)

        weighed = []
        for p in range(4):
            re, im = spread_row(2 * p), spread_row(2 * p + 1)
            weighed.append(
                jnp.concatenate([re * cos_u - im * sin_u, re * sin_u + im * cos_u], axis=1)
            )
        dims = (((1,), (1,)), ((), ()))
        image = lax.dot_general(
            jnp.concatenate(weighed, axis=0), table, dims, preferred_element_type=F32
        )
        return image.astype(BF)

    here_half, other_half = 16 * core, 16 * (1 - core)

    def relay(stage):
        if stage < 3:
            for k in ((0,), (1,), (2, 3))[stage]:
                y_copy(k).wait_recv()
                relayed(k, mine).start()
            if stage == 2:
                c_copy(0, here_half).start()
        elif stage == 3:
            for k in (0, 1):
                relayed(k, others).wait_recv()
            c_copy(2, here_half).start()
        else:
            y_copy(4).wait_recv()
            c_copy(1, here_half).start()
            for k in (2, 3):
                relayed(k, others).wait_recv()
            c_copy(3, here_half).start()

    def loop(group, carry):
        @pl.when(group == CAP // IMAGES_AT_ONCE)
        def _():
            for i in range(4):
                for copy in moves(i):
                    copy.wait_recv()
            samples[8 * CAP :] = got_data[8 * CAP :].astype(F32)
            spread[CAP:] = widen(got_labels[CAP:])

        for stage, at in enumerate(RELAY_AT):

            @pl.when(group == at)
            def _():
                relay(stage)

        made = [block(IMAGES_AT_ONCE * group + i) for i in range(IMAGES_AT_ONCE)]
        for i in range(IMAGES_AT_ONCE):
            images[IMAGES_AT_ONCE * group + i] = made[i]
        return carry

    lax.fori_loop(0, SLOTS // IMAGES_AT_ONCE, loop, 0)
    listing[...] = list_blocks(got_labels[...])
    for copy in loads[7:]:
        copy.wait()
    for i in range(4):
        for copy in moves(i):
            copy.wait_send()
    for k in range(5):
        y_copy(k).wait_send()
    for k in range(4):
        relayed(k, mine).wait_send()
        c_copy(k, here_half).wait_send()
        c_copy(k, other_half).wait_recv()


def folded(x):
    middle = x.shape[1] // 2
    lane = lax.broadcasted_iota(jnp.int32, (1, 1, 128), 2)
    return jnp.where(lane < S, x[:, :middle], swap_halves(x[:, middle:])).astype(BF)


def edge_u_kernel(listing, images, screens, right, left, canvas_in, canvas, edge_u, corner):
    grid_blocks(images, screens, canvas, right, left, listing, 0, listing[5, 0])
    edge_u[...] = canvas[:, TU : TU + S, :TV].astype(BF)
    corner[...] = folded(canvas[:, TU : TU + S, TV:])


def edge_v_kernel(listing, images, screens, right, left, canvas_in, canvas, *edge_v):
    grid_blocks(images, screens, canvas, right, left, listing, listing[5, 0], listing[6, 0])
    each = 8 // V_SPLIT
    for i, edge in enumerate(edge_v):
        edge[...] = folded(canvas[i * each : (i + 1) * each, :TU, TV:])


def late_kernel(listing, images, screens, right, left, canvas_in, canvas):
    grid_blocks(images, screens, canvas, right, left, listing, listing[6, 0], listing[7, 0])


def grid_blocks(images, screens, canvas, right, left, listing, first, last):
    here = screens.shape[0] // 2
    band = lax.axis_index("ch")

    def screen_place(station):
        owner = station // here
        local = station - owner * here
        return jnp.where(owner == band, local, here + local)

    def block(index):
        slot = listing[0, index]
        off_u = listing[1, index]
        off_v = listing[2, index]
        one = screen_place(listing[3, index])
        two = screen_place(listing[4, index])
        two_s = [screens[two, f].astype(F32) for f in range(2)]
        fixed = []
        for f in range(2):
            one_s = screens[one, f].astype(F32)
            one_swapped = swap_halves(one_s)
            for e in range(2):
                p = 2 * f + e
                same = one_s * two_s[e]
                cross = one_swapped * two_s[e]
                gain_re = same + swap_halves(same)
                gain_im = swap_halves(cross) - cross
                part = images[slot, p * S : (p + 1) * S].astype(F32)
                fixed.append((part * gain_re + swap_halves(part) * gain_im).astype(BF))
        tile = off_v // 128
        shift = off_v - tile * 128
        moved = pltpu.roll(right[...], shift, 1).astype(BF)
        table_re, table_im = moved[:S], moved[S:]
        shifted = jnp.concatenate(
            [
                jnp.concatenate([table_re, -table_im], axis=0),
                jnp.concatenate([table_im, table_re], axis=0),
            ],
            axis=1,
        )
        half = jnp.dot(
            jnp.concatenate(fixed, axis=0), shifted, preferred_element_type=F32
        ).astype(BF)
        eighth = off_u // 8
        placed = left[off_u - eighth * 8]
        start_u = pl.multiple_of(eighth * 8, 8)
        start_v = pl.multiple_of(tile * 128, 128)
        return start_u, start_v, shift, placed, half

    lane = lax.broadcasted_iota(jnp.int32, (1, 128), 1)

    def loop(group, carry):
        ready = [block(AT_ONCE * group + i) for i in range(AT_ONCE)]
        for start_u, start_v, shift, placed, half in ready:
            for f in range(2):
                both = []
                for p in (2 * f, 2 * f + 1):
                    part = half[p * S : (p + 1) * S]
                    both.append(jnp.concatenate([part[:, :128], part[:, 128:]], axis=0))
                grid = jnp.dot(
                    placed, jnp.concatenate(both, axis=1), preferred_element_type=F32
                )
                for e in range(2):
                    for r in range(2):
                        cells = grid[r * ROWS : (r + 1) * ROWS, 128 * e : 128 * (e + 1)]
                        cells = jnp.concatenate(
                            [
                                jnp.where(lane >= shift, cells, 0.0),
                                jnp.where(lane < shift, cells, 0.0),
                            ],
                            axis=1,
                        )
                        where = (
                            4 * f + 2 * e + r, pl.ds(start_u, ROWS), pl.ds(start_v, 256)
                        )
                        canvas[where] += cells
        return carry

    lax.fori_loop(first, last, loop, 0)


def lower_kernel(canvas, *refs):
    *got_v, out, top, side, sems = refs
    rest = pltpu.make_async_copy(
        canvas.at[:, S:TU, 128:TV], out.at[:, S:, 128:], sems.at[0]
    )
    rest.start()
    lane = lax.broadcasted_iota(jnp.int32, (1, 1, 128), 2)
    both = jnp.concatenate([x[...] for x in got_v], axis=0).astype(F32)
    low = jnp.where(lane < S, both, 0.0)
    high = jnp.where(lane < S, swap_halves(both), 0.0)
    side[:, : TU // 2 - S] = canvas[:, S : TU // 2, :128] + low[:, S:]
    side[:, TU // 2 - S :] = canvas[:, TU // 2 : TU, :128] + high
    store_side = pltpu.make_async_copy(side, out.at[:, S:, :128], sems.at[1])
    store_side.start()
    top[:, :, :128] = canvas[:, :S, :128] + low[:, :S]
    top[:, :, 128:] = canvas[:, :S, 128:TV]
    rest.wait()
    store_side.wait()


def upper_kernel(lower, top, got_u, got_c, out, rows, sems):
    lane = lax.broadcasted_iota(jnp.int32, (1, 1, 128), 2)
    stores = []
    for i in range(2):
        planes = slice(4 * i, 4 * i + 4)
        rows[planes] = top[planes] + got_u[planes].astype(F32)
        both = got_c[planes].astype(F32)
        rows[planes, : S // 2, :128] += jnp.where(lane < S, both, 0.0)
        rows[planes, S // 2 :, :128] += jnp.where(lane < S, swap_halves(both), 0.0)
        stores.append(
            pltpu.make_async_copy(rows.at[planes], out.at[planes, :S, :], sems.at[i])
        )
        stores[-1].start()
    for store in stores:
        store.wait()


def body(visibilities, tracks, offset_u, offset_v, heading, baseline, station_pair, screens):
    smem = pl.BlockSpec(memory_space=pltpu.SMEM)
    vmem = pl.BlockSpec(memory_space=pltpu.VMEM)
    hbm = pl.BlockSpec(memory_space=pltpu.HBM)
    n_au, n_vert = (lax.axis_size(axis) for axis in ("au", "vert"))
    here = screens.shape[0]
    canvas_shape = jax.ShapeDtypeStruct((8, TU + S + ROWS, TV + 128), F32)
    right_shape = jax.ShapeDtypeStruct((2 * S, 128), F32)
    left_shape = jax.ShapeDtypeStruct((8, 2 * ROWS, 2 * S), BF)
    dma = pltpu.SemaphoreType.DMA
    number = pltpu.VMEM((1, B_DEV), jnp.int32)
    images, all_screens, listing, canvas, right, left = pl.pallas_call(
        image_kernel,
        out_shape=(
            jax.ShapeDtypeStruct((SLOTS, 4 * S, 2 * S), BF),
            jax.ShapeDtypeStruct((2 * here, 2, S, 2 * S), BF),
            jax.ShapeDtypeStruct((8, 128), jnp.int32),
            canvas_shape,
            right_shape,
            left_shape,
        ),
        in_specs=[hbm] * 10,
        out_specs=(vmem,) * 6,
        scratch_shapes=[
            number,
            number,
            number,
            number,
            pltpu.VMEM(station_pair.shape, jnp.int32),
            pltpu.VMEM((2 * TB, B_DEV), BF),
            pltpu.VMEM((8 * B_DEV, K), BF),
            dma((9,)),
            pltpu.VMEM((8 * SLOTS, K), BF),
            pltpu.VMEM((SLOTS, 128), F32),
            pltpu.VMEM((8 * SLOTS, K), BF),
            pltpu.VMEM((SLOTS, 128), F32),
            pltpu.VMEM((8 * SLOTS, K), F32),
            pltpu.VMEM((SLOTS, 2 * K), F32),
            pltpu.VMEM((32, K), F32),
            pltpu.VMEM((here, 4, S * S), BF),
            pltpu.VMEM((2, 4 * S, 128), F32),
            dma((4,)),
            dma((4, 2)),
            dma((4, 2)),
            dma((5,)),
            dma((5,)),
            dma((4,)),
            dma((4,)),
            dma((4,)),
            dma((4,)),
        ],
        compiler_params=pltpu.CompilerParams(
            collective_id=0, has_side_effects=True, vmem_limit_bytes=20 << 20
        ),
    )(*(pltpu.with_memory_space_constraint(x, pltpu.HBM) for x in (
        heading.reshape(1, B_DEV), offset_u[None], offset_v[None], baseline[None],
        station_pair, tracks.transpose(1, 2, 0).reshape(2 * TB, B_DEV),
        visibilities.reshape(8 * B_DEV, K), screens,
        jnp.asarray(right_table()), jnp.asarray(left_table()),
    )))

    def grid(kernel, canvas, flops, *edges):
        return pl.pallas_call(
            kernel,
            out_shape=(canvas_shape, *edges),
            in_specs=[smem] + [vmem] * 5,
            out_specs=(vmem,) * (1 + len(edges)),
            input_output_aliases={5: 0},
            compiler_params=pltpu.CompilerParams(vmem_limit_bytes=12 << 20),
            cost_estimate=pl.CostEstimate(
                flops=flops, bytes_accessed=1 << 20, transcendentals=0
            ),
        )(listing, images, all_screens, right, left, canvas)

    canvas, edge_u, corner = grid(
        edge_u_kernel,
        canvas,
        10**9,
        jax.ShapeDtypeStruct((8, S, TV), BF),
        jax.ShapeDtypeStruct((8, S // 2, 128), BF),
    )
    got_u = lax.ppermute(edge_u, "au", [(i, (i + 1) % n_au) for i in range(n_au)])
    diagonal = [
        (u * n_vert + v, (u + 1) % n_au * n_vert + (v + 1) % n_vert)
        for u in range(n_au)
        for v in range(n_vert)
    ]
    got_c = lax.ppermute(corner, ("au", "vert"), diagonal)
    canvas, *edge_v = grid(
        edge_v_kernel, canvas, 4 * 10**9, *[jax.ShapeDtypeStruct((8 // V_SPLIT, TU // 2, 128), BF)] * V_SPLIT
    )
    got_v = [
        lax.ppermute(x, "vert", [(i, (i + 1) % n_vert) for i in range(n_vert)]) for x in edge_v
    ]
    (canvas,) = grid(late_kernel, canvas, 10**6)
    tile = jax.ShapeDtypeStruct((8, TU, TV), F32)
    out, top = pl.pallas_call(
        lower_kernel,
        out_shape=(tile, jax.ShapeDtypeStruct((8, S, TV), F32)),
        in_specs=[vmem] * (1 + V_SPLIT),
        out_specs=(pl.BlockSpec(memory_space=pl.ANY), vmem),
        scratch_shapes=[pltpu.VMEM((8, TU - S, 128), F32), dma((2,))],
        compiler_params=pltpu.CompilerParams(vmem_limit_bytes=8 << 20),
    )(canvas, *got_v)
    out = pl.pallas_call(
        upper_kernel,
        out_shape=tile,
        in_specs=[pl.BlockSpec(memory_space=pl.ANY)] + [vmem] * 3,
        out_specs=pl.BlockSpec(memory_space=pl.ANY),
        scratch_shapes=[pltpu.VMEM((8, S, TV), F32), dma((2,))],
        input_output_aliases={0: 0},
        compiler_params=pltpu.CompilerParams(vmem_limit_bytes=8 << 20),
    )(out, top, got_u, got_c)
    return out[None]


def solution(mesh):
    placed = (
        P(("au", "vert"), None, "ch"),
        P(("au", "vert"), None, None),
        P(("au", "vert")),
        P(("au", "vert")),
        P(("au", "vert"), None),
        P(("au", "vert")),
        P(),
        P("ch", None, None),
    )
    return jax.shard_map(
        body, mesh=mesh, in_specs=placed, out_specs=P("ch", None, "au", "vert"), check_vma=False
    )
```

```python
import math

import jax
import jax.numpy as jnp
import ml_dtypes
import numpy as np
from jax import lax
from jax.experimental import pallas as pl
from jax.experimental.pallas import tpu as pltpu
from jax.sharding import PartitionSpec as P

S = 64
CH_DEV = 32
TB = 8
K = TB * CH_DEV
B_DEV = 32
CAP = B_DEV // 4
SLOTS = 5 * CAP
TU = 256
TV = 256
ROWS = 72
AT_ONCE = 4
U_GROUPS = 3
V_GROUPS = 5
V_SPLIT = 4
IMAGES_AT_ONCE = 8
RELAY_AT = (0, 1, 2, 3, 4)
MESH = pl.DeviceIdType.MESH
BF = jnp.bfloat16
F32 = jnp.float32


def series(values, degree):
    nodes = (np.cos(np.pi * (np.arange(400) + 0.5) / 400) + 1.0) * 0.125
    fitted = np.polynomial.chebyshev.Chebyshev.fit(nodes, values(nodes), degree, domain=[0, 0.25])
    return [float(c) for c in fitted.convert(kind=np.polynomial.Polynomial).coef]


COS_COEF = series(lambda q: np.cos(2 * np.pi * np.sqrt(q)), 5)
SIN_COEF = series(lambda q: np.sin(2 * np.pi * np.sqrt(q)) / np.sqrt(q), 5)


def horner(coefs, q):
    total = jnp.full_like(q, coefs[-1])
    for c in coefs[-2::-1]:
        total = total * q + jnp.float32(c)
    return total


def dft_tables():
    centred = np.arange(S) - S // 2
    product = (centred[:, None] * centred[None, :]) % S
    angles = np.float32(2.0 * math.pi / S) * product.astype(np.float32)
    scale = np.float32(1.0 / math.sqrt(S))
    re = (np.cos(angles) * scale).astype(ml_dtypes.bfloat16).astype(np.float32)
    im = (-np.sin(angles) * scale).astype(ml_dtypes.bfloat16).astype(np.float32)
    return re, im


def right_table():
    re, im = dft_tables()
    norm = np.float32(1.0 / math.sqrt(K))
    table = np.zeros((2 * S, 128), np.float32)
    table[:S, :S] = re.T * norm
    table[S:, :S] = im.T * norm
    return table


def left_table():
    re, im = dft_tables()
    order = np.concatenate([np.arange(0, S, 2), np.arange(1, S, 2)])
    re, im = re[:, order], im[:, order]
    table = np.zeros((8, 2, ROWS, 2 * S), np.float32)
    for shift in range(8):
        table[shift, 0, shift : shift + S, :S] = re
        table[shift, 0, shift : shift + S, S:] = -im
        table[shift, 1, shift : shift + S, :S] = im
        table[shift, 1, shift : shift + S, S:] = re
    return table.reshape(8, 2 * ROWS, 2 * S).astype(ml_dtypes.bfloat16)


def swap_halves(x):
    return pltpu.roll(x, S, x.ndim - 1)


def arrange_station(raw, tall):
    value = raw.astype(F32)
    for i in range(S // 2):
        tall[8 * i : 8 * i + 4, :] = value[:, 128 * i : 128 * (i + 1)]
    lane = lax.broadcasted_iota(jnp.int32, (S // 2, 128), 1)
    feeds = []
    for f in range(2):
        re = tall[pl.ds(2 * f, S // 2, stride=8), :]
        im = tall[pl.ds(2 * f + 1, S // 2, stride=8), :]
        even = jnp.where(lane < S, re, swap_halves(im))
        odd = jnp.where(lane < S, swap_halves(re), im)
        feeds.append(jnp.concatenate([even, odd], axis=0).astype(BF))
    return feeds


def pack_blocks(head, off_u, off_v, base, pairs, track, data):
    heads = head[...]
    kind = lax.broadcasted_iota(jnp.int32, (8, B_DEV), 0)
    named = jnp.where(kind == heads, 1.0, 0.0)
    before = lax.broadcasted_iota(jnp.int32, (B_DEV, B_DEV), 0)
    after = lax.broadcasted_iota(jnp.int32, (B_DEV, B_DEV), 1)
    strict = jnp.where(before < after, 1.0, 0.0).astype(BF)
    counts = jnp.dot(named.astype(BF), strict, preferred_element_type=F32)
    rank = jnp.sum(named * counts, axis=0, keepdims=True)
    slot = heads.astype(F32) * CAP + rank
    which = lax.broadcasted_iota(jnp.int32, (SLOTS, B_DEV), 0).astype(F32)
    chosen = jnp.where(which == slot, 1.0, 0.0).astype(BF)

    label = lax.broadcasted_iota(jnp.int32, (pairs.shape[1], B_DEV), 0)
    listed = jnp.where(label == base[...], 1.0, 0.0).astype(BF)
    station = jnp.dot(pairs[...].astype(F32).astype(BF), listed, preferred_element_type=F32)
    rows = jnp.concatenate(
        [
            jnp.ones((1, B_DEV), F32),
            off_u[...].astype(F32),
            off_v[...].astype(F32),
            station,
            jnp.zeros((3, B_DEV), F32),
            track[...].astype(F32),
            jnp.zeros((128 - 8 - 2 * TB, B_DEV), F32),
        ],
        axis=0,
    ).astype(BF)
    dims = (((1,), (1,)), ((), ()))
    labels = lax.dot_general(chosen, rows, dims, preferred_element_type=F32)

    owner = lax.broadcasted_iota(jnp.int32, (B_DEV, 8 * B_DEV), 0)
    column = lax.broadcasted_iota(jnp.int32, (B_DEV, 8 * B_DEV), 1)
    widen = jnp.where(owner == column // 8, 1.0, 0.0).astype(BF)
    wide = jnp.dot(
        jnp.broadcast_to(slot, (8, B_DEV)).astype(BF), widen, preferred_element_type=F32
    )[:1]
    lane = lax.broadcasted_iota(jnp.int32, (1, 8 * B_DEV), 1) % 8
    place = wide * 8.0 + lane.astype(F32)
    target = lax.broadcasted_iota(jnp.int32, (8 * SLOTS, 8 * B_DEV), 0).astype(F32)
    moved = jnp.where(target == place, 1.0, 0.0).astype(BF)
    return jnp.dot(moved, data[...], preferred_element_type=F32).astype(BF), labels


def list_blocks(labels):
    dims = (((1,), (1,)), ((), ()))
    quantity = lax.broadcasted_iota(jnp.int32, (8, 128), 0)
    lane = lax.broadcasted_iota(jnp.int32, (8, 128), 1)
    pick = jnp.where(quantity == lane, 1.0, 0.0).astype(BF)
    rows = lax.dot_general(pick, labels.astype(BF), dims, preferred_element_type=F32)
    filled, at_u, at_v = rows[0:1], rows[1:2], rows[2:3]
    past_u = at_u > TU - S
    past = jnp.logical_or(past_u, at_v > TV - S)
    first = jnp.where(past_u, filled, 0.0)
    early = jnp.where(past, filled, 0.0)
    kind = lax.broadcasted_iota(jnp.int32, (8, SLOTS), 0)
    both = jnp.where(
        kind == 0,
        first,
        jnp.where(kind == 1, early - first, jnp.where(kind == 2, filled - early, 0.0)),
    )
    before = lax.broadcasted_iota(jnp.int32, (SLOTS, SLOTS), 0)
    after = lax.broadcasted_iota(jnp.int32, (SLOTS, SLOTS), 1)
    strict = jnp.where(before < after, 1.0, 0.0).astype(BF)
    ahead = jnp.dot(both.astype(BF), strict, preferred_element_type=F32)
    number_first = jnp.sum(first, axis=1, keepdims=True)
    number_early = jnp.sum(early, axis=1, keepdims=True)
    number = jnp.sum(filled, axis=1, keepdims=True)
    place = jnp.where(past, number_first + ahead[1:2], number_early + ahead[2:3])
    place = jnp.where(past_u, ahead[0:1], place)
    place = jnp.where(filled > 0.5, place, -1.0)
    target = lax.broadcasted_iota(jnp.int32, (128, SLOTS), 0).astype(F32)
    moved = jnp.where(target == place, 1.0, 0.0).astype(BF)
    slot = lax.broadcasted_iota(jnp.int32, (8, SLOTS), 1).astype(F32)
    rows = jnp.where(kind == 0, slot, rows)
    table = lax.dot_general(rows.astype(BF), moved, dims, preferred_element_type=F32)
    spare = jnp.where(lane.astype(F32) >= number, float(TU + S), 0.0)
    table = table + jnp.where(quantity == 1, spare, 0.0)
    groups = jnp.floor((number + (AT_ONCE - 1.0)) / AT_ONCE)
    ends = []
    for count, least in ((number_first, U_GROUPS), (number_early, V_GROUPS)):
        enough = jnp.minimum(groups, float(least))
        needed = jnp.floor((count + (AT_ONCE - 1.0)) / AT_ONCE)
        ends.append(jnp.maximum(needed, enough))
    for row, end in enumerate((*ends, groups)):
        table = jnp.where(quantity == 5 + row, end, table)
    return table.astype(jnp.int32)


def image_kernel(
    head_in, off_u_in, off_v_in, base_in, pairs_in, track_in, data_in, own_screens,
    right_in, left_in,
    images, screens, listing, canvas, right, left,
    head, off_u, off_v, base, pairs, track, data, in_sems,
    packed, labels, got_data, got_labels, samples, spread, mult, raw, tall,
    own_sems, send_sems, recv_sems, y_send, y_recv, relay_send, relay_recv, c_send, c_recv,
):
    au, vert, band = (lax.axis_index(axis) for axis in ("au", "vert", "ch"))
    n_au, n_vert, n_ch = (lax.axis_size(axis) for axis in ("au", "vert", "ch"))
    here = own_screens.shape[0]
    unit = here // 32
    core = lax.rem(vert, 2)
    colour = lax.rem(vert // 2 + au, 2)
    mine = 16 * core + 10 * colour
    common = 16 * core + 6
    others = 16 * core + 10 * (1 - colour)

    def turned(step):
        return lax.rem(vert + step, n_vert)

    near = (
        {"au": lax.rem(au + 1, n_au)},
        {"au": lax.rem(au + n_au - 1, n_au)},
        {"vert": turned(1)},
        {"vert": turned(n_vert - 1)},
    )
    across = {"ch": lax.rem(band + 1, n_ch)}
    sibling = {"vert": vert + 1 - 2 * core}
    beside = {"vert": vert + 2 - 4 * lax.rem(vert // 2, 2)}
    along = {"au": au + 1 - 2 * lax.rem(au, 2)}

    inputs = (
        (head_in, head), (off_u_in, off_u), (off_v_in, off_v), (base_in, base),
        (pairs_in, pairs), (track_in, track), (data_in, data),
        (right_in, right), (left_in, left),
    )
    loads = [
        pltpu.make_async_copy(source, target, in_sems.at[j])
        for j, (source, target) in enumerate(inputs)
    ]
    for copy in loads:
        copy.start()
    fetches = []
    spans = ((mine, 6), (common, 4), (others, 6), (16 * (1 - core), 16))
    for j, (first, count) in enumerate(spans):
        rows = pl.ds(first * unit, count * unit)
        fetches.append(
            pltpu.make_async_copy(own_screens.at[rows], raw.at[rows], own_sems.at[j])
        )
        fetches[-1].start()
    barrier = pltpu.get_barrier_semaphore()
    for device in (*near, across, beside):
        pl.semaphore_signal(barrier, inc=1, device_id=device, device_id_type=MESH)

    def arrange(first, number):
        def one(pair, carry):
            for i in range(2):
                station = first * unit + 2 * pair + i
                feeds = arrange_station(raw[station], tall.at[i])
                for f in range(2):
                    screens[station, f] = feeds[f]
            return carry

        lax.fori_loop(0, number * unit // 2, one, 0)

    fetches[0].wait()
    arrange(mine, 6)
    fetches[1].wait()
    arrange(common, 4)
    pl.semaphore_wait(barrier, 6)

    def moves(i):
        pairs_of = ((packed, got_data, 8 * CAP), (labels, got_labels, CAP))
        for j, (source, target, rows) in enumerate(pairs_of):
            where = pl.ds((i + 1) * rows, rows)
            yield pltpu.make_async_remote_copy(
                src_ref=source.at[where],
                dst_ref=target.at[where],
                send_sem=send_sems.at[i, j],
                recv_sem=recv_sems.at[i, j],
                device_id=near[i],
                device_id_type=MESH,
            )

    def send(number, count, send_sem, recv_sem, device, own=False):
        where = number * unit
        return pltpu.make_async_remote_copy(
            src_ref=screens.at[pl.ds(where if own else here + where, count * unit)],
            dst_ref=screens.at[pl.ds(here + where, count * unit)],
            send_sem=send_sem,
            recv_sem=recv_sem,
            device_id=device,
            device_id_type=MESH,
        )

    runs = ((0, 2), (2, 2), (4, 1), (5, 1))

    def y_copy(k):
        first, count = (common, 4) if k == 4 else (mine + runs[k][0], runs[k][1])
        return send(first, count, y_send.at[k], y_recv.at[k], across, True)

    def relayed(k, first):
        device = beside if k % 2 == 0 else along
        start, count = runs[k]
        return send(first + start, count, relay_send.at[k], relay_recv.at[k], device)

    def c_copy(k, half):
        first = (
            half + 10 * colour, half + 6, half + 10 * (1 - colour), half + 10 * (1 - colour) + 4
        )[k]
        return send(first, (6, 4, 4, 2)[k], c_send.at[k], c_recv.at[k], sibling)

    for k in range(5):
        y_copy(k).start()

    for copy in loads[:7]:
        copy.wait()
    values, rows = pack_blocks(head, off_u, off_v, base, pairs, track, data)
    packed[...] = values
    labels[...] = rows

    for i in range(4):
        for copy in moves(i):
            copy.start()

    canvas[...] = jnp.zeros_like(canvas)
    for copy in fetches[2:]:
        copy.wait()
    arrange(others, 6)
    arrange(16 * (1 - core), 16)

    row = lax.broadcasted_iota(jnp.int32, (32, K), 0)
    channel = band * CH_DEV + lax.broadcasted_iota(jnp.int32, (32, K), 1) % CH_DEV
    ratio = 1.0 + channel.astype(F32) / jnp.float32(2 * CH_DEV * n_ch)
    coarse = row - 8
    coarse_u = 16 * (coarse % 4) + coarse // 4 - S // 2
    fine_v = row - 16
    coarse_v = (row - 24) * 8 - S // 2
    step = jnp.where(
        row < 16, jnp.where(row < 8, 2 * row, coarse_u), jnp.where(row < 24, fine_v, coarse_v)
    )
    mult[...] = step.astype(F32) / S * ratio

    def widen(rows):
        source = lax.broadcasted_iota(jnp.int32, (128, 2 * K), 0)
        column = lax.broadcasted_iota(jnp.int32, (128, 2 * K), 1)
        chosen = jnp.where(source == 8 + column // CH_DEV, 1.0, 0.0).astype(BF)
        lane = lax.broadcasted_iota(jnp.int32, rows.shape, 1)
        only = jnp.where(lane < 8, 0.0, rows).astype(BF)
        return jnp.dot(only, chosen, preferred_element_type=F32)

    got_labels[:CAP] = labels[:CAP]
    samples[: 8 * CAP] = packed[: 8 * CAP].astype(F32)
    spread[:CAP] = widen(labels[:CAP])

    def block(slot):
        sample = samples[pl.ds(8 * slot, 8), :]
        track = spread[pl.ds(slot, 1), :]
        turns = jnp.concatenate(
            [track[:, :K] * mult[:16], track[:, K:] * mult[16:]], axis=0
        )
        frac = turns - jnp.floor(turns + 0.5)
        square = frac * frac
        cos = horner(COS_COEF, square)
        sin = horner(SIN_COEF, square) * frac

        def phasors(first):
            cos_fine, sin_fine = cos[first : first + 8], sin[first : first + 8]
            all_cos, all_sin = [], []
            for a in range(8):
                at = first + 8 + a
                cos_a, sin_a = cos[at : at + 1], sin[at : at + 1]
                all_cos.append(cos_fine * cos_a - sin_fine * sin_a)
                all_sin.append(sin_fine * cos_a + cos_fine * sin_a)
            return (
                jnp.concatenate(all_cos, axis=0).astype(BF),
                jnp.concatenate(all_sin, axis=0).astype(BF),
            )

        cos_u, sin_u = phasors(0)
        cos_v, sin_v = phasors(16)
        table = jnp.concatenate(
            [
                jnp.concatenate([cos_v, -sin_v], axis=1),
                jnp.concatenate([sin_v, cos_v], axis=1),
            ],
            axis=0,
        )

        def spread_row(r):
            row = jnp.broadcast_to(sample[r : r + 1], (16, K)).astype(BF)
            return jnp.concatenate([row] * (S // 16), axis=0)

        weighed = []
        for p in range(4):
            re, im = spread_row(2 * p), spread_row(2 * p + 1)
            weighed.append(
                jnp.concatenate([re * cos_u - im * sin_u, re * sin_u + im * cos_u], axis=1)
            )
        dims = (((1,), (1,)), ((), ()))
        image = lax.dot_general(
            jnp.concatenate(weighed, axis=0), table, dims, preferred_element_type=F32
        )
        return image.astype(BF)

    here_half, other_half = 16 * core, 16 * (1 - core)

    def relay(stage):
        if stage < 3:
            for k in ((0,), (1,), (2, 3))[stage]:
                y_copy(k).wait_recv()
                relayed(k, mine).start()
            if stage == 2:
                c_copy(0, here_half).start()
        elif stage == 3:
            for k in (0, 1):
                relayed(k, others).wait_recv()
            c_copy(2, here_half).start()
        else:
            y_copy(4).wait_recv()
            c_copy(1, here_half).start()
            for k in (2, 3):
                relayed(k, others).wait_recv()
            c_copy(3, here_half).start()

    def loop(group, carry):
        @pl.when(group == CAP // IMAGES_AT_ONCE)
        def _():
            for i in range(4):
                for copy in moves(i):
                    copy.wait_recv()
            samples[8 * CAP :] = got_data[8 * CAP :].astype(F32)
            spread[CAP:] = widen(got_labels[CAP:])
            listing[...] = list_blocks(got_labels[...])

        for stage, at in enumerate(RELAY_AT):

            @pl.when(group == at)
            def _():
                relay(stage)

        made = [block(IMAGES_AT_ONCE * group + i) for i in range(IMAGES_AT_ONCE)]
        for i in range(IMAGES_AT_ONCE):
            images[IMAGES_AT_ONCE * group + i] = made[i]
        return carry

    lax.fori_loop(0, SLOTS // IMAGES_AT_ONCE, loop, 0)
    for copy in loads[7:]:
        copy.wait()
    for i in range(4):
        for copy in moves(i):
            copy.wait_send()
    for k in range(5):
        y_copy(k).wait_send()
    for k in range(4):
        relayed(k, mine).wait_send()
        c_copy(k, here_half).wait_send()
        c_copy(k, other_half).wait_recv()


def folded(x):
    middle = x.shape[1] // 2
    lane = lax.broadcasted_iota(jnp.int32, (1, 1, 128), 2)
    return jnp.where(lane < S, x[:, :middle], swap_halves(x[:, middle:])).astype(BF)


def edge_u_kernel(listing, images, screens, right, left, canvas_in, canvas, edge_u, corner):
    grid_blocks(images, screens, canvas, right, left, listing, 0, listing[5, 0])
    edge_u[...] = canvas[:, TU : TU + S, :TV].astype(BF)
    corner[...] = folded(canvas[:, TU : TU + S, TV:])


def edge_v_kernel(listing, images, screens, right, left, canvas_in, canvas, *edge_v):
    grid_blocks(images, screens, canvas, right, left, listing, listing[5, 0], listing[6, 0])
    each = 8 // V_SPLIT
    for i, edge in enumerate(edge_v):
        edge[...] = folded(canvas[i * each : (i + 1) * each, :TU, TV:])


def late_kernel(listing, images, screens, right, left, canvas_in, got_c, canvas):
    lane = lax.broadcasted_iota(jnp.int32, (1, 1, 128), 2)
    both = got_c[...].astype(F32)
    canvas[:, : S // 2, :128] += jnp.where(lane < S, both, 0.0)
    canvas[:, S // 2 : S, :128] += jnp.where(lane < S, swap_halves(both), 0.0)
    grid_blocks(images, screens, canvas, right, left, listing, listing[6, 0], listing[7, 0])


def grid_blocks(images, screens, canvas, right, left, listing, first, last):
    here = screens.shape[0] // 2
    band = lax.axis_index("ch")

    def screen_place(station):
        owner = station // here
        local = station - owner * here
        return jnp.where(owner == band, local, here + local)

    def block(index):
        slot = listing[0, index]
        off_u = listing[1, index]
        off_v = listing[2, index]
        one = screen_place(listing[3, index])
        two = screen_place(listing[4, index])
        two_s = [screens[two, f].astype(F32) for f in range(2)]
        fixed = []
        for f in range(2):
            one_s = screens[one, f].astype(F32)
            one_swapped = swap_halves(one_s)
            for e in range(2):
                p = 2 * f + e
                same = one_s * two_s[e]
                cross = one_swapped * two_s[e]
                gain_re = same + swap_halves(same)
                gain_im = swap_halves(cross) - cross
                part = images[slot, p * S : (p + 1) * S].astype(F32)
                fixed.append((part * gain_re + swap_halves(part) * gain_im).astype(BF))
        tile = off_v // 128
        shift = off_v - tile * 128
        moved = pltpu.roll(right[...], shift, 1).astype(BF)
        table_re, table_im = moved[:S], moved[S:]
        shifted = jnp.concatenate(
            [
                jnp.concatenate([table_re, -table_im], axis=0),
                jnp.concatenate([table_im, table_re], axis=0),
            ],
            axis=1,
        )
        half = jnp.dot(
            jnp.concatenate(fixed, axis=0), shifted, preferred_element_type=F32
        ).astype(BF)
        eighth = off_u // 8
        placed = left[off_u - eighth * 8]
        start_u = pl.multiple_of(eighth * 8, 8)
        start_v = pl.multiple_of(tile * 128, 128)
        return start_u, start_v, shift, placed, half

    lane = lax.broadcasted_iota(jnp.int32, (1, 128), 1)

    def loop(group, carry):
        ready = [block(AT_ONCE * group + i) for i in range(AT_ONCE)]
        for start_u, start_v, shift, placed, half in ready:
            for f in range(2):
                both = []
                for p in (2 * f, 2 * f + 1):
                    part = half[p * S : (p + 1) * S]
                    both.append(jnp.concatenate([part[:, :128], part[:, 128:]], axis=0))
                grid = jnp.dot(
                    placed, jnp.concatenate(both, axis=1), preferred_element_type=F32
                )
                for e in range(2):
                    for r in range(2):
                        cells = grid[r * ROWS : (r + 1) * ROWS, 128 * e : 128 * (e + 1)]
                        cells = jnp.concatenate(
                            [
                                jnp.where(lane >= shift, cells, 0.0),
                                jnp.where(lane < shift, cells, 0.0),
                            ],
                            axis=1,
                        )
                        where = (
                            4 * f + 2 * e + r, pl.ds(start_u, ROWS), pl.ds(start_v, 256)
                        )
                        canvas[where] += cells
        return carry

    lax.fori_loop(first, last, loop, 0)


def finish_kernel(canvas, got_u, *refs):
    *got_v, out, top, side, sems = refs
    rest = pltpu.make_async_copy(
        canvas.at[:, S:TU, 128:TV], out.at[:, S:, 128:], sems.at[2]
    )
    rest.start()
    lane = lax.broadcasted_iota(jnp.int32, (1, 1, 128), 2)
    both = jnp.concatenate([x[...] for x in got_v], axis=0).astype(F32)
    low = jnp.where(lane < S, both, 0.0)
    high = jnp.where(lane < S, swap_halves(both), 0.0)
    side[:, : TU // 2 - S] = canvas[:, S : TU // 2, :128] + low[:, S:]
    side[:, TU // 2 - S :] = canvas[:, TU // 2 : TU, :128] + high
    store_side = pltpu.make_async_copy(side, out.at[:, S:, :128], sems.at[1])
    store_side.start()
    top[...] = canvas[:, :S, :TV] + got_u[...].astype(F32)
    top[:, :, :128] += low[:, :S]
    store_top = pltpu.make_async_copy(top, out.at[:, :S, :], sems.at[0])
    store_top.start()
    rest.wait()
    store_side.wait()
    store_top.wait()


def body(visibilities, tracks, offset_u, offset_v, heading, baseline, station_pair, screens):
    smem = pl.BlockSpec(memory_space=pltpu.SMEM)
    vmem = pl.BlockSpec(memory_space=pltpu.VMEM)
    hbm = pl.BlockSpec(memory_space=pltpu.HBM)
    n_au, n_vert = (lax.axis_size(axis) for axis in ("au", "vert"))
    here = screens.shape[0]
    canvas_shape = jax.ShapeDtypeStruct((8, TU + S + ROWS, TV + 128), F32)
    right_shape = jax.ShapeDtypeStruct((2 * S, 128), F32)
    left_shape = jax.ShapeDtypeStruct((8, 2 * ROWS, 2 * S), BF)
    dma = pltpu.SemaphoreType.DMA
    number = pltpu.VMEM((1, B_DEV), jnp.int32)
    images, all_screens, listing, canvas, right, left = pl.pallas_call(
        image_kernel,
        out_shape=(
            jax.ShapeDtypeStruct((SLOTS, 4 * S, 2 * S), BF),
            jax.ShapeDtypeStruct((2 * here, 2, S, 2 * S), BF),
            jax.ShapeDtypeStruct((8, 128), jnp.int32),
            canvas_shape,
            right_shape,
            left_shape,
        ),
        in_specs=[hbm] * 10,
        out_specs=(vmem,) * 6,
        scratch_shapes=[
            number,
            number,
            number,
            number,
            pltpu.VMEM(station_pair.shape, jnp.int32),
            pltpu.VMEM((2 * TB, B_DEV), BF),
            pltpu.VMEM((8 * B_DEV, K), BF),
            dma((9,)),
            pltpu.VMEM((8 * SLOTS, K), BF),
            pltpu.VMEM((SLOTS, 128), F32),
            pltpu.VMEM((8 * SLOTS, K), BF),
            pltpu.VMEM((SLOTS, 128), F32),
            pltpu.VMEM((8 * SLOTS, K), F32),
            pltpu.VMEM((SLOTS, 2 * K), F32),
            pltpu.VMEM((32, K), F32),
            pltpu.VMEM((here, 4, S * S), BF),
            pltpu.VMEM((2, 4 * S, 128), F32),
            dma((4,)),
            dma((4, 2)),
            dma((4, 2)),
            dma((5,)),
            dma((5,)),
            dma((4,)),
            dma((4,)),
            dma((4,)),
            dma((4,)),
        ],
        compiler_params=pltpu.CompilerParams(
            collective_id=0, has_side_effects=True, vmem_limit_bytes=20 << 20
        ),
    )(*(pltpu.with_memory_space_constraint(x, pltpu.HBM) for x in (
        heading.reshape(1, B_DEV), offset_u[None], offset_v[None], baseline[None],
        station_pair, tracks.transpose(1, 2, 0).reshape(2 * TB, B_DEV),
        visibilities.reshape(8 * B_DEV, K), screens,
        jnp.asarray(right_table()), jnp.asarray(left_table()),
    )))

    def grid(kernel, canvas, flops, *edges, got=()):
        return pl.pallas_call(
            kernel,
            out_shape=(canvas_shape, *edges),
            in_specs=[smem] + [vmem] * (5 + len(got)),
            out_specs=(vmem,) * (1 + len(edges)),
            input_output_aliases={5: 0},
            compiler_params=pltpu.CompilerParams(vmem_limit_bytes=12 << 20),
            cost_estimate=pl.CostEstimate(
                flops=flops, bytes_accessed=1 << 20, transcendentals=0
            ),
        )(listing, images, all_screens, right, left, canvas, *got)

    canvas, edge_u, corner = grid(
        edge_u_kernel,
        canvas,
        10**9,
        jax.ShapeDtypeStruct((8, S, TV), BF),
        jax.ShapeDtypeStruct((8, S // 2, 128), BF),
    )
    got_u = lax.ppermute(edge_u, "au", [(i, (i + 1) % n_au) for i in range(n_au)])
    diagonal = [
        (u * n_vert + v, (u + 1) % n_au * n_vert + (v + 1) % n_vert)
        for u in range(n_au)
        for v in range(n_vert)
    ]
    got_c = lax.ppermute(corner, ("au", "vert"), diagonal)
    canvas, *edge_v = grid(
        edge_v_kernel, canvas, 4 * 10**9, *[jax.ShapeDtypeStruct((8 // V_SPLIT, TU // 2, 128), BF)] * V_SPLIT
    )
    got_v = [
        lax.ppermute(x, "vert", [(i, (i + 1) % n_vert) for i in range(n_vert)]) for x in edge_v
    ]
    (canvas,) = grid(late_kernel, canvas, 10**6, got=(got_c,))
    out = pl.pallas_call(
        finish_kernel,
        out_shape=jax.ShapeDtypeStruct((8, TU, TV), F32),
        in_specs=[vmem] * (2 + V_SPLIT),
        out_specs=pl.BlockSpec(memory_space=pl.ANY),
        scratch_shapes=[
            pltpu.VMEM((8, S, TV), F32),
            pltpu.VMEM((8, TU - S, 128), F32),
            dma((3,)),
        ],
        compiler_params=pltpu.CompilerParams(vmem_limit_bytes=8 << 20),
    )(canvas, got_u, *got_v)
    return out[None]


def solution(mesh):
    placed = (
        P(("au", "vert"), None, "ch"),
        P(("au", "vert"), None, None),
        P(("au", "vert")),
        P(("au", "vert")),
        P(("au", "vert"), None),
        P(("au", "vert")),
        P(),
        P("ch", None, None),
    )
    return jax.shard_map(
        body, mesh=mesh, in_specs=placed, out_specs=P("ch", None, "au", "vert"), check_vma=False
    )
```

```python
import math

import jax
import jax.numpy as jnp
import ml_dtypes
import numpy as np
from jax import lax
from jax.experimental import pallas as pl
from jax.experimental.pallas import tpu as pltpu
from jax.sharding import PartitionSpec as P

S = 64
CH_DEV = 32
TB = 8
K = TB * CH_DEV
B_DEV = 32
CAP = B_DEV // 4
SLOTS = 5 * CAP
TU = 256
TV = 256
ROWS = 72
AT_ONCE = 4
U_GROUPS = 3
V_GROUPS = 5
V_SPLIT = 2
IMAGES_AT_ONCE = 8
RELAY_AT = (0, 1, 2, 3, 4)
MESH = pl.DeviceIdType.MESH
BF = jnp.bfloat16
F32 = jnp.float32


def series(values, degree):
    nodes = (np.cos(np.pi * (np.arange(400) + 0.5) / 400) + 1.0) * 0.125
    fitted = np.polynomial.chebyshev.Chebyshev.fit(nodes, values(nodes), degree, domain=[0, 0.25])
    return [float(c) for c in fitted.convert(kind=np.polynomial.Polynomial).coef]


COS_COEF = series(lambda q: np.cos(2 * np.pi * np.sqrt(q)), 5)
SIN_COEF = series(lambda q: np.sin(2 * np.pi * np.sqrt(q)) / np.sqrt(q), 5)


def horner(coefs, q):
    total = jnp.full_like(q, coefs[-1])
    for c in coefs[-2::-1]:
        total = total * q + jnp.float32(c)
    return total


def dft_tables():
    centred = np.arange(S) - S // 2
    product = (centred[:, None] * centred[None, :]) % S
    angles = np.float32(2.0 * math.pi / S) * product.astype(np.float32)
    scale = np.float32(1.0 / math.sqrt(S))
    re = (np.cos(angles) * scale).astype(ml_dtypes.bfloat16).astype(np.float32)
    im = (-np.sin(angles) * scale).astype(ml_dtypes.bfloat16).astype(np.float32)
    return re, im


def right_table():
    re, im = dft_tables()
    norm = np.float32(1.0 / math.sqrt(K))
    table = np.zeros((2 * S, 128), np.float32)
    table[:S, :S] = re.T * norm
    table[S:, :S] = im.T * norm
    return table


def left_table():
    re, im = dft_tables()
    order = np.concatenate([np.arange(0, S, 2), np.arange(1, S, 2)])
    re, im = re[:, order], im[:, order]
    table = np.zeros((8, 2, ROWS, 2 * S), np.float32)
    for shift in range(8):
        table[shift, 0, shift : shift + S, :S] = re
        table[shift, 0, shift : shift + S, S:] = -im
        table[shift, 1, shift : shift + S, :S] = im
        table[shift, 1, shift : shift + S, S:] = re
    return table.reshape(8, 2 * ROWS, 2 * S).astype(ml_dtypes.bfloat16)


def swap_halves(x):
    return pltpu.roll(x, S, x.ndim - 1)


def arrange_station(raw, tall):
    value = raw.astype(F32)
    for i in range(S // 2):
        tall[8 * i : 8 * i + 4, :] = value[:, 128 * i : 128 * (i + 1)]
    lane = lax.broadcasted_iota(jnp.int32, (S // 2, 128), 1)
    feeds = []
    for f in range(2):
        re = tall[pl.ds(2 * f, S // 2, stride=8), :]
        im = tall[pl.ds(2 * f + 1, S // 2, stride=8), :]
        even = jnp.where(lane < S, re, swap_halves(im))
        odd = jnp.where(lane < S, swap_halves(re), im)
        feeds.append(jnp.concatenate([even, odd], axis=0).astype(BF))
    return feeds


def pack_blocks(head, off_u, off_v, base, pairs, track, data):
    heads = head[...]
    kind = lax.broadcasted_iota(jnp.int32, (8, B_DEV), 0)
    named = jnp.where(kind == heads, 1.0, 0.0)
    before = lax.broadcasted_iota(jnp.int32, (B_DEV, B_DEV), 0)
    after = lax.broadcasted_iota(jnp.int32, (B_DEV, B_DEV), 1)
    strict = jnp.where(before < after, 1.0, 0.0).astype(BF)
    counts = jnp.dot(named.astype(BF), strict, preferred_element_type=F32)
    rank = jnp.sum(named * counts, axis=0, keepdims=True)
    slot = heads.astype(F32) * CAP + rank
    which = lax.broadcasted_iota(jnp.int32, (SLOTS, B_DEV), 0).astype(F32)
    chosen = jnp.where(which == slot, 1.0, 0.0).astype(BF)

    label = lax.broadcasted_iota(jnp.int32, (pairs.shape[1], B_DEV), 0)
    listed = jnp.where(label == base[...], 1.0, 0.0).astype(BF)
    station = jnp.dot(pairs[...].astype(F32).astype(BF), listed, preferred_element_type=F32)
    rows = jnp.concatenate(
        [
            jnp.ones((1, B_DEV), F32),
            off_u[...].astype(F32),
            off_v[...].astype(F32),
            station,
            jnp.zeros((3, B_DEV), F32),
            track[...].astype(F32),
            jnp.zeros((128 - 8 - 2 * TB, B_DEV), F32),
        ],
        axis=0,
    ).astype(BF)
    dims = (((1,), (1,)), ((), ()))
    labels = lax.dot_general(chosen, rows, dims, preferred_element_type=F32)

    owner = lax.broadcasted_iota(jnp.int32, (B_DEV, 8 * B_DEV), 0)
    column = lax.broadcasted_iota(jnp.int32, (B_DEV, 8 * B_DEV), 1)
    widen = jnp.where(owner == column // 8, 1.0, 0.0).astype(BF)
    wide = jnp.dot(
        jnp.broadcast_to(slot, (8, B_DEV)).astype(BF), widen, preferred_element_type=F32
    )[:1]
    lane = lax.broadcasted_iota(jnp.int32, (1, 8 * B_DEV), 1) % 8
    place = wide * 8.0 + lane.astype(F32)
    target = lax.broadcasted_iota(jnp.int32, (8 * SLOTS, 8 * B_DEV), 0).astype(F32)
    moved = jnp.where(target == place, 1.0, 0.0).astype(BF)
    return jnp.dot(moved, data[...], preferred_element_type=F32).astype(BF), labels


def list_blocks(labels):
    dims = (((1,), (1,)), ((), ()))
    quantity = lax.broadcasted_iota(jnp.int32, (8, 128), 0)
    lane = lax.broadcasted_iota(jnp.int32, (8, 128), 1)
    pick = jnp.where(quantity == lane, 1.0, 0.0).astype(BF)
    rows = lax.dot_general(pick, labels.astype(BF), dims, preferred_element_type=F32)
    filled, at_u, at_v = rows[0:1], rows[1:2], rows[2:3]
    past_u = at_u > TU - S
    past = jnp.logical_or(past_u, at_v > TV - S)
    first = jnp.where(past_u, filled, 0.0)
    early = jnp.where(past, filled, 0.0)
    kind = lax.broadcasted_iota(jnp.int32, (8, SLOTS), 0)
    both = jnp.where(
        kind == 0,
        first,
        jnp.where(kind == 1, early - first, jnp.where(kind == 2, filled - early, 0.0)),
    )
    before = lax.broadcasted_iota(jnp.int32, (SLOTS, SLOTS), 0)
    after = lax.broadcasted_iota(jnp.int32, (SLOTS, SLOTS), 1)
    strict = jnp.where(before < after, 1.0, 0.0).astype(BF)
    ahead = jnp.dot(both.astype(BF), strict, preferred_element_type=F32)
    number_first = jnp.sum(first, axis=1, keepdims=True)
    number_early = jnp.sum(early, axis=1, keepdims=True)
    number = jnp.sum(filled, axis=1, keepdims=True)
    place = jnp.where(past, number_first + ahead[1:2], number_early + ahead[2:3])
    place = jnp.where(past_u, ahead[0:1], place)
    place = jnp.where(filled > 0.5, place, -1.0)
    target = lax.broadcasted_iota(jnp.int32, (128, SLOTS), 0).astype(F32)
    moved = jnp.where(target == place, 1.0, 0.0).astype(BF)
    slot = lax.broadcasted_iota(jnp.int32, (8, SLOTS), 1).astype(F32)
    rows = jnp.where(kind == 0, slot, rows)
    table = lax.dot_general(rows.astype(BF), moved, dims, preferred_element_type=F32)
    spare = jnp.where(lane.astype(F32) >= number, float(TU + S), 0.0)
    table = table + jnp.where(quantity == 1, spare, 0.0)
    groups = jnp.floor((number + (AT_ONCE - 1.0)) / AT_ONCE)
    ends = []
    for count, least in ((number_first, U_GROUPS), (number_early, V_GROUPS)):
        enough = jnp.minimum(groups, float(least))
        needed = jnp.floor((count + (AT_ONCE - 1.0)) / AT_ONCE)
        ends.append(jnp.maximum(needed, enough))
    for row, end in enumerate((*ends, groups)):
        table = jnp.where(quantity == 5 + row, end, table)
    return table.astype(jnp.int32)


def image_kernel(
    head_in, off_u_in, off_v_in, base_in, pairs_in, track_in, data_in, own_screens,
    right_in, left_in,
    images, screens, listing, canvas, right, left,
    head, off_u, off_v, base, pairs, track, data, table, in_sems,
    packed, labels, got_data, got_labels, samples, spread, mult, raw, tall,
    own_sems, send_sems, recv_sems, y_send, y_recv, relay_send, relay_recv, c_send, c_recv,
):
    au, vert, band = (lax.axis_index(axis) for axis in ("au", "vert", "ch"))
    n_au, n_vert, n_ch = (lax.axis_size(axis) for axis in ("au", "vert", "ch"))
    here = own_screens.shape[0]
    unit = here // 32
    core = lax.rem(vert, 2)
    colour = lax.rem(vert // 2 + au, 2)
    mine = 16 * core + 10 * colour
    common = 16 * core + 6
    others = 16 * core + 10 * (1 - colour)

    def turned(step):
        return lax.rem(vert + step, n_vert)

    near = (
        {"au": lax.rem(au + 1, n_au)},
        {"au": lax.rem(au + n_au - 1, n_au)},
        {"vert": turned(1)},
        {"vert": turned(n_vert - 1)},
    )
    across = {"ch": lax.rem(band + 1, n_ch)}
    sibling = {"vert": vert + 1 - 2 * core}
    beside = {"vert": vert + 2 - 4 * lax.rem(vert // 2, 2)}
    along = {"au": au + 1 - 2 * lax.rem(au, 2)}

    inputs = (
        (head_in, head), (off_u_in, off_u), (off_v_in, off_v), (base_in, base),
        (pairs_in, pairs), (track_in, track), (data_in, data),
        (right_in, right), (left_in, left),
    )
    loads = [
        pltpu.make_async_copy(source, target, in_sems.at[j])
        for j, (source, target) in enumerate(inputs)
    ]
    for copy in loads:
        copy.start()
    fetches = []
    spans = ((mine, 6), (common, 4), (others, 6), (16 * (1 - core), 16))
    for j, (first, count) in enumerate(spans):
        rows = pl.ds(first * unit, count * unit)
        fetches.append(
            pltpu.make_async_copy(own_screens.at[rows], raw.at[rows], own_sems.at[j])
        )
        fetches[-1].start()
    barrier = pltpu.get_barrier_semaphore()
    for device in (*near, across, beside):
        pl.semaphore_signal(barrier, inc=1, device_id=device, device_id_type=MESH)

    def arrange(first, number):
        def one(pair, carry):
            for i in range(2):
                station = first * unit + 2 * pair + i
                feeds = arrange_station(raw[station], tall.at[i])
                for f in range(2):
                    screens[station, f] = feeds[f]
            return carry

        lax.fori_loop(0, number * unit // 2, one, 0)

    fetches[0].wait()
    arrange(mine, 6)
    fetches[1].wait()
    arrange(common, 4)
    pl.semaphore_wait(barrier, 6)

    def moves(i):
        pairs_of = ((packed, got_data, 8 * CAP), (labels, got_labels, CAP))
        for j, (source, target, rows) in enumerate(pairs_of):
            where = pl.ds((i + 1) * rows, rows)
            yield pltpu.make_async_remote_copy(
                src_ref=source.at[where],
                dst_ref=target.at[where],
                send_sem=send_sems.at[i, j],
                recv_sem=recv_sems.at[i, j],
                device_id=near[i],
                device_id_type=MESH,
            )

    def send(number, count, send_sem, recv_sem, device, own=False):
        where = number * unit
        return pltpu.make_async_remote_copy(
            src_ref=screens.at[pl.ds(where if own else here + where, count * unit)],
            dst_ref=screens.at[pl.ds(here + where, count * unit)],
            send_sem=send_sem,
            recv_sem=recv_sem,
            device_id=device,
            device_id_type=MESH,
        )

    runs = ((0, 2), (2, 2), (4, 1), (5, 1))

    def y_copy(k):
        first, count = (common, 4) if k == 4 else (mine + runs[k][0], runs[k][1])
        return send(first, count, y_send.at[k], y_recv.at[k], across, True)

    def relayed(k, first):
        device = beside if k % 2 == 0 else along
        start, count = runs[k]
        return send(first + start, count, relay_send.at[k], relay_recv.at[k], device)

    def c_copy(k, half):
        first = (
            half + 10 * colour, half + 6, half + 10 * (1 - colour), half + 10 * (1 - colour) + 4
        )[k]
        return send(first, (6, 4, 4, 2)[k], c_send.at[k], c_recv.at[k], sibling)

    for k in range(5):
        y_copy(k).start()

    for copy in loads[:7]:
        copy.wait()
    values, rows = pack_blocks(head, off_u, off_v, base, pairs, track, data)
    packed[...] = values
    labels[...] = rows

    for i in range(4):
        for copy in moves(i):
            copy.start()

    canvas[...] = jnp.zeros_like(canvas)
    for copy in fetches[2:]:
        copy.wait()
    arrange(others, 6)
    arrange(16 * (1 - core), 16)

    row = lax.broadcasted_iota(jnp.int32, (32, K), 0)
    channel = band * CH_DEV + lax.broadcasted_iota(jnp.int32, (32, K), 1) % CH_DEV
    ratio = 1.0 + channel.astype(F32) / jnp.float32(2 * CH_DEV * n_ch)
    coarse = row - 8
    coarse_u = 16 * (coarse % 4) + coarse // 4 - S // 2
    fine_v = row - 16
    coarse_v = (row - 24) * 8 - S // 2
    step = jnp.where(
        row < 16, jnp.where(row < 8, 2 * row, coarse_u), jnp.where(row < 24, fine_v, coarse_v)
    )
    mult[...] = step.astype(F32) / S * ratio

    def widen(rows):
        source = lax.broadcasted_iota(jnp.int32, (128, 2 * K), 0)
        column = lax.broadcasted_iota(jnp.int32, (128, 2 * K), 1)
        chosen = jnp.where(source == 8 + column // CH_DEV, 1.0, 0.0).astype(BF)
        lane = lax.broadcasted_iota(jnp.int32, rows.shape, 1)
        only = jnp.where(lane < 8, 0.0, rows).astype(BF)
        return jnp.dot(only, chosen, preferred_element_type=F32)

    got_labels[:CAP] = labels[:CAP]
    samples[: 8 * CAP] = packed[: 8 * CAP].astype(F32)
    spread[:CAP] = widen(labels[:CAP])

    def block(slot):
        sample = samples[pl.ds(8 * slot, 8), :]
        track = spread[pl.ds(slot, 1), :]
        turns = jnp.concatenate(
            [track[:, :K] * mult[:16], track[:, K:] * mult[16:]], axis=0
        )
        frac = turns - jnp.floor(turns + 0.5)
        square = frac * frac
        cos = horner(COS_COEF, square)
        sin = horner(SIN_COEF, square) * frac

        def phasors(first):
            cos_fine, sin_fine = cos[first : first + 8], sin[first : first + 8]
            all_cos, all_sin = [], []
            for a in range(8):
                at = first + 8 + a
                cos_a, sin_a = cos[at : at + 1], sin[at : at + 1]
                all_cos.append(cos_fine * cos_a - sin_fine * sin_a)
                all_sin.append(sin_fine * cos_a + cos_fine * sin_a)
            return (
                jnp.concatenate(all_cos, axis=0).astype(BF),
                jnp.concatenate(all_sin, axis=0).astype(BF),
            )

        cos_u, sin_u = phasors(0)
        cos_v, sin_v = phasors(16)
        table = jnp.concatenate(
            [
                jnp.concatenate([cos_v, -sin_v], axis=1),
                jnp.concatenate([sin_v, cos_v], axis=1),
            ],
            axis=0,
        )

        def spread_row(r):
            row = jnp.broadcast_to(sample[r : r + 1], (16, K)).astype(BF)
            return jnp.concatenate([row] * (S // 16), axis=0)

        weighed = []
        for p in range(4):
            re, im = spread_row(2 * p), spread_row(2 * p + 1)
            weighed.append(
                jnp.concatenate([re * cos_u - im * sin_u, re * sin_u + im * cos_u], axis=1)
            )
        dims = (((1,), (1,)), ((), ()))
        image = lax.dot_general(
            jnp.concatenate(weighed, axis=0), table, dims, preferred_element_type=F32
        )
        return image.astype(BF)

    keep = pltpu.make_async_copy(table, listing, in_sems.at[9])
    here_half, other_half = 16 * core, 16 * (1 - core)

    def relay(stage):
        if stage < 3:
            for k in ((0,), (1,), (2, 3))[stage]:
                y_copy(k).wait_recv()
                relayed(k, mine).start()
            if stage == 2:
                c_copy(0, here_half).start()
        elif stage == 3:
            for k in (0, 1):
                relayed(k, others).wait_recv()
            c_copy(2, here_half).start()
        else:
            y_copy(4).wait_recv()
            c_copy(1, here_half).start()
            for k in (2, 3):
                relayed(k, others).wait_recv()
            c_copy(3, here_half).start()

    def loop(group, carry):
        @pl.when(group == CAP // IMAGES_AT_ONCE)
        def _():
            for i in range(4):
                for copy in moves(i):
                    copy.wait_recv()
            samples[8 * CAP :] = got_data[8 * CAP :].astype(F32)
            spread[CAP:] = widen(got_labels[CAP:])
            table[...] = list_blocks(got_labels[...])
            keep.start()

        for stage, at in enumerate(RELAY_AT):

            @pl.when(group == at)
            def _():
                relay(stage)

        made = [block(IMAGES_AT_ONCE * group + i) for i in range(IMAGES_AT_ONCE)]
        for i in range(IMAGES_AT_ONCE):
            images[IMAGES_AT_ONCE * group + i] = made[i]
        return carry

    lax.fori_loop(0, SLOTS // IMAGES_AT_ONCE, loop, 0)
    for copy in loads[7:]:
        copy.wait()
    keep.wait()
    for i in range(4):
        for copy in moves(i):
            copy.wait_send()
    for k in range(5):
        y_copy(k).wait_send()
    for k in range(4):
        relayed(k, mine).wait_send()
        c_copy(k, here_half).wait_send()
        c_copy(k, other_half).wait_recv()


def folded(x):
    middle = x.shape[1] // 2
    lane = lax.broadcasted_iota(jnp.int32, (1, 1, 128), 2)
    return jnp.where(lane < S, x[:, :middle], swap_halves(x[:, middle:])).astype(BF)


def edge_u_kernel(listing, images, screens, right, left, canvas_in, canvas, edge_u, corner):
    grid_blocks(images, screens, canvas, right, left, listing, 0, listing[5, 0])
    edge_u[...] = canvas[:, TU : TU + S, :TV].astype(BF)
    corner[...] = folded(canvas[:, TU : TU + S, TV:])


def edge_v_kernel(listing, images, screens, right, left, canvas_in, canvas, *edge_v):
    grid_blocks(images, screens, canvas, right, left, listing, listing[5, 0], listing[6, 0])
    each = 8 // V_SPLIT
    for i, edge in enumerate(edge_v):
        edge[...] = folded(canvas[i * each : (i + 1) * each, :TU, TV:])


def late_kernel(listing, images, screens, right, left, canvas_in, canvas):
    grid_blocks(images, screens, canvas, right, left, listing, listing[6, 0], listing[7, 0])


def grid_blocks(images, screens, canvas, right, left, listing, first, last):
    here = screens.shape[0] // 2
    band = lax.axis_index("ch")

    def screen_place(station):
        owner = station // here
        local = station - owner * here
        return jnp.where(owner == band, local, here + local)

    def block(index):
        slot = listing[0, index]
        off_u = listing[1, index]
        off_v = listing[2, index]
        one = screen_place(listing[3, index])
        two = screen_place(listing[4, index])
        two_s = [screens[two, f].astype(F32) for f in range(2)]
        fixed = []
        for f in range(2):
            one_s = screens[one, f].astype(F32)
            one_swapped = swap_halves(one_s)
            for e in range(2):
                p = 2 * f + e
                same = one_s * two_s[e]
                cross = one_swapped * two_s[e]
                gain_re = same + swap_halves(same)
                gain_im = swap_halves(cross) - cross
                part = images[slot, p * S : (p + 1) * S].astype(F32)
                fixed.append((part * gain_re + swap_halves(part) * gain_im).astype(BF))
        tile = off_v // 128
        shift = off_v - tile * 128
        moved = pltpu.roll(right[...], shift, 1).astype(BF)
        table_re, table_im = moved[:S], moved[S:]
        shifted = jnp.concatenate(
            [
                jnp.concatenate([table_re, -table_im], axis=0),
                jnp.concatenate([table_im, table_re], axis=0),
            ],
            axis=1,
        )
        half = jnp.dot(
            jnp.concatenate(fixed, axis=0), shifted, preferred_element_type=F32
        ).astype(BF)
        eighth = off_u // 8
        placed = left[off_u - eighth * 8]
        start_u = pl.multiple_of(eighth * 8, 8)
        start_v = pl.multiple_of(tile * 128, 128)
        return start_u, start_v, shift, placed, half

    lane = lax.broadcasted_iota(jnp.int32, (1, 128), 1)

    def loop(group, carry):
        ready = [block(AT_ONCE * group + i) for i in range(AT_ONCE)]
        for start_u, start_v, shift, placed, half in ready:
            for f in range(2):
                both = []
                for p in (2 * f, 2 * f + 1):
                    part = half[p * S : (p + 1) * S]
                    both.append(jnp.concatenate([part[:, :128], part[:, 128:]], axis=0))
                grid = jnp.dot(
                    placed, jnp.concatenate(both, axis=1), preferred_element_type=F32
                )
                for e in range(2):
                    for r in range(2):
                        cells = grid[r * ROWS : (r + 1) * ROWS, 128 * e : 128 * (e + 1)]
                        cells = jnp.concatenate(
                            [
                                jnp.where(lane >= shift, cells, 0.0),
                                jnp.where(lane < shift, cells, 0.0),
                            ],
                            axis=1,
                        )
                        where = (
                            4 * f + 2 * e + r, pl.ds(start_u, ROWS), pl.ds(start_v, 256)
                        )
                        canvas[where] += cells
        return carry

    lax.fori_loop(first, last, loop, 0)


def lower_kernel(canvas, *refs):
    *got_v, out, top, side, sems = refs
    rest = pltpu.make_async_copy(
        canvas.at[:, S:TU, 128:TV], out.at[:, S:, 128:], sems.at[0]
    )
    rest.start()
    lane = lax.broadcasted_iota(jnp.int32, (1, 1, 128), 2)
    both = jnp.concatenate([x[...] for x in got_v], axis=0).astype(F32)
    low = jnp.where(lane < S, both, 0.0)
    high = jnp.where(lane < S, swap_halves(both), 0.0)
    side[:, : TU // 2 - S] = canvas[:, S : TU // 2, :128] + low[:, S:]
    side[:, TU // 2 - S :] = canvas[:, TU // 2 : TU, :128] + high
    store_side = pltpu.make_async_copy(side, out.at[:, S:, :128], sems.at[1])
    store_side.start()
    top[:, :, :128] = canvas[:, :S, :128] + low[:, :S]
    top[:, :, 128:] = canvas[:, :S, 128:TV]
    rest.wait()
    store_side.wait()


def upper_kernel(lower, top, got_u, got_c, out, rows, sems):
    lane = lax.broadcasted_iota(jnp.int32, (1, 1, 128), 2)
    stores = []
    for i in range(2):
        planes = slice(4 * i, 4 * i + 4)
        rows[planes] = top[planes] + got_u[planes].astype(F32)
        both = got_c[planes].astype(F32)
        rows[planes, : S // 2, :128] += jnp.where(lane < S, both, 0.0)
        rows[planes, S // 2 :, :128] += jnp.where(lane < S, swap_halves(both), 0.0)
        stores.append(
            pltpu.make_async_copy(rows.at[planes], out.at[planes, :S, :], sems.at[i])
        )
        stores[-1].start()
    for store in stores:
        store.wait()


def body(visibilities, tracks, offset_u, offset_v, heading, baseline, station_pair, screens):
    smem = pl.BlockSpec(memory_space=pltpu.SMEM)
    vmem = pl.BlockSpec(memory_space=pltpu.VMEM)
    hbm = pl.BlockSpec(memory_space=pltpu.HBM)
    n_au, n_vert = (lax.axis_size(axis) for axis in ("au", "vert"))
    here = screens.shape[0]
    canvas_shape = jax.ShapeDtypeStruct((8, TU + S + ROWS, TV + 128), F32)
    right_shape = jax.ShapeDtypeStruct((2 * S, 128), F32)
    left_shape = jax.ShapeDtypeStruct((8, 2 * ROWS, 2 * S), BF)
    dma = pltpu.SemaphoreType.DMA
    number = pltpu.VMEM((1, B_DEV), jnp.int32)
    images, all_screens, listing, canvas, right, left = pl.pallas_call(
        image_kernel,
        out_shape=(
            jax.ShapeDtypeStruct((SLOTS, 4 * S, 2 * S), BF),
            jax.ShapeDtypeStruct((2 * here, 2, S, 2 * S), BF),
            pltpu.SMEM((8, 128), jnp.int32),
            canvas_shape,
            right_shape,
            left_shape,
        ),
        in_specs=[hbm] * 10,
        out_specs=(vmem, vmem, smem, vmem, vmem, vmem),
        scratch_shapes=[
            number,
            number,
            number,
            number,
            pltpu.VMEM(station_pair.shape, jnp.int32),
            pltpu.VMEM((2 * TB, B_DEV), BF),
            pltpu.VMEM((8 * B_DEV, K), BF),
            pltpu.VMEM((8, 128), jnp.int32),
            dma((10,)),
            pltpu.VMEM((8 * SLOTS, K), BF),
            pltpu.VMEM((SLOTS, 128), F32),
            pltpu.VMEM((8 * SLOTS, K), BF),
            pltpu.VMEM((SLOTS, 128), F32),
            pltpu.VMEM((8 * SLOTS, K), F32),
            pltpu.VMEM((SLOTS, 2 * K), F32),
            pltpu.VMEM((32, K), F32),
            pltpu.VMEM((here, 4, S * S), BF),
            pltpu.VMEM((2, 4 * S, 128), F32),
            dma((4,)),
            dma((4, 2)),
            dma((4, 2)),
            dma((5,)),
            dma((5,)),
            dma((4,)),
            dma((4,)),
            dma((4,)),
            dma((4,)),
        ],
        compiler_params=pltpu.CompilerParams(
            collective_id=0, has_side_effects=True, vmem_limit_bytes=20 << 20
        ),
    )(*(pltpu.with_memory_space_constraint(x, pltpu.HBM) for x in (
        heading.reshape(1, B_DEV), offset_u[None], offset_v[None], baseline[None],
        station_pair, tracks.transpose(1, 2, 0).reshape(2 * TB, B_DEV),
        visibilities.reshape(8 * B_DEV, K), screens,
        jnp.asarray(right_table()), jnp.asarray(left_table()),
    )))

    def grid(kernel, canvas, flops, *edges):
        return pl.pallas_call(
            kernel,
            out_shape=(canvas_shape, *edges),
            in_specs=[smem] + [vmem] * 5,
            out_specs=(vmem,) * (1 + len(edges)),
            input_output_aliases={5: 0},
            compiler_params=pltpu.CompilerParams(vmem_limit_bytes=12 << 20),
            cost_estimate=pl.CostEstimate(
                flops=flops, bytes_accessed=1 << 20, transcendentals=0
            ),
        )(listing, images, all_screens, right, left, canvas)

    canvas, edge_u, corner = grid(
        edge_u_kernel,
        canvas,
        10**9,
        jax.ShapeDtypeStruct((8, S, TV), BF),
        jax.ShapeDtypeStruct((8, S // 2, 128), BF),
    )
    got_u = lax.ppermute(edge_u, "au", [(i, (i + 1) % n_au) for i in range(n_au)])
    diagonal = [
        (u * n_vert + v, (u + 1) % n_au * n_vert + (v + 1) % n_vert)
        for u in range(n_au)
        for v in range(n_vert)
    ]
    got_c = lax.ppermute(corner, ("au", "vert"), diagonal)
    canvas, *edge_v = grid(
        edge_v_kernel, canvas, 4 * 10**9, *[jax.ShapeDtypeStruct((8 // V_SPLIT, TU // 2, 128), BF)] * V_SPLIT
    )
    got_v = [
        lax.ppermute(x, "vert", [(i, (i + 1) % n_vert) for i in range(n_vert)]) for x in edge_v
    ]
    (canvas,) = grid(late_kernel, canvas, 10**6)
    tile = jax.ShapeDtypeStruct((8, TU, TV), F32)
    out, top = pl.pallas_call(
        lower_kernel,
        out_shape=(tile, jax.ShapeDtypeStruct((8, S, TV), F32)),
        in_specs=[vmem] * (1 + V_SPLIT),
        out_specs=(pl.BlockSpec(memory_space=pl.ANY), vmem),
        scratch_shapes=[pltpu.VMEM((8, TU - S, 128), F32), dma((2,))],
        compiler_params=pltpu.CompilerParams(vmem_limit_bytes=8 << 20),
    )(canvas, *got_v)
    out = pl.pallas_call(
        upper_kernel,
        out_shape=tile,
        in_specs=[pl.BlockSpec(memory_space=pl.ANY)] + [vmem] * 3,
        out_specs=pl.BlockSpec(memory_space=pl.ANY),
        scratch_shapes=[pltpu.VMEM((8, S, TV), F32), dma((2,))],
        input_output_aliases={0: 0},
        compiler_params=pltpu.CompilerParams(vmem_limit_bytes=8 << 20),
    )(out, top, got_u, got_c)
    return out[None]


def solution(mesh):
    placed = (
        P(("au", "vert"), None, "ch"),
        P(("au", "vert"), None, None),
        P(("au", "vert")),
        P(("au", "vert")),
        P(("au", "vert"), None),
        P(("au", "vert")),
        P(),
        P("ch", None, None),
    )
    return jax.shard_map(
        body, mesh=mesh, in_specs=placed, out_specs=P("ch", None, "au", "vert"), check_vma=False
    )
```

```python
import math

import jax
import jax.numpy as jnp
import ml_dtypes
import numpy as np
from jax import lax
from jax.experimental import pallas as pl
from jax.experimental.pallas import tpu as pltpu
from jax.sharding import PartitionSpec as P

S = 64
CH_DEV = 32
TB = 8
K = TB * CH_DEV
B_DEV = 32
CAP = B_DEV // 4
SLOTS = 5 * CAP
TU = 256
TV = 256
ROWS = 72
AT_ONCE = 4
U_GROUPS = 3
V_GROUPS = 5
V_SPLIT = 2
IMAGES_AT_ONCE = 8
RELAY_AT = (0, 1, 2, 3, 4)
MESH = pl.DeviceIdType.MESH
BF = jnp.bfloat16
F32 = jnp.float32


def series(values, degree):
    nodes = (np.cos(np.pi * (np.arange(400) + 0.5) / 400) + 1.0) * 0.125
    fitted = np.polynomial.chebyshev.Chebyshev.fit(nodes, values(nodes), degree, domain=[0, 0.25])
    return [float(c) for c in fitted.convert(kind=np.polynomial.Polynomial).coef]


COS_COEF = series(lambda q: np.cos(2 * np.pi * np.sqrt(q)), 5)
SIN_COEF = series(lambda q: np.sin(2 * np.pi * np.sqrt(q)) / np.sqrt(q), 5)


def horner(coefs, q):
    total = jnp.full_like(q, coefs[-1])
    for c in coefs[-2::-1]:
        total = total * q + jnp.float32(c)
    return total


def dft_tables():
    centred = np.arange(S) - S // 2
    product = (centred[:, None] * centred[None, :]) % S
    angles = np.float32(2.0 * math.pi / S) * product.astype(np.float32)
    scale = np.float32(1.0 / math.sqrt(S))
    re = (np.cos(angles) * scale).astype(ml_dtypes.bfloat16).astype(np.float32)
    im = (-np.sin(angles) * scale).astype(ml_dtypes.bfloat16).astype(np.float32)
    return re, im


def right_table():
    re, im = dft_tables()
    norm = np.float32(1.0 / math.sqrt(K))
    table = np.zeros((2 * S, 128), np.float32)
    table[:S, :S] = re.T * norm
    table[S:, :S] = im.T * norm
    return table


def left_table():
    re, im = dft_tables()
    order = np.concatenate([np.arange(0, S, 2), np.arange(1, S, 2)])
    re, im = re[:, order], im[:, order]
    table = np.zeros((8, 2, ROWS, 2 * S), np.float32)
    for shift in range(8):
        table[shift, 0, shift : shift + S, :S] = re
        table[shift, 0, shift : shift + S, S:] = -im
        table[shift, 1, shift : shift + S, :S] = im
        table[shift, 1, shift : shift + S, S:] = re
    return table.reshape(8, 2 * ROWS, 2 * S).astype(ml_dtypes.bfloat16)


def swap_halves(x):
    return pltpu.roll(x, S, x.ndim - 1)


def arrange_station(raw, tall):
    value = raw.astype(F32)
    for i in range(S // 2):
        tall[8 * i : 8 * i + 4, :] = value[:, 128 * i : 128 * (i + 1)]
    lane = lax.broadcasted_iota(jnp.int32, (S // 2, 128), 1)
    feeds = []
    for f in range(2):
        re = tall[pl.ds(2 * f, S // 2, stride=8), :]
        im = tall[pl.ds(2 * f + 1, S // 2, stride=8), :]
        even = jnp.where(lane < S, re, swap_halves(im))
        odd = jnp.where(lane < S, swap_halves(re), im)
        feeds.append(jnp.concatenate([even, odd], axis=0).astype(BF))
    return feeds


def pack_blocks(head, off_u, off_v, base, pairs, track, data):
    heads = head[...]
    kind = lax.broadcasted_iota(jnp.int32, (8, B_DEV), 0)
    named = jnp.where(kind == heads, 1.0, 0.0)
    before = lax.broadcasted_iota(jnp.int32, (B_DEV, B_DEV), 0)
    after = lax.broadcasted_iota(jnp.int32, (B_DEV, B_DEV), 1)
    strict = jnp.where(before < after, 1.0, 0.0).astype(BF)
    counts = jnp.dot(named.astype(BF), strict, preferred_element_type=F32)
    rank = jnp.sum(named * counts, axis=0, keepdims=True)
    slot = heads.astype(F32) * CAP + rank
    which = lax.broadcasted_iota(jnp.int32, (SLOTS, B_DEV), 0).astype(F32)
    chosen = jnp.where(which == slot, 1.0, 0.0).astype(BF)

    label = lax.broadcasted_iota(jnp.int32, (pairs.shape[1], B_DEV), 0)
    listed = jnp.where(label == base[...], 1.0, 0.0).astype(BF)
    station = jnp.dot(pairs[...].astype(F32).astype(BF), listed, preferred_element_type=F32)
    rows = jnp.concatenate(
        [
            jnp.ones((1, B_DEV), F32),
            off_u[...].astype(F32),
            off_v[...].astype(F32),
            station,
            jnp.zeros((3, B_DEV), F32),
            track[...].astype(F32),
            jnp.zeros((128 - 8 - 2 * TB, B_DEV), F32),
        ],
        axis=0,
    ).astype(BF)
    dims = (((1,), (1,)), ((), ()))
    labels = lax.dot_general(chosen, rows, dims, preferred_element_type=F32)

    owner = lax.broadcasted_iota(jnp.int32, (B_DEV, 8 * B_DEV), 0)
    column = lax.broadcasted_iota(jnp.int32, (B_DEV, 8 * B_DEV), 1)
    widen = jnp.where(owner == column // 8, 1.0, 0.0).astype(BF)
    wide = jnp.dot(
        jnp.broadcast_to(slot, (8, B_DEV)).astype(BF), widen, preferred_element_type=F32
    )[:1]
    lane = lax.broadcasted_iota(jnp.int32, (1, 8 * B_DEV), 1) % 8
    place = wide * 8.0 + lane.astype(F32)
    target = lax.broadcasted_iota(jnp.int32, (8 * SLOTS, 8 * B_DEV), 0).astype(F32)
    moved = jnp.where(target == place, 1.0, 0.0).astype(BF)
    return jnp.dot(moved, data[...], preferred_element_type=F32).astype(BF), labels


def list_blocks(labels):
    dims = (((1,), (1,)), ((), ()))
    quantity = lax.broadcasted_iota(jnp.int32, (8, 128), 0)
    lane = lax.broadcasted_iota(jnp.int32, (8, 128), 1)
    pick = jnp.where(quantity == lane, 1.0, 0.0).astype(BF)
    rows = lax.dot_general(pick, labels.astype(BF), dims, preferred_element_type=F32)
    filled, at_u, at_v = rows[0:1], rows[1:2], rows[2:3]
    past_u = at_u > TU - S
    past = jnp.logical_or(past_u, at_v > TV - S)
    first = jnp.where(past_u, filled, 0.0)
    early = jnp.where(past, filled, 0.0)
    kind = lax.broadcasted_iota(jnp.int32, (8, SLOTS), 0)
    both = jnp.where(
        kind == 0,
        first,
        jnp.where(kind == 1, early - first, jnp.where(kind == 2, filled - early, 0.0)),
    )
    before = lax.broadcasted_iota(jnp.int32, (SLOTS, SLOTS), 0)
    after = lax.broadcasted_iota(jnp.int32, (SLOTS, SLOTS), 1)
    strict = jnp.where(before < after, 1.0, 0.0).astype(BF)
    ahead = jnp.dot(both.astype(BF), strict, preferred_element_type=F32)
    number_first = jnp.sum(first, axis=1, keepdims=True)
    number_early = jnp.sum(early, axis=1, keepdims=True)
    number = jnp.sum(filled, axis=1, keepdims=True)
    place = jnp.where(past, number_first + ahead[1:2], number_early + ahead[2:3])
    place = jnp.where(past_u, ahead[0:1], place)
    place = jnp.where(filled > 0.5, place, -1.0)
    target = lax.broadcasted_iota(jnp.int32, (128, SLOTS), 0).astype(F32)
    moved = jnp.where(target == place, 1.0, 0.0).astype(BF)
    slot = lax.broadcasted_iota(jnp.int32, (8, SLOTS), 1).astype(F32)
    rows = jnp.where(kind == 0, slot, rows)
    table = lax.dot_general(rows.astype(BF), moved, dims, preferred_element_type=F32)
    spare = jnp.where(lane.astype(F32) >= number, float(TU + S), 0.0)
    table = table + jnp.where(quantity == 1, spare, 0.0)
    groups = jnp.floor((number + (AT_ONCE - 1.0)) / AT_ONCE)
    ends = []
    for count, least in ((number_first, U_GROUPS), (number_early, V_GROUPS)):
        enough = jnp.minimum(groups, float(least))
        needed = jnp.floor((count + (AT_ONCE - 1.0)) / AT_ONCE)
        ends.append(jnp.maximum(needed, enough))
    for row, end in enumerate((*ends, groups)):
        table = jnp.where(quantity == 5 + row, end, table)
    return table.astype(jnp.int32)


def image_kernel(
    head_in, off_u_in, off_v_in, base_in, pairs_in, track_in, data_in, own_screens,
    right_in, left_in,
    images, screens, listing, canvas, right, left,
    head, off_u, off_v, base, pairs, track, data, table, in_sems,
    packed, labels, got_data, got_labels, samples, spread, mult, raw, tall,
    own_sems, send_sems, recv_sems, y_send, y_recv, relay_send, relay_recv, c_send, c_recv,
):
    au, vert, band = (lax.axis_index(axis) for axis in ("au", "vert", "ch"))
    n_au, n_vert, n_ch = (lax.axis_size(axis) for axis in ("au", "vert", "ch"))
    here = own_screens.shape[0]
    unit = here // 32
    core = lax.rem(vert, 2)
    colour = lax.rem(vert // 2 + au, 2)
    mine = 16 * core + 10 * colour
    common = 16 * core + 6
    others = 16 * core + 10 * (1 - colour)

    def turned(step):
        return lax.rem(vert + step, n_vert)

    near = (
        {"au": lax.rem(au + 1, n_au)},
        {"au": lax.rem(au + n_au - 1, n_au)},
        {"vert": turned(1)},
        {"vert": turned(n_vert - 1)},
    )
    across = {"ch": lax.rem(band + 1, n_ch)}
    sibling = {"vert": vert + 1 - 2 * core}
    beside = {"vert": vert + 2 - 4 * lax.rem(vert // 2, 2)}
    along = {"au": au + 1 - 2 * lax.rem(au, 2)}

    inputs = (
        (head_in, head), (off_u_in, off_u), (off_v_in, off_v), (base_in, base),
        (pairs_in, pairs), (track_in, track), (data_in, data),
        (right_in, right), (left_in, left),
    )
    loads = [
        pltpu.make_async_copy(source, target, in_sems.at[j])
        for j, (source, target) in enumerate(inputs)
    ]
    for copy in loads:
        copy.start()
    fetches = []
    spans = ((mine, 6), (common, 4), (others, 6), (16 * (1 - core), 16))
    for j, (first, count) in enumerate(spans):
        rows = pl.ds(first * unit, count * unit)
        fetches.append(
            pltpu.make_async_copy(own_screens.at[rows], raw.at[rows], own_sems.at[j])
        )
        fetches[-1].start()
    barrier = pltpu.get_barrier_semaphore()
    for device in (*near, across, beside):
        pl.semaphore_signal(barrier, inc=1, device_id=device, device_id_type=MESH)

    def arrange(first, number):
        def one(pair, carry):
            for i in range(2):
                station = first * unit + 2 * pair + i
                feeds = arrange_station(raw[station], tall.at[i])
                for f in range(2):
                    screens[station, f] = feeds[f]
            return carry

        lax.fori_loop(0, number * unit // 2, one, 0)

    fetches[0].wait()
    arrange(mine, 6)
    fetches[1].wait()
    arrange(common, 4)
    pl.semaphore_wait(barrier, 6)

    def moves(i):
        pairs_of = ((packed, got_data, 8 * CAP), (labels, got_labels, CAP))
        for j, (source, target, rows) in enumerate(pairs_of):
            where = pl.ds((i + 1) * rows, rows)
            yield pltpu.make_async_remote_copy(
                src_ref=source.at[where],
                dst_ref=target.at[where],
                send_sem=send_sems.at[i, j],
                recv_sem=recv_sems.at[i, j],
                device_id=near[i],
                device_id_type=MESH,
            )

    def send(number, count, send_sem, recv_sem, device, own=False):
        where = number * unit
        return pltpu.make_async_remote_copy(
            src_ref=screens.at[pl.ds(where if own else here + where, count * unit)],
            dst_ref=screens.at[pl.ds(here + where, count * unit)],
            send_sem=send_sem,
            recv_sem=recv_sem,
            device_id=device,
            device_id_type=MESH,
        )

    runs = ((0, 2), (2, 2), (4, 1), (5, 1))

    def y_copy(k):
        first, count = (common, 4) if k == 4 else (mine + runs[k][0], runs[k][1])
        return send(first, count, y_send.at[k], y_recv.at[k], across, True)

    def relayed(k, first):
        device = beside if k % 2 == 0 else along
        start, count = runs[k]
        return send(first + start, count, relay_send.at[k], relay_recv.at[k], device)

    def c_copy(k, half):
        first = (
            half + 10 * colour, half + 6, half + 10 * (1 - colour), half + 10 * (1 - colour) + 4
        )[k]
        return send(first, (6, 4, 4, 2)[k], c_send.at[k], c_recv.at[k], sibling)

    for k in range(5):
        y_copy(k).start()

    for copy in loads[:7]:
        copy.wait()
    values, rows = pack_blocks(head, off_u, off_v, base, pairs, track, data)
    packed[...] = values
    labels[...] = rows

    for i in range(4):
        for copy in moves(i):
            copy.start()

    canvas[...] = jnp.zeros_like(canvas)
    for copy in fetches[2:]:
        copy.wait()
    arrange(others, 6)
    arrange(16 * (1 - core), 16)

    row = lax.broadcasted_iota(jnp.int32, (32, K), 0)
    channel = band * CH_DEV + lax.broadcasted_iota(jnp.int32, (32, K), 1) % CH_DEV
    ratio = 1.0 + channel.astype(F32) / jnp.float32(2 * CH_DEV * n_ch)
    coarse = row - 8
    coarse_u = 16 * (coarse % 4) + coarse // 4 - S // 2
    fine_v = row - 16
    coarse_v = (row - 24) * 8 - S // 2
    step = jnp.where(
        row < 16, jnp.where(row < 8, 2 * row, coarse_u), jnp.where(row < 24, fine_v, coarse_v)
    )
    mult[...] = step.astype(F32) / S * ratio

    def widen(rows):
        source = lax.broadcasted_iota(jnp.int32, (128, 2 * K), 0)
        column = lax.broadcasted_iota(jnp.int32, (128, 2 * K), 1)
        chosen = jnp.where(source == 8 + column // CH_DEV, 1.0, 0.0).astype(BF)
        lane = lax.broadcasted_iota(jnp.int32, rows.shape, 1)
        only = jnp.where(lane < 8, 0.0, rows).astype(BF)
        return jnp.dot(only, chosen, preferred_element_type=F32)

    got_labels[:CAP] = labels[:CAP]
    samples[: 8 * CAP] = packed[: 8 * CAP].astype(F32)
    spread[:CAP] = widen(labels[:CAP])

    def block(slot):
        sample = samples[pl.ds(8 * slot, 8), :]
        track = spread[pl.ds(slot, 1), :]
        turns = jnp.concatenate(
            [track[:, :K] * mult[:16], track[:, K:] * mult[16:]], axis=0
        )
        frac = turns - jnp.floor(turns + 0.5)
        square = frac * frac
        cos = horner(COS_COEF, square)
        sin = horner(SIN_COEF, square) * frac

        def phasors(first):
            cos_fine, sin_fine = cos[first : first + 8], sin[first : first + 8]
            all_cos, all_sin = [], []
            for a in range(8):
                at = first + 8 + a
                cos_a, sin_a = cos[at : at + 1], sin[at : at + 1]
                all_cos.append(cos_fine * cos_a - sin_fine * sin_a)
                all_sin.append(sin_fine * cos_a + cos_fine * sin_a)
            return (
                jnp.concatenate(all_cos, axis=0).astype(BF),
                jnp.concatenate(all_sin, axis=0).astype(BF),
            )

        cos_u, sin_u = phasors(0)
        cos_v, sin_v = phasors(16)
        table = jnp.concatenate(
            [
                jnp.concatenate([cos_v, -sin_v], axis=1),
                jnp.concatenate([sin_v, cos_v], axis=1),
            ],
            axis=0,
        )

        def spread_row(r):
            row = jnp.broadcast_to(sample[r : r + 1], (16, K)).astype(BF)
            return jnp.concatenate([row] * (S // 16), axis=0)

        weighed = []
        for p in range(4):
            re, im = spread_row(2 * p), spread_row(2 * p + 1)
            weighed.append(
                jnp.concatenate([re * cos_u - im * sin_u, re * sin_u + im * cos_u], axis=1)
            )
        dims = (((1,), (1,)), ((), ()))
        image = lax.dot_general(
            jnp.concatenate(weighed, axis=0), table, dims, preferred_element_type=F32
        )
        return image.astype(BF)

    keep = pltpu.make_async_copy(table, listing, in_sems.at[9])
    here_half, other_half = 16 * core, 16 * (1 - core)

    def relay(stage):
        if stage < 3:
            for k in ((0,), (1,), (2, 3))[stage]:
                y_copy(k).wait_recv()
                relayed(k, mine).start()
            if stage == 2:
                c_copy(0, here_half).start()
        elif stage == 3:
            for k in (0, 1):
                relayed(k, others).wait_recv()
            c_copy(2, here_half).start()
        else:
            y_copy(4).wait_recv()
            c_copy(1, here_half).start()
            for k in (2, 3):
                relayed(k, others).wait_recv()
            c_copy(3, here_half).start()

    def loop(group, carry):
        @pl.when(group == CAP // IMAGES_AT_ONCE)
        def _():
            for i in range(4):
                for copy in moves(i):
                    copy.wait_recv()
            samples[8 * CAP :] = got_data[8 * CAP :].astype(F32)
            spread[CAP:] = widen(got_labels[CAP:])
            table[...] = list_blocks(got_labels[...])
            keep.start()

        for stage, at in enumerate(RELAY_AT):

            @pl.when(group == at)
            def _():
                relay(stage)

        made = [block(IMAGES_AT_ONCE * group + i) for i in range(IMAGES_AT_ONCE)]
        for i in range(IMAGES_AT_ONCE):
            images[IMAGES_AT_ONCE * group + i] = made[i]
        return carry

    lax.fori_loop(0, SLOTS // IMAGES_AT_ONCE, loop, 0)
    for copy in loads[7:]:
        copy.wait()
    keep.wait()
    for i in range(4):
        for copy in moves(i):
            copy.wait_send()
    for k in range(5):
        y_copy(k).wait_send()
    for k in range(4):
        relayed(k, mine).wait_send()
        c_copy(k, here_half).wait_send()
        c_copy(k, other_half).wait_recv()


def folded(x):
    middle = x.shape[1] // 2
    lane = lax.broadcasted_iota(jnp.int32, (1, 1, 128), 2)
    return jnp.where(lane < S, x[:, :middle], swap_halves(x[:, middle:])).astype(BF)


def edge_u_kernel(listing, images, screens, right, left, canvas_in, canvas, edge_u, corner):
    grid_blocks(images, screens, canvas, right, left, listing, 0, listing[5, 0])
    edge_u[...] = canvas[:, TU : TU + S, :TV].astype(BF)
    corner[...] = canvas[:, TU : TU + S, TV:].astype(BF)


def edge_v_kernel(listing, images, screens, right, left, canvas_in, canvas, *edge_v):
    grid_blocks(images, screens, canvas, right, left, listing, listing[5, 0], listing[6, 0])
    each = 8 // V_SPLIT
    for i, edge in enumerate(edge_v):
        edge[...] = folded(canvas[i * each : (i + 1) * each, :TU, TV:])


def late_kernel(listing, images, screens, right, left, canvas_in, canvas):
    grid_blocks(images, screens, canvas, right, left, listing, listing[6, 0], listing[7, 0])


def grid_blocks(images, screens, canvas, right, left, listing, first, last):
    here = screens.shape[0] // 2
    band = lax.axis_index("ch")

    def screen_place(station):
        owner = station // here
        local = station - owner * here
        return jnp.where(owner == band, local, here + local)

    def block(index):
        slot = listing[0, index]
        off_u = listing[1, index]
        off_v = listing[2, index]
        one = screen_place(listing[3, index])
        two = screen_place(listing[4, index])
        two_s = [screens[two, f].astype(F32) for f in range(2)]
        fixed = []
        for f in range(2):
            one_s = screens[one, f].astype(F32)
            one_swapped = swap_halves(one_s)
            for e in range(2):
                p = 2 * f + e
                same = one_s * two_s[e]
                cross = one_swapped * two_s[e]
                gain_re = same + swap_halves(same)
                gain_im = swap_halves(cross) - cross
                part = images[slot, p * S : (p + 1) * S].astype(F32)
                fixed.append((part * gain_re + swap_halves(part) * gain_im).astype(BF))
        tile = off_v // 128
        shift = off_v - tile * 128
        moved = pltpu.roll(right[...], shift, 1).astype(BF)
        table_re, table_im = moved[:S], moved[S:]
        shifted = jnp.concatenate(
            [
                jnp.concatenate([table_re, -table_im], axis=0),
                jnp.concatenate([table_im, table_re], axis=0),
            ],
            axis=1,
        )
        half = jnp.dot(
            jnp.concatenate(fixed, axis=0), shifted, preferred_element_type=F32
        ).astype(BF)
        eighth = off_u // 8
        placed = left[off_u - eighth * 8]
        start_u = pl.multiple_of(eighth * 8, 8)
        start_v = pl.multiple_of(tile * 128, 128)
        return start_u, start_v, shift, placed, half

    lane = lax.broadcasted_iota(jnp.int32, (1, 128), 1)

    def loop(group, carry):
        ready = [block(AT_ONCE * group + i) for i in range(AT_ONCE)]
        for start_u, start_v, shift, placed, half in ready:
            for f in range(2):
                both = []
                for p in (2 * f, 2 * f + 1):
                    part = half[p * S : (p + 1) * S]
                    both.append(jnp.concatenate([part[:, :128], part[:, 128:]], axis=0))
                grid = jnp.dot(
                    placed, jnp.concatenate(both, axis=1), preferred_element_type=F32
                )
                for e in range(2):
                    for r in range(2):
                        cells = grid[r * ROWS : (r + 1) * ROWS, 128 * e : 128 * (e + 1)]
                        cells = jnp.concatenate(
                            [
                                jnp.where(lane >= shift, cells, 0.0),
                                jnp.where(lane < shift, cells, 0.0),
                            ],
                            axis=1,
                        )
                        where = (
                            4 * f + 2 * e + r, pl.ds(start_u, ROWS), pl.ds(start_v, 256)
                        )
                        canvas[where] += cells
        return carry

    lax.fori_loop(first, last, loop, 0)


def lower_kernel(canvas, got_c, *refs):
    *got_v, out, top, side, sems = refs
    rest = pltpu.make_async_copy(
        canvas.at[:, S:TU, 128:TV], out.at[:, S:, 128:], sems.at[0]
    )
    rest.start()
    lane = lax.broadcasted_iota(jnp.int32, (1, 1, 128), 2)
    both = jnp.concatenate([x[...] for x in got_v], axis=0).astype(F32)
    low = jnp.where(lane < S, both, 0.0)
    high = jnp.where(lane < S, swap_halves(both), 0.0)
    side[:, : TU // 2 - S] = canvas[:, S : TU // 2, :128] + low[:, S:]
    side[:, TU // 2 - S :] = canvas[:, TU // 2 : TU, :128] + high
    store_side = pltpu.make_async_copy(side, out.at[:, S:, :128], sems.at[1])
    store_side.start()
    top[:, :, :128] = canvas[:, :S, :128] + low[:, :S] + got_c[...].astype(F32)
    top[:, :, 128:] = canvas[:, :S, 128:TV]
    rest.wait()
    store_side.wait()


def upper_kernel(lower, top, got_u, out, rows, sems):
    stores = []
    for i in range(2):
        planes = slice(4 * i, 4 * i + 4)
        rows[planes] = top[planes] + got_u[planes].astype(F32)
        stores.append(
            pltpu.make_async_copy(rows.at[planes], out.at[planes, :S, :], sems.at[i])
        )
        stores[-1].start()
    for store in stores:
        store.wait()


def body(visibilities, tracks, offset_u, offset_v, heading, baseline, station_pair, screens):
    smem = pl.BlockSpec(memory_space=pltpu.SMEM)
    vmem = pl.BlockSpec(memory_space=pltpu.VMEM)
    hbm = pl.BlockSpec(memory_space=pltpu.HBM)
    n_au, n_vert = (lax.axis_size(axis) for axis in ("au", "vert"))
    here = screens.shape[0]
    canvas_shape = jax.ShapeDtypeStruct((8, TU + S + ROWS, TV + 128), F32)
    right_shape = jax.ShapeDtypeStruct((2 * S, 128), F32)
    left_shape = jax.ShapeDtypeStruct((8, 2 * ROWS, 2 * S), BF)
    dma = pltpu.SemaphoreType.DMA
    number = pltpu.VMEM((1, B_DEV), jnp.int32)
    images, all_screens, listing, canvas, right, left = pl.pallas_call(
        image_kernel,
        out_shape=(
            jax.ShapeDtypeStruct((SLOTS, 4 * S, 2 * S), BF),
            jax.ShapeDtypeStruct((2 * here, 2, S, 2 * S), BF),
            pltpu.SMEM((8, 128), jnp.int32),
            canvas_shape,
            right_shape,
            left_shape,
        ),
        in_specs=[hbm] * 10,
        out_specs=(vmem, vmem, smem, vmem, vmem, vmem),
        scratch_shapes=[
            number,
            number,
            number,
            number,
            pltpu.VMEM(station_pair.shape, jnp.int32),
            pltpu.VMEM((2 * TB, B_DEV), BF),
            pltpu.VMEM((8 * B_DEV, K), BF),
            pltpu.VMEM((8, 128), jnp.int32),
            dma((10,)),
            pltpu.VMEM((8 * SLOTS, K), BF),
            pltpu.VMEM((SLOTS, 128), F32),
            pltpu.VMEM((8 * SLOTS, K), BF),
            pltpu.VMEM((SLOTS, 128), F32),
            pltpu.VMEM((8 * SLOTS, K), F32),
            pltpu.VMEM((SLOTS, 2 * K), F32),
            pltpu.VMEM((32, K), F32),
            pltpu.VMEM((here, 4, S * S), BF),
            pltpu.VMEM((2, 4 * S, 128), F32),
            dma((4,)),
            dma((4, 2)),
            dma((4, 2)),
            dma((5,)),
            dma((5,)),
            dma((4,)),
            dma((4,)),
            dma((4,)),
            dma((4,)),
        ],
        compiler_params=pltpu.CompilerParams(
            collective_id=0, has_side_effects=True, vmem_limit_bytes=20 << 20
        ),
    )(*(pltpu.with_memory_space_constraint(x, pltpu.HBM) for x in (
        heading.reshape(1, B_DEV), offset_u[None], offset_v[None], baseline[None],
        station_pair, tracks.transpose(1, 2, 0).reshape(2 * TB, B_DEV),
        visibilities.reshape(8 * B_DEV, K), screens,
        jnp.asarray(right_table()), jnp.asarray(left_table()),
    )))

    def grid(kernel, canvas, flops, *edges):
        return pl.pallas_call(
            kernel,
            out_shape=(canvas_shape, *edges),
            in_specs=[smem] + [vmem] * 5,
            out_specs=(vmem,) * (1 + len(edges)),
            input_output_aliases={5: 0},
            compiler_params=pltpu.CompilerParams(vmem_limit_bytes=12 << 20),
            cost_estimate=pl.CostEstimate(
                flops=flops, bytes_accessed=1 << 20, transcendentals=0
            ),
        )(listing, images, all_screens, right, left, canvas)

    canvas, edge_u, corner = grid(
        edge_u_kernel,
        canvas,
        10**9,
        jax.ShapeDtypeStruct((8, S, TV), BF),
        jax.ShapeDtypeStruct((8, S, 128), BF),
    )
    got_u = lax.ppermute(edge_u, "au", [(i, (i + 1) % n_au) for i in range(n_au)])
    diagonal = [
        (u * n_vert + v, (u + 1) % n_au * n_vert + (v + 1) % n_vert)
        for u in range(n_au)
        for v in range(n_vert)
    ]
    got_c = lax.ppermute(corner, ("au", "vert"), diagonal)
    canvas, *edge_v = grid(
        edge_v_kernel, canvas, 4 * 10**9, *[jax.ShapeDtypeStruct((8 // V_SPLIT, TU // 2, 128), BF)] * V_SPLIT
    )
    got_v = [
        lax.ppermute(x, "vert", [(i, (i + 1) % n_vert) for i in range(n_vert)]) for x in edge_v
    ]
    (canvas,) = grid(late_kernel, canvas, 10**6)
    tile = jax.ShapeDtypeStruct((8, TU, TV), F32)
    out, top = pl.pallas_call(
        lower_kernel,
        out_shape=(tile, jax.ShapeDtypeStruct((8, S, TV), F32)),
        in_specs=[vmem] * (2 + V_SPLIT),
        out_specs=(pl.BlockSpec(memory_space=pl.ANY), vmem),
        scratch_shapes=[pltpu.VMEM((8, TU - S, 128), F32), dma((2,))],
        compiler_params=pltpu.CompilerParams(vmem_limit_bytes=8 << 20),
    )(canvas, got_c, *got_v)
    out = pl.pallas_call(
        upper_kernel,
        out_shape=tile,
        in_specs=[pl.BlockSpec(memory_space=pl.ANY)] + [vmem] * 2,
        out_specs=pl.BlockSpec(memory_space=pl.ANY),
        scratch_shapes=[pltpu.VMEM((8, S, TV), F32), dma((2,))],
        input_output_aliases={0: 0},
        compiler_params=pltpu.CompilerParams(vmem_limit_bytes=8 << 20),
    )(out, top, got_u)
    return out[None]


def solution(mesh):
    placed = (
        P(("au", "vert"), None, "ch"),
        P(("au", "vert"), None, None),
        P(("au", "vert")),
        P(("au", "vert")),
        P(("au", "vert"), None),
        P(("au", "vert")),
        P(),
        P("ch", None, None),
    )
    return jax.shard_map(
        body, mesh=mesh, in_specs=placed, out_specs=P("ch", None, "au", "vert"), check_vma=False
    )
```

```python
import math

import jax
import jax.numpy as jnp
import ml_dtypes
import numpy as np
from jax import lax
from jax.experimental import pallas as pl
from jax.experimental.pallas import tpu as pltpu
from jax.sharding import PartitionSpec as P

S = 64
CH_DEV = 32
TB = 8
K = TB * CH_DEV
B_DEV = 32
CAP = B_DEV // 4
SLOTS = 5 * CAP
TU = 256
TV = 256
ROWS = 72
AT_ONCE = 4
U_GROUPS = 2
V_GROUPS = 5
V_SPLIT = 2
IMAGES_AT_ONCE = 8
RELAY_AT = (0, 1, 2, 4, 4)
MESH = pl.DeviceIdType.MESH
BF = jnp.bfloat16
F32 = jnp.float32


def series(values, degree):
    nodes = (np.cos(np.pi * (np.arange(400) + 0.5) / 400) + 1.0) * 0.125
    fitted = np.polynomial.chebyshev.Chebyshev.fit(nodes, values(nodes), degree, domain=[0, 0.25])
    return [float(c) for c in fitted.convert(kind=np.polynomial.Polynomial).coef]


COS_COEF = series(lambda q: np.cos(2 * np.pi * np.sqrt(q)), 5)
SIN_COEF = series(lambda q: np.sin(2 * np.pi * np.sqrt(q)) / np.sqrt(q), 5)


def horner(coefs, q):
    total = jnp.full_like(q, coefs[-1])
    for c in coefs[-2::-1]:
        total = total * q + jnp.float32(c)
    return total


def dft_tables():
    centred = np.arange(S) - S // 2
    product = (centred[:, None] * centred[None, :]) % S
    angles = np.float32(2.0 * math.pi / S) * product.astype(np.float32)
    scale = np.float32(1.0 / math.sqrt(S))
    re = (np.cos(angles) * scale).astype(ml_dtypes.bfloat16).astype(np.float32)
    im = (-np.sin(angles) * scale).astype(ml_dtypes.bfloat16).astype(np.float32)
    return re, im


def right_table():
    re, im = dft_tables()
    norm = np.float32(1.0 / math.sqrt(K))
    table = np.zeros((2 * S, 128), np.float32)
    table[:S, :S] = re.T * norm
    table[S:, :S] = im.T * norm
    return table


def left_table():
    re, im = dft_tables()
    order = np.concatenate([np.arange(0, S, 2), np.arange(1, S, 2)])
    re, im = re[:, order], im[:, order]
    table = np.zeros((8, 2, ROWS, 2 * S), np.float32)
    for shift in range(8):
        table[shift, 0, shift : shift + S, :S] = re
        table[shift, 0, shift : shift + S, S:] = -im
        table[shift, 1, shift : shift + S, :S] = im
        table[shift, 1, shift : shift + S, S:] = re
    return table.reshape(8, 2 * ROWS, 2 * S).astype(ml_dtypes.bfloat16)


def swap_halves(x):
    return pltpu.roll(x, S, x.ndim - 1)


def arrange_station(raw, tall):
    value = raw.astype(F32)
    for i in range(S // 2):
        tall[8 * i : 8 * i + 4, :] = value[:, 128 * i : 128 * (i + 1)]
    lane = lax.broadcasted_iota(jnp.int32, (S // 2, 128), 1)
    feeds = []
    for f in range(2):
        re = tall[pl.ds(2 * f, S // 2, stride=8), :]
        im = tall[pl.ds(2 * f + 1, S // 2, stride=8), :]
        even = jnp.where(lane < S, re, swap_halves(im))
        odd = jnp.where(lane < S, swap_halves(re), im)
        feeds.append(jnp.concatenate([even, odd], axis=0).astype(BF))
    return feeds


def pack_blocks(head, off_u, off_v, base, pairs, track, data):
    heads = head[...]
    kind = lax.broadcasted_iota(jnp.int32, (8, B_DEV), 0)
    named = jnp.where(kind == heads, 1.0, 0.0)
    before = lax.broadcasted_iota(jnp.int32, (B_DEV, B_DEV), 0)
    after = lax.broadcasted_iota(jnp.int32, (B_DEV, B_DEV), 1)
    strict = jnp.where(before < after, 1.0, 0.0).astype(BF)
    counts = jnp.dot(named.astype(BF), strict, preferred_element_type=F32)
    rank = jnp.sum(named * counts, axis=0, keepdims=True)
    slot = heads.astype(F32) * CAP + rank
    which = lax.broadcasted_iota(jnp.int32, (SLOTS, B_DEV), 0).astype(F32)
    chosen = jnp.where(which == slot, 1.0, 0.0).astype(BF)

    label = lax.broadcasted_iota(jnp.int32, (pairs.shape[1], B_DEV), 0)
    listed = jnp.where(label == base[...], 1.0, 0.0).astype(BF)
    station = jnp.dot(pairs[...].astype(F32).astype(BF), listed, preferred_element_type=F32)
    rows = jnp.concatenate(
        [
            jnp.ones((1, B_DEV), F32),
            off_u[...].astype(F32),
            off_v[...].astype(F32),
            station,
            jnp.zeros((3, B_DEV), F32),
            track[...].astype(F32),
            jnp.zeros((128 - 8 - 2 * TB, B_DEV), F32),
        ],
        axis=0,
    ).astype(BF)
    dims = (((1,), (1,)), ((), ()))
    labels = lax.dot_general(chosen, rows, dims, preferred_element_type=F32)

    owner = lax.broadcasted_iota(jnp.int32, (B_DEV, 8 * B_DEV), 0)
    column = lax.broadcasted_iota(jnp.int32, (B_DEV, 8 * B_DEV), 1)
    widen = jnp.where(owner == column // 8, 1.0, 0.0).astype(BF)
    wide = jnp.dot(
        jnp.broadcast_to(slot, (8, B_DEV)).astype(BF), widen, preferred_element_type=F32
    )[:1]
    lane = lax.broadcasted_iota(jnp.int32, (1, 8 * B_DEV), 1) % 8
    place = wide * 8.0 + lane.astype(F32)
    target = lax.broadcasted_iota(jnp.int32, (8 * SLOTS, 8 * B_DEV), 0).astype(F32)
    moved = jnp.where(target == place, 1.0, 0.0).astype(BF)
    return jnp.dot(moved, data[...], preferred_element_type=F32).astype(BF), labels


def list_blocks(labels):
    dims = (((1,), (1,)), ((), ()))
    quantity = lax.broadcasted_iota(jnp.int32, (8, 128), 0)
    lane = lax.broadcasted_iota(jnp.int32, (8, 128), 1)
    pick = jnp.where(quantity == lane, 1.0, 0.0).astype(BF)
    rows = lax.dot_general(pick, labels.astype(BF), dims, preferred_element_type=F32)
    filled, at_u, at_v = rows[0:1], rows[1:2], rows[2:3]
    past_u = at_u > TU - S
    past = jnp.logical_or(past_u, at_v > TV - S)
    first = jnp.where(past_u, filled, 0.0)
    early = jnp.where(past, filled, 0.0)
    kind = lax.broadcasted_iota(jnp.int32, (8, SLOTS), 0)
    both = jnp.where(
        kind == 0,
        first,
        jnp.where(kind == 1, early - first, jnp.where(kind == 2, filled - early, 0.0)),
    )
    before = lax.broadcasted_iota(jnp.int32, (SLOTS, SLOTS), 0)
    after = lax.broadcasted_iota(jnp.int32, (SLOTS, SLOTS), 1)
    strict = jnp.where(before < after, 1.0, 0.0).astype(BF)
    ahead = jnp.dot(both.astype(BF), strict, preferred_element_type=F32)
    number_first = jnp.sum(first, axis=1, keepdims=True)
    number_early = jnp.sum(early, axis=1, keepdims=True)
    number = jnp.sum(filled, axis=1, keepdims=True)
    place = jnp.where(past, number_first + ahead[1:2], number_early + ahead[2:3])
    place = jnp.where(past_u, ahead[0:1], place)
    place = jnp.where(filled > 0.5, place, -1.0)
    target = lax.broadcasted_iota(jnp.int32, (128, SLOTS), 0).astype(F32)
    moved = jnp.where(target == place, 1.0, 0.0).astype(BF)
    slot = lax.broadcasted_iota(jnp.int32, (8, SLOTS), 1).astype(F32)
    rows = jnp.where(kind == 0, slot, rows)
    table = lax.dot_general(rows.astype(BF), moved, dims, preferred_element_type=F32)
    spare = jnp.where(lane.astype(F32) >= number, float(TU + S), 0.0)
    table = table + jnp.where(quantity == 1, spare, 0.0)
    groups = jnp.floor((number + (AT_ONCE - 1.0)) / AT_ONCE)
    ends = []
    for count, least in ((number_first, U_GROUPS), (number_early, V_GROUPS)):
        enough = jnp.minimum(groups, float(least))
        needed = jnp.floor((count + (AT_ONCE - 1.0)) / AT_ONCE)
        ends.append(jnp.maximum(needed, enough))
    for row, end in enumerate((*ends, groups)):
        table = jnp.where(quantity == 5 + row, end, table)
    return table.astype(jnp.int32)


def image_kernel(
    head_in, off_u_in, off_v_in, base_in, pairs_in, track_in, data_in, own_screens,
    right_in, left_in,
    images, screens, listing, canvas, right, left,
    head, off_u, off_v, base, pairs, track, data, table, in_sems,
    packed, labels, got_data, got_labels, samples, spread, mult, raw, tall,
    own_sems, send_sems, recv_sems, y_send, y_recv, relay_send, relay_recv, c_send, c_recv,
):
    au, vert, band = (lax.axis_index(axis) for axis in ("au", "vert", "ch"))
    n_au, n_vert, n_ch = (lax.axis_size(axis) for axis in ("au", "vert", "ch"))
    here = own_screens.shape[0]
    unit = here // 32
    core = lax.rem(vert, 2)
    colour = lax.rem(vert // 2 + au, 2)
    mine = 16 * core + 10 * colour
    common = 16 * core + 6
    others = 16 * core + 10 * (1 - colour)

    def turned(step):
        return lax.rem(vert + step, n_vert)

    near = (
        {"au": lax.rem(au + 1, n_au)},
        {"au": lax.rem(au + n_au - 1, n_au)},
        {"vert": turned(1)},
        {"vert": turned(n_vert - 1)},
    )
    across = {"ch": lax.rem(band + 1, n_ch)}
    sibling = {"vert": vert + 1 - 2 * core}
    beside = {"vert": vert + 2 - 4 * lax.rem(vert // 2, 2)}
    along = {"au": au + 1 - 2 * lax.rem(au, 2)}

    inputs = (
        (head_in, head), (off_u_in, off_u), (off_v_in, off_v), (base_in, base),
        (pairs_in, pairs), (track_in, track), (data_in, data),
        (right_in, right), (left_in, left),
    )
    loads = [
        pltpu.make_async_copy(source, target, in_sems.at[j])
        for j, (source, target) in enumerate(inputs)
    ]
    for copy in loads:
        copy.start()
    fetches = []
    spans = ((mine, 6), (common, 4), (others, 6), (16 * (1 - core), 16))
    for j, (first, count) in enumerate(spans):
        rows = pl.ds(first * unit, count * unit)
        fetches.append(
            pltpu.make_async_copy(own_screens.at[rows], raw.at[rows], own_sems.at[j])
        )
        fetches[-1].start()
    barrier = pltpu.get_barrier_semaphore()
    for device in (*near, across, beside):
        pl.semaphore_signal(barrier, inc=1, device_id=device, device_id_type=MESH)

    def arrange(first, number):
        def one(pair, carry):
            for i in range(2):
                station = first * unit + 2 * pair + i
                feeds = arrange_station(raw[station], tall.at[i])
                for f in range(2):
                    screens[station, f] = feeds[f]
            return carry

        lax.fori_loop(0, number * unit // 2, one, 0)

    fetches[0].wait()
    arrange(mine, 6)
    fetches[1].wait()
    arrange(common, 4)
    pl.semaphore_wait(barrier, 6)

    def moves(i):
        pairs_of = ((packed, got_data, 8 * CAP), (labels, got_labels, CAP))
        for j, (source, target, rows) in enumerate(pairs_of):
            where = pl.ds((i + 1) * rows, rows)
            yield pltpu.make_async_remote_copy(
                src_ref=source.at[where],
                dst_ref=target.at[where],
                send_sem=send_sems.at[i, j],
                recv_sem=recv_sems.at[i, j],
                device_id=near[i],
                device_id_type=MESH,
            )

    def send(number, count, send_sem, recv_sem, device, own=False):
        where = number * unit
        return pltpu.make_async_remote_copy(
            src_ref=screens.at[pl.ds(where if own else here + where, count * unit)],
            dst_ref=screens.at[pl.ds(here + where, count * unit)],
            send_sem=send_sem,
            recv_sem=recv_sem,
            device_id=device,
            device_id_type=MESH,
        )

    runs = ((0, 2), (2, 2), (4, 1), (5, 1))

    def y_copy(k):
        first, count = (common, 4) if k == 4 else (mine + runs[k][0], runs[k][1])
        return send(first, count, y_send.at[k], y_recv.at[k], across, True)

    def relayed(k, first):
        device = beside if k % 2 == 0 else along
        start, count = runs[k]
        return send(first + start, count, relay_send.at[k], relay_recv.at[k], device)

    def c_copy(k, half):
        first = (
            half + 10 * colour, half + 6, half + 10 * (1 - colour), half + 10 * (1 - colour) + 4
        )[k]
        return send(first, (6, 4, 4, 2)[k], c_send.at[k], c_recv.at[k], sibling)

    for k in range(5):
        y_copy(k).start()

    for copy in loads[:7]:
        copy.wait()
    values, rows = pack_blocks(head, off_u, off_v, base, pairs, track, data)
    packed[...] = values
    labels[...] = rows

    for i in range(4):
        for copy in moves(i):
            copy.start()

    canvas[...] = jnp.zeros_like(canvas)
    for copy in fetches[2:]:
        copy.wait()
    arrange(others, 6)
    arrange(16 * (1 - core), 16)

    row = lax.broadcasted_iota(jnp.int32, (32, K), 0)
    channel = band * CH_DEV + lax.broadcasted_iota(jnp.int32, (32, K), 1) % CH_DEV
    ratio = 1.0 + channel.astype(F32) / jnp.float32(2 * CH_DEV * n_ch)
    coarse = row - 8
    coarse_u = 16 * (coarse % 4) + coarse // 4 - S // 2
    fine_v = row - 16
    coarse_v = (row - 24) * 8 - S // 2
    step = jnp.where(
        row < 16, jnp.where(row < 8, 2 * row, coarse_u), jnp.where(row < 24, fine_v, coarse_v)
    )
    mult[...] = step.astype(F32) / S * ratio

    def widen(rows):
        source = lax.broadcasted_iota(jnp.int32, (128, 2 * K), 0)
        column = lax.broadcasted_iota(jnp.int32, (128, 2 * K), 1)
        chosen = jnp.where(source == 8 + column // CH_DEV, 1.0, 0.0).astype(BF)
        lane = lax.broadcasted_iota(jnp.int32, rows.shape, 1)
        only = jnp.where(lane < 8, 0.0, rows).astype(BF)
        return jnp.dot(only, chosen, preferred_element_type=F32)

    got_labels[:CAP] = labels[:CAP]
    samples[: 8 * CAP] = packed[: 8 * CAP].astype(F32)
    spread[:CAP] = widen(labels[:CAP])

    def block(slot):
        sample = samples[pl.ds(8 * slot, 8), :]
        track = spread[pl.ds(slot, 1), :]
        turns = jnp.concatenate(
            [track[:, :K] * mult[:16], track[:, K:] * mult[16:]], axis=0
        )
        frac = turns - jnp.floor(turns + 0.5)
        square = frac * frac
        cos = horner(COS_COEF, square)
        sin = horner(SIN_COEF, square) * frac

        def phasors(first):
            cos_fine, sin_fine = cos[first : first + 8], sin[first : first + 8]
            all_cos, all_sin = [], []
            for a in range(8):
                at = first + 8 + a
                cos_a, sin_a = cos[at : at + 1], sin[at : at + 1]
                all_cos.append(cos_fine * cos_a - sin_fine * sin_a)
                all_sin.append(sin_fine * cos_a + cos_fine * sin_a)
            return (
                jnp.concatenate(all_cos, axis=0).astype(BF),
                jnp.concatenate(all_sin, axis=0).astype(BF),
            )

        cos_u, sin_u = phasors(0)
        cos_v, sin_v = phasors(16)
        table = jnp.concatenate(
            [
                jnp.concatenate([cos_v, -sin_v], axis=1),
                jnp.concatenate([sin_v, cos_v], axis=1),
            ],
            axis=0,
        )

        def spread_row(r):
            row = jnp.broadcast_to(sample[r : r + 1], (16, K)).astype(BF)
            return jnp.concatenate([row] * (S // 16), axis=0)

        weighed = []
        for p in range(4):
            re, im = spread_row(2 * p), spread_row(2 * p + 1)
            weighed.append(
                jnp.concatenate([re * cos_u - im * sin_u, re * sin_u + im * cos_u], axis=1)
            )
        dims = (((1,), (1,)), ((), ()))
        image = lax.dot_general(
            jnp.concatenate(weighed, axis=0), table, dims, preferred_element_type=F32
        )
        return image.astype(BF)

    keep = pltpu.make_async_copy(table, listing, in_sems.at[9])
    here_half, other_half = 16 * core, 16 * (1 - core)

    def relay(stage):
        if stage < 3:
            for k in ((0,), (1,), (2, 3))[stage]:
                y_copy(k).wait_recv()
                relayed(k, mine).start()
            if stage == 2:
                c_copy(0, here_half).start()
        elif stage == 3:
            for k in (0, 1):
                relayed(k, others).wait_recv()
            c_copy(2, here_half).start()
        else:
            y_copy(4).wait_recv()
            c_copy(1, here_half).start()
            for k in (2, 3):
                relayed(k, others).wait_recv()
            c_copy(3, here_half).start()

    def loop(group, carry):
        @pl.when(group == CAP // IMAGES_AT_ONCE)
        def _():
            for i in range(4):
                for copy in moves(i):
                    copy.wait_recv()
            samples[8 * CAP :] = got_data[8 * CAP :].astype(F32)
            spread[CAP:] = widen(got_labels[CAP:])
            table[...] = list_blocks(got_labels[...])
            keep.start()

        for stage, at in enumerate(RELAY_AT):

            @pl.when(group == at)
            def _():
                relay(stage)

        made = [block(IMAGES_AT_ONCE * group + i) for i in range(IMAGES_AT_ONCE)]
        for i in range(IMAGES_AT_ONCE):
            images[IMAGES_AT_ONCE * group + i] = made[i]
        return carry

    lax.fori_loop(0, SLOTS // IMAGES_AT_ONCE, loop, 0)
    for copy in loads[7:]:
        copy.wait()
    keep.wait()
    for i in range(4):
        for copy in moves(i):
            copy.wait_send()
    for k in range(5):
        y_copy(k).wait_send()
    for k in range(4):
        relayed(k, mine).wait_send()
        c_copy(k, here_half).wait_send()
        c_copy(k, other_half).wait_recv()


def folded(x):
    middle = x.shape[1] // 2
    lane = lax.broadcasted_iota(jnp.int32, (1, 1, 128), 2)
    return jnp.where(lane < S, x[:, :middle], swap_halves(x[:, middle:])).astype(BF)


def edge_u_kernel(listing, images, screens, right, left, canvas_in, canvas, edge_u, corner):
    grid_blocks(images, screens, canvas, right, left, listing, 0, listing[5, 0])
    edge_u[...] = canvas[:, TU : TU + S, :TV].astype(BF)
    corner[...] = folded(canvas[:, TU : TU + S, TV:])


def edge_v_kernel(listing, images, screens, right, left, canvas_in, canvas, *edge_v):
    grid_blocks(images, screens, canvas, right, left, listing, listing[5, 0], listing[6, 0])
    each = 8 // V_SPLIT
    for i, edge in enumerate(edge_v):
        edge[...] = folded(canvas[i * each : (i + 1) * each, :TU, TV:])


def late_kernel(listing, images, screens, right, left, canvas_in, canvas):
    grid_blocks(images, screens, canvas, right, left, listing, listing[6, 0], listing[7, 0])


def grid_blocks(images, screens, canvas, right, left, listing, first, last):
    here = screens.shape[0] // 2
    band = lax.axis_index("ch")

    def screen_place(station):
        owner = station // here
        local = station - owner * here
        return jnp.where(owner == band, local, here + local)

    def block(index):
        slot = listing[0, index]
        off_u = listing[1, index]
        off_v = listing[2, index]
        one = screen_place(listing[3, index])
        two = screen_place(listing[4, index])
        two_s = [screens[two, f].astype(F32) for f in range(2)]
        fixed = []
        for f in range(2):
            one_s = screens[one, f].astype(F32)
            one_swapped = swap_halves(one_s)
            for e in range(2):
                p = 2 * f + e
                same = one_s * two_s[e]
                cross = one_swapped * two_s[e]
                gain_re = same + swap_halves(same)
                gain_im = swap_halves(cross) - cross
                part = images[slot, p * S : (p + 1) * S].astype(F32)
                fixed.append((part * gain_re + swap_halves(part) * gain_im).astype(BF))
        tile = off_v // 128
        shift = off_v - tile * 128
        moved = pltpu.roll(right[...], shift, 1).astype(BF)
        table_re, table_im = moved[:S], moved[S:]
        shifted = jnp.concatenate(
            [
                jnp.concatenate([table_re, -table_im], axis=0),
                jnp.concatenate([table_im, table_re], axis=0),
            ],
            axis=1,
        )
        half = jnp.dot(
            jnp.concatenate(fixed, axis=0), shifted, preferred_element_type=F32
        ).astype(BF)
        eighth = off_u // 8
        placed = left[off_u - eighth * 8]
        start_u = pl.multiple_of(eighth * 8, 8)
        start_v = pl.multiple_of(tile * 128, 128)
        return start_u, start_v, shift, placed, half

    lane = lax.broadcasted_iota(jnp.int32, (1, 128), 1)

    def loop(group, carry):
        ready = [block(AT_ONCE * group + i) for i in range(AT_ONCE)]
        for start_u, start_v, shift, placed, half in ready:
            for f in range(2):
                both = []
                for p in (2 * f, 2 * f + 1):
                    part = half[p * S : (p + 1) * S]
                    both.append(jnp.concatenate([part[:, :128], part[:, 128:]], axis=0))
                grid = jnp.dot(
                    placed, jnp.concatenate(both, axis=1), preferred_element_type=F32
                )
                for e in range(2):
                    for r in range(2):
                        cells = grid[r * ROWS : (r + 1) * ROWS, 128 * e : 128 * (e + 1)]
                        cells = jnp.concatenate(
                            [
                                jnp.where(lane >= shift, cells, 0.0),
                                jnp.where(lane < shift, cells, 0.0),
                            ],
                            axis=1,
                        )
                        where = (
                            4 * f + 2 * e + r, pl.ds(start_u, ROWS), pl.ds(start_v, 256)
                        )
                        canvas[where] += cells
        return carry

    lax.fori_loop(first, last, loop, 0)


def lower_kernel(canvas, *refs):
    *got_v, out, top, side, sems = refs
    rest = pltpu.make_async_copy(
        canvas.at[:, S:TU, 128:TV], out.at[:, S:, 128:], sems.at[0]
    )
    rest.start()
    lane = lax.broadcasted_iota(jnp.int32, (1, 1, 128), 2)
    both = jnp.concatenate([x[...] for x in got_v], axis=0).astype(F32)
    low = jnp.where(lane < S, both, 0.0)
    high = jnp.where(lane < S, swap_halves(both), 0.0)
    side[:, : TU // 2 - S] = canvas[:, S : TU // 2, :128] + low[:, S:]
    side[:, TU // 2 - S :] = canvas[:, TU // 2 : TU, :128] + high
    store_side = pltpu.make_async_copy(side, out.at[:, S:, :128], sems.at[1])
    store_side.start()
    top[:, :, :128] = canvas[:, :S, :128] + low[:, :S]
    top[:, :, 128:] = canvas[:, :S, 128:TV]
    rest.wait()
    store_side.wait()


def upper_kernel(lower, top, got_u, got_c, out, rows, sems):
    lane = lax.broadcasted_iota(jnp.int32, (1, 1, 128), 2)
    stores = []
    for i in range(2):
        planes = slice(4 * i, 4 * i + 4)
        rows[planes] = top[planes] + got_u[planes].astype(F32)
        both = got_c[planes].astype(F32)
        rows[planes, : S // 2, :128] += jnp.where(lane < S, both, 0.0)
        rows[planes, S // 2 :, :128] += jnp.where(lane < S, swap_halves(both), 0.0)
        stores.append(
            pltpu.make_async_copy(rows.at[planes], out.at[planes, :S, :], sems.at[i])
        )
        stores[-1].start()
    for store in stores:
        store.wait()


def body(visibilities, tracks, offset_u, offset_v, heading, baseline, station_pair, screens):
    smem = pl.BlockSpec(memory_space=pltpu.SMEM)
    vmem = pl.BlockSpec(memory_space=pltpu.VMEM)
    hbm = pl.BlockSpec(memory_space=pltpu.HBM)
    n_au, n_vert = (lax.axis_size(axis) for axis in ("au", "vert"))
    here = screens.shape[0]
    canvas_shape = jax.ShapeDtypeStruct((8, TU + S + ROWS, TV + 128), F32)
    right_shape = jax.ShapeDtypeStruct((2 * S, 128), F32)
    left_shape = jax.ShapeDtypeStruct((8, 2 * ROWS, 2 * S), BF)
    dma = pltpu.SemaphoreType.DMA
    number = pltpu.VMEM((1, B_DEV), jnp.int32)
    images, all_screens, listing, canvas, right, left = pl.pallas_call(
        image_kernel,
        out_shape=(
            jax.ShapeDtypeStruct((SLOTS, 4 * S, 2 * S), BF),
            jax.ShapeDtypeStruct((2 * here, 2, S, 2 * S), BF),
            pltpu.SMEM((8, 128), jnp.int32),
            canvas_shape,
            right_shape,
            left_shape,
        ),
        in_specs=[hbm] * 10,
        out_specs=(vmem, vmem, smem, vmem, vmem, vmem),
        scratch_shapes=[
            number,
            number,
            number,
            number,
            pltpu.VMEM(station_pair.shape, jnp.int32),
            pltpu.VMEM((2 * TB, B_DEV), BF),
            pltpu.VMEM((8 * B_DEV, K), BF),
            pltpu.VMEM((8, 128), jnp.int32),
            dma((10,)),
            pltpu.VMEM((8 * SLOTS, K), BF),
            pltpu.VMEM((SLOTS, 128), F32),
            pltpu.VMEM((8 * SLOTS, K), BF),
            pltpu.VMEM((SLOTS, 128), F32),
            pltpu.VMEM((8 * SLOTS, K), F32),
            pltpu.VMEM((SLOTS, 2 * K), F32),
            pltpu.VMEM((32, K), F32),
            pltpu.VMEM((here, 4, S * S), BF),
            pltpu.VMEM((2, 4 * S, 128), F32),
            dma((4,)),
            dma((4, 2)),
            dma((4, 2)),
            dma((5,)),
            dma((5,)),
            dma((4,)),
            dma((4,)),
            dma((4,)),
            dma((4,)),
        ],
        compiler_params=pltpu.CompilerParams(
            collective_id=0, has_side_effects=True, vmem_limit_bytes=20 << 20
        ),
    )(*(pltpu.with_memory_space_constraint(x, pltpu.HBM) for x in (
        heading.reshape(1, B_DEV), offset_u[None], offset_v[None], baseline[None],
        station_pair, tracks.transpose(1, 2, 0).reshape(2 * TB, B_DEV),
        visibilities.reshape(8 * B_DEV, K), screens,
        jnp.asarray(right_table()), jnp.asarray(left_table()),
    )))

    def grid(kernel, canvas, flops, *edges):
        return pl.pallas_call(
            kernel,
            out_shape=(canvas_shape, *edges),
            in_specs=[smem] + [vmem] * 5,
            out_specs=(vmem,) * (1 + len(edges)),
            input_output_aliases={5: 0},
            compiler_params=pltpu.CompilerParams(vmem_limit_bytes=12 << 20),
            cost_estimate=pl.CostEstimate(
                flops=flops, bytes_accessed=1 << 20, transcendentals=0
            ),
        )(listing, images, all_screens, right, left, canvas)

    canvas, edge_u, corner = grid(
        edge_u_kernel,
        canvas,
        10**9,
        jax.ShapeDtypeStruct((8, S, TV), BF),
        jax.ShapeDtypeStruct((8, S // 2, 128), BF),
    )
    got_u = lax.ppermute(edge_u, "au", [(i, (i + 1) % n_au) for i in range(n_au)])
    diagonal = [
        (u * n_vert + v, (u + 1) % n_au * n_vert + (v + 1) % n_vert)
        for u in range(n_au)
        for v in range(n_vert)
    ]
    got_c = lax.ppermute(corner, ("au", "vert"), diagonal)
    canvas, *edge_v = grid(
        edge_v_kernel, canvas, 4 * 10**9, *[jax.ShapeDtypeStruct((8 // V_SPLIT, TU // 2, 128), BF)] * V_SPLIT
    )
    got_v = [
        lax.ppermute(x, "vert", [(i, (i + 1) % n_vert) for i in range(n_vert)]) for x in edge_v
    ]
    (canvas,) = grid(late_kernel, canvas, 10**6)
    tile = jax.ShapeDtypeStruct((8, TU, TV), F32)
    out, top = pl.pallas_call(
        lower_kernel,
        out_shape=(tile, jax.ShapeDtypeStruct((8, S, TV), F32)),
        in_specs=[vmem] * (1 + V_SPLIT),
        out_specs=(pl.BlockSpec(memory_space=pl.ANY), vmem),
        scratch_shapes=[pltpu.VMEM((8, TU - S, 128), F32), dma((2,))],
        compiler_params=pltpu.CompilerParams(vmem_limit_bytes=8 << 20),
    )(canvas, *got_v)
    out = pl.pallas_call(
        upper_kernel,
        out_shape=tile,
        in_specs=[pl.BlockSpec(memory_space=pl.ANY)] + [vmem] * 3,
        out_specs=pl.BlockSpec(memory_space=pl.ANY),
        scratch_shapes=[pltpu.VMEM((8, S, TV), F32), dma((2,))],
        input_output_aliases={0: 0},
        compiler_params=pltpu.CompilerParams(vmem_limit_bytes=8 << 20),
    )(out, top, got_u, got_c)
    return out[None]


def solution(mesh):
    placed = (
        P(("au", "vert"), None, "ch"),
        P(("au", "vert"), None, None),
        P(("au", "vert")),
        P(("au", "vert")),
        P(("au", "vert"), None),
        P(("au", "vert")),
        P(),
        P("ch", None, None),
    )
    return jax.shard_map(
        body, mesh=mesh, in_specs=placed, out_specs=P("ch", None, "au", "vert"), check_vma=False
    )
```

```python
import math

import jax
import jax.numpy as jnp
import ml_dtypes
import numpy as np
from jax import lax
from jax.experimental import pallas as pl
from jax.experimental.pallas import tpu as pltpu
from jax.sharding import PartitionSpec as P

S = 64
CH_DEV = 32
TB = 8
K = TB * CH_DEV
B_DEV = 32
CAP = B_DEV // 4
SLOTS = 5 * CAP
TU = 256
TV = 256
ROWS = 72
AT_ONCE = 4
U_GROUPS = 2
V_GROUPS = 4
V_SPLIT = 2
IMAGES_AT_ONCE = 8
RELAY_AT = (0, 1, 2, 4, 4)
MESH = pl.DeviceIdType.MESH
BF = jnp.bfloat16
F32 = jnp.float32


def series(values, degree):
    nodes = (np.cos(np.pi * (np.arange(400) + 0.5) / 400) + 1.0) * 0.125
    fitted = np.polynomial.chebyshev.Chebyshev.fit(nodes, values(nodes), degree, domain=[0, 0.25])
    return [float(c) for c in fitted.convert(kind=np.polynomial.Polynomial).coef]


COS_COEF = series(lambda q: np.cos(2 * np.pi * np.sqrt(q)), 5)
SIN_COEF = series(lambda q: np.sin(2 * np.pi * np.sqrt(q)) / np.sqrt(q), 5)


def horner(coefs, q):
    total = jnp.full_like(q, coefs[-1])
    for c in coefs[-2::-1]:
        total = total * q + jnp.float32(c)
    return total


def dft_tables():
    centred = np.arange(S) - S // 2
    product = (centred[:, None] * centred[None, :]) % S
    angles = np.float32(2.0 * math.pi / S) * product.astype(np.float32)
    scale = np.float32(1.0 / math.sqrt(S))
    re = (np.cos(angles) * scale).astype(ml_dtypes.bfloat16).astype(np.float32)
    im = (-np.sin(angles) * scale).astype(ml_dtypes.bfloat16).astype(np.float32)
    return re, im


def right_table():
    re, im = dft_tables()
    norm = np.float32(1.0 / math.sqrt(K))
    table = np.zeros((2 * S, 128), np.float32)
    table[:S, :S] = re.T * norm
    table[S:, :S] = im.T * norm
    return table


def left_table():
    re, im = dft_tables()
    order = np.concatenate([np.arange(0, S, 2), np.arange(1, S, 2)])
    re, im = re[:, order], im[:, order]
    table = np.zeros((8, 2, ROWS, 2 * S), np.float32)
    for shift in range(8):
        table[shift, 0, shift : shift + S, :S] = re
        table[shift, 0, shift : shift + S, S:] = -im
        table[shift, 1, shift : shift + S, :S] = im
        table[shift, 1, shift : shift + S, S:] = re
    return table.reshape(8, 2 * ROWS, 2 * S).astype(ml_dtypes.bfloat16)


def swap_halves(x):
    return pltpu.roll(x, S, x.ndim - 1)


def arrange_station(raw, tall):
    value = raw.astype(F32)
    for i in range(S // 2):
        tall[8 * i : 8 * i + 4, :] = value[:, 128 * i : 128 * (i + 1)]
    lane = lax.broadcasted_iota(jnp.int32, (S // 2, 128), 1)
    feeds = []
    for f in range(2):
        re = tall[pl.ds(2 * f, S // 2, stride=8), :]
        im = tall[pl.ds(2 * f + 1, S // 2, stride=8), :]
        even = jnp.where(lane < S, re, swap_halves(im))
        odd = jnp.where(lane < S, swap_halves(re), im)
        feeds.append(jnp.concatenate([even, odd], axis=0).astype(BF))
    return feeds


def pack_blocks(head, off_u, off_v, base, pairs, track, data):
    heads = head[...]
    kind = lax.broadcasted_iota(jnp.int32, (8, B_DEV), 0)
    named = jnp.where(kind == heads, 1.0, 0.0)
    before = lax.broadcasted_iota(jnp.int32, (B_DEV, B_DEV), 0)
    after = lax.broadcasted_iota(jnp.int32, (B_DEV, B_DEV), 1)
    strict = jnp.where(before < after, 1.0, 0.0).astype(BF)
    counts = jnp.dot(named.astype(BF), strict, preferred_element_type=F32)
    rank = jnp.sum(named * counts, axis=0, keepdims=True)
    slot = heads.astype(F32) * CAP + rank
    which = lax.broadcasted_iota(jnp.int32, (SLOTS, B_DEV), 0).astype(F32)
    chosen = jnp.where(which == slot, 1.0, 0.0).astype(BF)

    label = lax.broadcasted_iota(jnp.int32, (pairs.shape[1], B_DEV), 0)
    listed = jnp.where(label == base[...], 1.0, 0.0).astype(BF)
    station = jnp.dot(pairs[...].astype(F32).astype(BF), listed, preferred_element_type=F32)
    rows = jnp.concatenate(
        [
            jnp.ones((1, B_DEV), F32),
            off_u[...].astype(F32),
            off_v[...].astype(F32),
            station,
            jnp.zeros((3, B_DEV), F32),
            track[...].astype(F32),
            jnp.zeros((128 - 8 - 2 * TB, B_DEV), F32),
        ],
        axis=0,
    ).astype(BF)
    dims = (((1,), (1,)), ((), ()))
    labels = lax.dot_general(chosen, rows, dims, preferred_element_type=F32)

    owner = lax.broadcasted_iota(jnp.int32, (B_DEV, 8 * B_DEV), 0)
    column = lax.broadcasted_iota(jnp.int32, (B_DEV, 8 * B_DEV), 1)
    widen = jnp.where(owner == column // 8, 1.0, 0.0).astype(BF)
    wide = jnp.dot(
        jnp.broadcast_to(slot, (8, B_DEV)).astype(BF), widen, preferred_element_type=F32
    )[:1]
    lane = lax.broadcasted_iota(jnp.int32, (1, 8 * B_DEV), 1) % 8
    place = wide * 8.0 + lane.astype(F32)
    target = lax.broadcasted_iota(jnp.int32, (8 * SLOTS, 8 * B_DEV), 0).astype(F32)
    moved = jnp.where(target == place, 1.0, 0.0).astype(BF)
    return jnp.dot(moved, data[...], preferred_element_type=F32).astype(BF), labels


def list_blocks(labels):
    dims = (((1,), (1,)), ((), ()))
    quantity = lax.broadcasted_iota(jnp.int32, (8, 128), 0)
    lane = lax.broadcasted_iota(jnp.int32, (8, 128), 1)
    pick = jnp.where(quantity == lane, 1.0, 0.0).astype(BF)
    rows = lax.dot_general(pick, labels.astype(BF), dims, preferred_element_type=F32)
    filled, at_u, at_v = rows[0:1], rows[1:2], rows[2:3]
    past_u = at_u > TU - S
    past = jnp.logical_or(past_u, at_v > TV - S)
    first = jnp.where(past_u, filled, 0.0)
    early = jnp.where(past, filled, 0.0)
    kind = lax.broadcasted_iota(jnp.int32, (8, SLOTS), 0)
    both = jnp.where(
        kind == 0,
        first,
        jnp.where(kind == 1, early - first, jnp.where(kind == 2, filled - early, 0.0)),
    )
    before = lax.broadcasted_iota(jnp.int32, (SLOTS, SLOTS), 0)
    after = lax.broadcasted_iota(jnp.int32, (SLOTS, SLOTS), 1)
    strict = jnp.where(before < after, 1.0, 0.0).astype(BF)
    ahead = jnp.dot(both.astype(BF), strict, preferred_element_type=F32)
    number_first = jnp.sum(first, axis=1, keepdims=True)
    number_early = jnp.sum(early, axis=1, keepdims=True)
    number = jnp.sum(filled, axis=1, keepdims=True)
    place = jnp.where(past, number_first + ahead[1:2], number_early + ahead[2:3])
    place = jnp.where(past_u, ahead[0:1], place)
    place = jnp.where(filled > 0.5, place, -1.0)
    target = lax.broadcasted_iota(jnp.int32, (128, SLOTS), 0).astype(F32)
    moved = jnp.where(target == place, 1.0, 0.0).astype(BF)
    slot = lax.broadcasted_iota(jnp.int32, (8, SLOTS), 1).astype(F32)
    rows = jnp.where(kind == 0, slot, rows)
    table = lax.dot_general(rows.astype(BF), moved, dims, preferred_element_type=F32)
    spare = jnp.where(lane.astype(F32) >= number, float(TU + S), 0.0)
    table = table + jnp.where(quantity == 1, spare, 0.0)
    groups = jnp.floor((number + (AT_ONCE - 1.0)) / AT_ONCE)
    ends = []
    for count, least in ((number_first, U_GROUPS), (number_early, V_GROUPS)):
        enough = jnp.minimum(groups, float(least))
        needed = jnp.floor((count + (AT_ONCE - 1.0)) / AT_ONCE)
        ends.append(jnp.maximum(needed, enough))
    for row, end in enumerate((*ends, groups)):
        table = jnp.where(quantity == 5 + row, end, table)
    return table.astype(jnp.int32)


def image_kernel(
    head_in, off_u_in, off_v_in, base_in, pairs_in, track_in, data_in, own_screens,
    right_in, left_in,
    images, screens, listing, canvas, right, left,
    head, off_u, off_v, base, pairs, track, data, table, in_sems,
    packed, labels, got_data, got_labels, samples, spread, mult, raw, tall,
    own_sems, send_sems, recv_sems, y_send, y_recv, relay_send, relay_recv, c_send, c_recv,
):
    au, vert, band = (lax.axis_index(axis) for axis in ("au", "vert", "ch"))
    n_au, n_vert, n_ch = (lax.axis_size(axis) for axis in ("au", "vert", "ch"))
    here = own_screens.shape[0]
    unit = here // 32
    core = lax.rem(vert, 2)
    colour = lax.rem(vert // 2 + au, 2)
    mine = 16 * core + 10 * colour
    common = 16 * core + 6
    others = 16 * core + 10 * (1 - colour)

    def turned(step):
        return lax.rem(vert + step, n_vert)

    near = (
        {"au": lax.rem(au + 1, n_au)},
        {"au": lax.rem(au + n_au - 1, n_au)},
        {"vert": turned(1)},
        {"vert": turned(n_vert - 1)},
    )
    across = {"ch": lax.rem(band + 1, n_ch)}
    sibling = {"vert": vert + 1 - 2 * core}
    beside = {"vert": vert + 2 - 4 * lax.rem(vert // 2, 2)}
    along = {"au": au + 1 - 2 * lax.rem(au, 2)}

    inputs = (
        (head_in, head), (off_u_in, off_u), (off_v_in, off_v), (base_in, base),
        (pairs_in, pairs), (track_in, track), (data_in, data),
        (right_in, right), (left_in, left),
    )
    loads = [
        pltpu.make_async_copy(source, target, in_sems.at[j])
        for j, (source, target) in enumerate(inputs)
    ]
    for copy in loads:
        copy.start()
    fetches = []
    spans = ((mine, 6), (common, 4), (others, 6), (16 * (1 - core), 16))
    for j, (first, count) in enumerate(spans):
        rows = pl.ds(first * unit, count * unit)
        fetches.append(
            pltpu.make_async_copy(own_screens.at[rows], raw.at[rows], own_sems.at[j])
        )
        fetches[-1].start()
    barrier = pltpu.get_barrier_semaphore()
    for device in (*near, across, beside):
        pl.semaphore_signal(barrier, inc=1, device_id=device, device_id_type=MESH)

    def arrange(first, number):
        def one(pair, carry):
            for i in range(2):
                station = first * unit + 2 * pair + i
                feeds = arrange_station(raw[station], tall.at[i])
                for f in range(2):
                    screens[station, f] = feeds[f]
            return carry

        lax.fori_loop(0, number * unit // 2, one, 0)

    fetches[0].wait()
    arrange(mine, 6)
    fetches[1].wait()
    arrange(common, 4)
    pl.semaphore_wait(barrier, 6)

    def moves(i):
        pairs_of = ((packed, got_data, 8 * CAP), (labels, got_labels, CAP))
        for j, (source, target, rows) in enumerate(pairs_of):
            where = pl.ds((i + 1) * rows, rows)
            yield pltpu.make_async_remote_copy(
                src_ref=source.at[where],
                dst_ref=target.at[where],
                send_sem=send_sems.at[i, j],
                recv_sem=recv_sems.at[i, j],
                device_id=near[i],
                device_id_type=MESH,
            )

    def send(number, count, send_sem, recv_sem, device, own=False):
        where = number * unit
        return pltpu.make_async_remote_copy(
            src_ref=screens.at[pl.ds(where if own else here + where, count * unit)],
            dst_ref=screens.at[pl.ds(here + where, count * unit)],
            send_sem=send_sem,
            recv_sem=recv_sem,
            device_id=device,
            device_id_type=MESH,
        )

    runs = ((0, 2), (2, 2), (4, 1), (5, 1))

    def y_copy(k):
        first, count = (common, 4) if k == 4 else (mine + runs[k][0], runs[k][1])
        return send(first, count, y_send.at[k], y_recv.at[k], across, True)

    def relayed(k, first):
        device = beside if k % 2 == 0 else along
        start, count = runs[k]
        return send(first + start, count, relay_send.at[k], relay_recv.at[k], device)

    def c_copy(k, half):
        first = (
            half + 10 * colour, half + 6, half + 10 * (1 - colour), half + 10 * (1 - colour) + 4
        )[k]
        return send(first, (6, 4, 4, 2)[k], c_send.at[k], c_recv.at[k], sibling)

    for k in range(5):
        y_copy(k).start()

    for copy in loads[:7]:
        copy.wait()
    values, rows = pack_blocks(head, off_u, off_v, base, pairs, track, data)
    packed[...] = values
    labels[...] = rows

    for i in range(4):
        for copy in moves(i):
            copy.start()

    canvas[...] = jnp.zeros_like(canvas)
    for copy in fetches[2:]:
        copy.wait()
    arrange(others, 6)
    arrange(16 * (1 - core), 16)

    row = lax.broadcasted_iota(jnp.int32, (32, K), 0)
    channel = band * CH_DEV + lax.broadcasted_iota(jnp.int32, (32, K), 1) % CH_DEV
    ratio = 1.0 + channel.astype(F32) / jnp.float32(2 * CH_DEV * n_ch)
    coarse = row - 8
    coarse_u = 16 * (coarse % 4) + coarse // 4 - S // 2
    fine_v = row - 16
    coarse_v = (row - 24) * 8 - S // 2
    step = jnp.where(
        row < 16, jnp.where(row < 8, 2 * row, coarse_u), jnp.where(row < 24, fine_v, coarse_v)
    )
    mult[...] = step.astype(F32) / S * ratio

    def widen(rows):
        source = lax.broadcasted_iota(jnp.int32, (128, 2 * K), 0)
        column = lax.broadcasted_iota(jnp.int32, (128, 2 * K), 1)
        chosen = jnp.where(source == 8 + column // CH_DEV, 1.0, 0.0).astype(BF)
        lane = lax.broadcasted_iota(jnp.int32, rows.shape, 1)
        only = jnp.where(lane < 8, 0.0, rows).astype(BF)
        return jnp.dot(only, chosen, preferred_element_type=F32)

    got_labels[:CAP] = labels[:CAP]
    samples[: 8 * CAP] = packed[: 8 * CAP].astype(F32)
    spread[:CAP] = widen(labels[:CAP])

    def block(slot):
        sample = samples[pl.ds(8 * slot, 8), :]
        track = spread[pl.ds(slot, 1), :]
        turns = jnp.concatenate(
            [track[:, :K] * mult[:16], track[:, K:] * mult[16:]], axis=0
        )
        frac = turns - jnp.floor(turns + 0.5)
        square = frac * frac
        cos = horner(COS_COEF, square)
        sin = horner(SIN_COEF, square) * frac

        def phasors(first):
            cos_fine, sin_fine = cos[first : first + 8], sin[first : first + 8]
            all_cos, all_sin = [], []
            for a in range(8):
                at = first + 8 + a
                cos_a, sin_a = cos[at : at + 1], sin[at : at + 1]
                all_cos.append(cos_fine * cos_a - sin_fine * sin_a)
                all_sin.append(sin_fine * cos_a + cos_fine * sin_a)
            return (
                jnp.concatenate(all_cos, axis=0).astype(BF),
                jnp.concatenate(all_sin, axis=0).astype(BF),
            )

        cos_u, sin_u = phasors(0)
        cos_v, sin_v = phasors(16)
        table = jnp.concatenate(
            [
                jnp.concatenate([cos_v, -sin_v], axis=1),
                jnp.concatenate([sin_v, cos_v], axis=1),
            ],
            axis=0,
        )

        def spread_row(r):
            row = jnp.broadcast_to(sample[r : r + 1], (16, K)).astype(BF)
            return jnp.concatenate([row] * (S // 16), axis=0)

        weighed = []
        for p in range(4):
            re, im = spread_row(2 * p), spread_row(2 * p + 1)
            weighed.append(
                jnp.concatenate([re * cos_u - im * sin_u, re * sin_u + im * cos_u], axis=1)
            )
        dims = (((1,), (1,)), ((), ()))
        image = lax.dot_general(
            jnp.concatenate(weighed, axis=0), table, dims, preferred_element_type=F32
        )
        return image.astype(BF)

    keep = pltpu.make_async_copy(table, listing, in_sems.at[9])
    here_half, other_half = 16 * core, 16 * (1 - core)

    def relay(stage):
        if stage < 3:
            for k in ((0,), (1,), (2, 3))[stage]:
                y_copy(k).wait_recv()
                relayed(k, mine).start()
            if stage == 2:
                c_copy(0, here_half).start()
        elif stage == 3:
            for k in (0, 1):
                relayed(k, others).wait_recv()
            c_copy(2, here_half).start()
        else:
            y_copy(4).wait_recv()
            c_copy(1, here_half).start()
            for k in (2, 3):
                relayed(k, others).wait_recv()
            c_copy(3, here_half).start()

    def loop(group, carry):
        @pl.when(group == CAP // IMAGES_AT_ONCE)
        def _():
            for i in range(4):
                for copy in moves(i):
                    copy.wait_recv()
            samples[8 * CAP :] = got_data[8 * CAP :].astype(F32)
            spread[CAP:] = widen(got_labels[CAP:])
            table[...] = list_blocks(got_labels[...])
            keep.start()

        for stage, at in enumerate(RELAY_AT):

            @pl.when(group == at)
            def _():
                relay(stage)

        made = [block(IMAGES_AT_ONCE * group + i) for i in range(IMAGES_AT_ONCE)]
        for i in range(IMAGES_AT_ONCE):
            images[IMAGES_AT_ONCE * group + i] = made[i]
        return carry

    lax.fori_loop(0, SLOTS // IMAGES_AT_ONCE, loop, 0)
    for copy in loads[7:]:
        copy.wait()
    keep.wait()
    for i in range(4):
        for copy in moves(i):
            copy.wait_send()
    for k in range(5):
        y_copy(k).wait_send()
    for k in range(4):
        relayed(k, mine).wait_send()
        c_copy(k, here_half).wait_send()
        c_copy(k, other_half).wait_recv()


def folded(x):
    middle = x.shape[1] // 2
    lane = lax.broadcasted_iota(jnp.int32, (1, 1, 128), 2)
    return jnp.where(lane < S, x[:, :middle], swap_halves(x[:, middle:])).astype(BF)


def edge_u_kernel(listing, images, screens, right, left, canvas_in, canvas, edge_u, corner):
    grid_blocks(images, screens, canvas, right, left, listing, 0, listing[5, 0])
    edge_u[...] = canvas[:, TU : TU + S, :TV].astype(BF)
    corner[...] = folded(canvas[:, TU : TU + S, TV:])


def edge_v_kernel(listing, images, screens, right, left, canvas_in, canvas, *edge_v):
    grid_blocks(images, screens, canvas, right, left, listing, listing[5, 0], listing[6, 0])
    each = 8 // V_SPLIT
    for i, edge in enumerate(edge_v):
        edge[...] = folded(canvas[i * each : (i + 1) * each, :TU, TV:])


def late_kernel(listing, images, screens, right, left, canvas_in, canvas):
    grid_blocks(images, screens, canvas, right, left, listing, listing[6, 0], listing[7, 0])


def grid_blocks(images, screens, canvas, right, left, listing, first, last):
    here = screens.shape[0] // 2
    band = lax.axis_index("ch")

    def screen_place(station):
        owner = station // here
        local = station - owner * here
        return jnp.where(owner == band, local, here + local)

    def block(index):
        slot = listing[0, index]
        off_u = listing[1, index]
        off_v = listing[2, index]
        one = screen_place(listing[3, index])
        two = screen_place(listing[4, index])
        two_s = [screens[two, f].astype(F32) for f in range(2)]
        fixed = []
        for f in range(2):
            one_s = screens[one, f].astype(F32)
            one_swapped = swap_halves(one_s)
            for e in range(2):
                p = 2 * f + e
                same = one_s * two_s[e]
                cross = one_swapped * two_s[e]
                gain_re = same + swap_halves(same)
                gain_im = swap_halves(cross) - cross
                part = images[slot, p * S : (p + 1) * S].astype(F32)
                fixed.append((part * gain_re + swap_halves(part) * gain_im).astype(BF))
        tile = off_v // 128
        shift = off_v - tile * 128
        moved = pltpu.roll(right[...], shift, 1).astype(BF)
        table_re, table_im = moved[:S], moved[S:]
        shifted = jnp.concatenate(
            [
                jnp.concatenate([table_re, -table_im], axis=0),
                jnp.concatenate([table_im, table_re], axis=0),
            ],
            axis=1,
        )
        half = jnp.dot(
            jnp.concatenate(fixed, axis=0), shifted, preferred_element_type=F32
        ).astype(BF)
        eighth = off_u // 8
        placed = left[off_u - eighth * 8]
        start_u = pl.multiple_of(eighth * 8, 8)
        start_v = pl.multiple_of(tile * 128, 128)
        return start_u, start_v, shift, placed, half

    lane = lax.broadcasted_iota(jnp.int32, (1, 128), 1)

    def loop(group, carry):
        ready = [block(AT_ONCE * group + i) for i in range(AT_ONCE)]
        for start_u, start_v, shift, placed, half in ready:
            for f in range(2):
                both = []
                for p in (2 * f, 2 * f + 1):
                    part = half[p * S : (p + 1) * S]
                    both.append(jnp.concatenate([part[:, :128], part[:, 128:]], axis=0))
                grid = jnp.dot(
                    placed, jnp.concatenate(both, axis=1), preferred_element_type=F32
                )
                for e in range(2):
                    for r in range(2):
                        cells = grid[r * ROWS : (r + 1) * ROWS, 128 * e : 128 * (e + 1)]
                        cells = jnp.concatenate(
                            [
                                jnp.where(lane >= shift, cells, 0.0),
                                jnp.where(lane < shift, cells, 0.0),
                            ],
                            axis=1,
                        )
                        where = (
                            4 * f + 2 * e + r, pl.ds(start_u, ROWS), pl.ds(start_v, 256)
                        )
                        canvas[where] += cells
        return carry

    lax.fori_loop(first, last, loop, 0)


def lower_kernel(canvas, *refs):
    *got_v, out, top, side, sems = refs
    rest = pltpu.make_async_copy(
        canvas.at[:, S:TU, 128:TV], out.at[:, S:, 128:], sems.at[0]
    )
    rest.start()
    lane = lax.broadcasted_iota(jnp.int32, (1, 1, 128), 2)
    both = jnp.concatenate([x[...] for x in got_v], axis=0).astype(F32)
    low = jnp.where(lane < S, both, 0.0)
    high = jnp.where(lane < S, swap_halves(both), 0.0)
    side[:, : TU // 2 - S] = canvas[:, S : TU // 2, :128] + low[:, S:]
    side[:, TU // 2 - S :] = canvas[:, TU // 2 : TU, :128] + high
    store_side = pltpu.make_async_copy(side, out.at[:, S:, :128], sems.at[1])
    store_side.start()
    top[:, :, :128] = canvas[:, :S, :128] + low[:, :S]
    top[:, :, 128:] = canvas[:, :S, 128:TV]
    rest.wait()
    store_side.wait()


def upper_kernel(lower, top, got_u, got_c, out, rows, sems):
    lane = lax.broadcasted_iota(jnp.int32, (1, 1, 128), 2)
    stores = []
    for i in range(2):
        planes = slice(4 * i, 4 * i + 4)
        rows[planes] = top[planes] + got_u[planes].astype(F32)
        both = got_c[planes].astype(F32)
        rows[planes, : S // 2, :128] += jnp.where(lane < S, both, 0.0)
        rows[planes, S // 2 :, :128] += jnp.where(lane < S, swap_halves(both), 0.0)
        stores.append(
            pltpu.make_async_copy(rows.at[planes], out.at[planes, :S, :], sems.at[i])
        )
        stores[-1].start()
    for store in stores:
        store.wait()


def body(visibilities, tracks, offset_u, offset_v, heading, baseline, station_pair, screens):
    smem = pl.BlockSpec(memory_space=pltpu.SMEM)
    vmem = pl.BlockSpec(memory_space=pltpu.VMEM)
    hbm = pl.BlockSpec(memory_space=pltpu.HBM)
    n_au, n_vert = (lax.axis_size(axis) for axis in ("au", "vert"))
    here = screens.shape[0]
    canvas_shape = jax.ShapeDtypeStruct((8, TU + S + ROWS, TV + 128), F32)
    right_shape = jax.ShapeDtypeStruct((2 * S, 128), F32)
    left_shape = jax.ShapeDtypeStruct((8, 2 * ROWS, 2 * S), BF)
    dma = pltpu.SemaphoreType.DMA
    number = pltpu.VMEM((1, B_DEV), jnp.int32)
    images, all_screens, listing, canvas, right, left = pl.pallas_call(
        image_kernel,
        out_shape=(
            jax.ShapeDtypeStruct((SLOTS, 4 * S, 2 * S), BF),
            jax.ShapeDtypeStruct((2 * here, 2, S, 2 * S), BF),
            pltpu.SMEM((8, 128), jnp.int32),
            canvas_shape,
            right_shape,
            left_shape,
        ),
        in_specs=[hbm] * 10,
        out_specs=(vmem, vmem, smem, vmem, vmem, vmem),
        scratch_shapes=[
            number,
            number,
            number,
            number,
            pltpu.VMEM(station_pair.shape, jnp.int32),
            pltpu.VMEM((2 * TB, B_DEV), BF),
            pltpu.VMEM((8 * B_DEV, K), BF),
            pltpu.VMEM((8, 128), jnp.int32),
            dma((10,)),
            pltpu.VMEM((8 * SLOTS, K), BF),
            pltpu.VMEM((SLOTS, 128), F32),
            pltpu.VMEM((8 * SLOTS, K), BF),
            pltpu.VMEM((SLOTS, 128), F32),
            pltpu.VMEM((8 * SLOTS, K), F32),
            pltpu.VMEM((SLOTS, 2 * K), F32),
            pltpu.VMEM((32, K), F32),
            pltpu.VMEM((here, 4, S * S), BF),
            pltpu.VMEM((2, 4 * S, 128), F32),
            dma((4,)),
            dma((4, 2)),
            dma((4, 2)),
            dma((5,)),
            dma((5,)),
            dma((4,)),
            dma((4,)),
            dma((4,)),
            dma((4,)),
        ],
        compiler_params=pltpu.CompilerParams(
            collective_id=0, has_side_effects=True, vmem_limit_bytes=20 << 20
        ),
    )(*(pltpu.with_memory_space_constraint(x, pltpu.HBM) for x in (
        heading.reshape(1, B_DEV), offset_u[None], offset_v[None], baseline[None],
        station_pair, tracks.transpose(1, 2, 0).reshape(2 * TB, B_DEV),
        visibilities.reshape(8 * B_DEV, K), screens,
        jnp.asarray(right_table()), jnp.asarray(left_table()),
    )))

    def grid(kernel, canvas, flops, *edges):
        return pl.pallas_call(
            kernel,
            out_shape=(canvas_shape, *edges),
            in_specs=[smem] + [vmem] * 5,
            out_specs=(vmem,) * (1 + len(edges)),
            input_output_aliases={5: 0},
            compiler_params=pltpu.CompilerParams(vmem_limit_bytes=12 << 20),
            cost_estimate=pl.CostEstimate(
                flops=flops, bytes_accessed=1 << 20, transcendentals=0
            ),
        )(listing, images, all_screens, right, left, canvas)

    canvas, edge_u, corner = grid(
        edge_u_kernel,
        canvas,
        10**9,
        jax.ShapeDtypeStruct((8, S, TV), BF),
        jax.ShapeDtypeStruct((8, S // 2, 128), BF),
    )
    got_u = lax.ppermute(edge_u, "au", [(i, (i + 1) % n_au) for i in range(n_au)])
    diagonal = [
        (u * n_vert + v, (u + 1) % n_au * n_vert + (v + 1) % n_vert)
        for u in range(n_au)
        for v in range(n_vert)
    ]
    got_c = lax.ppermute(corner, ("au", "vert"), diagonal)
    canvas, *edge_v = grid(
        edge_v_kernel, canvas, 4 * 10**9, *[jax.ShapeDtypeStruct((8 // V_SPLIT, TU // 2, 128), BF)] * V_SPLIT
    )
    got_v = [
        lax.ppermute(x, "vert", [(i, (i + 1) % n_vert) for i in range(n_vert)]) for x in edge_v
    ]
    (canvas,) = grid(late_kernel, canvas, 10**6)
    tile = jax.ShapeDtypeStruct((8, TU, TV), F32)
    out, top = pl.pallas_call(
        lower_kernel,
        out_shape=(tile, jax.ShapeDtypeStruct((8, S, TV), F32)),
        in_specs=[vmem] * (1 + V_SPLIT),
        out_specs=(pl.BlockSpec(memory_space=pl.ANY), vmem),
        scratch_shapes=[pltpu.VMEM((8, TU - S, 128), F32), dma((2,))],
        compiler_params=pltpu.CompilerParams(vmem_limit_bytes=8 << 20),
    )(canvas, *got_v)
    out = pl.pallas_call(
        upper_kernel,
        out_shape=tile,
        in_specs=[pl.BlockSpec(memory_space=pl.ANY)] + [vmem] * 3,
        out_specs=pl.BlockSpec(memory_space=pl.ANY),
        scratch_shapes=[pltpu.VMEM((8, S, TV), F32), dma((2,))],
        input_output_aliases={0: 0},
        compiler_params=pltpu.CompilerParams(vmem_limit_bytes=8 << 20),
    )(out, top, got_u, got_c)
    return out[None]


def solution(mesh):
    placed = (
        P(("au", "vert"), None, "ch"),
        P(("au", "vert"), None, None),
        P(("au", "vert")),
        P(("au", "vert")),
        P(("au", "vert"), None),
        P(("au", "vert")),
        P(),
        P("ch", None, None),
    )
    return jax.shard_map(
        body, mesh=mesh, in_specs=placed, out_specs=P("ch", None, "au", "vert"), check_vma=False
    )
```

```python
import math

import jax
import jax.numpy as jnp
import ml_dtypes
import numpy as np
from jax import lax
from jax.experimental import pallas as pl
from jax.experimental.pallas import tpu as pltpu
from jax.sharding import PartitionSpec as P

S = 64
CH_DEV = 32
TB = 8
K = TB * CH_DEV
B_DEV = 32
CAP = B_DEV // 4
SLOTS = 5 * CAP
TU = 256
TV = 256
ROWS = 72
AT_ONCE = 4
U_GROUPS = 2
V_GROUPS = 4
V_SPLIT = 2
IMAGES_AT_ONCE = 8
RELAY_AT = (0, 1, 2, 4, 4)
MESH = pl.DeviceIdType.MESH
BF = jnp.bfloat16
F32 = jnp.float32


def series(values, degree):
    nodes = (np.cos(np.pi * (np.arange(400) + 0.5) / 400) + 1.0) * 0.125
    fitted = np.polynomial.chebyshev.Chebyshev.fit(nodes, values(nodes), degree, domain=[0, 0.25])
    return [float(c) for c in fitted.convert(kind=np.polynomial.Polynomial).coef]


COS_COEF = series(lambda q: np.cos(2 * np.pi * np.sqrt(q)), 5)
SIN_COEF = series(lambda q: np.sin(2 * np.pi * np.sqrt(q)) / np.sqrt(q), 5)


def horner(coefs, q):
    total = jnp.full_like(q, coefs[-1])
    for c in coefs[-2::-1]:
        total = total * q + jnp.float32(c)
    return total


def dft_tables():
    centred = np.arange(S) - S // 2
    product = (centred[:, None] * centred[None, :]) % S
    angles = np.float32(2.0 * math.pi / S) * product.astype(np.float32)
    scale = np.float32(1.0 / math.sqrt(S))
    re = (np.cos(angles) * scale).astype(ml_dtypes.bfloat16).astype(np.float32)
    im = (-np.sin(angles) * scale).astype(ml_dtypes.bfloat16).astype(np.float32)
    return re, im


def right_table():
    re, im = dft_tables()
    norm = np.float32(1.0 / math.sqrt(K))
    table = np.zeros((2 * S, 128), np.float32)
    table[:S, :S] = re.T * norm
    table[S:, :S] = im.T * norm
    return table


def left_table():
    re, im = dft_tables()
    order = np.concatenate([np.arange(0, S, 2), np.arange(1, S, 2)])
    re, im = re[:, order], im[:, order]
    table = np.zeros((8, 2, ROWS, 2 * S), np.float32)
    for shift in range(8):
        table[shift, 0, shift : shift + S, :S] = re
        table[shift, 0, shift : shift + S, S:] = -im
        table[shift, 1, shift : shift + S, :S] = im
        table[shift, 1, shift : shift + S, S:] = re
    return table.reshape(8, 2 * ROWS, 2 * S).astype(ml_dtypes.bfloat16)


def swap_halves(x):
    return pltpu.roll(x, S, x.ndim - 1)


def arrange_station(raw, tall):
    value = raw.astype(F32)
    for i in range(S // 2):
        tall[8 * i : 8 * i + 4, :] = value[:, 128 * i : 128 * (i + 1)]
    lane = lax.broadcasted_iota(jnp.int32, (S // 2, 128), 1)
    feeds = []
    for f in range(2):
        re = tall[pl.ds(2 * f, S // 2, stride=8), :]
        im = tall[pl.ds(2 * f + 1, S // 2, stride=8), :]
        even = jnp.where(lane < S, re, swap_halves(im))
        odd = jnp.where(lane < S, swap_halves(re), im)
        feeds.append(jnp.concatenate([even, odd], axis=0).astype(BF))
    return feeds


def pack_blocks(head, off_u, off_v, base, pairs, track, data):
    heads = head[...]
    kind = lax.broadcasted_iota(jnp.int32, (8, B_DEV), 0)
    named = jnp.where(kind == heads, 1.0, 0.0)
    before = lax.broadcasted_iota(jnp.int32, (B_DEV, B_DEV), 0)
    after = lax.broadcasted_iota(jnp.int32, (B_DEV, B_DEV), 1)
    strict = jnp.where(before < after, 1.0, 0.0).astype(BF)
    counts = jnp.dot(named.astype(BF), strict, preferred_element_type=F32)
    rank = jnp.sum(named * counts, axis=0, keepdims=True)
    slot = heads.astype(F32) * CAP + rank
    which = lax.broadcasted_iota(jnp.int32, (SLOTS, B_DEV), 0).astype(F32)
    chosen = jnp.where(which == slot, 1.0, 0.0).astype(BF)

    label = lax.broadcasted_iota(jnp.int32, (pairs.shape[1], B_DEV), 0)
    listed = jnp.where(label == base[...], 1.0, 0.0).astype(BF)
    station = jnp.dot(pairs[...].astype(F32).astype(BF), listed, preferred_element_type=F32)
    rows = jnp.concatenate(
        [
            jnp.ones((1, B_DEV), F32),
            off_u[...].astype(F32),
            off_v[...].astype(F32),
            station,
            jnp.zeros((3, B_DEV), F32),
            track[...].astype(F32),
            jnp.zeros((128 - 8 - 2 * TB, B_DEV), F32),
        ],
        axis=0,
    ).astype(BF)
    dims = (((1,), (1,)), ((), ()))
    labels = lax.dot_general(chosen, rows, dims, preferred_element_type=F32)

    owner = lax.broadcasted_iota(jnp.int32, (B_DEV, 8 * B_DEV), 0)
    column = lax.broadcasted_iota(jnp.int32, (B_DEV, 8 * B_DEV), 1)
    widen = jnp.where(owner == column // 8, 1.0, 0.0).astype(BF)
    wide = jnp.dot(
        jnp.broadcast_to(slot, (8, B_DEV)).astype(BF), widen, preferred_element_type=F32
    )[:1]
    lane = lax.broadcasted_iota(jnp.int32, (1, 8 * B_DEV), 1) % 8
    place = wide * 8.0 + lane.astype(F32)
    target = lax.broadcasted_iota(jnp.int32, (8 * SLOTS, 8 * B_DEV), 0).astype(F32)
    moved = jnp.where(target == place, 1.0, 0.0).astype(BF)
    return jnp.dot(moved, data[...], preferred_element_type=F32).astype(BF), labels


def list_blocks(labels):
    dims = (((1,), (1,)), ((), ()))
    quantity = lax.broadcasted_iota(jnp.int32, (8, 128), 0)
    lane = lax.broadcasted_iota(jnp.int32, (8, 128), 1)
    pick = jnp.where(quantity == lane, 1.0, 0.0).astype(BF)
    rows = lax.dot_general(pick, labels.astype(BF), dims, preferred_element_type=F32)
    filled, at_u, at_v = rows[0:1], rows[1:2], rows[2:3]
    past_u = at_u > TU - S
    past = jnp.logical_or(past_u, at_v > TV - S)
    first = jnp.where(past_u, filled, 0.0)
    early = jnp.where(past, filled, 0.0)
    kind = lax.broadcasted_iota(jnp.int32, (8, SLOTS), 0)
    both = jnp.where(
        kind == 0,
        first,
        jnp.where(kind == 1, early - first, jnp.where(kind == 2, filled - early, 0.0)),
    )
    before = lax.broadcasted_iota(jnp.int32, (SLOTS, SLOTS), 0)
    after = lax.broadcasted_iota(jnp.int32, (SLOTS, SLOTS), 1)
    strict = jnp.where(before < after, 1.0, 0.0).astype(BF)
    ahead = jnp.dot(both.astype(BF), strict, preferred_element_type=F32)
    number_first = jnp.sum(first, axis=1, keepdims=True)
    number_early = jnp.sum(early, axis=1, keepdims=True)
    number = jnp.sum(filled, axis=1, keepdims=True)
    place = jnp.where(past, number_first + ahead[1:2], number_early + ahead[2:3])
    place = jnp.where(past_u, ahead[0:1], place)
    place = jnp.where(filled > 0.5, place, -1.0)
    target = lax.broadcasted_iota(jnp.int32, (128, SLOTS), 0).astype(F32)
    moved = jnp.where(target == place, 1.0, 0.0).astype(BF)
    slot = lax.broadcasted_iota(jnp.int32, (8, SLOTS), 1).astype(F32)
    rows = jnp.where(kind == 0, slot, rows)
    table = lax.dot_general(rows.astype(BF), moved, dims, preferred_element_type=F32)
    spare = jnp.where(lane.astype(F32) >= number, float(TU + S), 0.0)
    table = table + jnp.where(quantity == 1, spare, 0.0)
    groups = jnp.floor((number + (AT_ONCE - 1.0)) / AT_ONCE)
    ends = []
    for count, least in ((number_first, U_GROUPS), (number_early, V_GROUPS)):
        enough = jnp.minimum(groups, float(least))
        needed = jnp.floor((count + (AT_ONCE - 1.0)) / AT_ONCE)
        ends.append(jnp.maximum(needed, enough))
    for row, end in enumerate((*ends, groups)):
        table = jnp.where(quantity == 5 + row, end, table)
    return table.astype(jnp.int32)


def image_kernel(
    head_in, off_u_in, off_v_in, base_in, pairs_in, track_in, data_in, own_screens,
    right_in, left_in,
    images, screens, listing, canvas, right, left,
    head, off_u, off_v, base, pairs, track, data, table, in_sems,
    packed, labels, got_data, got_labels, samples, spread, mult, raw, tall,
    own_sems, send_sems, recv_sems, y_send, y_recv, relay_send, relay_recv, c_send, c_recv,
):
    au, vert, band = (lax.axis_index(axis) for axis in ("au", "vert", "ch"))
    n_au, n_vert, n_ch = (lax.axis_size(axis) for axis in ("au", "vert", "ch"))
    here = own_screens.shape[0]
    unit = here // 32
    core = lax.rem(vert, 2)
    colour = lax.rem(vert // 2 + au, 2)
    mine = 16 * core + 10 * colour
    common = 16 * core + 6
    others = 16 * core + 10 * (1 - colour)

    def turned(step):
        return lax.rem(vert + step, n_vert)

    near = (
        {"au": lax.rem(au + 1, n_au)},
        {"au": lax.rem(au + n_au - 1, n_au)},
        {"vert": turned(1)},
        {"vert": turned(n_vert - 1)},
    )
    across = {"ch": lax.rem(band + 1, n_ch)}
    sibling = {"vert": vert + 1 - 2 * core}
    beside = {"vert": vert + 2 - 4 * lax.rem(vert // 2, 2)}
    along = {"au": au + 1 - 2 * lax.rem(au, 2)}

    inputs = (
        (head_in, head), (off_u_in, off_u), (off_v_in, off_v), (base_in, base),
        (pairs_in, pairs), (track_in, track), (data_in, data),
        (right_in, right), (left_in, left),
    )
    loads = [
        pltpu.make_async_copy(source, target, in_sems.at[j])
        for j, (source, target) in enumerate(inputs)
    ]
    for copy in loads:
        copy.start()
    fetches = []
    spans = ((mine, 6), (common, 4), (others, 6), (16 * (1 - core), 16))
    for j, (first, count) in enumerate(spans):
        rows = pl.ds(first * unit, count * unit)
        fetches.append(
            pltpu.make_async_copy(own_screens.at[rows], raw.at[rows], own_sems.at[j])
        )
        fetches[-1].start()
    barrier = pltpu.get_barrier_semaphore()
    for device in (*near, across, beside):
        pl.semaphore_signal(barrier, inc=1, device_id=device, device_id_type=MESH)

    def arrange(first, number):
        def one(pair, carry):
            for i in range(2):
                station = first * unit + 2 * pair + i
                feeds = arrange_station(raw[station], tall.at[i])
                for f in range(2):
                    screens[station, f] = feeds[f]
            return carry

        lax.fori_loop(0, number * unit // 2, one, 0)

    fetches[0].wait()
    arrange(mine, 6)
    fetches[1].wait()
    arrange(common, 4)
    pl.semaphore_wait(barrier, 6)

    def moves(i):
        pairs_of = ((packed, got_data, 8 * CAP), (labels, got_labels, CAP))
        for j, (source, target, rows) in enumerate(pairs_of):
            where = pl.ds((i + 1) * rows, rows)
            yield pltpu.make_async_remote_copy(
                src_ref=source.at[where],
                dst_ref=target.at[where],
                send_sem=send_sems.at[i, j],
                recv_sem=recv_sems.at[i, j],
                device_id=near[i],
                device_id_type=MESH,
            )

    def send(number, count, send_sem, recv_sem, device, own=False):
        where = number * unit
        return pltpu.make_async_remote_copy(
            src_ref=screens.at[pl.ds(where if own else here + where, count * unit)],
            dst_ref=screens.at[pl.ds(here + where, count * unit)],
            send_sem=send_sem,
            recv_sem=recv_sem,
            device_id=device,
            device_id_type=MESH,
        )

    runs = ((0, 2), (2, 2), (4, 1), (5, 1))

    def y_copy(k):
        first, count = (common, 4) if k == 4 else (mine + runs[k][0], runs[k][1])
        return send(first, count, y_send.at[k], y_recv.at[k], across, True)

    def relayed(k, first):
        device = beside if k % 2 == 0 else along
        start, count = runs[k]
        return send(first + start, count, relay_send.at[k], relay_recv.at[k], device)

    def c_copy(k, half):
        first = (
            half + 10 * colour, half + 6, half + 10 * (1 - colour), half + 10 * (1 - colour) + 4
        )[k]
        return send(first, (6, 4, 4, 2)[k], c_send.at[k], c_recv.at[k], sibling)

    for k in range(5):
        y_copy(k).start()

    for copy in loads[:7]:
        copy.wait()
    values, rows = pack_blocks(head, off_u, off_v, base, pairs, track, data)
    packed[...] = values
    labels[...] = rows

    for i in range(4):
        for copy in moves(i):
            copy.start()

    canvas[...] = jnp.zeros_like(canvas)
    for copy in fetches[2:]:
        copy.wait()
    arrange(others, 6)
    arrange(16 * (1 - core), 16)

    row = lax.broadcasted_iota(jnp.int32, (32, K), 0)
    channel = band * CH_DEV + lax.broadcasted_iota(jnp.int32, (32, K), 1) % CH_DEV
    ratio = 1.0 + channel.astype(F32) / jnp.float32(2 * CH_DEV * n_ch)
    coarse = row - 8
    coarse_u = 16 * (coarse % 4) + coarse // 4 - S // 2
    fine_v = row - 16
    coarse_v = (row - 24) * 8 - S // 2
    step = jnp.where(
        row < 16, jnp.where(row < 8, 2 * row, coarse_u), jnp.where(row < 24, fine_v, coarse_v)
    )
    mult[...] = step.astype(F32) / S * ratio

    def widen(rows):
        source = lax.broadcasted_iota(jnp.int32, (128, 2 * K), 0)
        column = lax.broadcasted_iota(jnp.int32, (128, 2 * K), 1)
        chosen = jnp.where(source == 8 + column // CH_DEV, 1.0, 0.0).astype(BF)
        lane = lax.broadcasted_iota(jnp.int32, rows.shape, 1)
        only = jnp.where(lane < 8, 0.0, rows).astype(BF)
        return jnp.dot(only, chosen, preferred_element_type=F32)

    got_labels[:CAP] = labels[:CAP]
    samples[: 8 * CAP] = packed[: 8 * CAP].astype(F32)
    spread[:CAP] = widen(labels[:CAP])

    def block(slot):
        sample = samples[pl.ds(8 * slot, 8), :]
        track = spread[pl.ds(slot, 1), :]
        turns = jnp.concatenate(
            [track[:, :K] * mult[:16], track[:, K:] * mult[16:]], axis=0
        )
        frac = turns - jnp.floor(turns + 0.5)
        square = frac * frac
        cos = horner(COS_COEF, square)
        sin = horner(SIN_COEF, square) * frac

        def phasors(first):
            cos_fine, sin_fine = cos[first : first + 8], sin[first : first + 8]
            all_cos, all_sin = [], []
            for a in range(8):
                at = first + 8 + a
                cos_a, sin_a = cos[at : at + 1], sin[at : at + 1]
                all_cos.append(cos_fine * cos_a - sin_fine * sin_a)
                all_sin.append(sin_fine * cos_a + cos_fine * sin_a)
            return (
                jnp.concatenate(all_cos, axis=0).astype(BF),
                jnp.concatenate(all_sin, axis=0).astype(BF),
            )

        cos_u, sin_u = phasors(0)
        cos_v, sin_v = phasors(16)
        table = jnp.concatenate(
            [
                jnp.concatenate([cos_v, -sin_v], axis=1),
                jnp.concatenate([sin_v, cos_v], axis=1),
            ],
            axis=0,
        )

        def spread_row(r):
            row = jnp.broadcast_to(sample[r : r + 1], (16, K)).astype(BF)
            return jnp.concatenate([row] * (S // 16), axis=0)

        weighed = []
        for p in range(4):
            re, im = spread_row(2 * p), spread_row(2 * p + 1)
            weighed.append(
                jnp.concatenate([re * cos_u - im * sin_u, re * sin_u + im * cos_u], axis=1)
            )
        dims = (((1,), (1,)), ((), ()))
        image = lax.dot_general(
            jnp.concatenate(weighed, axis=0), table, dims, preferred_element_type=F32
        )
        return image.astype(BF)

    keep = pltpu.make_async_copy(table, listing, in_sems.at[9])
    here_half, other_half = 16 * core, 16 * (1 - core)

    def relay(stage):
        if stage < 3:
            for k in ((0,), (1,), (2, 3))[stage]:
                y_copy(k).wait_recv()
                relayed(k, mine).start()
            if stage == 2:
                c_copy(0, here_half).start()
        elif stage == 3:
            for k in (0, 1):
                relayed(k, others).wait_recv()
            c_copy(2, here_half).start()
        else:
            y_copy(4).wait_recv()
            c_copy(1, here_half).start()
            for k in (2, 3):
                relayed(k, others).wait_recv()
            c_copy(3, here_half).start()

    def loop(group, carry):
        @pl.when(group == CAP // IMAGES_AT_ONCE)
        def _():
            for i in range(4):
                for copy in moves(i):
                    copy.wait_recv()
            samples[8 * CAP :] = got_data[8 * CAP :].astype(F32)
            spread[CAP:] = widen(got_labels[CAP:])
            table[...] = list_blocks(got_labels[...])
            keep.start()

        for stage, at in enumerate(RELAY_AT):

            @pl.when(group == at)
            def _():
                relay(stage)

        made = [block(IMAGES_AT_ONCE * group + i) for i in range(IMAGES_AT_ONCE)]
        for i in range(IMAGES_AT_ONCE):
            images[IMAGES_AT_ONCE * group + i] = made[i]
        return carry

    lax.fori_loop(0, SLOTS // IMAGES_AT_ONCE, loop, 0)
    for copy in loads[7:]:
        copy.wait()
    keep.wait()
    for i in range(4):
        for copy in moves(i):
            copy.wait_send()
    for k in range(5):
        y_copy(k).wait_send()
    for k in range(4):
        relayed(k, mine).wait_send()
        c_copy(k, here_half).wait_send()
        c_copy(k, other_half).wait_recv()


def folded(x):
    middle = x.shape[1] // 2
    lane = lax.broadcasted_iota(jnp.int32, (1, 1, 128), 2)
    return jnp.where(lane < S, x[:, :middle], swap_halves(x[:, middle:])).astype(BF)


def edge_u_kernel(listing, images, screens, right, left, canvas_in, canvas, edge_u, corner):
    grid_blocks(images, screens, canvas, right, left, listing, 0, listing[5, 0])
    edge_u[...] = canvas[:, TU : TU + S, :TV].astype(BF)
    corner[...] = folded(canvas[:, TU : TU + S, TV:])


def edge_v_kernel(listing, images, screens, right, left, canvas_in, canvas, *edge_v):
    grid_blocks(images, screens, canvas, right, left, listing, listing[5, 0], listing[6, 0])
    each = 8 // V_SPLIT
    for i, edge in enumerate(edge_v):
        edge[...] = folded(canvas[i * each : (i + 1) * each, :TU, TV:])


def late_kernel(listing, images, screens, right, left, canvas_in, canvas):
    grid_blocks(images, screens, canvas, right, left, listing, listing[6, 0], listing[7, 0])


def grid_blocks(images, screens, canvas, right, left, listing, first, last):
    here = screens.shape[0] // 2
    band = lax.axis_index("ch")

    def screen_place(station):
        owner = station // here
        local = station - owner * here
        return jnp.where(owner == band, local, here + local)

    def block(index):
        slot = listing[0, index]
        off_u = listing[1, index]
        off_v = listing[2, index]
        one = screen_place(listing[3, index])
        two = screen_place(listing[4, index])
        two_s = [screens[two, f].astype(F32) for f in range(2)]
        fixed = []
        for f in range(2):
            one_s = screens[one, f].astype(F32)
            one_swapped = swap_halves(one_s)
            for e in range(2):
                p = 2 * f + e
                same = one_s * two_s[e]
                cross = one_swapped * two_s[e]
                gain_re = same + swap_halves(same)
                gain_im = swap_halves(cross) - cross
                part = images[slot, p * S : (p + 1) * S].astype(F32)
                fixed.append((part * gain_re + swap_halves(part) * gain_im).astype(BF))
        tile = off_v // 128
        shift = off_v - tile * 128
        moved = pltpu.roll(right[...], shift, 1).astype(BF)
        table_re, table_im = moved[:S], moved[S:]
        shifted = jnp.concatenate(
            [
                jnp.concatenate([table_re, -table_im], axis=0),
                jnp.concatenate([table_im, table_re], axis=0),
            ],
            axis=1,
        )
        half = jnp.dot(
            jnp.concatenate(fixed, axis=0), shifted, preferred_element_type=F32
        ).astype(BF)
        eighth = off_u // 8
        placed = left[off_u - eighth * 8]
        start_u = pl.multiple_of(eighth * 8, 8)
        start_v = pl.multiple_of(tile * 128, 128)
        return start_u, start_v, shift, placed, half

    lane = lax.broadcasted_iota(jnp.int32, (1, 128), 1)

    def loop(group, carry):
        ready = [block(AT_ONCE * group + i) for i in range(AT_ONCE)]
        for start_u, start_v, shift, placed, half in ready:
            for f in range(2):
                both = []
                for p in (2 * f, 2 * f + 1):
                    part = half[p * S : (p + 1) * S]
                    both.append(jnp.concatenate([part[:, :128], part[:, 128:]], axis=0))
                grid = jnp.dot(
                    placed, jnp.concatenate(both, axis=1), preferred_element_type=F32
                )
                for e in range(2):
                    for r in range(2):
                        cells = grid[r * ROWS : (r + 1) * ROWS, 128 * e : 128 * (e + 1)]
                        cells = jnp.concatenate(
                            [
                                jnp.where(lane >= shift, cells, 0.0),
                                jnp.where(lane < shift, cells, 0.0),
                            ],
                            axis=1,
                        )
                        where = (
                            4 * f + 2 * e + r, pl.ds(start_u, ROWS), pl.ds(start_v, 256)
                        )
                        canvas[where] += cells
        return carry

    lax.fori_loop(first, last, loop, 0)


def finish_kernel(canvas, got_u, got_c, *refs):
    *got_v, out, top, side, sems = refs
    rest = pltpu.make_async_copy(
        canvas.at[:, S:TU, 128:TV], out.at[:, S:, 128:], sems.at[2]
    )
    rest.start()
    lane = lax.broadcasted_iota(jnp.int32, (1, 1, 128), 2)
    both = jnp.concatenate([x[...] for x in got_v], axis=0).astype(F32)
    low = jnp.where(lane < S, both, 0.0)
    high = jnp.where(lane < S, swap_halves(both), 0.0)
    side[:, : TU // 2 - S] = canvas[:, S : TU // 2, :128] + low[:, S:]
    side[:, TU // 2 - S :] = canvas[:, TU // 2 : TU, :128] + high
    store_side = pltpu.make_async_copy(side, out.at[:, S:, :128], sems.at[1])
    store_side.start()
    top[...] = canvas[:, :S, :TV] + got_u[...].astype(F32)
    both = got_c[...].astype(F32)
    top[:, : S // 2, :128] += low[:, : S // 2] + jnp.where(lane < S, both, 0.0)
    top[:, S // 2 :, :128] += low[:, S // 2 : S] + jnp.where(
        lane < S, swap_halves(both), 0.0
    )
    store_top = pltpu.make_async_copy(top, out.at[:, :S, :], sems.at[0])
    store_top.start()
    rest.wait()
    store_side.wait()
    store_top.wait()


def body(visibilities, tracks, offset_u, offset_v, heading, baseline, station_pair, screens):
    smem = pl.BlockSpec(memory_space=pltpu.SMEM)
    vmem = pl.BlockSpec(memory_space=pltpu.VMEM)
    hbm = pl.BlockSpec(memory_space=pltpu.HBM)
    n_au, n_vert = (lax.axis_size(axis) for axis in ("au", "vert"))
    here = screens.shape[0]
    canvas_shape = jax.ShapeDtypeStruct((8, TU + S + ROWS, TV + 128), F32)
    right_shape = jax.ShapeDtypeStruct((2 * S, 128), F32)
    left_shape = jax.ShapeDtypeStruct((8, 2 * ROWS, 2 * S), BF)
    dma = pltpu.SemaphoreType.DMA
    number = pltpu.VMEM((1, B_DEV), jnp.int32)
    images, all_screens, listing, canvas, right, left = pl.pallas_call(
        image_kernel,
        out_shape=(
            jax.ShapeDtypeStruct((SLOTS, 4 * S, 2 * S), BF),
            jax.ShapeDtypeStruct((2 * here, 2, S, 2 * S), BF),
            pltpu.SMEM((8, 128), jnp.int32),
            canvas_shape,
            right_shape,
            left_shape,
        ),
        in_specs=[hbm] * 10,
        out_specs=(vmem, vmem, smem, vmem, vmem, vmem),
        scratch_shapes=[
            number,
            number,
            number,
            number,
            pltpu.VMEM(station_pair.shape, jnp.int32),
            pltpu.VMEM((2 * TB, B_DEV), BF),
            pltpu.VMEM((8 * B_DEV, K), BF),
            pltpu.VMEM((8, 128), jnp.int32),
            dma((10,)),
            pltpu.VMEM((8 * SLOTS, K), BF),
            pltpu.VMEM((SLOTS, 128), F32),
            pltpu.VMEM((8 * SLOTS, K), BF),
            pltpu.VMEM((SLOTS, 128), F32),
            pltpu.VMEM((8 * SLOTS, K), F32),
            pltpu.VMEM((SLOTS, 2 * K), F32),
            pltpu.VMEM((32, K), F32),
            pltpu.VMEM((here, 4, S * S), BF),
            pltpu.VMEM((2, 4 * S, 128), F32),
            dma((4,)),
            dma((4, 2)),
            dma((4, 2)),
            dma((5,)),
            dma((5,)),
            dma((4,)),
            dma((4,)),
            dma((4,)),
            dma((4,)),
        ],
        compiler_params=pltpu.CompilerParams(
            collective_id=0, has_side_effects=True, vmem_limit_bytes=20 << 20
        ),
    )(*(pltpu.with_memory_space_constraint(x, pltpu.HBM) for x in (
        heading.reshape(1, B_DEV), offset_u[None], offset_v[None], baseline[None],
        station_pair, tracks.transpose(1, 2, 0).reshape(2 * TB, B_DEV),
        visibilities.reshape(8 * B_DEV, K), screens,
        jnp.asarray(right_table()), jnp.asarray(left_table()),
    )))

    def grid(kernel, canvas, flops, *edges):
        return pl.pallas_call(
            kernel,
            out_shape=(canvas_shape, *edges),
            in_specs=[smem] + [vmem] * 5,
            out_specs=(vmem,) * (1 + len(edges)),
            input_output_aliases={5: 0},
            compiler_params=pltpu.CompilerParams(vmem_limit_bytes=12 << 20),
            cost_estimate=pl.CostEstimate(
                flops=flops, bytes_accessed=1 << 20, transcendentals=0
            ),
        )(listing, images, all_screens, right, left, canvas)

    canvas, edge_u, corner = grid(
        edge_u_kernel,
        canvas,
        10**9,
        jax.ShapeDtypeStruct((8, S, TV), BF),
        jax.ShapeDtypeStruct((8, S // 2, 128), BF),
    )
    got_u = lax.ppermute(edge_u, "au", [(i, (i + 1) % n_au) for i in range(n_au)])
    diagonal = [
        (u * n_vert + v, (u + 1) % n_au * n_vert + (v + 1) % n_vert)
        for u in range(n_au)
        for v in range(n_vert)
    ]
    got_c = lax.ppermute(corner, ("au", "vert"), diagonal)
    canvas, *edge_v = grid(
        edge_v_kernel, canvas, 4 * 10**9, *[jax.ShapeDtypeStruct((8 // V_SPLIT, TU // 2, 128), BF)] * V_SPLIT
    )
    got_v = [
        lax.ppermute(x, "vert", [(i, (i + 1) % n_vert) for i in range(n_vert)]) for x in edge_v
    ]
    (canvas,) = grid(late_kernel, canvas, 10**6)
    out = pl.pallas_call(
        finish_kernel,
        out_shape=jax.ShapeDtypeStruct((8, TU, TV), F32),
        in_specs=[vmem] * (3 + V_SPLIT),
        out_specs=pl.BlockSpec(memory_space=pl.ANY),
        scratch_shapes=[
            pltpu.VMEM((8, S, TV), F32),
            pltpu.VMEM((8, TU - S, 128), F32),
            dma((3,)),
        ],
        compiler_params=pltpu.CompilerParams(vmem_limit_bytes=8 << 20),
    )(canvas, got_u, got_c, *got_v)
    return out[None]


def solution(mesh):
    placed = (
        P(("au", "vert"), None, "ch"),
        P(("au", "vert"), None, None),
        P(("au", "vert")),
        P(("au", "vert")),
        P(("au", "vert"), None),
        P(("au", "vert")),
        P(),
        P("ch", None, None),
    )
    return jax.shard_map(
        body, mesh=mesh, in_specs=placed, out_specs=P("ch", None, "au", "vert"), check_vma=False
    )
```

```python
import math

import jax
import jax.numpy as jnp
import ml_dtypes
import numpy as np
from jax import lax
from jax.experimental import pallas as pl
from jax.experimental.pallas import tpu as pltpu
from jax.sharding import PartitionSpec as P

S = 64
CH_DEV = 32
TB = 8
K = TB * CH_DEV
B_DEV = 32
CAP = B_DEV // 4
SLOTS = 5 * CAP
TU = 256
TV = 256
ROWS = 72
AT_ONCE = 4
U_GROUPS = 2
V_GROUPS = 4
V_SPLIT = 2
IMAGES_AT_ONCE = 8
RELAY_AT = (0, 1, 2, 4, 4)
MESH = pl.DeviceIdType.MESH
BF = jnp.bfloat16
F32 = jnp.float32


def series(values, degree):
    nodes = (np.cos(np.pi * (np.arange(400) + 0.5) / 400) + 1.0) * 0.125
    fitted = np.polynomial.chebyshev.Chebyshev.fit(nodes, values(nodes), degree, domain=[0, 0.25])
    return [float(c) for c in fitted.convert(kind=np.polynomial.Polynomial).coef]


COS_COEF = series(lambda q: np.cos(2 * np.pi * np.sqrt(q)), 5)
SIN_COEF = series(lambda q: np.sin(2 * np.pi * np.sqrt(q)) / np.sqrt(q), 5)


def horner(coefs, q):
    total = jnp.full_like(q, coefs[-1])
    for c in coefs[-2::-1]:
        total = total * q + jnp.float32(c)
    return total


def dft_tables():
    centred = np.arange(S) - S // 2
    product = (centred[:, None] * centred[None, :]) % S
    angles = np.float32(2.0 * math.pi / S) * product.astype(np.float32)
    scale = np.float32(1.0 / math.sqrt(S))
    re = (np.cos(angles) * scale).astype(ml_dtypes.bfloat16).astype(np.float32)
    im = (-np.sin(angles) * scale).astype(ml_dtypes.bfloat16).astype(np.float32)
    return re, im


def right_table():
    re, im = dft_tables()
    norm = np.float32(1.0 / math.sqrt(K))
    table = np.zeros((2 * S, 128), np.float32)
    table[:S, :S] = re.T * norm
    table[S:, :S] = im.T * norm
    return table


def left_table():
    re, im = dft_tables()
    order = np.concatenate([np.arange(0, S, 2), np.arange(1, S, 2)])
    re, im = re[:, order], im[:, order]
    table = np.zeros((8, 2, ROWS, 2 * S), np.float32)
    for shift in range(8):
        table[shift, 0, shift : shift + S, :S] = re
        table[shift, 0, shift : shift + S, S:] = -im
        table[shift, 1, shift : shift + S, :S] = im
        table[shift, 1, shift : shift + S, S:] = re
    return table.reshape(8, 2 * ROWS, 2 * S).astype(ml_dtypes.bfloat16)


def swap_halves(x):
    return pltpu.roll(x, S, x.ndim - 1)


def arrange_station(raw, tall):
    value = raw.astype(F32)
    for i in range(S // 2):
        tall[8 * i : 8 * i + 4, :] = value[:, 128 * i : 128 * (i + 1)]
    lane = lax.broadcasted_iota(jnp.int32, (S // 2, 128), 1)
    planes = []
    for r in range(2):
        first = tall[pl.ds(r, S // 2, stride=8), :]
        second = tall[pl.ds(2 + r, S // 2, stride=8), :]
        even = jnp.where(lane < S, first, swap_halves(second))
        odd = jnp.where(lane < S, swap_halves(first), second)
        planes.append(jnp.concatenate([even, odd], axis=0).astype(BF))
    return planes


def pack_blocks(head, off_u, off_v, base, pairs, track, data):
    heads = head[...]
    kind = lax.broadcasted_iota(jnp.int32, (8, B_DEV), 0)
    named = jnp.where(kind == heads, 1.0, 0.0)
    before = lax.broadcasted_iota(jnp.int32, (B_DEV, B_DEV), 0)
    after = lax.broadcasted_iota(jnp.int32, (B_DEV, B_DEV), 1)
    strict = jnp.where(before < after, 1.0, 0.0).astype(BF)
    counts = jnp.dot(named.astype(BF), strict, preferred_element_type=F32)
    rank = jnp.sum(named * counts, axis=0, keepdims=True)
    slot = heads.astype(F32) * CAP + rank
    which = lax.broadcasted_iota(jnp.int32, (SLOTS, B_DEV), 0).astype(F32)
    chosen = jnp.where(which == slot, 1.0, 0.0).astype(BF)

    label = lax.broadcasted_iota(jnp.int32, (pairs.shape[1], B_DEV), 0)
    listed = jnp.where(label == base[...], 1.0, 0.0).astype(BF)
    station = jnp.dot(pairs[...].astype(F32).astype(BF), listed, preferred_element_type=F32)
    rows = jnp.concatenate(
        [
            jnp.ones((1, B_DEV), F32),
            off_u[...].astype(F32),
            off_v[...].astype(F32),
            station,
            jnp.zeros((3, B_DEV), F32),
            track[...].astype(F32),
            jnp.zeros((128 - 8 - 2 * TB, B_DEV), F32),
        ],
        axis=0,
    ).astype(BF)
    dims = (((1,), (1,)), ((), ()))
    labels = lax.dot_general(chosen, rows, dims, preferred_element_type=F32)

    owner = lax.broadcasted_iota(jnp.int32, (B_DEV, 8 * B_DEV), 0)
    column = lax.broadcasted_iota(jnp.int32, (B_DEV, 8 * B_DEV), 1)
    widen = jnp.where(owner == column // 8, 1.0, 0.0).astype(BF)
    wide = jnp.dot(
        jnp.broadcast_to(slot, (8, B_DEV)).astype(BF), widen, preferred_element_type=F32
    )[:1]
    lane = lax.broadcasted_iota(jnp.int32, (1, 8 * B_DEV), 1) % 8
    place = wide * 8.0 + lane.astype(F32)
    target = lax.broadcasted_iota(jnp.int32, (8 * SLOTS, 8 * B_DEV), 0).astype(F32)
    moved = jnp.where(target == place, 1.0, 0.0).astype(BF)
    return jnp.dot(moved, data[...], preferred_element_type=F32).astype(BF), labels


def list_blocks(labels):
    dims = (((1,), (1,)), ((), ()))
    quantity = lax.broadcasted_iota(jnp.int32, (8, 128), 0)
    lane = lax.broadcasted_iota(jnp.int32, (8, 128), 1)
    pick = jnp.where(quantity == lane, 1.0, 0.0).astype(BF)
    rows = lax.dot_general(pick, labels.astype(BF), dims, preferred_element_type=F32)
    filled, at_u, at_v = rows[0:1], rows[1:2], rows[2:3]
    past_u = at_u > TU - S
    past = jnp.logical_or(past_u, at_v > TV - S)
    first = jnp.where(past_u, filled, 0.0)
    early = jnp.where(past, filled, 0.0)
    kind = lax.broadcasted_iota(jnp.int32, (8, SLOTS), 0)
    both = jnp.where(
        kind == 0,
        first,
        jnp.where(kind == 1, early - first, jnp.where(kind == 2, filled - early, 0.0)),
    )
    before = lax.broadcasted_iota(jnp.int32, (SLOTS, SLOTS), 0)
    after = lax.broadcasted_iota(jnp.int32, (SLOTS, SLOTS), 1)
    strict = jnp.where(before < after, 1.0, 0.0).astype(BF)
    ahead = jnp.dot(both.astype(BF), strict, preferred_element_type=F32)
    number_first = jnp.sum(first, axis=1, keepdims=True)
    number_early = jnp.sum(early, axis=1, keepdims=True)
    number = jnp.sum(filled, axis=1, keepdims=True)
    place = jnp.where(past, number_first + ahead[1:2], number_early + ahead[2:3])
    place = jnp.where(past_u, ahead[0:1], place)
    place = jnp.where(filled > 0.5, place, -1.0)
    target = lax.broadcasted_iota(jnp.int32, (128, SLOTS), 0).astype(F32)
    moved = jnp.where(target == place, 1.0, 0.0).astype(BF)
    slot = lax.broadcasted_iota(jnp.int32, (8, SLOTS), 1).astype(F32)
    rows = jnp.where(kind == 0, slot, rows)
    table = lax.dot_general(rows.astype(BF), moved, dims, preferred_element_type=F32)
    spare = jnp.where(lane.astype(F32) >= number, float(TU + S), 0.0)
    table = table + jnp.where(quantity == 1, spare, 0.0)
    groups = jnp.floor((number + (AT_ONCE - 1.0)) / AT_ONCE)
    ends = []
    for count, least in ((number_first, U_GROUPS), (number_early, V_GROUPS)):
        enough = jnp.minimum(groups, float(least))
        needed = jnp.floor((count + (AT_ONCE - 1.0)) / AT_ONCE)
        ends.append(jnp.maximum(needed, enough))
    for row, end in enumerate((*ends, groups)):
        table = jnp.where(quantity == 5 + row, end, table)
    return table.astype(jnp.int32)


def image_kernel(
    head_in, off_u_in, off_v_in, base_in, pairs_in, track_in, data_in, own_screens,
    right_in, left_in,
    images, screens, listing, canvas, right, left,
    head, off_u, off_v, base, pairs, track, data, table, in_sems,
    packed, labels, got_data, got_labels, samples, spread, mult, raw, tall,
    own_sems, send_sems, recv_sems, y_send, y_recv, relay_send, relay_recv, c_send, c_recv,
):
    au, vert, band = (lax.axis_index(axis) for axis in ("au", "vert", "ch"))
    n_au, n_vert, n_ch = (lax.axis_size(axis) for axis in ("au", "vert", "ch"))
    here = own_screens.shape[0]
    unit = here // 32
    core = lax.rem(vert, 2)
    colour = lax.rem(vert // 2 + au, 2)
    mine = 16 * core + 10 * colour
    common = 16 * core + 6
    others = 16 * core + 10 * (1 - colour)

    def turned(step):
        return lax.rem(vert + step, n_vert)

    near = (
        {"au": lax.rem(au + 1, n_au)},
        {"au": lax.rem(au + n_au - 1, n_au)},
        {"vert": turned(1)},
        {"vert": turned(n_vert - 1)},
    )
    across = {"ch": lax.rem(band + 1, n_ch)}
    sibling = {"vert": vert + 1 - 2 * core}
    beside = {"vert": vert + 2 - 4 * lax.rem(vert // 2, 2)}
    along = {"au": au + 1 - 2 * lax.rem(au, 2)}

    inputs = (
        (head_in, head), (off_u_in, off_u), (off_v_in, off_v), (base_in, base),
        (pairs_in, pairs), (track_in, track), (data_in, data),
        (right_in, right), (left_in, left),
    )
    loads = [
        pltpu.make_async_copy(source, target, in_sems.at[j])
        for j, (source, target) in enumerate(inputs)
    ]
    for copy in loads:
        copy.start()
    fetches = []
    spans = ((mine, 6), (common, 4), (others, 6), (16 * (1 - core), 16))
    for j, (first, count) in enumerate(spans):
        rows = pl.ds(first * unit, count * unit)
        fetches.append(
            pltpu.make_async_copy(own_screens.at[rows], raw.at[rows], own_sems.at[j])
        )
        fetches[-1].start()
    barrier = pltpu.get_barrier_semaphore()
    for device in (*near, across, beside):
        pl.semaphore_signal(barrier, inc=1, device_id=device, device_id_type=MESH)

    def arrange(first, number):
        def one(pair, carry):
            for i in range(2):
                station = first * unit + 2 * pair + i
                planes = arrange_station(raw[station], tall.at[i])
                for r in range(2):
                    screens[station, r] = planes[r]
            return carry

        lax.fori_loop(0, number * unit // 2, one, 0)

    fetches[0].wait()
    arrange(mine, 6)
    fetches[1].wait()
    arrange(common, 4)
    pl.semaphore_wait(barrier, 6)

    def moves(i):
        pairs_of = ((packed, got_data, 8 * CAP), (labels, got_labels, CAP))
        for j, (source, target, rows) in enumerate(pairs_of):
            where = pl.ds((i + 1) * rows, rows)
            yield pltpu.make_async_remote_copy(
                src_ref=source.at[where],
                dst_ref=target.at[where],
                send_sem=send_sems.at[i, j],
                recv_sem=recv_sems.at[i, j],
                device_id=near[i],
                device_id_type=MESH,
            )

    def send(number, count, send_sem, recv_sem, device, own=False):
        where = number * unit
        return pltpu.make_async_remote_copy(
            src_ref=screens.at[pl.ds(where if own else here + where, count * unit)],
            dst_ref=screens.at[pl.ds(here + where, count * unit)],
            send_sem=send_sem,
            recv_sem=recv_sem,
            device_id=device,
            device_id_type=MESH,
        )

    runs = ((0, 2), (2, 2), (4, 1), (5, 1))

    def y_copy(k):
        first, count = (common, 4) if k == 4 else (mine + runs[k][0], runs[k][1])
        return send(first, count, y_send.at[k], y_recv.at[k], across, True)

    def relayed(k, first):
        device = beside if k % 2 == 0 else along
        start, count = runs[k]
        return send(first + start, count, relay_send.at[k], relay_recv.at[k], device)

    def c_copy(k, half):
        first = (
            half + 10 * colour, half + 6, half + 10 * (1 - colour), half + 10 * (1 - colour) + 4
        )[k]
        return send(first, (6, 4, 4, 2)[k], c_send.at[k], c_recv.at[k], sibling)

    for k in range(5):
        y_copy(k).start()

    for copy in loads[:7]:
        copy.wait()
    values, rows = pack_blocks(head, off_u, off_v, base, pairs, track, data)
    packed[...] = values
    labels[...] = rows

    for i in range(4):
        for copy in moves(i):
            copy.start()

    canvas[...] = jnp.zeros_like(canvas)
    for copy in fetches[2:]:
        copy.wait()
    arrange(others, 6)
    arrange(16 * (1 - core), 16)

    row = lax.broadcasted_iota(jnp.int32, (32, K), 0)
    channel = band * CH_DEV + lax.broadcasted_iota(jnp.int32, (32, K), 1) % CH_DEV
    ratio = 1.0 + channel.astype(F32) / jnp.float32(2 * CH_DEV * n_ch)
    coarse = row - 8
    coarse_u = 16 * (coarse % 4) + coarse // 4 - S // 2
    fine_v = row - 16
    coarse_v = (row - 24) * 8 - S // 2
    step = jnp.where(
        row < 16, jnp.where(row < 8, 2 * row, coarse_u), jnp.where(row < 24, fine_v, coarse_v)
    )
    mult[...] = step.astype(F32) / S * ratio

    def widen(rows):
        source = lax.broadcasted_iota(jnp.int32, (128, 2 * K), 0)
        column = lax.broadcasted_iota(jnp.int32, (128, 2 * K), 1)
        chosen = jnp.where(source == 8 + column // CH_DEV, 1.0, 0.0).astype(BF)
        lane = lax.broadcasted_iota(jnp.int32, rows.shape, 1)
        only = jnp.where(lane < 8, 0.0, rows).astype(BF)
        return jnp.dot(only, chosen, preferred_element_type=F32)

    got_labels[:CAP] = labels[:CAP]
    samples[: 8 * CAP] = packed[: 8 * CAP].astype(F32)
    spread[:CAP] = widen(labels[:CAP])

    half_lane = lax.broadcasted_iota(jnp.int32, (1, 128), 1)

    def block(slot):
        sample = samples[pl.ds(8 * slot, 8), :]
        track = spread[pl.ds(slot, 1), :]
        turns = jnp.concatenate(
            [track[:, :K] * mult[:16], track[:, K:] * mult[16:]], axis=0
        )
        frac = turns - jnp.floor(turns + 0.5)
        square = frac * frac
        cos = horner(COS_COEF, square)
        sin = horner(SIN_COEF, square) * frac

        def phasors(first):
            cos_fine, sin_fine = cos[first : first + 8], sin[first : first + 8]
            all_cos, all_sin = [], []
            for a in range(8):
                at = first + 8 + a
                cos_a, sin_a = cos[at : at + 1], sin[at : at + 1]
                all_cos.append(cos_fine * cos_a - sin_fine * sin_a)
                all_sin.append(sin_fine * cos_a + cos_fine * sin_a)
            return (
                jnp.concatenate(all_cos, axis=0).astype(BF),
                jnp.concatenate(all_sin, axis=0).astype(BF),
            )

        cos_u, sin_u = phasors(0)
        cos_v, sin_v = phasors(16)
        table = jnp.concatenate(
            [
                jnp.concatenate([cos_v, -sin_v], axis=1),
                jnp.concatenate([sin_v, cos_v], axis=1),
            ],
            axis=0,
        )

        def spread_row(r):
            row = jnp.broadcast_to(sample[r : r + 1], (16, K)).astype(BF)
            return jnp.concatenate([row] * (S // 16), axis=0)

        weighed = []
        for p in range(4):
            re, im = spread_row(2 * p), spread_row(2 * p + 1)
            weighed.append(
                jnp.concatenate([re * cos_u - im * sin_u, re * sin_u + im * cos_u], axis=1)
            )
        dims = (((1,), (1,)), ((), ()))
        image = lax.dot_general(
            jnp.concatenate(weighed, axis=0), table, dims, preferred_element_type=F32
        )
        planes = []
        for f in range(2):
            left_part = image[2 * f * S : (2 * f + 1) * S]
            right_part = image[(2 * f + 1) * S : (2 * f + 2) * S]
            planes.append(jnp.where(half_lane < S, left_part, swap_halves(right_part)))
            planes.append(jnp.where(half_lane < S, swap_halves(left_part), right_part))
        return jnp.concatenate(planes, axis=0).astype(BF)

    keep = pltpu.make_async_copy(table, listing, in_sems.at[9])
    here_half, other_half = 16 * core, 16 * (1 - core)

    def relay(stage):
        if stage < 3:
            for k in ((0,), (1,), (2, 3))[stage]:
                y_copy(k).wait_recv()
                relayed(k, mine).start()
            if stage == 2:
                c_copy(0, here_half).start()
        elif stage == 3:
            for k in (0, 1):
                relayed(k, others).wait_recv()
            c_copy(2, here_half).start()
        else:
            y_copy(4).wait_recv()
            c_copy(1, here_half).start()
            for k in (2, 3):
                relayed(k, others).wait_recv()
            c_copy(3, here_half).start()

    def loop(group, carry):
        @pl.when(group == CAP // IMAGES_AT_ONCE)
        def _():
            for i in range(4):
                for copy in moves(i):
                    copy.wait_recv()
            samples[8 * CAP :] = got_data[8 * CAP :].astype(F32)
            spread[CAP:] = widen(got_labels[CAP:])
            table[...] = list_blocks(got_labels[...])
            keep.start()

        for stage, at in enumerate(RELAY_AT):

            @pl.when(group == at)
            def _():
                relay(stage)

        made = [block(IMAGES_AT_ONCE * group + i) for i in range(IMAGES_AT_ONCE)]
        for i in range(IMAGES_AT_ONCE):
            images[IMAGES_AT_ONCE * group + i] = made[i]
        return carry

    lax.fori_loop(0, SLOTS // IMAGES_AT_ONCE, loop, 0)
    for copy in loads[7:]:
        copy.wait()
    keep.wait()
    for i in range(4):
        for copy in moves(i):
            copy.wait_send()
    for k in range(5):
        y_copy(k).wait_send()
    for k in range(4):
        relayed(k, mine).wait_send()
        c_copy(k, here_half).wait_send()
        c_copy(k, other_half).wait_recv()


def folded(x):
    middle = x.shape[1] // 2
    lane = lax.broadcasted_iota(jnp.int32, (1, 1, 128), 2)
    return jnp.where(lane < S, x[:, :middle], swap_halves(x[:, middle:])).astype(BF)


def edge_u_kernel(listing, images, screens, right, left, canvas_in, canvas, edge_u, corner):
    grid_blocks(images, screens, canvas, right, left, listing, 0, listing[5, 0])
    edge_u[...] = canvas[:, TU : TU + S, :TV].astype(BF)
    corner[...] = folded(canvas[:, TU : TU + S, TV:])


def edge_v_kernel(listing, images, screens, right, left, canvas_in, canvas, *edge_v):
    grid_blocks(images, screens, canvas, right, left, listing, listing[5, 0], listing[6, 0])
    each = 8 // V_SPLIT
    for i, edge in enumerate(edge_v):
        edge[...] = folded(canvas[i * each : (i + 1) * each, :TU, TV:])


def late_kernel(listing, images, screens, right, left, canvas_in, canvas):
    grid_blocks(images, screens, canvas, right, left, listing, listing[6, 0], listing[7, 0])


def grid_blocks(images, screens, canvas, right, left, listing, first, last):
    here = screens.shape[0] // 2
    band = lax.axis_index("ch")
    lane = lax.broadcasted_iota(jnp.int32, (1, 128), 1)

    def screen_place(station):
        owner = station // here
        local = station - owner * here
        return jnp.where(owner == band, local, here + local)

    def block(index):
        slot = listing[0, index]
        off_u = listing[1, index]
        off_v = listing[2, index]
        one = screen_place(listing[3, index])
        two = screen_place(listing[4, index])
        two_re, two_im = (screens[two, r].astype(F32) for r in range(2))
        one_re, one_im = (screens[one, r].astype(F32) for r in range(2))
        swapped_re, swapped_im = swap_halves(one_re), swap_halves(one_im)
        fixed = []
        for f in range(2):
            kept = (lane < S) if f == 0 else (lane >= S)
            feed_re = jnp.where(kept, one_re, swapped_re)
            feed_im = jnp.where(kept, one_im, swapped_im)
            gain_re = feed_re * two_re + feed_im * two_im
            gain_im = feed_im * two_re - feed_re * two_im
            image_re, image_im = (
                images[slot, (2 * f + r) * S : (2 * f + r + 1) * S].astype(F32)
                for r in range(2)
            )
            fixed.append(
                jnp.concatenate(
                    [
                        (image_re * gain_re - image_im * gain_im).astype(BF),
                        (image_re * gain_im + image_im * gain_re).astype(BF),
                    ],
                    axis=1,
                )
            )
        tile = off_v // 128
        shift = off_v - tile * 128
        moved = pltpu.roll(right[...], shift, 1).astype(BF)
        table_re, table_im = moved[:S], moved[S:]
        none = jnp.zeros_like(table_re)
        shifted = jnp.concatenate(
            [
                jnp.concatenate(row, axis=1)
                for row in (
                    (table_re, none, table_im, none),
                    (none, table_re, none, table_im),
                    (-table_im, none, table_re, none),
                    (none, -table_im, none, table_re),
                )
            ],
            axis=0,
        )
        half = jnp.dot(
            jnp.concatenate(fixed, axis=0), shifted, preferred_element_type=F32
        ).astype(BF)
        eighth = off_u // 8
        placed = left[off_u - eighth * 8]
        start_u = pl.multiple_of(eighth * 8, 8)
        start_v = pl.multiple_of(tile * 128, 128)
        return start_u, start_v, shift, placed, half

    def loop(group, carry):
        ready = [block(AT_ONCE * group + i) for i in range(AT_ONCE)]
        for start_u, start_v, shift, placed, half in ready:
            for f in range(2):
                part = half[f * S : (f + 1) * S]
                both = jnp.concatenate([part[:, :256], part[:, 256:]], axis=0)
                grid = jnp.dot(placed, both, preferred_element_type=F32)
                for e in range(2):
                    for r in range(2):
                        cells = grid[r * ROWS : (r + 1) * ROWS, 128 * e : 128 * (e + 1)]
                        cells = jnp.concatenate(
                            [
                                jnp.where(lane >= shift, cells, 0.0),
                                jnp.where(lane < shift, cells, 0.0),
                            ],
                            axis=1,
                        )
                        where = (
                            4 * f + 2 * e + r, pl.ds(start_u, ROWS), pl.ds(start_v, 256)
                        )
                        canvas[where] += cells
        return carry

    lax.fori_loop(first, last, loop, 0)


def lower_kernel(canvas, *refs):
    *got_v, out, top, side, sems = refs
    rest = pltpu.make_async_copy(
        canvas.at[:, S:TU, 128:TV], out.at[:, S:, 128:], sems.at[0]
    )
    rest.start()
    lane = lax.broadcasted_iota(jnp.int32, (1, 1, 128), 2)
    both = jnp.concatenate([x[...] for x in got_v], axis=0).astype(F32)
    low = jnp.where(lane < S, both, 0.0)
    high = jnp.where(lane < S, swap_halves(both), 0.0)
    side[:, : TU // 2 - S] = canvas[:, S : TU // 2, :128] + low[:, S:]
    side[:, TU // 2 - S :] = canvas[:, TU // 2 : TU, :128] + high
    store_side = pltpu.make_async_copy(side, out.at[:, S:, :128], sems.at[1])
    store_side.start()
    top[:, :, :128] = canvas[:, :S, :128] + low[:, :S]
    top[:, :, 128:] = canvas[:, :S, 128:TV]
    rest.wait()
    store_side.wait()


def upper_kernel(lower, top, got_u, got_c, out, rows, sems):
    lane = lax.broadcasted_iota(jnp.int32, (1, 1, 128), 2)
    stores = []
    for i in range(2):
        planes = slice(4 * i, 4 * i + 4)
        rows[planes] = top[planes] + got_u[planes].astype(F32)
        both = got_c[planes].astype(F32)
        rows[planes, : S // 2, :128] += jnp.where(lane < S, both, 0.0)
        rows[planes, S // 2 :, :128] += jnp.where(lane < S, swap_halves(both), 0.0)
        stores.append(
            pltpu.make_async_copy(rows.at[planes], out.at[planes, :S, :], sems.at[i])
        )
        stores[-1].start()
    for store in stores:
        store.wait()


def body(visibilities, tracks, offset_u, offset_v, heading, baseline, station_pair, screens):
    smem = pl.BlockSpec(memory_space=pltpu.SMEM)
    vmem = pl.BlockSpec(memory_space=pltpu.VMEM)
    hbm = pl.BlockSpec(memory_space=pltpu.HBM)
    n_au, n_vert = (lax.axis_size(axis) for axis in ("au", "vert"))
    here = screens.shape[0]
    canvas_shape = jax.ShapeDtypeStruct((8, TU + S + ROWS, TV + 128), F32)
    right_shape = jax.ShapeDtypeStruct((2 * S, 128), F32)
    left_shape = jax.ShapeDtypeStruct((8, 2 * ROWS, 2 * S), BF)
    dma = pltpu.SemaphoreType.DMA
    number = pltpu.VMEM((1, B_DEV), jnp.int32)
    images, all_screens, listing, canvas, right, left = pl.pallas_call(
        image_kernel,
        out_shape=(
            jax.ShapeDtypeStruct((SLOTS, 4 * S, 2 * S), BF),
            jax.ShapeDtypeStruct((2 * here, 2, S, 2 * S), BF),
            pltpu.SMEM((8, 128), jnp.int32),
            canvas_shape,
            right_shape,
            left_shape,
        ),
        in_specs=[hbm] * 10,
        out_specs=(vmem, vmem, smem, vmem, vmem, vmem),
        scratch_shapes=[
            number,
            number,
            number,
            number,
            pltpu.VMEM(station_pair.shape, jnp.int32),
            pltpu.VMEM((2 * TB, B_DEV), BF),
            pltpu.VMEM((8 * B_DEV, K), BF),
            pltpu.VMEM((8, 128), jnp.int32),
            dma((10,)),
            pltpu.VMEM((8 * SLOTS, K), BF),
            pltpu.VMEM((SLOTS, 128), F32),
            pltpu.VMEM((8 * SLOTS, K), BF),
            pltpu.VMEM((SLOTS, 128), F32),
            pltpu.VMEM((8 * SLOTS, K), F32),
            pltpu.VMEM((SLOTS, 2 * K), F32),
            pltpu.VMEM((32, K), F32),
            pltpu.VMEM((here, 4, S * S), BF),
            pltpu.VMEM((2, 4 * S, 128), F32),
            dma((4,)),
            dma((4, 2)),
            dma((4, 2)),
            dma((5,)),
            dma((5,)),
            dma((4,)),
            dma((4,)),
            dma((4,)),
            dma((4,)),
        ],
        compiler_params=pltpu.CompilerParams(
            collective_id=0, has_side_effects=True, vmem_limit_bytes=20 << 20
        ),
    )(*(pltpu.with_memory_space_constraint(x, pltpu.HBM) for x in (
        heading.reshape(1, B_DEV), offset_u[None], offset_v[None], baseline[None],
        station_pair, tracks.transpose(1, 2, 0).reshape(2 * TB, B_DEV),
        visibilities.reshape(8 * B_DEV, K), screens,
        jnp.asarray(right_table()), jnp.asarray(left_table()),
    )))

    def grid(kernel, canvas, flops, *edges):
        return pl.pallas_call(
            kernel,
            out_shape=(canvas_shape, *edges),
            in_specs=[smem] + [vmem] * 5,
            out_specs=(vmem,) * (1 + len(edges)),
            input_output_aliases={5: 0},
            compiler_params=pltpu.CompilerParams(vmem_limit_bytes=12 << 20),
            cost_estimate=pl.CostEstimate(
                flops=flops, bytes_accessed=1 << 20, transcendentals=0
            ),
        )(listing, images, all_screens, right, left, canvas)

    canvas, edge_u, corner = grid(
        edge_u_kernel,
        canvas,
        10**9,
        jax.ShapeDtypeStruct((8, S, TV), BF),
        jax.ShapeDtypeStruct((8, S // 2, 128), BF),
    )
    got_u = lax.ppermute(edge_u, "au", [(i, (i + 1) % n_au) for i in range(n_au)])
    diagonal = [
        (u * n_vert + v, (u + 1) % n_au * n_vert + (v + 1) % n_vert)
        for u in range(n_au)
        for v in range(n_vert)
    ]
    got_c = lax.ppermute(corner, ("au", "vert"), diagonal)
    canvas, *edge_v = grid(
        edge_v_kernel, canvas, 4 * 10**9, *[jax.ShapeDtypeStruct((8 // V_SPLIT, TU // 2, 128), BF)] * V_SPLIT
    )
    got_v = [
        lax.ppermute(x, "vert", [(i, (i + 1) % n_vert) for i in range(n_vert)]) for x in edge_v
    ]
    (canvas,) = grid(late_kernel, canvas, 10**6)
    tile = jax.ShapeDtypeStruct((8, TU, TV), F32)
    out, top = pl.pallas_call(
        lower_kernel,
        out_shape=(tile, jax.ShapeDtypeStruct((8, S, TV), F32)),
        in_specs=[vmem] * (1 + V_SPLIT),
        out_specs=(pl.BlockSpec(memory_space=pl.ANY), vmem),
        scratch_shapes=[pltpu.VMEM((8, TU - S, 128), F32), dma((2,))],
        compiler_params=pltpu.CompilerParams(vmem_limit_bytes=8 << 20),
    )(canvas, *got_v)
    out = pl.pallas_call(
        upper_kernel,
        out_shape=tile,
        in_specs=[pl.BlockSpec(memory_space=pl.ANY)] + [vmem] * 3,
        out_specs=pl.BlockSpec(memory_space=pl.ANY),
        scratch_shapes=[pltpu.VMEM((8, S, TV), F32), dma((2,))],
        input_output_aliases={0: 0},
        compiler_params=pltpu.CompilerParams(vmem_limit_bytes=8 << 20),
    )(out, top, got_u, got_c)
    return out[None]


def solution(mesh):
    placed = (
        P(("au", "vert"), None, "ch"),
        P(("au", "vert"), None, None),
        P(("au", "vert")),
        P(("au", "vert")),
        P(("au", "vert"), None),
        P(("au", "vert")),
        P(),
        P("ch", None, None),
    )
    return jax.shard_map(
        body, mesh=mesh, in_specs=placed, out_specs=P("ch", None, "au", "vert"), check_vma=False
    )
```

```python
import math

import jax
import jax.numpy as jnp
import ml_dtypes
import numpy as np
from jax import lax
from jax.experimental import pallas as pl
from jax.experimental.pallas import tpu as pltpu
from jax.sharding import PartitionSpec as P

S = 64
CH_DEV = 32
TB = 8
K = TB * CH_DEV
B_DEV = 32
CAP = B_DEV // 4
SLOTS = 5 * CAP
TU = 256
TV = 256
ROWS = 72
AT_ONCE = 5
U_GROUPS = 2
V_GROUPS = 3
V_SPLIT = 2
IMAGES_AT_ONCE = 8
RELAY_AT = (0, 1, 2, 4, 4)
MESH = pl.DeviceIdType.MESH
BF = jnp.bfloat16
F32 = jnp.float32


def series(values, degree):
    nodes = (np.cos(np.pi * (np.arange(400) + 0.5) / 400) + 1.0) * 0.125
    fitted = np.polynomial.chebyshev.Chebyshev.fit(nodes, values(nodes), degree, domain=[0, 0.25])
    return [float(c) for c in fitted.convert(kind=np.polynomial.Polynomial).coef]


COS_COEF = series(lambda q: np.cos(2 * np.pi * np.sqrt(q)), 5)
SIN_COEF = series(lambda q: np.sin(2 * np.pi * np.sqrt(q)) / np.sqrt(q), 5)


def horner(coefs, q):
    total = jnp.full_like(q, coefs[-1])
    for c in coefs[-2::-1]:
        total = total * q + jnp.float32(c)
    return total


def dft_tables():
    centred = np.arange(S) - S // 2
    product = (centred[:, None] * centred[None, :]) % S
    angles = np.float32(2.0 * math.pi / S) * product.astype(np.float32)
    scale = np.float32(1.0 / math.sqrt(S))
    re = (np.cos(angles) * scale).astype(ml_dtypes.bfloat16).astype(np.float32)
    im = (-np.sin(angles) * scale).astype(ml_dtypes.bfloat16).astype(np.float32)
    return re, im


def right_table():
    re, im = dft_tables()
    norm = np.float32(1.0 / math.sqrt(K))
    table = np.zeros((2 * S, 128), np.float32)
    table[:S, :S] = re.T * norm
    table[S:, :S] = im.T * norm
    return table


def left_table():
    re, im = dft_tables()
    order = np.concatenate([np.arange(0, S, 2), np.arange(1, S, 2)])
    re, im = re[:, order], im[:, order]
    table = np.zeros((8, 2, ROWS, 2 * S), np.float32)
    for shift in range(8):
        table[shift, 0, shift : shift + S, :S] = re
        table[shift, 0, shift : shift + S, S:] = -im
        table[shift, 1, shift : shift + S, :S] = im
        table[shift, 1, shift : shift + S, S:] = re
    return table.reshape(8, 2 * ROWS, 2 * S).astype(ml_dtypes.bfloat16)


def swap_halves(x):
    return pltpu.roll(x, S, x.ndim - 1)


def arrange_station(raw, tall):
    value = raw.astype(F32)
    for i in range(S // 2):
        tall[8 * i : 8 * i + 4, :] = value[:, 128 * i : 128 * (i + 1)]
    lane = lax.broadcasted_iota(jnp.int32, (S // 2, 128), 1)
    planes = []
    for r in range(2):
        first = tall[pl.ds(r, S // 2, stride=8), :]
        second = tall[pl.ds(2 + r, S // 2, stride=8), :]
        even = jnp.where(lane < S, first, swap_halves(second))
        odd = jnp.where(lane < S, swap_halves(first), second)
        planes.append(jnp.concatenate([even, odd], axis=0).astype(BF))
    return planes


def pack_blocks(head, off_u, off_v, base, pairs, track, data):
    heads = head[...]
    kind = lax.broadcasted_iota(jnp.int32, (8, B_DEV), 0)
    named = jnp.where(kind == heads, 1.0, 0.0)
    before = lax.broadcasted_iota(jnp.int32, (B_DEV, B_DEV), 0)
    after = lax.broadcasted_iota(jnp.int32, (B_DEV, B_DEV), 1)
    strict = jnp.where(before < after, 1.0, 0.0).astype(BF)
    counts = jnp.dot(named.astype(BF), strict, preferred_element_type=F32)
    rank = jnp.sum(named * counts, axis=0, keepdims=True)
    slot = heads.astype(F32) * CAP + rank
    which = lax.broadcasted_iota(jnp.int32, (SLOTS, B_DEV), 0).astype(F32)
    chosen = jnp.where(which == slot, 1.0, 0.0).astype(BF)

    label = lax.broadcasted_iota(jnp.int32, (pairs.shape[1], B_DEV), 0)
    listed = jnp.where(label == base[...], 1.0, 0.0).astype(BF)
    station = jnp.dot(pairs[...].astype(F32).astype(BF), listed, preferred_element_type=F32)
    rows = jnp.concatenate(
        [
            jnp.ones((1, B_DEV), F32),
            off_u[...].astype(F32),
            off_v[...].astype(F32),
            station,
            jnp.zeros((3, B_DEV), F32),
            track[...].astype(F32),
            jnp.zeros((128 - 8 - 2 * TB, B_DEV), F32),
        ],
        axis=0,
    ).astype(BF)
    dims = (((1,), (1,)), ((), ()))
    labels = lax.dot_general(chosen, rows, dims, preferred_element_type=F32)

    owner = lax.broadcasted_iota(jnp.int32, (B_DEV, 8 * B_DEV), 0)
    column = lax.broadcasted_iota(jnp.int32, (B_DEV, 8 * B_DEV), 1)
    widen = jnp.where(owner == column // 8, 1.0, 0.0).astype(BF)
    wide = jnp.dot(
        jnp.broadcast_to(slot, (8, B_DEV)).astype(BF), widen, preferred_element_type=F32
    )[:1]
    lane = lax.broadcasted_iota(jnp.int32, (1, 8 * B_DEV), 1) % 8
    place = wide * 8.0 + lane.astype(F32)
    target = lax.broadcasted_iota(jnp.int32, (8 * SLOTS, 8 * B_DEV), 0).astype(F32)
    moved = jnp.where(target == place, 1.0, 0.0).astype(BF)
    return jnp.dot(moved, data[...], preferred_element_type=F32).astype(BF), labels


def list_blocks(labels):
    dims = (((1,), (1,)), ((), ()))
    quantity = lax.broadcasted_iota(jnp.int32, (8, 128), 0)
    lane = lax.broadcasted_iota(jnp.int32, (8, 128), 1)
    pick = jnp.where(quantity == lane, 1.0, 0.0).astype(BF)
    rows = lax.dot_general(pick, labels.astype(BF), dims, preferred_element_type=F32)
    filled, at_u, at_v = rows[0:1], rows[1:2], rows[2:3]
    past_u = at_u > TU - S
    past = jnp.logical_or(past_u, at_v > TV - S)
    first = jnp.where(past_u, filled, 0.0)
    early = jnp.where(past, filled, 0.0)
    kind = lax.broadcasted_iota(jnp.int32, (8, SLOTS), 0)
    both = jnp.where(
        kind == 0,
        first,
        jnp.where(kind == 1, early - first, jnp.where(kind == 2, filled - early, 0.0)),
    )
    before = lax.broadcasted_iota(jnp.int32, (SLOTS, SLOTS), 0)
    after = lax.broadcasted_iota(jnp.int32, (SLOTS, SLOTS), 1)
    strict = jnp.where(before < after, 1.0, 0.0).astype(BF)
    ahead = jnp.dot(both.astype(BF), strict, preferred_element_type=F32)
    number_first = jnp.sum(first, axis=1, keepdims=True)
    number_early = jnp.sum(early, axis=1, keepdims=True)
    number = jnp.sum(filled, axis=1, keepdims=True)
    place = jnp.where(past, number_first + ahead[1:2], number_early + ahead[2:3])
    place = jnp.where(past_u, ahead[0:1], place)
    place = jnp.where(filled > 0.5, place, -1.0)
    target = lax.broadcasted_iota(jnp.int32, (128, SLOTS), 0).astype(F32)
    moved = jnp.where(target == place, 1.0, 0.0).astype(BF)
    slot = lax.broadcasted_iota(jnp.int32, (8, SLOTS), 1).astype(F32)
    rows = jnp.where(kind == 0, slot, rows)
    table = lax.dot_general(rows.astype(BF), moved, dims, preferred_element_type=F32)
    spare = jnp.where(lane.astype(F32) >= number, float(TU + S), 0.0)
    table = table + jnp.where(quantity == 1, spare, 0.0)
    groups = jnp.floor((number + (AT_ONCE - 0.5)) / AT_ONCE)
    ends = []
    for count, least in ((number_first, U_GROUPS), (number_early, V_GROUPS)):
        enough = jnp.minimum(groups, float(least))
        needed = jnp.floor((count + (AT_ONCE - 0.5)) / AT_ONCE)
        ends.append(jnp.maximum(needed, enough))
    for row, end in enumerate((*ends, groups)):
        table = jnp.where(quantity == 5 + row, end, table)
    return table.astype(jnp.int32)


def image_kernel(
    head_in, off_u_in, off_v_in, base_in, pairs_in, track_in, data_in, own_screens,
    right_in, left_in,
    images, screens, listing, canvas, right, left,
    head, off_u, off_v, base, pairs, track, data, table, in_sems,
    packed, labels, got_data, got_labels, samples, spread, mult, raw, tall,
    own_sems, send_sems, recv_sems, y_send, y_recv, relay_send, relay_recv, c_send, c_recv,
):
    au, vert, band = (lax.axis_index(axis) for axis in ("au", "vert", "ch"))
    n_au, n_vert, n_ch = (lax.axis_size(axis) for axis in ("au", "vert", "ch"))
    here = own_screens.shape[0]
    unit = here // 32
    core = lax.rem(vert, 2)
    colour = lax.rem(vert // 2 + au, 2)
    mine = 16 * core + 10 * colour
    common = 16 * core + 6
    others = 16 * core + 10 * (1 - colour)

    def turned(step):
        return lax.rem(vert + step, n_vert)

    near = (
        {"au": lax.rem(au + 1, n_au)},
        {"au": lax.rem(au + n_au - 1, n_au)},
        {"vert": turned(1)},
        {"vert": turned(n_vert - 1)},
    )
    across = {"ch": lax.rem(band + 1, n_ch)}
    sibling = {"vert": vert + 1 - 2 * core}
    beside = {"vert": vert + 2 - 4 * lax.rem(vert // 2, 2)}
    along = {"au": au + 1 - 2 * lax.rem(au, 2)}

    inputs = (
        (head_in, head), (off_u_in, off_u), (off_v_in, off_v), (base_in, base),
        (pairs_in, pairs), (track_in, track), (data_in, data),
        (right_in, right), (left_in, left),
    )
    loads = [
        pltpu.make_async_copy(source, target, in_sems.at[j])
        for j, (source, target) in enumerate(inputs)
    ]
    for copy in loads:
        copy.start()
    fetches = []
    spans = ((mine, 6), (common, 4), (others, 6), (16 * (1 - core), 16))
    for j, (first, count) in enumerate(spans):
        rows = pl.ds(first * unit, count * unit)
        fetches.append(
            pltpu.make_async_copy(own_screens.at[rows], raw.at[rows], own_sems.at[j])
        )
        fetches[-1].start()
    barrier = pltpu.get_barrier_semaphore()
    for device in (*near, across, beside):
        pl.semaphore_signal(barrier, inc=1, device_id=device, device_id_type=MESH)

    def arrange(first, number):
        def one(pair, carry):
            for i in range(2):
                station = first * unit + 2 * pair + i
                planes = arrange_station(raw[station], tall.at[i])
                for r in range(2):
                    screens[station, r] = planes[r]
            return carry

        lax.fori_loop(0, number * unit // 2, one, 0)

    fetches[0].wait()
    arrange(mine, 6)
    fetches[1].wait()
    arrange(common, 4)
    pl.semaphore_wait(barrier, 6)

    def moves(i):
        pairs_of = ((packed, got_data, 8 * CAP), (labels, got_labels, CAP))
        for j, (source, target, rows) in enumerate(pairs_of):
            where = pl.ds((i + 1) * rows, rows)
            yield pltpu.make_async_remote_copy(
                src_ref=source.at[where],
                dst_ref=target.at[where],
                send_sem=send_sems.at[i, j],
                recv_sem=recv_sems.at[i, j],
                device_id=near[i],
                device_id_type=MESH,
            )

    def send(number, count, send_sem, recv_sem, device, own=False):
        where = number * unit
        return pltpu.make_async_remote_copy(
            src_ref=screens.at[pl.ds(where if own else here + where, count * unit)],
            dst_ref=screens.at[pl.ds(here + where, count * unit)],
            send_sem=send_sem,
            recv_sem=recv_sem,
            device_id=device,
            device_id_type=MESH,
        )

    runs = ((0, 2), (2, 2), (4, 1), (5, 1))

    def y_copy(k):
        first, count = (common, 4) if k == 4 else (mine + runs[k][0], runs[k][1])
        return send(first, count, y_send.at[k], y_recv.at[k], across, True)

    def relayed(k, first):
        device = beside if k % 2 == 0 else along
        start, count = runs[k]
        return send(first + start, count, relay_send.at[k], relay_recv.at[k], device)

    def c_copy(k, half):
        first = (
            half + 10 * colour, half + 6, half + 10 * (1 - colour), half + 10 * (1 - colour) + 4
        )[k]
        return send(first, (6, 4, 4, 2)[k], c_send.at[k], c_recv.at[k], sibling)

    for k in range(5):
        y_copy(k).start()

    for copy in loads[:7]:
        copy.wait()
    values, rows = pack_blocks(head, off_u, off_v, base, pairs, track, data)
    packed[...] = values
    labels[...] = rows

    for i in range(4):
        for copy in moves(i):
            copy.start()

    canvas[...] = jnp.zeros_like(canvas)
    for copy in fetches[2:]:
        copy.wait()
    arrange(others, 6)
    arrange(16 * (1 - core), 16)

    row = lax.broadcasted_iota(jnp.int32, (32, K), 0)
    channel = band * CH_DEV + lax.broadcasted_iota(jnp.int32, (32, K), 1) % CH_DEV
    ratio = 1.0 + channel.astype(F32) / jnp.float32(2 * CH_DEV * n_ch)
    coarse = row - 8
    coarse_u = 16 * (coarse % 4) + coarse // 4 - S // 2
    fine_v = row - 16
    coarse_v = (row - 24) * 8 - S // 2
    step = jnp.where(
        row < 16, jnp.where(row < 8, 2 * row, coarse_u), jnp.where(row < 24, fine_v, coarse_v)
    )
    mult[...] = step.astype(F32) / S * ratio

    def widen(rows):
        source = lax.broadcasted_iota(jnp.int32, (128, 2 * K), 0)
        column = lax.broadcasted_iota(jnp.int32, (128, 2 * K), 1)
        chosen = jnp.where(source == 8 + column // CH_DEV, 1.0, 0.0).astype(BF)
        lane = lax.broadcasted_iota(jnp.int32, rows.shape, 1)
        only = jnp.where(lane < 8, 0.0, rows).astype(BF)
        return jnp.dot(only, chosen, preferred_element_type=F32)

    got_labels[:CAP] = labels[:CAP]
    samples[: 8 * CAP] = packed[: 8 * CAP].astype(F32)
    spread[:CAP] = widen(labels[:CAP])

    half_lane = lax.broadcasted_iota(jnp.int32, (1, 128), 1)

    def block(slot):
        sample = samples[pl.ds(8 * slot, 8), :]
        track = spread[pl.ds(slot, 1), :]
        turns = jnp.concatenate(
            [track[:, :K] * mult[:16], track[:, K:] * mult[16:]], axis=0
        )
        frac = turns - jnp.floor(turns + 0.5)
        square = frac * frac
        cos = horner(COS_COEF, square)
        sin = horner(SIN_COEF, square) * frac

        def phasors(first):
            cos_fine, sin_fine = cos[first : first + 8], sin[first : first + 8]
            all_cos, all_sin = [], []
            for a in range(8):
                at = first + 8 + a
                cos_a, sin_a = cos[at : at + 1], sin[at : at + 1]
                all_cos.append(cos_fine * cos_a - sin_fine * sin_a)
                all_sin.append(sin_fine * cos_a + cos_fine * sin_a)
            return (
                jnp.concatenate(all_cos, axis=0).astype(BF),
                jnp.concatenate(all_sin, axis=0).astype(BF),
            )

        cos_u, sin_u = phasors(0)
        cos_v, sin_v = phasors(16)
        table = jnp.concatenate(
            [
                jnp.concatenate([cos_v, -sin_v], axis=1),
                jnp.concatenate([sin_v, cos_v], axis=1),
            ],
            axis=0,
        )

        def spread_row(r):
            row = jnp.broadcast_to(sample[r : r + 1], (16, K)).astype(BF)
            return jnp.concatenate([row] * (S // 16), axis=0)

        weighed = []
        for p in range(4):
            re, im = spread_row(2 * p), spread_row(2 * p + 1)
            weighed.append(
                jnp.concatenate([re * cos_u - im * sin_u, re * sin_u + im * cos_u], axis=1)
            )
        dims = (((1,), (1,)), ((), ()))
        image = lax.dot_general(
            jnp.concatenate(weighed, axis=0), table, dims, preferred_element_type=F32
        )
        planes = []
        for f in range(2):
            left_part = image[2 * f * S : (2 * f + 1) * S]
            right_part = image[(2 * f + 1) * S : (2 * f + 2) * S]
            planes.append(jnp.where(half_lane < S, left_part, swap_halves(right_part)))
            planes.append(jnp.where(half_lane < S, swap_halves(left_part), right_part))
        return jnp.concatenate(planes, axis=0).astype(BF)

    keep = pltpu.make_async_copy(table, listing, in_sems.at[9])
    here_half, other_half = 16 * core, 16 * (1 - core)

    def relay(stage):
        if stage < 3:
            for k in ((0,), (1,), (2, 3))[stage]:
                y_copy(k).wait_recv()
                relayed(k, mine).start()
            if stage == 2:
                c_copy(0, here_half).start()
        elif stage == 3:
            for k in (0, 1):
                relayed(k, others).wait_recv()
            c_copy(2, here_half).start()
        else:
            y_copy(4).wait_recv()
            c_copy(1, here_half).start()
            for k in (2, 3):
                relayed(k, others).wait_recv()
            c_copy(3, here_half).start()

    def loop(group, carry):
        @pl.when(group == CAP // IMAGES_AT_ONCE)
        def _():
            for i in range(4):
                for copy in moves(i):
                    copy.wait_recv()
            samples[8 * CAP :] = got_data[8 * CAP :].astype(F32)
            spread[CAP:] = widen(got_labels[CAP:])
            table[...] = list_blocks(got_labels[...])
            keep.start()

        for stage, at in enumerate(RELAY_AT):

            @pl.when(group == at)
            def _():
                relay(stage)

        made = [block(IMAGES_AT_ONCE * group + i) for i in range(IMAGES_AT_ONCE)]
        for i in range(IMAGES_AT_ONCE):
            images[IMAGES_AT_ONCE * group + i] = made[i]
        return carry

    lax.fori_loop(0, SLOTS // IMAGES_AT_ONCE, loop, 0)
    for copy in loads[7:]:
        copy.wait()
    keep.wait()
    for i in range(4):
        for copy in moves(i):
            copy.wait_send()
    for k in range(5):
        y_copy(k).wait_send()
    for k in range(4):
        relayed(k, mine).wait_send()
        c_copy(k, here_half).wait_send()
        c_copy(k, other_half).wait_recv()


def folded(x):
    middle = x.shape[1] // 2
    lane = lax.broadcasted_iota(jnp.int32, (1, 1, 128), 2)
    return jnp.where(lane < S, x[:, :middle], swap_halves(x[:, middle:])).astype(BF)


def edge_u_kernel(listing, images, screens, right, left, canvas_in, canvas, edge_u, corner):
    grid_blocks(images, screens, canvas, right, left, listing, 0, listing[5, 0])
    edge_u[...] = canvas[:, TU : TU + S, :TV].astype(BF)
    corner[...] = folded(canvas[:, TU : TU + S, TV:])


def edge_v_kernel(listing, images, screens, right, left, canvas_in, canvas, *edge_v):
    grid_blocks(images, screens, canvas, right, left, listing, listing[5, 0], listing[6, 0])
    each = 8 // V_SPLIT
    for i, edge in enumerate(edge_v):
        edge[...] = folded(canvas[i * each : (i + 1) * each, :TU, TV:])


def late_kernel(listing, images, screens, right, left, canvas_in, canvas):
    grid_blocks(images, screens, canvas, right, left, listing, listing[6, 0], listing[7, 0])


def grid_blocks(images, screens, canvas, right, left, listing, first, last):
    here = screens.shape[0] // 2
    band = lax.axis_index("ch")
    lane = lax.broadcasted_iota(jnp.int32, (1, 128), 1)

    def screen_place(station):
        owner = station // here
        local = station - owner * here
        return jnp.where(owner == band, local, here + local)

    def block(index):
        slot = listing[0, index]
        off_u = listing[1, index]
        off_v = listing[2, index]
        one = screen_place(listing[3, index])
        two = screen_place(listing[4, index])
        two_re, two_im = (screens[two, r].astype(F32) for r in range(2))
        one_re, one_im = (screens[one, r].astype(F32) for r in range(2))
        swapped_re, swapped_im = swap_halves(one_re), swap_halves(one_im)
        fixed = []
        for f in range(2):
            kept = (lane < S) if f == 0 else (lane >= S)
            feed_re = jnp.where(kept, one_re, swapped_re)
            feed_im = jnp.where(kept, one_im, swapped_im)
            gain_re = feed_re * two_re + feed_im * two_im
            gain_im = feed_im * two_re - feed_re * two_im
            image_re, image_im = (
                images[slot, (2 * f + r) * S : (2 * f + r + 1) * S].astype(F32)
                for r in range(2)
            )
            fixed.append(
                jnp.concatenate(
                    [
                        (image_re * gain_re - image_im * gain_im).astype(BF),
                        (image_re * gain_im + image_im * gain_re).astype(BF),
                    ],
                    axis=1,
                )
            )
        tile = off_v // 128
        shift = off_v - tile * 128
        moved = pltpu.roll(right[...], shift, 1).astype(BF)
        table_re, table_im = moved[:S], moved[S:]
        none = jnp.zeros_like(table_re)
        shifted = jnp.concatenate(
            [
                jnp.concatenate(row, axis=1)
                for row in (
                    (table_re, none, table_im, none),
                    (none, table_re, none, table_im),
                    (-table_im, none, table_re, none),
                    (none, -table_im, none, table_re),
                )
            ],
            axis=0,
        )
        half = jnp.dot(
            jnp.concatenate(fixed, axis=0), shifted, preferred_element_type=F32
        ).astype(BF)
        eighth = off_u // 8
        placed = left[off_u - eighth * 8]
        start_u = pl.multiple_of(eighth * 8, 8)
        start_v = pl.multiple_of(tile * 128, 128)
        return start_u, start_v, shift, placed, half

    def loop(group, carry):
        ready = [block(AT_ONCE * group + i) for i in range(AT_ONCE)]
        for start_u, start_v, shift, placed, half in ready:
            for f in range(2):
                part = half[f * S : (f + 1) * S]
                both = jnp.concatenate([part[:, :256], part[:, 256:]], axis=0)
                grid = jnp.dot(placed, both, preferred_element_type=F32)
                for e in range(2):
                    for r in range(2):
                        cells = grid[r * ROWS : (r + 1) * ROWS, 128 * e : 128 * (e + 1)]
                        cells = jnp.concatenate(
                            [
                                jnp.where(lane >= shift, cells, 0.0),
                                jnp.where(lane < shift, cells, 0.0),
                            ],
                            axis=1,
                        )
                        where = (
                            4 * f + 2 * e + r, pl.ds(start_u, ROWS), pl.ds(start_v, 256)
                        )
                        canvas[where] += cells
        return carry

    lax.fori_loop(first, last, loop, 0)


def lower_kernel(canvas, *refs):
    *got_v, out, top, side, sems = refs
    rest = pltpu.make_async_copy(
        canvas.at[:, S:TU, 128:TV], out.at[:, S:, 128:], sems.at[0]
    )
    rest.start()
    lane = lax.broadcasted_iota(jnp.int32, (1, 1, 128), 2)
    both = jnp.concatenate([x[...] for x in got_v], axis=0).astype(F32)
    low = jnp.where(lane < S, both, 0.0)
    high = jnp.where(lane < S, swap_halves(both), 0.0)
    side[:, : TU // 2 - S] = canvas[:, S : TU // 2, :128] + low[:, S:]
    side[:, TU // 2 - S :] = canvas[:, TU // 2 : TU, :128] + high
    store_side = pltpu.make_async_copy(side, out.at[:, S:, :128], sems.at[1])
    store_side.start()
    top[:, :, :128] = canvas[:, :S, :128] + low[:, :S]
    top[:, :, 128:] = canvas[:, :S, 128:TV]
    rest.wait()
    store_side.wait()


def upper_kernel(lower, top, got_u, got_c, out, rows, sems):
    lane = lax.broadcasted_iota(jnp.int32, (1, 1, 128), 2)
    stores = []
    for i in range(2):
        planes = slice(4 * i, 4 * i + 4)
        rows[planes] = top[planes] + got_u[planes].astype(F32)
        both = got_c[planes].astype(F32)
        rows[planes, : S // 2, :128] += jnp.where(lane < S, both, 0.0)
        rows[planes, S // 2 :, :128] += jnp.where(lane < S, swap_halves(both), 0.0)
        stores.append(
            pltpu.make_async_copy(rows.at[planes], out.at[planes, :S, :], sems.at[i])
        )
        stores[-1].start()
    for store in stores:
        store.wait()


def body(visibilities, tracks, offset_u, offset_v, heading, baseline, station_pair, screens):
    smem = pl.BlockSpec(memory_space=pltpu.SMEM)
    vmem = pl.BlockSpec(memory_space=pltpu.VMEM)
    hbm = pl.BlockSpec(memory_space=pltpu.HBM)
    n_au, n_vert = (lax.axis_size(axis) for axis in ("au", "vert"))
    here = screens.shape[0]
    canvas_shape = jax.ShapeDtypeStruct((8, TU + S + ROWS, TV + 128), F32)
    right_shape = jax.ShapeDtypeStruct((2 * S, 128), F32)
    left_shape = jax.ShapeDtypeStruct((8, 2 * ROWS, 2 * S), BF)
    dma = pltpu.SemaphoreType.DMA
    number = pltpu.VMEM((1, B_DEV), jnp.int32)
    images, all_screens, listing, canvas, right, left = pl.pallas_call(
        image_kernel,
        out_shape=(
            jax.ShapeDtypeStruct((SLOTS, 4 * S, 2 * S), BF),
            jax.ShapeDtypeStruct((2 * here, 2, S, 2 * S), BF),
            pltpu.SMEM((8, 128), jnp.int32),
            canvas_shape,
            right_shape,
            left_shape,
        ),
        in_specs=[hbm] * 10,
        out_specs=(vmem, vmem, smem, vmem, vmem, vmem),
        scratch_shapes=[
            number,
            number,
            number,
            number,
            pltpu.VMEM(station_pair.shape, jnp.int32),
            pltpu.VMEM((2 * TB, B_DEV), BF),
            pltpu.VMEM((8 * B_DEV, K), BF),
            pltpu.VMEM((8, 128), jnp.int32),
            dma((10,)),
            pltpu.VMEM((8 * SLOTS, K), BF),
            pltpu.VMEM((SLOTS, 128), F32),
            pltpu.VMEM((8 * SLOTS, K), BF),
            pltpu.VMEM((SLOTS, 128), F32),
            pltpu.VMEM((8 * SLOTS, K), F32),
            pltpu.VMEM((SLOTS, 2 * K), F32),
            pltpu.VMEM((32, K), F32),
            pltpu.VMEM((here, 4, S * S), BF),
            pltpu.VMEM((2, 4 * S, 128), F32),
            dma((4,)),
            dma((4, 2)),
            dma((4, 2)),
            dma((5,)),
            dma((5,)),
            dma((4,)),
            dma((4,)),
            dma((4,)),
            dma((4,)),
        ],
        compiler_params=pltpu.CompilerParams(
            collective_id=0, has_side_effects=True, vmem_limit_bytes=20 << 20
        ),
    )(*(pltpu.with_memory_space_constraint(x, pltpu.HBM) for x in (
        heading.reshape(1, B_DEV), offset_u[None], offset_v[None], baseline[None],
        station_pair, tracks.transpose(1, 2, 0).reshape(2 * TB, B_DEV),
        visibilities.reshape(8 * B_DEV, K), screens,
        jnp.asarray(right_table()), jnp.asarray(left_table()),
    )))

    def grid(kernel, canvas, flops, *edges):
        return pl.pallas_call(
            kernel,
            out_shape=(canvas_shape, *edges),
            in_specs=[smem] + [vmem] * 5,
            out_specs=(vmem,) * (1 + len(edges)),
            input_output_aliases={5: 0},
            compiler_params=pltpu.CompilerParams(vmem_limit_bytes=12 << 20),
            cost_estimate=pl.CostEstimate(
                flops=flops, bytes_accessed=1 << 20, transcendentals=0
            ),
        )(listing, images, all_screens, right, left, canvas)

    canvas, edge_u, corner = grid(
        edge_u_kernel,
        canvas,
        10**9,
        jax.ShapeDtypeStruct((8, S, TV), BF),
        jax.ShapeDtypeStruct((8, S // 2, 128), BF),
    )
    got_u = lax.ppermute(edge_u, "au", [(i, (i + 1) % n_au) for i in range(n_au)])
    diagonal = [
        (u * n_vert + v, (u + 1) % n_au * n_vert + (v + 1) % n_vert)
        for u in range(n_au)
        for v in range(n_vert)
    ]
    got_c = lax.ppermute(corner, ("au", "vert"), diagonal)
    canvas, *edge_v = grid(
        edge_v_kernel, canvas, 4 * 10**9, *[jax.ShapeDtypeStruct((8 // V_SPLIT, TU // 2, 128), BF)] * V_SPLIT
    )
    got_v = [
        lax.ppermute(x, "vert", [(i, (i + 1) % n_vert) for i in range(n_vert)]) for x in edge_v
    ]
    (canvas,) = grid(late_kernel, canvas, 10**6)
    tile = jax.ShapeDtypeStruct((8, TU, TV), F32)
    out, top = pl.pallas_call(
        lower_kernel,
        out_shape=(tile, jax.ShapeDtypeStruct((8, S, TV), F32)),
        in_specs=[vmem] * (1 + V_SPLIT),
        out_specs=(pl.BlockSpec(memory_space=pl.ANY), vmem),
        scratch_shapes=[pltpu.VMEM((8, TU - S, 128), F32), dma((2,))],
        compiler_params=pltpu.CompilerParams(vmem_limit_bytes=8 << 20),
    )(canvas, *got_v)
    out = pl.pallas_call(
        upper_kernel,
        out_shape=tile,
        in_specs=[pl.BlockSpec(memory_space=pl.ANY)] + [vmem] * 3,
        out_specs=pl.BlockSpec(memory_space=pl.ANY),
        scratch_shapes=[pltpu.VMEM((8, S, TV), F32), dma((2,))],
        input_output_aliases={0: 0},
        compiler_params=pltpu.CompilerParams(vmem_limit_bytes=8 << 20),
    )(out, top, got_u, got_c)
    return out[None]


def solution(mesh):
    placed = (
        P(("au", "vert"), None, "ch"),
        P(("au", "vert"), None, None),
        P(("au", "vert")),
        P(("au", "vert")),
        P(("au", "vert"), None),
        P(("au", "vert")),
        P(),
        P("ch", None, None),
    )
    return jax.shard_map(
        body, mesh=mesh, in_specs=placed, out_specs=P("ch", None, "au", "vert"), check_vma=False
    )
```
